32 devices in a mesh: dp: 8 (over y, x, core), mp: 4 (over z).
Axes of the slice: x: 2, y: 2, z: 4, core: 2. Of those that a mesh axis runs over, the one named last changes fastest.
Arguments:
- tokens: bfloat16 [8, 1024, 2048], P('dp', 'mp'), may hold values from -6 to 6
- mixed_grad: bfloat16 [8, 1024, 2048], P('dp', 'mp'), may hold values from -6 to 6
- doc_ids: int32 [8, 1024], P('dp'), may hold values from 0 to 7, never falling along the last dimension, each value on 1 to 512 neighbouring positions
- head_count: int32 [8, 1024], P('dp'), may hold values from 1 to 16
- width_bucket: int32 [8, 1024], P('dp'), may hold values from 0 to 3
- first_gain: float32 [2048], replicated, may hold values from 0.5 to 1.5
- first_shift: float32 [2048], replicated, may hold values from -3 to 3
- query_weight: bfloat16 [2048, 2048], P(None, 'mp'), may hold values from -0.125 to 0.125
- key_weight: bfloat16 [2048, 2048], P(None, 'mp'), may hold values from -0.125 to 0.125
- value_weight: bfloat16 [2048, 2048], P(None, 'mp'), may hold values from -0.125 to 0.125
- output_weight: bfloat16 [2048, 2048], P(None, 'mp'), may hold values from -0.375 to 0.375
- second_gain: float32 [2048], replicated, may hold values from 0.5 to 1.5
- second_shift: float32 [2048], replicated, may hold values from -3 to 3
- up_weight: bfloat16 [2048, 8192], P(None, 'mp'), may hold values from -0.125 to 0.125
- down_weight: bfloat16 [2048, 8192], P(None, 'mp'), may hold values from -0.0625 to 0.0625
Outputs:
- mixed: bfloat16 [8, 1024, 2048], P('dp', 'mp')
- input_grad: bfloat16 [8, 1024, 2048], P('dp', 'mp')
- first_gain_grad: float32 [2048], replicated
- first_shift_grad: float32 [2048], replicated
- query_grad: float32 [2048, 2048], P('dp', 'mp')
- key_grad: float32 [2048, 2048], P('dp', 'mp')
- value_grad: float32 [2048, 2048], P('dp', 'mp')
- output_grad: float32 [2048, 2048], P('dp', 'mp')
- second_gain_grad: float32 [2048], replicated
- second_shift_grad: float32 [2048], replicated
- up_grad: float32 [2048, 8192], P('dp', 'mp')
- down_grad: float32 [2048, 8192], P('dp', 'mp')
- bucket_tally: int32 [4], replicated
- head_tally: int32 [16], replicated
The draws below stay inside these ranges and needn't reach their ends.
Inputs may be any that keep to these rules, and one draw needn't show every extreme that they name: `doc_ids`: within each sequence, document numbers never fall; a document has 1 to 512 tokens.
All inputs are finite; a program needn't handle non-finite values.
Results may differ from the reference program's by a relative error of at most 0.023.
Values may be sent and summed in bfloat16 or wider, within the bound.
No kernel may reach another device: no remote copies, remote signals or barrier semaphores. Data moves between devices by JAX's collectives and lax.ppermute only.
A program may use at most 192 MiB of HBM per device.

```python
import math
import jax
import jax.numpy as jnp
import numpy as np
from jax import lax

D = 2048
HEADS = 16
E = 128
FF = 8192
SEQ = 1024
SEQS = 8
N_MP = 4


def touch_ends(drawn, rng, least, top_value):
    longest = drawn.shape.index(max(drawn.shape))
    spots = []
    for shift in (0, 1):
        where = [jax.random.randint(jax.random.fold_in(rng, axis), (), 0, length) for axis, length in enumerate(drawn.shape)]
        where[longest] = (where[longest] + shift) % drawn.shape[longest]
        spots.append(tuple(where))
    return drawn.at[spots[0]].set(least).at[spots[1]].set(top_value)


def block_levels(key, shape, pieces, low, top_value):
    level, own = 1.0, jax.random.fold_in(key, 6)
    for axis_at, shards_of in pieces:
        heights = jnp.exp(jax.random.uniform(jax.random.fold_in(own, axis_at), (shards_of,), jnp.float32, low / len(pieces), top_value / len(pieces)))
        level = level * jnp.repeat(heights, shape[axis_at] // shards_of).reshape([-1 if axis == axis_at else 1 for axis in range(len(shape))])
    return level


def profile(amount, total, reach, lean):
    portions = [(1 << 20) // math.isqrt(grade ** lean) + 1 for grade in range(2, amount + 1)]
    spare, given = total - reach - (amount - 1), [1] * (amount - 1)
    while spare > 0:
        candidates = [i for i in range(amount - 1) if given[i] < reach]
        pool, left = sum([portions[i] for i in candidates]), spare
        for i in candidates:
            more = min(reach - given[i], max(1, left * portions[i] // pool), spare)
            given[i] = given[i] + more
            spare = spare - more
    return np.array([reach] + given)


def uneven_parts(key, count, total, bound, skew):
    if count == 2:
        one = jax.random.randint(key, (), max(1, total - bound), min(bound, total - 1) + 1)
        return jnp.stack([one, total - one])
    lengths = jnp.asarray(profile(count, total, bound, skew), jnp.int32)
    twos = (count - 1) // 2
    source_of, receiver = lengths[1:1 + 2 * twos:2], lengths[2:2 + 2 * twos:2]
    margin = jnp.minimum(source_of - 1, bound - receiver)
    moved = jax.random.randint(jax.random.fold_in(key, 1), (twos,), 0, 1 << 20) % (margin + 1)
    lengths = lengths.at[1:1 + 2 * twos:2].set(source_of - moved).at[2:2 + 2 * twos:2].set(receiver + moved)
    return lengths[jax.random.permutation(jax.random.fold_in(key, 2), count)]


def normal_values(own_key, dims, deviation, limit, cuts=(), kind=jnp.bfloat16):
    level = block_levels(own_key, dims, cuts, -0.22, 0.18) if cuts else 1.0
    drawn = jax.random.normal(own_key, dims, jnp.float32) * deviation * level
    return jnp.minimum(jnp.maximum(drawn, -limit), limit).astype(kind)


def setup_inputs(seed: int = 0) -> dict:
    key_list = jax.random.split(jax.random.key(seed), 16)
    return {
        "tokens": normal_values(key_list[0], (SEQS, SEQ, D), 1.0, 6.0, ((0, 8), (1, 4))),
        "mixed_grad": normal_values(key_list[1], (SEQS, SEQ, D), 1.0, 6.0, ((0, 8), (1, 4))),
        "doc_ids": jax.vmap(lambda own: jnp.searchsorted(jnp.cumsum(uneven_parts(own, 8, SEQ, SEQ // 2, 2)), jnp.arange(SEQ), side="right"))(jax.random.split(key_list[2], SEQS)).reshape((SEQS, SEQ)).astype(jnp.int32),
        "head_count": touch_ends(jax.random.randint(key_list[3], (SEQS, SEQ), 1, HEADS + 1), jax.random.fold_in(key_list[3], 1), 1, HEADS).astype(jnp.int32),
        "width_bucket": touch_ends(jax.random.randint(key_list[4], (SEQS, SEQ), 0, 4), jax.random.fold_in(key_list[4], 1), 0, 3).astype(jnp.int32),
        "first_gain": jnp.clip(1.0 + 0.1 * jax.random.normal(key_list[5], (D,), jnp.float32), 0.5, 1.5),
        "first_shift": normal_values(key_list[6], (D,), 0.5, 3.0, (), jnp.float32),
        "query_weight": normal_values(key_list[7], (D, D), D ** -0.5, 0.125, ((1, 4),)),
        "key_weight": normal_values(key_list[8], (D, D), D ** -0.5, 0.125, ((1, 4),)),
        "value_weight": normal_values(key_list[9], (D, D), D ** -0.5, 0.125, ((1, 4),)),
        "output_weight": normal_values(key_list[10], (D, D), (D // 8) ** -0.5, 0.375, ((1, 4),)),
        "second_gain": jnp.clip(1.0 + 0.1 * jax.random.normal(key_list[11], (D,), jnp.float32), 0.5, 1.5),
        "second_shift": normal_values(key_list[12], (D,), 0.5, 3.0, (), jnp.float32),
        "up_weight": normal_values(key_list[13], (D, FF), D ** -0.5, 0.125, ((1, 4),)),
        "down_weight": normal_values(key_list[14], (D, FF), FF ** -0.5, 0.0625, ((1, 4),)),
    }


EPS = 1e-05

@jax.custom_vjp
def low(v):
    return lax.optimization_barrier(v.astype(jnp.bfloat16)).astype(jnp.float32)

@jax.custom_vjp
def low_back(v):
    return v

def low_keep(v):
    return (low(v), None)

def low_pass(kept, grad):
    return (grad,)

def back_keep(v):
    return (v, None)

def back_low(kept, grad):
    return (low(grad),)
low.defvjp(low_keep, low_pass)
low_back.defvjp(back_keep, back_low)

def layer_norm(values, gain, shift):
    mean = lax.optimization_barrier(jnp.mean(values, axis=-1, keepdims=True))
    cent = values - mean
    var = lax.optimization_barrier(jnp.mean(cent * cent, axis=-1, keepdims=True))
    return cent * lax.rsqrt(var + EPS) * gain + shift

def rotary_tables(length, size):
    half = size // 2
    freq = 10000.0 ** (-(jnp.arange(half, dtype=jnp.float32) * 2.0 / size))
    angle = jnp.arange(length, dtype=jnp.float32)[:, None] * freq[None, :]
    return (jnp.cos(angle)[:, None, :], jnp.sin(angle)[:, None, :])

def rotate(values, cosine, sine):
    half = values.shape[-1] // 2
    first = values[..., :half]
    second = values[..., half:]
    return jnp.concatenate([first * cosine - second * sine, second * cosine + first * sine], axis=-1)

def attention(query, keys, vals, docs):
    length = query.shape[0]
    span = min(512, length)
    blocks = length // span
    positions = jnp.arange(length, dtype=jnp.int32)
    scale = E ** (-0.5)

    def block(item):
        q_blk, q_pos, q_doc = item
        scores = jnp.einsum('qhe,khe->hqk', q_blk, keys, precision=lax.Precision.HIGHEST) * scale
        scores = low_back(scores)
        allowed = (positions[None, :] <= q_pos[:, None]) & (docs[None, :] == q_doc[:, None])
        scores = jnp.where(allowed[None], scores, -1e+30)
        prob = low(jax.nn.softmax(scores, axis=-1))
        return jnp.einsum('hqk,khe->qhe', prob, vals, precision=lax.Precision.HIGHEST)
    outs = lax.map(jax.checkpoint(block), (query.reshape(blocks, span, HEADS, E), positions.reshape(blocks, span), docs.reshape(blocks, span)))
    return outs.reshape(length, HEADS, E)

def forward_seq(seq_x, params, docs, heads, bucket, cosine, sine):
    gain_one, shift_one, wquery, wkey, wvalue, wout, gain_two, shift_two, wup, wdown = params
    length = seq_x.shape[0]
    groups = N_MP
    local = D // groups
    hidden = FF // groups
    high = lax.Precision.HIGHEST
    normed_one = low(layer_norm(seq_x, gain_one, shift_one))
    copies_one = low_back(jnp.broadcast_to(normed_one, (groups, length, D)))

    def project(matrix):
        return jnp.einsum('gtd,dgc->tgc', copies_one, matrix.reshape(D, groups, local), precision=high).reshape(length, HEADS, E)
    q_lin = low_back(project(wquery))
    k_lin = low_back(project(wkey))
    vals = low(low_back(project(wvalue)))
    query = low(rotate(q_lin, cosine, sine))
    keys = low(rotate(k_lin, cosine, sine))
    attended = attention(query, keys, vals, docs)
    head_mask = (jnp.arange(HEADS, dtype=jnp.int32)[None, :] < heads[:, None]).astype(jnp.float32)
    masked = low(low_back(attended * head_mask[:, :, None])).reshape(length, groups, local)
    terms = low(jnp.einsum('tgc,dgc->gtd', masked, wout.reshape(D, groups, local), precision=high))
    state = seq_x + low_back(lax.optimization_barrier(jnp.sum(terms, axis=0)))
    normed_two = low(layer_norm(state, gain_two, shift_two))
    copies_two = low_back(jnp.broadcast_to(normed_two, (groups, length, D)))
    upper = jnp.einsum('gtd,dgc->tgc', copies_two, wup.reshape(D, groups, hidden), precision=high).reshape(length, FF)
    upper = low_back(upper)
    width_mask = (jnp.arange(FF, dtype=jnp.int32)[None, :] < (bucket[:, None] + 1) * (FF // 4)).astype(jnp.float32)
    active = low(low_back(jnp.square(jax.nn.relu(upper)) * width_mask)).reshape(length, groups, hidden)
    terms_two = low(jnp.einsum('tgc,dgc->gtd', active, wdown.reshape(D, groups, hidden), precision=high))
    return state + lax.optimization_barrier(jnp.sum(terms_two, axis=0))

def reference(tokens, mixed_grad, doc_ids, head_count, width_bucket, first_gain, first_shift, query_weight, key_weight, value_weight, output_weight, second_gain, second_shift, up_weight, down_weight):
    params = (first_gain, first_shift, query_weight.astype(jnp.float32), key_weight.astype(jnp.float32), value_weight.astype(jnp.float32), output_weight.astype(jnp.float32), second_gain, second_shift, up_weight.astype(jnp.float32), down_weight.astype(jnp.float32))
    cosine, sine = rotary_tables(SEQ, E)

    def one(carry, item):
        seq_x, seq_g, docs, heads, bucket = item

        def run(values, *rest):
            return forward_seq(values, rest, docs, heads, bucket, cosine, sine)
        result, pull = jax.vjp(run, seq_x.astype(jnp.float32), *params)
        grads = pull(seq_g.astype(jnp.float32))
        carry = tuple((total + piece for total, piece in zip(carry, grads[1:])))
        return (carry, (result.astype(jnp.bfloat16), grads[0].astype(jnp.bfloat16)))
    start = tuple((jnp.zeros(p.shape, jnp.float32) for p in params))
    totals, (mixed, input_grad) = lax.scan(one, start, (tokens, mixed_grad, doc_ids, head_count, width_bucket))
    bucket_tally = lax.optimization_barrier(jnp.sum((width_bucket.reshape(-1)[:, None] == jnp.arange(4, dtype=jnp.int32)[None, :]).astype(jnp.int32), axis=0))
    head_tally = lax.optimization_barrier(jnp.sum((head_count.reshape(-1)[:, None] == jnp.arange(1, HEADS + 1, dtype=jnp.int32)[None, :]).astype(jnp.int32), axis=0))
    return (mixed, input_grad, totals[0], totals[1], totals[2], totals[3], totals[4], totals[5], totals[6], totals[7], totals[8], totals[9], bucket_tally, head_tally)
```

```python
import functools
import jax
import jax.numpy as jnp
from jax import lax
from jax.experimental import pallas as pl
from jax.experimental.pallas import tpu as pltpu
from jax.sharding import PartitionSpec as P

HEADS = 16
E = 128
FF = 8192
EPS = 1e-05
DOC_MAX = 512
LOG2E = 1.4426950408889634
F32 = jnp.float32
BF16 = jnp.bfloat16
VMEM_LIMIT = 56 * 1024 * 1024


def params(**kw):
    return pltpu.CompilerParams(vmem_limit_bytes=VMEM_LIMIT, **kw)


def cost(flops, nbytes, trans=0):
    return pl.CostEstimate(flops=int(flops), bytes_accessed=int(nbytes), transcendentals=int(trans))


def norm_forward(values, gain, shift):
    mean = jnp.mean(values, axis=-1, keepdims=True)
    cent = values - mean
    inverse = lax.rsqrt(jnp.mean(cent * cent, axis=-1, keepdims=True) + EPS)
    normed = cent * inverse
    return (normed * gain + shift, normed, inverse)


def norm_backward(grad_out, normed, inverse, gain):
    scaled = grad_out * gain
    return inverse * (
        scaled
        - jnp.mean(scaled, axis=-1, keepdims=True)
        - normed * jnp.mean(scaled * normed, axis=-1, keepdims=True)
    )


def rotary_tables(length):
    half = E // 2
    freq = 10000.0 ** (-(jnp.arange(half, dtype=F32) * 2.0 / E))
    angle = jnp.arange(length, dtype=F32)[:, None] * freq[None, :]
    cos, sin = jnp.cos(angle), jnp.sin(angle)
    return jnp.concatenate([cos, cos], axis=1), jnp.concatenate([-sin, sin], axis=1)


def dot_t(left, right):
    return lax.dot_general(left, right, (((1,), (1,)), ((), ())), preferred_element_type=F32)


def dot_n(left, right):
    return lax.dot_general(left, right, (((1,), (0,)), ((), ())), preferred_element_type=F32)


def outer(left, right):
    return lax.dot_general(left, right, (((0,), (0,)), ((), ())), preferred_element_type=F32)


def qkv_body(rank_ref, x_ref, gain_ref, shift_ref, wq_ref, wk_ref, wv_ref, cos_ref, sin_ref, *rest):
    a_ref, q_ref, k_ref, v_ref = rest[-4:]

    @pl.when(pl.program_id(0) == 0)
    def _():
        out, _, _ = norm_forward(x_ref[...].astype(F32), gain_ref[...], shift_ref[...])
        a_ref[0] = out.astype(BF16)

    act = a_ref[0]
    cos, sin = cos_ref[0], sin_ref[0]
    v_ref[0] = dot_n(act, wv_ref[...]).astype(BF16)
    for w_ref, o_ref in ((wq_ref, q_ref), (wk_ref, k_ref)):
        lin = dot_n(act, w_ref[...])
        for j in range(lin.shape[1] // E):
            part = lin[:, j * E : (j + 1) * E]
            turned = part * cos + pltpu.roll(part, E // 2, 1) * sin
            o_ref[0, :, j * E : (j + 1) * E] = turned.astype(BF16)


def qkv_slot(slot, n, rank, x, gain, shift, wq, wk, wv, cos, sin, held):
    rows, d = x.shape
    local = wq.shape[1]
    cb = min(256, local)
    whole = lambda j, r: (0, 0)
    wspec = pl.BlockSpec((d, cb), lambda j, r: (0, j))
    tspec = pl.BlockSpec((1, rows, E), lambda j, r: (lax.rem(r[0] + slot, n), 0, 0))
    in_specs = [
        pl.BlockSpec((rows, d), whole),
        pl.BlockSpec((1, d), whole),
        pl.BlockSpec((1, d), whole),
        wspec,
        wspec,
        wspec,
        tspec,
        tspec,
    ]
    extra = [] if held is None else list(held)
    aliases = {} if held is None else {9 + i: i for i in range(4)}
    ospec = pl.BlockSpec((1, rows, cb), lambda j, r: (slot, 0, j))
    return pl.pallas_call(
        qkv_body,
        grid_spec=pltpu.PrefetchScalarGridSpec(
            num_scalar_prefetch=1,
            grid=(local // cb,),
            in_specs=in_specs + [pl.BlockSpec(memory_space=pl.ANY)] * len(extra),
            out_specs=[pl.BlockSpec((1, rows, d), lambda j, r: (slot, 0, 0)), ospec, ospec, ospec],
        ),
        out_shape=[jax.ShapeDtypeStruct((n, rows, d), BF16)]
        + [jax.ShapeDtypeStruct((n, rows, local), BF16)] * 3,
        input_output_aliases=aliases,
        compiler_params=params(),
        cost_estimate=cost(6 * rows * d * local, 6 * d * local + 4 * rows * d),
        name="qkv_slot",
    )(rank, x, gain, shift, wq, wk, wv, cos, sin, *extra)


def first_key(block, rows):
    return max(0, block - (DOC_MAX - 1 + rows - 1) // rows)


def attend_body(rank_ref, q_ref, k_ref, v_ref, dcol_ref, drow_ref, hc_ref, o_ref):
    n, rows, _ = q_ref.shape
    rank = rank_ref[0]
    head = rank_ref[1] + pl.program_id(0)
    slot = lambda b: lax.rem(b + n - rank, n)
    factor = E ** (-0.5) * LOG2E
    low = lax.broadcasted_iota(jnp.int32, (rows, rows), 0) >= lax.broadcasted_iota(
        jnp.int32, (rows, rows), 1
    )
    for b in range(n):
        q = q_ref[slot(b)]
        doc = dcol_ref[b]
        keys = range(first_key(b, rows), b + 1)
        scores = []
        for c in keys:
            s = dot_t(q, k_ref[slot(c)])
            ok = doc == drow_ref[c]
            if c == b:
                ok = ok & low
            scores.append(jnp.where(ok, s, -1e30))
        top = scores[0]
        for s in scores[1:]:
            top = jnp.maximum(top, s)
        top = jnp.max(top, axis=1, keepdims=True)
        total = None
        out = None
        for c, s in zip(keys, scores):
            p = jnp.exp2((s - top) * factor)
            total = p if total is None else total + p
            o = dot_n(p.astype(BF16), v_ref[slot(c)])
            out = o if out is None else out + o
        total = jnp.sum(total, axis=1, keepdims=True)
        gate = jnp.where(hc_ref[b] > head, 1.0, 0.0)
        o_ref[slot(b)] = (out * (gate / total)).astype(BF16)


def attend(rank, q, k, v, docs_col, docs_row, heads_col):
    n, rows, local = q.shape
    spec = pl.BlockSpec((n, rows, E), lambda h, r: (0, 0, h))
    col = pl.BlockSpec((n, rows, 1), lambda h, r: (0, 0, 0))
    row = pl.BlockSpec((n, 1, rows), lambda h, r: (0, 0, 0))
    t = n * rows
    return pl.pallas_call(
        attend_body,
        grid_spec=pltpu.PrefetchScalarGridSpec(
            num_scalar_prefetch=1,
            grid=(local // E,),
            in_specs=[spec, spec, spec, col, row, col],
            out_specs=spec,
        ),
        out_shape=jax.ShapeDtypeStruct((n, rows, local), BF16),
        compiler_params=params(),
        cost_estimate=cost(4 * t * t * local, 8 * t * local, t * t * local // E),
        name="attend",
    )(rank, q, k, v, docs_col, docs_row, heads_col)


def attend_back_body(
    rank_ref, q_ref, k_ref, v_ref, do_ref, dcol_ref, drow_ref, hc_ref, cos_ref, sin_ref, out_ref, dk_ref, dv_ref
):
    n, rows, _ = q_ref.shape
    rank = rank_ref[0]
    head = rank_ref[1] + pl.program_id(0)
    slot = lambda b: lax.rem(b + n - rank, n)
    scale = E ** (-0.5)
    factor = scale * LOG2E
    low = lax.broadcasted_iota(jnp.int32, (rows, rows), 0) <= lax.broadcasted_iota(
        jnp.int32, (rows, rows), 1
    )
    dk_ref[...] = jnp.zeros_like(dk_ref)
    dv_ref[...] = jnp.zeros_like(dv_ref)

    def unrotate(w, b):
        w = w * scale
        return (w * cos_ref[b] - pltpu.roll(w, E // 2, 1) * sin_ref[b]).astype(BF16)

    for b in range(n):
        q = q_ref[slot(b)]
        grad = jnp.where(hc_ref[b] > head, do_ref[slot(b)].astype(F32), 0.0).astype(BF16)
        keys = range(first_key(b, rows), b + 1)
        scores = []
        for c in keys:
            s = dot_t(k_ref[slot(c)], q)
            ok = dcol_ref[c] == drow_ref[b]
            if c == b:
                ok = ok & low
            scores.append(jnp.where(ok, s, -1e30))
        top = scores[0]
        for s in scores[1:]:
            top = jnp.maximum(top, s)
        top = jnp.max(top, axis=0, keepdims=True)
        probs = [jnp.exp2((s - top) * factor) for s in scores]
        total = probs[0]
        for p in probs[1:]:
            total = total + p
        inv = 1.0 / jnp.sum(total, axis=0, keepdims=True)
        probs = [p * inv for p in probs]
        dprobs = [dot_t(v_ref[slot(c)], grad) for c in keys]
        delta = None
        for p, g in zip(probs, dprobs):
            delta = p * g if delta is None else delta + p * g
        delta = jnp.sum(delta, axis=0, keepdims=True)
        dq = None
        for c, p, g in zip(keys, probs, dprobs):
            ds = (p * (g - delta)).astype(BF16)
            dk_ref[c] += dot_n(ds, q)
            dv_ref[c] += dot_n(p.astype(BF16), grad)
            part = outer(ds, k_ref[slot(c)])
            dq = part if dq is None else dq + part
        out_ref[slot(b), :, :E] = unrotate(dq, b)
    for b in range(n):
        out_ref[slot(b), :, E : 2 * E] = unrotate(dk_ref[b], b)
        out_ref[slot(b), :, 2 * E :] = dv_ref[b].astype(BF16)


def attend_back(rank, q, k, v, do, docs_col, docs_row, heads_col, cos, sin):
    n, rows, local = q.shape
    spec = pl.BlockSpec((n, rows, E), lambda h, r: (0, 0, h))
    col = pl.BlockSpec((n, rows, 1), lambda h, r: (0, 0, 0))
    row = pl.BlockSpec((n, 1, rows), lambda h, r: (0, 0, 0))
    table = pl.BlockSpec((n, rows, E), lambda h, r: (0, 0, 0))
    t = n * rows
    return pl.pallas_call(
        attend_back_body,
        grid_spec=pltpu.PrefetchScalarGridSpec(
            num_scalar_prefetch=1,
            grid=(local // E,),
            in_specs=[spec, spec, spec, spec, col, row, col, table, table],
            out_specs=pl.BlockSpec((n, rows, 3 * E), lambda h, r: (0, 0, h)),
            scratch_shapes=[pltpu.VMEM((n, rows, E), F32), pltpu.VMEM((n, rows, E), F32)],
        ),
        out_shape=jax.ShapeDtypeStruct((n, rows, 3 * local), BF16),
        compiler_params=params(),
        cost_estimate=cost(8 * t * t * local, 14 * t * local, t * t * local // E),
        name="attend_back",
    )(rank, q, k, v, do, docs_col, docs_row, heads_col, cos, sin)


def mlp_body(rank_ref, a_ref, g_ref, up_ref, down_ref, bucket_ref, *rest):
    r_ref, du_ref, aa_ref, ga_ref = rest[-4:]
    rows, cb = a_ref.shape[0], up_ref.shape[1]

    @pl.when(pl.program_id(0) == 0)
    def _():
        aa_ref[0] = a_ref[...]
        ga_ref[0] = g_ref[...]

    u = dot_n(a_ref[...], up_ref[...])
    dr = dot_n(g_ref[...], down_ref[...]).astype(BF16).astype(F32)
    column = rank_ref[2] + pl.program_id(0) * cb + lax.broadcasted_iota(jnp.int32, (rows, cb), 1)
    lifted = jnp.where(column < (bucket_ref[0] + 1) * (FF // 4), jnp.maximum(u, 0.0), 0.0)
    r_ref[0] = (lifted * lifted).astype(BF16)
    du_ref[0] = (dr * (2.0 * lifted)).astype(BF16)


def mlp_slot(slot, n, rank, act, grad, up, down, bucket_col, held):
    rows, d = act.shape
    hidden = up.shape[1]
    cb = min(512, hidden)
    whole = lambda j, r: (0, 0)
    wspec = pl.BlockSpec((d, cb), lambda j, r: (0, j))
    extra = [] if held is None else list(held)
    aliases = {} if held is None else {6 + i: i for i in range(4)}
    ospec = pl.BlockSpec((1, rows, cb), lambda j, r: (slot, 0, j))
    aspec = pl.BlockSpec((1, rows, d), lambda j, r: (slot, 0, 0))
    return pl.pallas_call(
        mlp_body,
        grid_spec=pltpu.PrefetchScalarGridSpec(
            num_scalar_prefetch=1,
            grid=(hidden // cb,),
            in_specs=[
                pl.BlockSpec((rows, d), whole),
                pl.BlockSpec((rows, d), whole),
                wspec,
                wspec,
                pl.BlockSpec((1, rows, 1), lambda j, r: (lax.rem(r[0] + slot, n), 0, 0)),
            ]
            + [pl.BlockSpec(memory_space=pl.ANY)] * len(extra),
            out_specs=[ospec, ospec, aspec, aspec],
        ),
        out_shape=[jax.ShapeDtypeStruct((n, rows, hidden), BF16)] * 2
        + [jax.ShapeDtypeStruct((n, rows, d), BF16)] * 2,
        input_output_aliases=aliases,
        compiler_params=params(),
        cost_estimate=cost(4 * rows * d * hidden, 4 * d * hidden + 4 * rows * (d + hidden)),
        name="mlp_slot",
    )(rank, act, grad, up, down, bucket_col, *extra)


def xor_sum(vec, axis, size):
    step = 1
    while step < size:
        vec = vec + lax.ppermute(vec, axis, [(i, i ^ step) for i in range(size)])
        step *= 2
    return vec


def per_device(
    n,
    n_dp,
    tokens,
    mixed_grad,
    doc_ids,
    head_count,
    width_bucket,
    first_gain,
    first_shift,
    query_weight,
    key_weight,
    value_weight,
    output_weight,
    second_gain,
    second_shift,
    up_weight,
    down_weight,
):
    rank = lax.axis_index("mp")
    rows, d = tokens.shape[1:]
    local = query_weight.shape[1]
    local_heads = local // E
    hidden = up_weight.shape[1]
    length = n * rows
    own = tokens[0]
    ring = [(i, (i - 1) % n) for i in range(n)]
    hop = lambda v: lax.ppermute(v, "mp", ring)
    where = jnp.stack([rank, rank * local_heads, rank * hidden]).astype(jnp.int32)
    docs_col = doc_ids.reshape(n, rows, 1)
    docs_row = doc_ids.reshape(n, 1, rows)
    heads_col = head_count.reshape(n, rows, 1)
    bucket_col = width_bucket.reshape(n, rows, 1)
    cos, sin = (t.reshape(n, rows, E) for t in rotary_tables(length))
    gain1, shift1 = first_gain[None], first_shift[None]
    gain2, shift2 = second_gain[None], second_shift[None]

    held, block = None, own
    for s in range(n):
        after = hop(block) if s < n - 1 else None
        held = qkv_slot(
            s, n, where, block, gain1, shift1, query_weight, key_weight, value_weight, cos, sin, held
        )
        block = after
    first_all, query, keys, vals = held
    masked = attend(where, query, keys, vals, docs_col, docs_row, heads_col)

    grads = [mixed_grad[0]]
    for s in range(n - 1):
        grads.append(hop(grads[-1]))

    def scatter_ring(term):
        moved = None
        for s in range(1, n):
            t = term(s)
            moved = hop((t if moved is None else t + moved.astype(F32)).astype(BF16))
        return term(0).astype(BF16).astype(F32) + moved.astype(F32)

    attn = scatter_ring(lambda s: dot_t(masked[s], output_weight))
    x_rows = own.astype(F32)
    state = x_rows + attn
    second_out, normed_two, inverse_two = norm_forward(state, gain2, shift2)

    held, block = None, second_out.astype(BF16)
    for s in range(n):
        after = hop(block) if s < n - 1 else None
        held = mlp_slot(s, n, where, block, grads[s], up_weight, down_weight, bucket_col, held)
        block = after
    active, grad_upper, second_all, grad_all = held
    grad_second = scatter_ring(lambda s: dot_t(grad_upper[s], up_weight))
    back_two = norm_backward(grad_second, normed_two, inverse_two, gain2)
    second_gain_part = jnp.sum(grad_second * normed_two, axis=0)
    second_shift_part = jnp.sum(grad_second, axis=0)
    grad_state = mixed_grad[0].astype(F32) + back_two

    flat = lambda v: v.reshape(length, v.shape[-1])
    scatter = lambda v: lax.psum_scatter(v.astype(BF16), "dp", scatter_dimension=0, tiled=True)
    down_grad = scatter(outer(flat(grad_all), flat(active)))
    up_grad = scatter(outer(flat(second_all), flat(grad_upper)))

    states = [grad_state.astype(BF16)]
    for s in range(n - 1):
        states.append(hop(states[-1]))
    grad_masked = jnp.stack([dot_n(v, output_weight).astype(BF16) for v in states])
    state_all = jnp.concatenate(states)
    output_grad = scatter(outer(state_all, flat(masked)))
    mixed = (state + scatter_ring(lambda s: dot_t(active[s], down_weight))).astype(BF16)

    dqkv = attend_back(
        where, query, keys, vals, grad_masked, docs_col, docs_row, heads_col, cos, sin
    )
    weights = jnp.stack(
        [w.reshape(d, local_heads, E) for w in (query_weight, key_weight, value_weight)], axis=2
    ).reshape(d, 3 * local)
    term = outer(flat(first_all), flat(dqkv)).astype(BF16)
    qkv_grad = scatter(term)
    grad_first = scatter_ring(lambda s: dot_t(dqkv[s], weights))
    n1_out, normed_one, inverse_one = norm_forward(x_rows, gain1, shift1)
    back_one = norm_backward(grad_first, normed_one, inverse_one, gain1)
    input_grad = (grad_state + back_one).astype(BF16)

    wide = weights.astype(F32)
    total_d = jnp.sum(flat(dqkv).astype(F32), axis=0)
    first_shift_part = jnp.sum(wide * total_d[None], axis=1)
    product = jnp.sum(wide * term.astype(F32), axis=1)
    first_gain_part = (product - first_shift * first_shift_part) / first_gain

    lead = (rank == 0).astype(F32)
    bucket_part = lead * jnp.sum(
        (width_bucket[0][:, None] == jnp.arange(4, dtype=jnp.int32)[None, :]).astype(F32), axis=0
    )
    head_part = lead * jnp.sum(
        (head_count[0][:, None] == jnp.arange(1, HEADS + 1, dtype=jnp.int32)[None, :]).astype(F32),
        axis=0,
    )
    small = jnp.concatenate(
        [
            first_gain_part,
            first_shift_part,
            second_gain_part,
            second_shift_part,
            bucket_part,
            head_part,
            jnp.zeros((128 - 4 - HEADS,), F32),
        ]
    )
    small = xor_sum(xor_sum(small, "dp", n_dp), "mp", n)
    qkv_grad = qkv_grad.reshape(-1, local_heads, 3, E).astype(F32)
    pick = lambda i: qkv_grad[:, :, i].reshape(-1, local)
    return (
        mixed[None],
        input_grad[None],
        small[:d],
        small[d : 2 * d],
        pick(0),
        pick(1),
        pick(2),
        output_grad.astype(F32),
        small[2 * d : 3 * d],
        small[3 * d : 4 * d],
        up_grad.astype(F32),
        down_grad.astype(F32),
        small[4 * d : 4 * d + 4].astype(jnp.int32),
        small[4 * d + 4 : 4 * d + 4 + HEADS].astype(jnp.int32),
    )


def solution(mesh):
    token, seq, copy, col = P("dp", "mp", None), P("dp", None), P(), P(None, "mp")
    grad = P("dp", "mp")
    return jax.shard_map(
        functools.partial(per_device, mesh.shape["mp"], mesh.shape["dp"]),
        mesh=mesh,
        in_specs=(token, token, seq, seq, seq, copy, copy, col, col, col, col, copy, copy, col, col),
        out_specs=(token, token, copy, copy, grad, grad, grad, grad, copy, copy, grad, grad, copy, copy),
        check_vma=False,
    )
```

```python
import functools
import jax
import jax.numpy as jnp
from jax import lax
from jax.experimental import pallas as pl
from jax.experimental.pallas import tpu as pltpu
from jax.sharding import PartitionSpec as P

HEADS = 16
E = 128
FF = 8192
EPS = 1e-05
DOC_MAX = 512
LOG2E = 1.4426950408889634
F32 = jnp.float32
BF16 = jnp.bfloat16
VMEM_LIMIT = 56 * 1024 * 1024


def params(**kw):
    return pltpu.CompilerParams(vmem_limit_bytes=VMEM_LIMIT, **kw)


def cost(flops, nbytes, trans=0):
    return pl.CostEstimate(flops=int(flops), bytes_accessed=int(nbytes), transcendentals=int(trans))


def norm_forward(values, gain, shift):
    mean = jnp.mean(values, axis=-1, keepdims=True)
    cent = values - mean
    inverse = lax.rsqrt(jnp.mean(cent * cent, axis=-1, keepdims=True) + EPS)
    normed = cent * inverse
    return (normed * gain + shift, normed, inverse)


def norm_backward(grad_out, normed, inverse, gain):
    scaled = grad_out * gain
    return inverse * (
        scaled
        - jnp.mean(scaled, axis=-1, keepdims=True)
        - normed * jnp.mean(scaled * normed, axis=-1, keepdims=True)
    )


def rotary_tables(length):
    half = E // 2
    freq = 10000.0 ** (-(jnp.arange(half, dtype=F32) * 2.0 / E))
    angle = jnp.arange(length, dtype=F32)[:, None] * freq[None, :]
    cos, sin = jnp.cos(angle), jnp.sin(angle)
    return jnp.concatenate([cos, cos], axis=1), jnp.concatenate([-sin, sin], axis=1)


def dot_t(left, right):
    return lax.dot_general(left, right, (((1,), (1,)), ((), ())), preferred_element_type=F32)


def dot_n(left, right):
    return lax.dot_general(left, right, (((1,), (0,)), ((), ())), preferred_element_type=F32)


def outer(left, right):
    return lax.dot_general(left, right, (((0,), (0,)), ((), ())), preferred_element_type=F32)


def qkv_body(rank_ref, xa_ref, xb_ref, gain_ref, shift_ref, wq_ref, wk_ref, wv_ref, cos_ref, sin_ref, *rest):
    a_ref, q_ref, k_ref, v_ref = rest[-4:]

    @pl.when(pl.program_id(0) == 0)
    def _():
        x = jnp.concatenate([xa_ref[...], xb_ref[...]], axis=1).astype(F32)
        out, _, _ = norm_forward(x, gain_ref[...], shift_ref[...])
        a_ref[0] = out.astype(BF16)

    act = a_ref[0]
    cos, sin = cos_ref[0], sin_ref[0]
    v_ref[0] = dot_n(act, wv_ref[...]).astype(BF16)
    for w_ref, o_ref in ((wq_ref, q_ref), (wk_ref, k_ref)):
        lin = dot_n(act, w_ref[...])
        for j in range(lin.shape[1] // E):
            part = lin[:, j * E : (j + 1) * E]
            turned = part * cos + pltpu.roll(part, E // 2, 1) * sin
            o_ref[0, :, j * E : (j + 1) * E] = turned.astype(BF16)


def qkv_slot(slot, n, rank, xa, xb, gain, shift, wq, wk, wv, cos, sin, held):
    rows, half = xa.shape
    d = 2 * half
    local = wq.shape[1]
    cb = min(512, local)
    whole = lambda j, r: (0, 0)
    wspec = pl.BlockSpec((d, cb), lambda j, r: (0, j))
    tspec = pl.BlockSpec((1, rows, E), lambda j, r: (lax.rem(r[0] + slot, n), 0, 0))
    in_specs = [
        pl.BlockSpec((rows, half), whole),
        pl.BlockSpec((rows, half), whole),
        pl.BlockSpec((1, d), whole),
        pl.BlockSpec((1, d), whole),
        wspec,
        wspec,
        wspec,
        tspec,
        tspec,
    ]
    extra = [] if held is None else list(held)
    aliases = {} if held is None else {10 + i: i for i in range(4)}
    ospec = pl.BlockSpec((1, rows, cb), lambda j, r: (slot, 0, j))
    return pl.pallas_call(
        qkv_body,
        grid_spec=pltpu.PrefetchScalarGridSpec(
            num_scalar_prefetch=1,
            grid=(local // cb,),
            in_specs=in_specs + [pl.BlockSpec(memory_space=pl.ANY)] * len(extra),
            out_specs=[pl.BlockSpec((1, rows, d), lambda j, r: (slot, 0, 0)), ospec, ospec, ospec],
        ),
        out_shape=[jax.ShapeDtypeStruct((n, rows, d), BF16)]
        + [jax.ShapeDtypeStruct((n, rows, local), BF16)] * 3,
        input_output_aliases=aliases,
        compiler_params=params(),
        cost_estimate=cost(6 * rows * d * local, 6 * d * local + 4 * rows * d),
        name="qkv_slot",
    )(rank, xa, xb, gain, shift, wq, wk, wv, cos, sin, *extra)


def first_key(block, rows):
    return max(0, block - (DOC_MAX - 1 + rows - 1) // rows)


def attend_body(rank_ref, q_ref, k_ref, v_ref, dcol_ref, drow_ref, hc_ref, o_ref):
    n, rows, _ = q_ref.shape
    rank = rank_ref[0]
    head = rank_ref[1] + pl.program_id(0)
    slot = lambda b: lax.rem(b + n - rank, n)
    factor = E ** (-0.5) * LOG2E
    low = lax.broadcasted_iota(jnp.int32, (rows, rows), 0) >= lax.broadcasted_iota(
        jnp.int32, (rows, rows), 1
    )
    for b in range(n):
        q = q_ref[slot(b)]
        doc = dcol_ref[b]
        keys = range(first_key(b, rows), b + 1)
        scores = []
        for c in keys:
            s = dot_t(q, k_ref[slot(c)])
            ok = doc == drow_ref[c]
            if c == b:
                ok = ok & low
            scores.append(jnp.where(ok, s, -1e30))
        top = scores[0]
        for s in scores[1:]:
            top = jnp.maximum(top, s)
        top = jnp.max(top, axis=1, keepdims=True)
        total = None
        out = None
        for c, s in zip(keys, scores):
            p = jnp.exp2((s - top) * factor)
            total = p if total is None else total + p
            o = dot_n(p.astype(BF16), v_ref[slot(c)])
            out = o if out is None else out + o
        total = jnp.sum(total, axis=1, keepdims=True)
        gate = jnp.where(hc_ref[b] > head, 1.0, 0.0)
        o_ref[slot(b)] = (out * (gate / total)).astype(BF16)


def attend(rank, q, k, v, docs_col, docs_row, heads_col):
    n, rows, local = q.shape
    spec = pl.BlockSpec((n, rows, E), lambda h, r: (0, 0, h))
    col = pl.BlockSpec((n, rows, 1), lambda h, r: (0, 0, 0))
    row = pl.BlockSpec((n, 1, rows), lambda h, r: (0, 0, 0))
    t = n * rows
    return pl.pallas_call(
        attend_body,
        grid_spec=pltpu.PrefetchScalarGridSpec(
            num_scalar_prefetch=1,
            grid=(local // E,),
            in_specs=[spec, spec, spec, col, row, col],
            out_specs=spec,
        ),
        out_shape=jax.ShapeDtypeStruct((n, rows, local), BF16),
        compiler_params=params(),
        cost_estimate=cost(4 * t * t * local, 8 * t * local, t * t * local // E),
        name="attend",
    )(rank, q, k, v, docs_col, docs_row, heads_col)


def attend_back_body(
    rank_ref, q_ref, k_ref, v_ref, do_ref, dcol_ref, drow_ref, hc_ref, cos_ref, sin_ref, out_ref, dk_ref, dv_ref
):
    n, rows, _ = q_ref.shape
    rank = rank_ref[0]
    head = rank_ref[1] + pl.program_id(0)
    slot = lambda b: lax.rem(b + n - rank, n)
    scale = E ** (-0.5)
    factor = scale * LOG2E
    low = lax.broadcasted_iota(jnp.int32, (rows, rows), 0) <= lax.broadcasted_iota(
        jnp.int32, (rows, rows), 1
    )
    local = out_ref.shape[2] // 3
    lanes = lambda i: pl.ds(pl.multiple_of(i * local + pl.program_id(0) * E, E), E)
    dk_ref[...] = jnp.zeros_like(dk_ref)
    dv_ref[...] = jnp.zeros_like(dv_ref)

    def unrotate(w, b):
        w = w * scale
        return (w * cos_ref[b] - pltpu.roll(w, E // 2, 1) * sin_ref[b]).astype(BF16)

    for b in range(n):
        q = q_ref[slot(b)]
        grad = jnp.where(hc_ref[b] > head, do_ref[slot(b)].astype(F32), 0.0).astype(BF16)
        keys = range(first_key(b, rows), b + 1)
        scores = []
        for c in keys:
            s = dot_t(k_ref[slot(c)], q)
            ok = dcol_ref[c] == drow_ref[b]
            if c == b:
                ok = ok & low
            scores.append(jnp.where(ok, s, -1e30))
        top = scores[0]
        for s in scores[1:]:
            top = jnp.maximum(top, s)
        top = jnp.max(top, axis=0, keepdims=True)
        probs = [jnp.exp2((s - top) * factor) for s in scores]
        total = probs[0]
        for p in probs[1:]:
            total = total + p
        inv = 1.0 / jnp.sum(total, axis=0, keepdims=True)
        probs = [p * inv for p in probs]
        dprobs = [dot_t(v_ref[slot(c)], grad) for c in keys]
        delta = None
        for p, g in zip(probs, dprobs):
            delta = p * g if delta is None else delta + p * g
        delta = jnp.sum(delta, axis=0, keepdims=True)
        dq = None
        for c, p, g in zip(keys, probs, dprobs):
            ds = (p * (g - delta)).astype(BF16)
            dk_ref[c] += dot_n(ds, q)
            dv_ref[c] += dot_n(p.astype(BF16), grad)
            part = outer(ds, k_ref[slot(c)])
            dq = part if dq is None else dq + part
        out_ref[slot(b), :, lanes(0)] = unrotate(dq, b)
    for b in range(n):
        out_ref[slot(b), :, lanes(1)] = unrotate(dk_ref[b], b)
        out_ref[slot(b), :, lanes(2)] = dv_ref[b].astype(BF16)


def attend_back(rank, q, k, v, do, docs_col, docs_row, heads_col, cos, sin):
    n, rows, local = q.shape
    spec = pl.BlockSpec((n, rows, E), lambda h, r: (0, 0, h))
    col = pl.BlockSpec((n, rows, 1), lambda h, r: (0, 0, 0))
    row = pl.BlockSpec((n, 1, rows), lambda h, r: (0, 0, 0))
    table = pl.BlockSpec((n, rows, E), lambda h, r: (0, 0, 0))
    t = n * rows
    return pl.pallas_call(
        attend_back_body,
        grid_spec=pltpu.PrefetchScalarGridSpec(
            num_scalar_prefetch=1,
            grid=(local // E,),
            in_specs=[spec, spec, spec, spec, col, row, col, table, table],
            out_specs=pl.BlockSpec((n, rows, 3 * local), lambda h, r: (0, 0, 0)),
            scratch_shapes=[pltpu.VMEM((n, rows, E), F32), pltpu.VMEM((n, rows, E), F32)],
        ),
        out_shape=jax.ShapeDtypeStruct((n, rows, 3 * local), BF16),
        compiler_params=params(),
        cost_estimate=cost(200e9, 14 * t * local),
        name="attend_back",
    )(rank, q, k, v, do, docs_col, docs_row, heads_col, cos, sin)


def mlp_body(slot, n, rank_ref, a_ref, gl_ref, gr_ref, up_ref, down_ref, bucket_ref, *rest):
    r_ref, du_ref, aa_ref, ga_ref = rest[-4:]
    rows, cb = a_ref.shape[0], up_ref.shape[1]

    @pl.when(pl.program_id(0) == 0)
    def _():
        aa_ref[0] = a_ref[...]
        ahead = rank_ref[0] + slot < n


        @pl.when(ahead)
        def _():
            ga_ref[0] = gl_ref[...]

        @pl.when(jnp.logical_not(ahead))
        def _():
            ga_ref[0] = gr_ref[...]

    u = dot_n(a_ref[...], up_ref[...])
    dr = dot_n(ga_ref[0], down_ref[...]).astype(BF16).astype(F32)
    column = rank_ref[2] + pl.program_id(0) * cb + lax.broadcasted_iota(jnp.int32, (rows, cb), 1)
    lifted = jnp.where(column < (bucket_ref[0] + 1) * (FF // 4), jnp.maximum(u, 0.0), 0.0)
    r_ref[0] = (lifted * lifted).astype(BF16)
    du_ref[0] = (dr * (2.0 * lifted)).astype(BF16)


def mlp_slot(slot, n, rank, act, grads, up, down, bucket_col, held):
    rows, d = act.shape
    hidden = up.shape[1]
    cb = min(512, hidden)
    whole = lambda j, r: (0, 0)
    wspec = pl.BlockSpec((d, cb), lambda j, r: (0, j))
    extra = [] if held is None else list(held)
    aliases = {} if held is None else {7 + i: i for i in range(4)}
    ospec = pl.BlockSpec((1, rows, cb), lambda j, r: (slot, 0, j))
    aspec = pl.BlockSpec((1, rows, d), lambda j, r: (slot, 0, 0))
    return pl.pallas_call(
        functools.partial(mlp_body, slot, n),
        grid_spec=pltpu.PrefetchScalarGridSpec(
            num_scalar_prefetch=1,
            grid=(hidden // cb,),
            in_specs=[
                pl.BlockSpec((rows, d), whole),
            ]
            + [pl.BlockSpec((rows, d), whole)] * 2
            + [
                wspec,
                wspec,
                pl.BlockSpec((1, rows, 1), lambda j, r: (lax.rem(r[0] + slot, n), 0, 0)),
            ]
            + [pl.BlockSpec(memory_space=pl.ANY)] * len(extra),
            out_specs=[ospec, ospec, aspec, aspec],
        ),
        out_shape=[jax.ShapeDtypeStruct((n, rows, hidden), BF16)] * 2
        + [jax.ShapeDtypeStruct((n, rows, d), BF16)] * 2,
        input_output_aliases=aliases,
        compiler_params=params(),
        cost_estimate=cost(4 * rows * d * hidden, 4 * d * hidden + 4 * rows * (d + hidden)),
        name="mlp_slot",
    )(rank, act, *grads, up, down, bucket_col, *extra)


def dom_body(n, slots, rank_ref, slot_ref, *refs):
    dom_ref, all_ref = refs[-2:]
    count = sum(2 if s == 0 else 4 for s in slots)
    flows, w_ref = list(refs[:count]), refs[count]
    half = flows[0].shape[1]

    def fill(pair):
        all_ref[0, :, :half] = pair[0][...]
        all_ref[0, :, half:] = pair[1][...]

    for i, s in enumerate(slots):
        here = pl.program_id(0) == i
        if s == 0:
            pl.when(here)(functools.partial(fill, flows[:2]))
            flows = flows[2:]
        else:
            ahead = rank_ref[0] + s < n
            pl.when(here & ahead)(functools.partial(fill, flows[:2]))
            pl.when(here & jnp.logical_not(ahead))(functools.partial(fill, flows[2:4]))
            flows = flows[4:]
    dom_ref[0] = dot_n(all_ref[0], w_ref[...]).astype(BF16)


def dom_part(n, slots, rank, flows, weight, held):
    rows, half = flows[0].shape
    d, local = weight.shape
    whole = lambda i, r, s: (0, 0)
    extra = [] if held is None else list(held)
    at = 2 + len(flows) + 1
    return pl.pallas_call(
        functools.partial(dom_body, n, slots),
        grid_spec=pltpu.PrefetchScalarGridSpec(
            num_scalar_prefetch=2,
            grid=(len(slots),),
            in_specs=[pl.BlockSpec((rows, half), whole)] * len(flows)
            + [pl.BlockSpec((d, local), whole)]
            + [pl.BlockSpec(memory_space=pl.ANY)] * len(extra),
            out_specs=[
                pl.BlockSpec((1, rows, local), lambda i, r, s: (s[i], 0, 0)),
                pl.BlockSpec((1, rows, d), lambda i, r, s: (s[i], 0, 0)),
            ],
        ),
        out_shape=[
            jax.ShapeDtypeStruct((n, rows, local), BF16),
            jax.ShapeDtypeStruct((n, rows, d), BF16),
        ],
        input_output_aliases={at + i: i for i in range(len(extra))},
        compiler_params=params(),
        cost_estimate=cost(
            2 * len(slots) * rows * d * local, 2 * d * local + 6 * len(slots) * rows * d
        ),
        name="dom_part",
    )(rank, jnp.asarray(slots, jnp.int32), *flows, weight, *extra)


def grad_body(lhs_ref, rhs_ref, *rest):
    rest[-1][0] = outer(lhs_ref[...], rhs_ref[...]).astype(BF16)


def grad_part(which, lhs, rhs, held):
    t, d = lhs.shape
    width = rhs.shape[1]
    tile = min(512, d)
    extra = [] if held is None else [held]
    return pl.pallas_call(
        grad_body,
        grid=(d // tile,),
        in_specs=[
            pl.BlockSpec((t, tile), lambda j: (0, j)),
            pl.BlockSpec((t, width), lambda j: (0, 0)),
        ]
        + [pl.BlockSpec(memory_space=pl.ANY)] * len(extra),
        out_specs=pl.BlockSpec((1, tile, width), lambda j: (which, j, 0)),
        out_shape=jax.ShapeDtypeStruct((2, d, width), BF16),
        input_output_aliases={2: 0} if extra else {},
        compiler_params=params(),
        cost_estimate=cost(2 * t * d * width, 2 * t * (d + width) + 2 * d * width),
        name="grad_part",
    )(lhs, rhs, *extra)


def attn_grad_body(a_ref, s_ref, dqkv_ref, om_ref, wq_ref, wk_ref, wv_ref, out_ref, sum_ref, dot_ref, tot_ref):
    local = om_ref.shape[1]

    @pl.when(pl.program_id(0) == 0)
    def _():
        tot_ref[...] = jnp.sum(dqkv_ref[...].astype(F32), axis=0, keepdims=True)

    act = a_ref[...]
    plain = None
    for i, w_ref in enumerate((wq_ref, wk_ref, wv_ref)):
        cols = slice(i * local, (i + 1) * local)
        part = outer(act, dqkv_ref[:, cols])
        out_ref[:, cols] = part.astype(BF16)
        w = w_ref[...].astype(F32)
        one, two = w * tot_ref[:, cols], w * part
        plain = one if plain is None else plain + one
        mixed = two if i == 0 else mixed + two
    sum_ref[...] = jnp.sum(plain, axis=1, keepdims=True)
    dot_ref[...] = jnp.sum(mixed, axis=1, keepdims=True)
    out_ref[:, 3 * local :] = outer(s_ref[...], om_ref[...]).astype(BF16)


def attn_grads(act, states, dqkv, om, wq, wk, wv):
    t, d = act.shape
    local = om.shape[1]
    tile = min(512, d)
    col = pl.BlockSpec((t, tile), lambda j: (0, j))
    wspec = pl.BlockSpec((tile, local), lambda j: (j, 0))
    vec = pl.BlockSpec((tile, 1), lambda j: (j, 0))
    return pl.pallas_call(
        attn_grad_body,
        grid=(d // tile,),
        in_specs=[
            col,
            col,
            pl.BlockSpec((t, 3 * local), lambda j: (0, 0)),
            pl.BlockSpec((t, local), lambda j: (0, 0)),
            wspec,
            wspec,
            wspec,
        ],
        out_specs=[pl.BlockSpec((tile, 4 * local), lambda j: (j, 0)), vec, vec],
        out_shape=[
            jax.ShapeDtypeStruct((d, 4 * local), BF16),
            jax.ShapeDtypeStruct((d, 1), F32),
            jax.ShapeDtypeStruct((d, 1), F32),
        ],
        scratch_shapes=[pltpu.VMEM((1, 3 * local), F32)],
        compiler_params=params(),
        cost_estimate=cost(8 * t * d * local, 2 * t * (2 * d + 4 * local) + 14 * d * local),
        name="attn_grads",
    )(act, states, dqkv, om, wq, wk, wv)


def last_body(x_ref, gain_ref, term_ref, moved_ref, state_ref, out_ref):
    gain = gain_ref[...]
    _, normed, inverse = norm_forward(x_ref[...].astype(F32), gain, gain)
    back = norm_backward(term_ref[...].astype(F32) + moved_ref[...].astype(F32), normed, inverse, gain)
    out_ref[...] = (state_ref[...] + back).astype(BF16)


def last_step(x, gain, term, moved, state):
    rows, d = x.shape
    tile = min(64, rows)
    row = lambda w: pl.BlockSpec((tile, w), lambda i: (i, 0))
    return pl.pallas_call(
        last_body,
        grid=(rows // tile,),
        in_specs=[row(d), pl.BlockSpec((1, d), lambda i: (0, 0)), row(d), row(d), row(d)],
        out_specs=row(d),
        out_shape=jax.ShapeDtypeStruct((rows, d), BF16),
        compiler_params=params(),
        cost_estimate=cost(73e9, 12 * rows * d),
        name="last_step",
    )(x, gain, term, moved, state)


def tie(values, *others):
    values = tuple(values)
    return lax.optimization_barrier(values + others)[: len(values)]


def sum_over(vec, axis, moves):
    return sum((lax.ppermute(vec, axis, pairs) for pairs in moves), vec)


def per_device(
    n,
    n_dp,
    tokens,
    mixed_grad,
    doc_ids,
    head_count,
    width_bucket,
    first_gain,
    first_shift,
    query_weight,
    key_weight,
    value_weight,
    output_weight,
    second_gain,
    second_shift,
    up_weight,
    down_weight,
):
    rank = lax.axis_index("mp")
    rows, d = tokens.shape[1:]
    half = d // 2
    local = query_weight.shape[1]
    local_heads = local // E
    hidden = up_weight.shape[1]
    length = n * rows
    own = tokens[0]
    send = lambda v, pairs: lax.ppermute(v, "mp", pairs)
    ring = [(i, (i - 1) % n) for i in range(n)]
    hop = lambda v: send(v, ring)
    right_line = [(i, i + 1) for i in range(n - 1)]
    left_line = [(i + 1, i) for i in range(n - 1)]

    def tick(k, right, left, terms):
        width = d // len(right)
        for p in range(len(right)):
            cols = slice(p * width, (p + 1) * width)
            r, l = right[p], left[p]
            if k:
                r = low(r.astype(F32) + (rank < k).astype(F32) * terms[n - k][:, cols].astype(F32))
                l = low(l.astype(F32) + (rank >= n - k).astype(F32) * terms[k][:, cols].astype(F32))
            right[p], left[p] = send(r, right_line), send(l, left_line)

    def owned(terms, right, left):
        moved = [r.astype(F32) + l.astype(F32) for r, l in zip(right, left)]
        return terms[0].astype(F32) + (jnp.concatenate(moved, axis=1) if len(moved) > 1 else moved[0])

    low = lambda v: v.astype(BF16)
    flat = lambda v: v.reshape(length, v.shape[-1])
    add = lambda t, moved: (t.astype(F32) + moved.astype(F32)).astype(BF16)

    where = jnp.stack([rank, rank * local_heads, rank * hidden]).astype(jnp.int32)
    docs_col = doc_ids.reshape(n, rows, 1)
    docs_row = doc_ids.reshape(n, 1, rows)
    heads_col = head_count.reshape(n, rows, 1)
    bucket_col = width_bucket.reshape(n, rows, 1)
    cos, sin = (t.reshape(n, rows, E) for t in rotary_tables(length))
    gain1, shift1 = first_gain[None], first_shift[None]
    gain2, shift2 = second_gain[None], second_shift[None]

    held, block = None, [own[:, :half], own[:, half:]]
    for s in range(n):
        after = [None, None]
        for p in range(2):
            if s >= 1:
                block[p], *held = tie([block[p]] + list(held))
            if s < n - 1:
                after[p] = hop(block[p])
        held = qkv_slot(
            s, n, where, *block, gain1, shift1, query_weight, key_weight, value_weight, cos, sin, held
        )
        if s < n - 1:
            block = after
    first_all, query, keys, vals = held

    grad_own = mixed_grad[0]
    right = list(tie([grad_own], *block))
    left = list(right)
    grads_r, grads_l = [list(right)], [list(left)]
    tick(0, right, left, None)
    masked = attend(where, query, keys, vals, docs_col, docs_row, heads_col)
    terms = low(dot_t(flat(masked), output_weight)).reshape(n, rows, d)
    for k in range(1, n):
        grads_r.append(list(right))
        grads_l.append(list(left))
        tick(k, right, left, terms)
    attn = owned(terms, right, left)
    x_rows = own.astype(F32)
    state = x_rows + attn
    second_out, normed_two, inverse_two = norm_forward(state, gain2, shift2)

    weights = jnp.concatenate([query_weight, key_weight, value_weight], axis=1)
    held, moved = None, None
    (block,) = tie([low(second_out)], weights)
    for s in range(n):
        if s >= 1:
            block, *held = tie([block] + list(held) + ([term0] if s == n - 1 else []))
            if s == n - 1:
                term0, held = held[-1], held[:-1]
        after = hop(block) if s < n - 1 else None
        held = mlp_slot(
            s, n, where, block, grads_l[s] + grads_r[n - s if s else 0], up_weight, down_weight, bucket_col, held
        )
        if s >= 1:
            term = dot_t(held[1][s], up_weight)
            if s > 1:
                (term,) = tie([term])
            sent = low(term) if moved is None else add(term, moved)
            moved = hop(sent)
        else:
            term0 = dot_t(held[1][0], up_weight)
        block = after
    active, grad_upper, second_all, grad_all = held
    grad_all, active, second_all, grad_upper = tie([grad_all, active, second_all, grad_upper], sent)
    pair = grad_part(0, flat(grad_all), flat(active), None)
    pair = grad_part(1, flat(second_all), flat(grad_upper), pair)
    (moved,) = tie([moved], pair)
    grad_second = term0 + moved.astype(F32)
    back_two = norm_backward(grad_second, normed_two, inverse_two, gain2)
    second_gain_part = jnp.sum(grad_second * normed_two, axis=0)
    second_shift_part = jnp.sum(grad_second, axis=0)
    grad_state = grad_own.astype(F32) + back_two

    wide_grad = lax.psum_scatter(pair, "dp", scatter_dimension=1, tiled=True)

    start = low(grad_state)
    active, start = tie([active, start])
    ffn = low(dot_t(flat(active), down_weight)).reshape(n, rows, d)
    right = [start[:, :half], start[:, half:]]
    left = list(right)
    rights, lefts = [list(right)], [list(left)]
    tick(0, right, left, None)
    for k in range(1, n):
        rights.append(list(right))
        lefts.append(list(left))
        tick(k, right, left, ffn)
    late = sorted({1, n - 1})
    early = [s for s in range(n) if s not in late]
    pick = lambda slots: sum((rights[0] if s == 0 else lefts[s] + rights[n - s] for s in slots), [])
    held = dom_part(n, early, where, pick(early), output_weight, None)
    grad_masked, state_all = dom_part(n, late, where, pick(late), output_weight, held)
    dqkv = attend_back(
        where, query, keys, vals, grad_masked, docs_col, docs_row, heads_col, cos, sin
    )
    mixed = low(state + owned(ffn, right, left))

    (dqkv,) = tie([dqkv], *right, *left)
    terms = low(dot_t(flat(dqkv), weights)).reshape(n, rows, d)
    sent = terms[1]
    (dqkv,) = tie([dqkv], sent)
    moved = hop(sent)
    attn_term, sum_d, sum_da = attn_grads(
        flat(first_all), flat(state_all), flat(dqkv), flat(masked), query_weight, key_weight, value_weight
    )
    (late,) = tie([attn_term], wide_grad)
    attn_grad = lax.psum_scatter(late, "dp", scatter_dimension=0, tiled=True)
    (moved,) = tie([moved], attn_term)
    first_shift_part = sum_d[:, 0]
    first_gain_part = (sum_da[:, 0] - first_shift * first_shift_part) / first_gain

    lead = (rank == 0).astype(F32)
    bucket_part = lead * jnp.sum(
        (width_bucket[0][:, None] == jnp.arange(4, dtype=jnp.int32)[None, :]).astype(F32), axis=0
    )
    head_part = lead * jnp.sum(
        (head_count[0][:, None] == jnp.arange(1, HEADS + 1, dtype=jnp.int32)[None, :]).astype(F32),
        axis=0,
    )
    small = jnp.concatenate(
        [
            first_gain_part,
            first_shift_part,
            second_gain_part,
            second_shift_part,
            bucket_part,
            head_part,
            jnp.zeros((128 - 4 - HEADS,), F32),
        ]
    )
    small = sum_over(small, "dp", [[(i, i ^ 1) for i in range(n_dp)]])
    for s in range(2, n):
        sent = add(terms[s], moved)
        if s == 2:
            first_sent = sent
        moved = hop(sent)
    if n == 2:
        first_sent = sent

    planes = tie([send(small, [(i, (i + m) % n) for i in range(n)]) for m in range(1, n)], first_sent)
    small = small + sum(planes)
    others = [
        lax.ppermute(small, "dp", [(i, (i + 2 * m) % n_dp) for i in range(n_dp)])
        for m in range(1, n_dp // 2)
    ]
    small = small + sum(tie(others, moved))
    input_grad = last_step(own, gain1, terms[0], moved, grad_state)
    wide_grad, attn_grad = wide_grad.astype(F32), attn_grad.astype(F32)
    return (
        mixed[None],
        input_grad[None],
        small[:d],
        small[d : 2 * d],
        attn_grad[:, :local],
        attn_grad[:, local : 2 * local],
        attn_grad[:, 2 * local : 3 * local],
        attn_grad[:, 3 * local :],
        small[2 * d : 3 * d],
        small[3 * d : 4 * d],
        wide_grad[1],
        wide_grad[0],
        small[4 * d : 4 * d + 4].astype(jnp.int32),
        small[4 * d + 4 : 4 * d + 4 + HEADS].astype(jnp.int32),
    )


def solution(mesh):
    token, seq, copy, col = P("dp", "mp", None), P("dp", None), P(), P(None, "mp")
    grad = P("dp", "mp")
    return jax.shard_map(
        functools.partial(per_device, mesh.shape["mp"], mesh.shape["dp"]),
        mesh=mesh,
        in_specs=(token, token, seq, seq, seq, copy, copy, col, col, col, col, copy, copy, col, col),
        out_specs=(token, token, copy, copy, grad, grad, grad, grad, copy, copy, grad, grad, copy, copy),
        check_vma=False,
    )
```

```python
import functools
import jax
import jax.numpy as jnp
from jax import lax
from jax.experimental import pallas as pl
from jax.experimental.pallas import tpu as pltpu
from jax.sharding import PartitionSpec as P

HEADS = 16
E = 128
FF = 8192
EPS = 1e-05
DOC_MAX = 512
LOG2E = 1.4426950408889634
F32 = jnp.float32
BF16 = jnp.bfloat16
VMEM_LIMIT = 56 * 1024 * 1024


def params(**kw):
    return pltpu.CompilerParams(vmem_limit_bytes=VMEM_LIMIT, **kw)


def cost(flops, nbytes, trans=0):
    return pl.CostEstimate(flops=int(flops), bytes_accessed=int(nbytes), transcendentals=int(trans))


def norm_forward(values, gain, shift):
    mean = jnp.mean(values, axis=-1, keepdims=True)
    cent = values - mean
    inverse = lax.rsqrt(jnp.mean(cent * cent, axis=-1, keepdims=True) + EPS)
    normed = cent * inverse
    return (normed * gain + shift, normed, inverse)


def norm_backward(grad_out, normed, inverse, gain):
    scaled = grad_out * gain
    return inverse * (
        scaled
        - jnp.mean(scaled, axis=-1, keepdims=True)
        - normed * jnp.mean(scaled * normed, axis=-1, keepdims=True)
    )


def rotary_tables(length):
    half = E // 2
    freq = 10000.0 ** (-(jnp.arange(half, dtype=F32) * 2.0 / E))
    angle = jnp.arange(length, dtype=F32)[:, None] * freq[None, :]
    cos, sin = jnp.cos(angle), jnp.sin(angle)
    return jnp.concatenate([cos, cos], axis=1), jnp.concatenate([-sin, sin], axis=1)


def dot_t(left, right):
    return lax.dot_general(left, right, (((1,), (1,)), ((), ())), preferred_element_type=F32)


def dot_n(left, right):
    return lax.dot_general(left, right, (((1,), (0,)), ((), ())), preferred_element_type=F32)


def outer(left, right):
    return lax.dot_general(left, right, (((0,), (0,)), ((), ())), preferred_element_type=F32)


def qkv_body(rank_ref, xa_ref, xb_ref, gain_ref, shift_ref, wq_ref, wk_ref, wv_ref, cos_ref, sin_ref, *rest):
    a_ref, q_ref, k_ref, v_ref = rest[-4:]

    @pl.when(pl.program_id(0) == 0)
    def _():
        x = jnp.concatenate([xa_ref[...], xb_ref[...]], axis=1).astype(F32)
        out, _, _ = norm_forward(x, gain_ref[...], shift_ref[...])
        a_ref[0] = out.astype(BF16)

    act = a_ref[0]
    cos, sin = cos_ref[0], sin_ref[0]
    v_ref[0] = dot_n(act, wv_ref[...]).astype(BF16)
    for w_ref, o_ref in ((wq_ref, q_ref), (wk_ref, k_ref)):
        lin = dot_n(act, w_ref[...])
        for j in range(lin.shape[1] // E):
            part = lin[:, j * E : (j + 1) * E]
            turned = part * cos + pltpu.roll(part, E // 2, 1) * sin
            o_ref[0, :, j * E : (j + 1) * E] = turned.astype(BF16)


def qkv_slot(slot, n, rank, xa, xb, gain, shift, wq, wk, wv, cos, sin, held):
    rows, half = xa.shape
    d = 2 * half
    local = wq.shape[1]
    cb = min(512, local)
    whole = lambda j, r: (0, 0)
    wspec = pl.BlockSpec((d, cb), lambda j, r: (0, j))
    tspec = pl.BlockSpec((1, rows, E), lambda j, r: (lax.rem(r[0] + slot, n), 0, 0))
    in_specs = [
        pl.BlockSpec((rows, half), whole),
        pl.BlockSpec((rows, half), whole),
        pl.BlockSpec((1, d), whole),
        pl.BlockSpec((1, d), whole),
        wspec,
        wspec,
        wspec,
        tspec,
        tspec,
    ]
    extra = [] if held is None else list(held)
    aliases = {} if held is None else {10 + i: i for i in range(4)}
    ospec = pl.BlockSpec((1, rows, cb), lambda j, r: (slot, 0, j))
    return pl.pallas_call(
        qkv_body,
        grid_spec=pltpu.PrefetchScalarGridSpec(
            num_scalar_prefetch=1,
            grid=(local // cb,),
            in_specs=in_specs + [pl.BlockSpec(memory_space=pl.ANY)] * len(extra),
            out_specs=[pl.BlockSpec((1, rows, d), lambda j, r: (slot, 0, 0)), ospec, ospec, ospec],
        ),
        out_shape=[jax.ShapeDtypeStruct((n, rows, d), BF16)]
        + [jax.ShapeDtypeStruct((n, rows, local), BF16)] * 3,
        input_output_aliases=aliases,
        compiler_params=params(),
        cost_estimate=cost(6 * rows * d * local, 6 * d * local + 4 * rows * d),
        name="qkv_slot",
    )(rank, xa, xb, gain, shift, wq, wk, wv, cos, sin, *extra)


def first_key(block, rows):
    return max(0, block - (DOC_MAX - 1 + rows - 1) // rows)


def attend_body(rank_ref, q_ref, k_ref, v_ref, dcol_ref, drow_ref, hc_ref, o_ref):
    n, rows, _ = q_ref.shape
    rank = rank_ref[0]
    head = rank_ref[1] + pl.program_id(0)
    slot = lambda b: lax.rem(b + n - rank, n)
    factor = E ** (-0.5) * LOG2E
    low = lax.broadcasted_iota(jnp.int32, (rows, rows), 0) >= lax.broadcasted_iota(
        jnp.int32, (rows, rows), 1
    )
    for b in range(n):
        q = q_ref[slot(b)]
        doc = dcol_ref[b]
        keys = range(first_key(b, rows), b + 1)
        scores = []
        for c in keys:
            s = dot_t(q, k_ref[slot(c)])
            ok = doc == drow_ref[c]
            if c == b:
                ok = ok & low
            scores.append(jnp.where(ok, s, -1e30))
        top = scores[0]
        for s in scores[1:]:
            top = jnp.maximum(top, s)
        top = jnp.max(top, axis=1, keepdims=True)
        total = None
        out = None
        for c, s in zip(keys, scores):
            p = jnp.exp2((s - top) * factor)
            total = p if total is None else total + p
            o = dot_n(p.astype(BF16), v_ref[slot(c)])
            out = o if out is None else out + o
        total = jnp.sum(total, axis=1, keepdims=True)
        gate = jnp.where(hc_ref[b] > head, 1.0, 0.0)
        o_ref[slot(b)] = (out * (gate / total)).astype(BF16)


def attend(rank, q, k, v, docs_col, docs_row, heads_col):
    n, rows, local = q.shape
    spec = pl.BlockSpec((n, rows, E), lambda h, r: (0, 0, h))
    col = pl.BlockSpec((n, rows, 1), lambda h, r: (0, 0, 0))
    row = pl.BlockSpec((n, 1, rows), lambda h, r: (0, 0, 0))
    t = n * rows
    return pl.pallas_call(
        attend_body,
        grid_spec=pltpu.PrefetchScalarGridSpec(
            num_scalar_prefetch=1,
            grid=(local // E,),
            in_specs=[spec, spec, spec, col, row, col],
            out_specs=spec,
        ),
        out_shape=jax.ShapeDtypeStruct((n, rows, local), BF16),
        compiler_params=params(),
        cost_estimate=cost(4 * t * t * local, 8 * t * local, t * t * local // E),
        name="attend",
    )(rank, q, k, v, docs_col, docs_row, heads_col)


def attend_back_body(
    rank_ref, q_ref, k_ref, v_ref, do_ref, dcol_ref, drow_ref, hc_ref, cos_ref, sin_ref, out_ref, dk_ref, dv_ref
):
    n, rows, _ = q_ref.shape
    rank = rank_ref[0]
    head = rank_ref[1] + pl.program_id(0)
    slot = lambda b: lax.rem(b + n - rank, n)
    scale = E ** (-0.5)
    factor = scale * LOG2E
    low = lax.broadcasted_iota(jnp.int32, (rows, rows), 0) <= lax.broadcasted_iota(
        jnp.int32, (rows, rows), 1
    )
    local = out_ref.shape[2] // 3
    lanes = lambda i: pl.ds(pl.multiple_of(i * local + pl.program_id(0) * E, E), E)
    dk_ref[...] = jnp.zeros_like(dk_ref)
    dv_ref[...] = jnp.zeros_like(dv_ref)

    def unrotate(w, b):
        w = w * scale
        return (w * cos_ref[b] - pltpu.roll(w, E // 2, 1) * sin_ref[b]).astype(BF16)

    for b in range(n):
        q = q_ref[slot(b)]
        grad = jnp.where(hc_ref[b] > head, do_ref[slot(b)].astype(F32), 0.0).astype(BF16)
        keys = range(first_key(b, rows), b + 1)
        scores = []
        for c in keys:
            s = dot_t(k_ref[slot(c)], q)
            ok = dcol_ref[c] == drow_ref[b]
            if c == b:
                ok = ok & low
            scores.append(jnp.where(ok, s, -1e30))
        top = scores[0]
        for s in scores[1:]:
            top = jnp.maximum(top, s)
        top = jnp.max(top, axis=0, keepdims=True)
        probs = [jnp.exp2((s - top) * factor) for s in scores]
        total = probs[0]
        for p in probs[1:]:
            total = total + p
        inv = 1.0 / jnp.sum(total, axis=0, keepdims=True)
        probs = [p * inv for p in probs]
        dprobs = [dot_t(v_ref[slot(c)], grad) for c in keys]
        delta = None
        for p, g in zip(probs, dprobs):
            delta = p * g if delta is None else delta + p * g
        delta = jnp.sum(delta, axis=0, keepdims=True)
        dq = None
        for c, p, g in zip(keys, probs, dprobs):
            ds = (p * (g - delta)).astype(BF16)
            dk_ref[c] += dot_n(ds, q)
            dv_ref[c] += dot_n(p.astype(BF16), grad)
            part = outer(ds, k_ref[slot(c)])
            dq = part if dq is None else dq + part
        out_ref[slot(b), :, lanes(0)] = unrotate(dq, b)
    for b in range(n):
        out_ref[slot(b), :, lanes(1)] = unrotate(dk_ref[b], b)
        out_ref[slot(b), :, lanes(2)] = dv_ref[b].astype(BF16)


def attend_back(rank, q, k, v, do, docs_col, docs_row, heads_col, cos, sin):
    n, rows, local = q.shape
    spec = pl.BlockSpec((n, rows, E), lambda h, r: (0, 0, h))
    col = pl.BlockSpec((n, rows, 1), lambda h, r: (0, 0, 0))
    row = pl.BlockSpec((n, 1, rows), lambda h, r: (0, 0, 0))
    table = pl.BlockSpec((n, rows, E), lambda h, r: (0, 0, 0))
    t = n * rows
    return pl.pallas_call(
        attend_back_body,
        grid_spec=pltpu.PrefetchScalarGridSpec(
            num_scalar_prefetch=1,
            grid=(local // E,),
            in_specs=[spec, spec, spec, spec, col, row, col, table, table],
            out_specs=pl.BlockSpec((n, rows, 3 * local), lambda h, r: (0, 0, 0)),
            scratch_shapes=[pltpu.VMEM((n, rows, E), F32), pltpu.VMEM((n, rows, E), F32)],
        ),
        out_shape=jax.ShapeDtypeStruct((n, rows, 3 * local), BF16),
        compiler_params=params(),
        cost_estimate=cost(230e9, 14 * t * local),
        name="attend_back",
    )(rank, q, k, v, do, docs_col, docs_row, heads_col, cos, sin)


def mlp_body(slot, n, rank_ref, a_ref, gl_ref, gr_ref, up_ref, down_ref, bucket_ref, *rest):
    r_ref, du_ref, aa_ref, ga_ref = rest[-4:]
    rows, cb = a_ref.shape[0], up_ref.shape[1]

    @pl.when(pl.program_id(0) == 0)
    def _():
        aa_ref[0] = a_ref[...]
        ahead = rank_ref[0] + slot < n


        @pl.when(ahead)
        def _():
            ga_ref[0] = gl_ref[...]

        @pl.when(jnp.logical_not(ahead))
        def _():
            ga_ref[0] = gr_ref[...]

    u = dot_n(a_ref[...], up_ref[...])
    dr = dot_n(ga_ref[0], down_ref[...]).astype(BF16).astype(F32)
    column = rank_ref[2] + pl.program_id(0) * cb + lax.broadcasted_iota(jnp.int32, (rows, cb), 1)
    lifted = jnp.where(column < (bucket_ref[0] + 1) * (FF // 4), jnp.maximum(u, 0.0), 0.0)
    r_ref[0] = (lifted * lifted).astype(BF16)
    du_ref[0] = (dr * (2.0 * lifted)).astype(BF16)


def mlp_slot(slot, n, rank, act, grads, up, down, bucket_col, held):
    rows, d = act.shape
    hidden = up.shape[1]
    cb = min(512, hidden)
    whole = lambda j, r: (0, 0)
    wspec = pl.BlockSpec((d, cb), lambda j, r: (0, j))
    extra = [] if held is None else list(held)
    aliases = {} if held is None else {7 + i: i for i in range(4)}
    ospec = pl.BlockSpec((1, rows, cb), lambda j, r: (slot, 0, j))
    aspec = pl.BlockSpec((1, rows, d), lambda j, r: (slot, 0, 0))
    return pl.pallas_call(
        functools.partial(mlp_body, slot, n),
        grid_spec=pltpu.PrefetchScalarGridSpec(
            num_scalar_prefetch=1,
            grid=(hidden // cb,),
            in_specs=[
                pl.BlockSpec((rows, d), whole),
            ]
            + [pl.BlockSpec((rows, d), whole)] * 2
            + [
                wspec,
                wspec,
                pl.BlockSpec((1, rows, 1), lambda j, r: (lax.rem(r[0] + slot, n), 0, 0)),
            ]
            + [pl.BlockSpec(memory_space=pl.ANY)] * len(extra),
            out_specs=[ospec, ospec, aspec, aspec],
        ),
        out_shape=[jax.ShapeDtypeStruct((n, rows, hidden), BF16)] * 2
        + [jax.ShapeDtypeStruct((n, rows, d), BF16)] * 2,
        input_output_aliases=aliases,
        compiler_params=params(),
        cost_estimate=cost(4 * rows * d * hidden, 4 * d * hidden + 4 * rows * (d + hidden)),
        name="mlp_slot",
    )(rank, act, *grads, up, down, bucket_col, *extra)


def dom_body(n, slots, rank_ref, slot_ref, *refs):
    dom_ref, all_ref = refs[-2:]
    count = sum(1 if s == 0 else 2 for s in slots)
    flows, w_ref = list(refs[:count]), refs[count]

    def fill(ref):
        all_ref[0] = ref[...]

    for i, s in enumerate(slots):
        here = pl.program_id(0) == i
        if s == 0:
            pl.when(here)(functools.partial(fill, flows[0]))
            flows = flows[1:]
        else:
            ahead = rank_ref[0] + s < n
            pl.when(here & ahead)(functools.partial(fill, flows[0]))
            pl.when(here & jnp.logical_not(ahead))(functools.partial(fill, flows[1]))
            flows = flows[2:]
    dom_ref[0] = dot_n(all_ref[0], w_ref[...]).astype(BF16)


def dom_part(n, slots, rank, flows, weight, held):
    rows, d = flows[0].shape
    local = weight.shape[1]
    whole = lambda i, r, s: (0, 0)
    extra = [] if held is None else list(held)
    at = 2 + len(flows) + 1
    return pl.pallas_call(
        functools.partial(dom_body, n, slots),
        grid_spec=pltpu.PrefetchScalarGridSpec(
            num_scalar_prefetch=2,
            grid=(len(slots),),
            in_specs=[pl.BlockSpec((rows, d), whole)] * len(flows)
            + [pl.BlockSpec((d, local), whole)]
            + [pl.BlockSpec(memory_space=pl.ANY)] * len(extra),
            out_specs=[
                pl.BlockSpec((1, rows, local), lambda i, r, s: (s[i], 0, 0)),
                pl.BlockSpec((1, rows, d), lambda i, r, s: (s[i], 0, 0)),
            ],
        ),
        out_shape=[
            jax.ShapeDtypeStruct((n, rows, local), BF16),
            jax.ShapeDtypeStruct((n, rows, d), BF16),
        ],
        input_output_aliases={at + i: i for i in range(len(extra))},
        compiler_params=params(),
        cost_estimate=cost(
            2 * len(slots) * rows * d * local, 2 * d * local + 6 * len(slots) * rows * d
        ),
        name="dom_part",
    )(rank, jnp.asarray(slots, jnp.int32), *flows, weight, *extra)


def grad_body(lhs_ref, rhs_ref, *rest):
    rest[-1][0] = outer(lhs_ref[...], rhs_ref[...]).astype(BF16)


def grad_part(which, lhs, rhs, held):
    t, d = lhs.shape
    width = rhs.shape[1]
    tile = min(512, d)
    extra = [] if held is None else [held]
    return pl.pallas_call(
        grad_body,
        grid=(d // tile,),
        in_specs=[
            pl.BlockSpec((t, tile), lambda j: (0, j)),
            pl.BlockSpec((t, width), lambda j: (0, 0)),
        ]
        + [pl.BlockSpec(memory_space=pl.ANY)] * len(extra),
        out_specs=pl.BlockSpec((1, tile, width), lambda j: (which, j, 0)),
        out_shape=jax.ShapeDtypeStruct((2, d, width), BF16),
        input_output_aliases={2: 0} if extra else {},
        compiler_params=params(),
        cost_estimate=cost(2 * t * d * width, 2 * t * (d + width) + 2 * d * width),
        name="grad_part",
    )(lhs, rhs, *extra)


def attn_grad_body(a_ref, s_ref, dqkv_ref, om_ref, out_ref):
    wide = dqkv_ref.shape[1]
    out_ref[:, :wide] = outer(a_ref[...], dqkv_ref[...]).astype(BF16)
    out_ref[:, wide:] = outer(s_ref[...], om_ref[...]).astype(BF16)


def attn_grads(act, states, dqkv, om):
    t, d = act.shape
    local = om.shape[1]
    tile = min(512, d)
    col = pl.BlockSpec((t, tile), lambda j: (0, j))
    return pl.pallas_call(
        attn_grad_body,
        grid=(d // tile,),
        in_specs=[
            col,
            col,
            pl.BlockSpec((t, 3 * local), lambda j: (0, 0)),
            pl.BlockSpec((t, local), lambda j: (0, 0)),
        ],
        out_specs=pl.BlockSpec((tile, 4 * local), lambda j: (j, 0)),
        out_shape=jax.ShapeDtypeStruct((d, 4 * local), BF16),
        compiler_params=params(),
        cost_estimate=cost(8 * t * d * local, 2 * t * (2 * d + 4 * local) + 8 * d * local),
        name="attn_grads",
    )(act, states, dqkv, om)


def join_body(slot, first, rank_ref, moved_ref, term_ref, out_ref):
    adds = rank_ref[0] < first if slot >= 0 else rank_ref[0] >= first

    @pl.when(adds)
    def _():
        out_ref[...] = (moved_ref[...].astype(F32) + term_ref[0].astype(F32)).astype(BF16)

    @pl.when(jnp.logical_not(adds))
    def _():
        out_ref[...] = moved_ref[...]


def join(rank, moved, terms, slot, first, right):
    rows, d = moved.shape
    tile = min(64, rows)
    row = pl.BlockSpec((tile, d), lambda i, r: (i, 0))
    return pl.pallas_call(
        functools.partial(join_body, 0 if right else -1, first),
        grid_spec=pltpu.PrefetchScalarGridSpec(
            num_scalar_prefetch=1,
            grid=(rows // tile,),
            in_specs=[row, pl.BlockSpec((1, tile, d), lambda i, r: (slot, i, 0))],
            out_specs=row,
        ),
        out_shape=jax.ShapeDtypeStruct((rows, d), BF16),
        compiler_params=params(),
        cost_estimate=cost(rows * d, 6 * rows * d),
        name="join",
    )(rank, moved, terms)


def last_body(x_ref, gain_ref, term_ref, moved_ref, state_ref, out_ref):
    gain = gain_ref[...]
    _, normed, inverse = norm_forward(x_ref[...].astype(F32), gain, gain)
    back = norm_backward(term_ref[...].astype(F32) + moved_ref[...].astype(F32), normed, inverse, gain)
    out_ref[...] = (state_ref[...] + back).astype(BF16)


def last_step(x, gain, term, moved, state):
    rows, d = x.shape
    tile = min(64, rows)
    row = lambda w: pl.BlockSpec((tile, w), lambda i: (i, 0))
    return pl.pallas_call(
        last_body,
        grid=(rows // tile,),
        in_specs=[row(d), pl.BlockSpec((1, d), lambda i: (0, 0)), row(d), row(d), row(d)],
        out_specs=row(d),
        out_shape=jax.ShapeDtypeStruct((rows, d), BF16),
        compiler_params=params(),
        cost_estimate=cost(73e9, 12 * rows * d),
        name="last_step",
    )(x, gain, term, moved, state)


def tie(values, *others):
    values = tuple(values)
    return lax.optimization_barrier(values + others)[: len(values)]


def sum_over(vec, axis, moves):
    return sum((lax.ppermute(vec, axis, pairs) for pairs in moves), vec)


def per_device(
    n,
    n_dp,
    tokens,
    mixed_grad,
    doc_ids,
    head_count,
    width_bucket,
    first_gain,
    first_shift,
    query_weight,
    key_weight,
    value_weight,
    output_weight,
    second_gain,
    second_shift,
    up_weight,
    down_weight,
):
    rank = lax.axis_index("mp")
    rows, d = tokens.shape[1:]
    half = d // 2
    local = query_weight.shape[1]
    local_heads = local // E
    hidden = up_weight.shape[1]
    length = n * rows
    own = tokens[0]
    send = lambda v, pairs: lax.ppermute(v, "mp", pairs)
    ring = [(i, (i - 1) % n) for i in range(n)]
    hop = lambda v: send(v, ring)
    right_line = [(i, i + 1) for i in range(n - 1)]
    left_line = [(i + 1, i) for i in range(n - 1)]

    def tick(k, right, left, terms):
        if k:
            right = join(where, right, terms, n - k, k, True)
            left = join(where, left, terms, k, n - k, False)
        return send(right, right_line), send(left, left_line)

    def owned(terms, right, left):
        return terms[0].astype(F32) + right.astype(F32) + left.astype(F32)

    low = lambda v: v.astype(BF16)
    flat = lambda v: v.reshape(length, v.shape[-1])
    add = lambda t, moved: (t.astype(F32) + moved.astype(F32)).astype(BF16)

    where = jnp.stack([rank, rank * local_heads, rank * hidden]).astype(jnp.int32)
    docs_col = doc_ids.reshape(n, rows, 1)
    docs_row = doc_ids.reshape(n, 1, rows)
    heads_col = head_count.reshape(n, rows, 1)
    bucket_col = width_bucket.reshape(n, rows, 1)
    cos, sin = (t.reshape(n, rows, E) for t in rotary_tables(length))
    gain1, shift1 = first_gain[None], first_shift[None]
    gain2, shift2 = second_gain[None], second_shift[None]

    held, block = None, [own[:, :half], own[:, half:]]
    for s in range(n):
        after = [None, None]
        for p in range(2):
            if s >= 1:
                block[p], *held = tie([block[p]] + list(held))
            if s < n - 1:
                after[p] = hop(block[p])
        held = qkv_slot(
            s, n, where, *block, gain1, shift1, query_weight, key_weight, value_weight, cos, sin, held
        )
        if s < n - 1:
            block = after
    first_all, query, keys, vals = held

    grad_own = mixed_grad[0]
    (right,) = tie([grad_own], block[0])
    left = right
    grads_r, grads_l = [right], [left]
    right, left = tick(0, right, left, None)
    masked = attend(where, query, keys, vals, docs_col, docs_row, heads_col)
    terms = low(dot_t(flat(masked), output_weight)).reshape(n, rows, d)
    for k in range(1, n):
        grads_r.append(right)
        grads_l.append(left)
        right, left = tick(k, right, left, terms)
    attn = owned(terms, right, left)
    x_rows = own.astype(F32)
    state = x_rows + attn
    second_out, normed_two, inverse_two = norm_forward(state, gain2, shift2)

    weights = jnp.concatenate([query_weight, key_weight, value_weight], axis=1)
    held, moved = None, None
    (block,) = tie([low(second_out)], weights)
    for s in range(n):
        if s >= 1:
            block, *held = tie([block] + list(held) + ([term0] if s == n - 1 else []))
            if s == n - 1:
                term0, held = held[-1], held[:-1]
        after = hop(block) if s < n - 1 else None
        held = mlp_slot(
            s, n, where, block, [grads_l[s], grads_r[n - s if s else 0]], up_weight, down_weight, bucket_col, held
        )
        if s >= 1:
            term = dot_t(held[1][s], up_weight)
            if s > 1:
                (term,) = tie([term])
            sent = low(term) if moved is None else add(term, moved)
            moved = hop(sent)
        else:
            term0 = dot_t(held[1][0], up_weight)
        block = after
    active, grad_upper, second_all, grad_all = held
    grad_all, active = tie([grad_all, active], sent)
    pair = grad_part(0, flat(grad_all), flat(active), None)
    (active,) = tie([active], pair)
    ffn = low(dot_t(flat(active), down_weight)).reshape(n, rows, d)
    (moved,) = tie([moved], ffn)
    grad_second = term0 + moved.astype(F32)
    back_two = norm_backward(grad_second, normed_two, inverse_two, gain2)
    second_gain_part = jnp.sum(grad_second * normed_two, axis=0)
    second_shift_part = jnp.sum(grad_second, axis=0)
    grad_state = grad_own.astype(F32) + back_two

    start = low(grad_state)
    second_all, grad_upper, start = tie([second_all, grad_upper, start])
    right = left = start
    rights, lefts = [start], [start]
    right, left = tick(0, right, left, None)
    pair = grad_part(1, flat(second_all), flat(grad_upper), pair)
    wide_grad = lax.psum_scatter(pair, "dp", scatter_dimension=1, tiled=True)
    right, left = tie([right, left], pair)
    for k in range(1, n):
        rights.append(right)
        lefts.append(left)
        right, left = tick(k, right, left, ffn)
    late = sorted({1, n - 1})
    early = [s for s in range(n) if s not in late]
    pick = lambda slots: sum(([start] if s == 0 else [lefts[s], rights[n - s]] for s in slots), [])
    held = dom_part(n, early, where, pick(early), output_weight, None)
    grad_masked, state_all = dom_part(n, late, where, pick(late), output_weight, held)
    dqkv = attend_back(
        where, query, keys, vals, grad_masked, docs_col, docs_row, heads_col, cos, sin
    )
    mixed = low(state + owned(ffn, right, left))

    (dqkv,) = tie([dqkv], right, left)
    sent = low(dot_t(dqkv[1], weights))
    (dqkv,) = tie([dqkv], sent)
    moved = hop(sent)
    attn_term = attn_grads(flat(first_all), flat(state_all), flat(dqkv), flat(masked))
    (dqkv,) = tie([dqkv], attn_term)
    terms = low(dot_t(flat(dqkv), weights)).reshape(n, rows, d)
    sum_d = jnp.sum(terms.astype(F32), axis=(0, 1))
    sum_da = jnp.sum(terms.astype(F32) * first_all.astype(F32), axis=(0, 1))
    (late,) = tie([attn_term], wide_grad)
    attn_grad = lax.psum_scatter(late, "dp", scatter_dimension=0, tiled=True)
    (moved,) = tie([moved], terms)
    first_shift_part = sum_d
    first_gain_part = (sum_da - first_shift * sum_d) / first_gain

    lead = (rank == 0).astype(F32)
    bucket_part = lead * jnp.sum(
        (width_bucket[0][:, None] == jnp.arange(4, dtype=jnp.int32)[None, :]).astype(F32), axis=0
    )
    head_part = lead * jnp.sum(
        (head_count[0][:, None] == jnp.arange(1, HEADS + 1, dtype=jnp.int32)[None, :]).astype(F32),
        axis=0,
    )
    small = jnp.concatenate(
        [
            first_gain_part,
            first_shift_part,
            second_gain_part,
            second_shift_part,
            bucket_part,
            head_part,
            jnp.zeros((128 - 4 - HEADS,), F32),
        ]
    )
    small = sum_over(small, "dp", [[(i, i ^ 1) for i in range(n_dp)]])
    for s in range(2, n):
        sent = add(terms[s], moved)
        if s == 2:
            first_sent = sent
        moved = hop(sent)
    if n == 2:
        first_sent = sent

    planes = tie([send(small, [(i, (i + m) % n) for i in range(n)]) for m in range(1, n)], first_sent)
    small = small + sum(planes)
    others = [
        lax.ppermute(small, "dp", [(i, (i + 2 * m) % n_dp) for i in range(n_dp)])
        for m in range(1, n_dp // 2)
    ]
    input_grad = last_step(own, gain1, terms[0], moved, grad_state)
    small = small + sum(tie(others, input_grad))
    wide_grad, attn_grad = wide_grad.astype(F32), attn_grad.astype(F32)
    return (
        mixed[None],
        input_grad[None],
        small[:d],
        small[d : 2 * d],
        attn_grad[:, :local],
        attn_grad[:, local : 2 * local],
        attn_grad[:, 2 * local : 3 * local],
        attn_grad[:, 3 * local :],
        small[2 * d : 3 * d],
        small[3 * d : 4 * d],
        wide_grad[1],
        wide_grad[0],
        small[4 * d : 4 * d + 4].astype(jnp.int32),
        small[4 * d + 4 : 4 * d + 4 + HEADS].astype(jnp.int32),
    )


def solution(mesh):
    token, seq, copy, col = P("dp", "mp", None), P("dp", None), P(), P(None, "mp")
    grad = P("dp", "mp")
    return jax.shard_map(
        functools.partial(per_device, mesh.shape["mp"], mesh.shape["dp"]),
        mesh=mesh,
        in_specs=(token, token, seq, seq, seq, copy, copy, col, col, col, col, copy, copy, col, col),
        out_specs=(token, token, copy, copy, grad, grad, grad, grad, copy, copy, grad, grad, copy, copy),
        check_vma=False,
    )
```

```python
import functools
import jax
import jax.numpy as jnp
from jax import lax
from jax.experimental import pallas as pl
from jax.experimental.pallas import tpu as pltpu
from jax.sharding import PartitionSpec as P

HEADS = 16
E = 128
FF = 8192
EPS = 1e-05
DOC_MAX = 512
LOG2E = 1.4426950408889634
F32 = jnp.float32
BF16 = jnp.bfloat16


def params(mib):
    return pltpu.CompilerParams(vmem_limit_bytes=mib << 20)


def cost(flops, nbytes, trans=0):
    return pl.CostEstimate(flops=int(flops), bytes_accessed=int(nbytes), transcendentals=int(trans))


def norm_forward(values, gain, shift):
    mean = jnp.mean(values, axis=-1, keepdims=True)
    cent = values - mean
    inverse = lax.rsqrt(jnp.mean(cent * cent, axis=-1, keepdims=True) + EPS)
    normed = cent * inverse
    return (normed * gain + shift, normed, inverse)


def norm_backward(grad_out, normed, inverse, gain):
    scaled = grad_out * gain
    return inverse * (
        scaled
        - jnp.mean(scaled, axis=-1, keepdims=True)
        - normed * jnp.mean(scaled * normed, axis=-1, keepdims=True)
    )


def rotary_tables(length):
    half = E // 2
    freq = 10000.0 ** (-(jnp.arange(half, dtype=F32) * 2.0 / E))
    angle = jnp.arange(length, dtype=F32)[:, None] * freq[None, :]
    cos, sin = jnp.cos(angle), jnp.sin(angle)
    return jnp.concatenate([cos, cos], axis=1), jnp.concatenate([-sin, sin], axis=1)


def dot_t(left, right):
    return lax.dot_general(left, right, (((1,), (1,)), ((), ())), preferred_element_type=F32)


def dot_n(left, right):
    return lax.dot_general(left, right, (((1,), (0,)), ((), ())), preferred_element_type=F32)


def outer(left, right):
    return lax.dot_general(left, right, (((0,), (0,)), ((), ())), preferred_element_type=F32)


def qkv_body(rank_ref, xa_ref, xb_ref, gain_ref, shift_ref, wq_ref, wk_ref, wv_ref, cos_ref, sin_ref, *rest):
    a_ref, q_ref, k_ref, v_ref = rest[-4:]

    @pl.when(pl.program_id(0) == 0)
    def _():
        x = jnp.concatenate([xa_ref[...], xb_ref[...]], axis=1).astype(F32)
        out, _, _ = norm_forward(x, gain_ref[...], shift_ref[...])
        a_ref[0] = out.astype(BF16)

    act = a_ref[0]
    cos, sin = cos_ref[0], sin_ref[0]
    v_ref[0] = dot_n(act, wv_ref[...]).astype(BF16)
    for w_ref, o_ref in ((wq_ref, q_ref), (wk_ref, k_ref)):
        lin = dot_n(act, w_ref[...])
        for j in range(lin.shape[1] // E):
            part = lin[:, j * E : (j + 1) * E]
            turned = part * cos + pltpu.roll(part, E // 2, 1) * sin
            o_ref[0, :, j * E : (j + 1) * E] = turned.astype(BF16)


def qkv_slot(slot, n, rank, xa, xb, gain, shift, wq, wk, wv, cos, sin, held):
    rows, half = xa.shape
    d = 2 * half
    local = wq.shape[1]
    cb = min(512, local)
    whole = lambda j, r: (0, 0)
    wspec = pl.BlockSpec((d, cb), lambda j, r: (0, j))
    tspec = pl.BlockSpec((1, rows, E), lambda j, r: (lax.rem(r[0] + slot, n), 0, 0))
    in_specs = [
        pl.BlockSpec((rows, half), whole),
        pl.BlockSpec((rows, half), whole),
        pl.BlockSpec((1, d), whole),
        pl.BlockSpec((1, d), whole),
        wspec,
        wspec,
        wspec,
        tspec,
        tspec,
    ]
    extra = [] if held is None else list(held)
    aliases = {} if held is None else {10 + i: i for i in range(4)}
    ospec = pl.BlockSpec((1, rows, cb), lambda j, r: (slot, 0, j))
    return pl.pallas_call(
        qkv_body,
        grid_spec=pltpu.PrefetchScalarGridSpec(
            num_scalar_prefetch=1,
            grid=(local // cb,),
            in_specs=in_specs + [pl.BlockSpec(memory_space=pl.ANY)] * len(extra),
            out_specs=[pl.BlockSpec((1, rows, d), lambda j, r: (slot, 0, 0)), ospec, ospec, ospec],
        ),
        out_shape=[jax.ShapeDtypeStruct((n, rows, d), BF16)]
        + [jax.ShapeDtypeStruct((n, rows, local), BF16)] * 3,
        input_output_aliases=aliases,
        compiler_params=params(28),
        cost_estimate=cost(6 * rows * d * local, 6 * d * local + 4 * rows * d),
        name="qkv_slot",
    )(rank, xa, xb, gain, shift, wq, wk, wv, cos, sin, *extra)


def first_key(block, rows):
    return max(0, block - (DOC_MAX - 1 + rows - 1) // rows)


def attend_body(rank_ref, q_ref, k_ref, v_ref, dcol_ref, drow_ref, hc_ref, o_ref):
    n, rows, _ = q_ref.shape
    rank = rank_ref[0]
    head = rank_ref[1] + pl.program_id(0)
    slot = lambda b: lax.rem(b + n - rank, n)
    factor = E ** (-0.5) * LOG2E
    low = lax.broadcasted_iota(jnp.int32, (rows, rows), 0) >= lax.broadcasted_iota(
        jnp.int32, (rows, rows), 1
    )
    for b in range(n):
        q = q_ref[slot(b)]
        doc = dcol_ref[b]
        keys = range(first_key(b, rows), b + 1)
        scores = []
        for c in keys:
            s = dot_t(q, k_ref[slot(c)])
            ok = doc == drow_ref[c]
            if c == b:
                ok = ok & low
            scores.append(jnp.where(ok, s, -1e30))
        top = scores[0]
        for s in scores[1:]:
            top = jnp.maximum(top, s)
        top = jnp.max(top, axis=1, keepdims=True)
        total = None
        out = None
        for c, s in zip(keys, scores):
            p = jnp.exp2((s - top) * factor)
            total = p if total is None else total + p
            o = dot_n(p.astype(BF16), v_ref[slot(c)])
            out = o if out is None else out + o
        total = jnp.sum(total, axis=1, keepdims=True)
        gate = jnp.where(hc_ref[b] > head, 1.0, 0.0)
        o_ref[slot(b)] = (out * (gate / total)).astype(BF16)


def attend(rank, q, k, v, docs_col, docs_row, heads_col):
    n, rows, local = q.shape
    spec = pl.BlockSpec((n, rows, E), lambda h, r: (0, 0, h))
    col = pl.BlockSpec((n, rows, 1), lambda h, r: (0, 0, 0))
    row = pl.BlockSpec((n, 1, rows), lambda h, r: (0, 0, 0))
    t = n * rows
    return pl.pallas_call(
        attend_body,
        grid_spec=pltpu.PrefetchScalarGridSpec(
            num_scalar_prefetch=1,
            grid=(local // E,),
            in_specs=[spec, spec, spec, col, row, col],
            out_specs=spec,
        ),
        out_shape=jax.ShapeDtypeStruct((n, rows, local), BF16),
        compiler_params=params(16),
        cost_estimate=cost(4 * t * t * local, 8 * t * local, t * t * local // E),
        name="attend",
    )(rank, q, k, v, docs_col, docs_row, heads_col)


def attend_back_body(
    rank_ref, q_ref, k_ref, v_ref, do_ref, dcol_ref, drow_ref, hc_ref, cos_ref, sin_ref, out_ref, dk_ref, dv_ref
):
    n, rows, _ = q_ref.shape
    rank = rank_ref[0]
    head = rank_ref[1] + pl.program_id(0)
    slot = lambda b: lax.rem(b + n - rank, n)
    scale = E ** (-0.5)
    factor = scale * LOG2E
    low = lax.broadcasted_iota(jnp.int32, (rows, rows), 0) <= lax.broadcasted_iota(
        jnp.int32, (rows, rows), 1
    )
    local = out_ref.shape[2] // 3
    lanes = lambda i: pl.ds(pl.multiple_of(i * local + pl.program_id(0) * E, E), E)
    dk_ref[...] = jnp.zeros_like(dk_ref)
    dv_ref[...] = jnp.zeros_like(dv_ref)

    def unrotate(w, b):
        w = w * scale
        return (w * cos_ref[b] - pltpu.roll(w, E // 2, 1) * sin_ref[b]).astype(BF16)

    for b in range(n):
        q = q_ref[slot(b)]
        grad = jnp.where(hc_ref[b] > head, do_ref[slot(b)].astype(F32), 0.0).astype(BF16)
        keys = range(first_key(b, rows), b + 1)
        scores = []
        for c in keys:
            s = dot_t(k_ref[slot(c)], q)
            ok = dcol_ref[c] == drow_ref[b]
            if c == b:
                ok = ok & low
            scores.append(jnp.where(ok, s, -1e30))
        top = scores[0]
        for s in scores[1:]:
            top = jnp.maximum(top, s)
        top = jnp.max(top, axis=0, keepdims=True)
        probs = [jnp.exp2((s - top) * factor) for s in scores]
        total = probs[0]
        for p in probs[1:]:
            total = total + p
        inv = 1.0 / jnp.sum(total, axis=0, keepdims=True)
        probs = [p * inv for p in probs]
        dprobs = [dot_t(v_ref[slot(c)], grad) for c in keys]
        delta = None
        for p, g in zip(probs, dprobs):
            delta = p * g if delta is None else delta + p * g
        delta = jnp.sum(delta, axis=0, keepdims=True)
        dq = None
        for c, p, g in zip(keys, probs, dprobs):
            ds = (p * (g - delta)).astype(BF16)
            dk_ref[c] += dot_n(ds, q)
            dv_ref[c] += dot_n(p.astype(BF16), grad)
            part = outer(ds, k_ref[slot(c)])
            dq = part if dq is None else dq + part
        out_ref[slot(b), :, lanes(0)] = unrotate(dq, b)
    for b in range(n):
        out_ref[slot(b), :, lanes(1)] = unrotate(dk_ref[b], b)
        out_ref[slot(b), :, lanes(2)] = dv_ref[b].astype(BF16)


def attend_back(rank, q, k, v, do, docs_col, docs_row, heads_col, cos, sin):
    n, rows, local = q.shape
    spec = pl.BlockSpec((n, rows, E), lambda h, r: (0, 0, h))
    col = pl.BlockSpec((n, rows, 1), lambda h, r: (0, 0, 0))
    row = pl.BlockSpec((n, 1, rows), lambda h, r: (0, 0, 0))
    table = pl.BlockSpec((n, rows, E), lambda h, r: (0, 0, 0))
    t = n * rows
    return pl.pallas_call(
        attend_back_body,
        grid_spec=pltpu.PrefetchScalarGridSpec(
            num_scalar_prefetch=1,
            grid=(local // E,),
            in_specs=[spec, spec, spec, spec, col, row, col, table, table],
            out_specs=pl.BlockSpec((n, rows, 3 * local), lambda h, r: (0, 0, 0)),
            scratch_shapes=[pltpu.VMEM((n, rows, E), F32), pltpu.VMEM((n, rows, E), F32)],
        ),
        out_shape=jax.ShapeDtypeStruct((n, rows, 3 * local), BF16),
        compiler_params=params(24),
        cost_estimate=cost(108e9, 14 * t * local),
        name="attend_back",
    )(rank, q, k, v, do, docs_col, docs_row, heads_col, cos, sin)


def mlp_body(slot, n, rank_ref, a_ref, gl_ref, gr_ref, up_ref, down_ref, bucket_ref, *rest):
    r_ref, du_ref, aa_ref, ga_ref = rest[-4:]
    rows, cb = a_ref.shape[0], up_ref.shape[1]

    @pl.when(pl.program_id(0) == 0)
    def _():
        aa_ref[0] = a_ref[...]
        ahead = rank_ref[0] + slot < n


        @pl.when(ahead)
        def _():
            ga_ref[0] = gl_ref[...]

        @pl.when(jnp.logical_not(ahead))
        def _():
            ga_ref[0] = gr_ref[...]

    u = dot_n(a_ref[...], up_ref[...])
    dr = dot_n(ga_ref[0], down_ref[...]).astype(BF16).astype(F32)
    column = rank_ref[2] + pl.program_id(0) * cb + lax.broadcasted_iota(jnp.int32, (rows, cb), 1)
    lifted = jnp.where(column < (bucket_ref[0] + 1) * (FF // 4), jnp.maximum(u, 0.0), 0.0)
    r_ref[0] = (lifted * lifted).astype(BF16)
    du_ref[0] = (dr * (2.0 * lifted)).astype(BF16)


def mlp_slot(slot, n, rank, act, grads, up, down, bucket_col, held):
    rows, d = act.shape
    hidden = up.shape[1]
    cb = min(512, hidden)
    whole = lambda j, r: (0, 0)
    wspec = pl.BlockSpec((d, cb), lambda j, r: (0, j))
    extra = [] if held is None else list(held)
    aliases = {} if held is None else {7 + i: i for i in range(4)}
    ospec = pl.BlockSpec((1, rows, cb), lambda j, r: (slot, 0, j))
    aspec = pl.BlockSpec((1, rows, d), lambda j, r: (slot, 0, 0))
    return pl.pallas_call(
        functools.partial(mlp_body, slot, n),
        grid_spec=pltpu.PrefetchScalarGridSpec(
            num_scalar_prefetch=1,
            grid=(hidden // cb,),
            in_specs=[
                pl.BlockSpec((rows, d), whole),
            ]
            + [pl.BlockSpec((rows, d), whole)] * 2
            + [
                wspec,
                wspec,
                pl.BlockSpec((1, rows, 1), lambda j, r: (lax.rem(r[0] + slot, n), 0, 0)),
            ]
            + [pl.BlockSpec(memory_space=pl.ANY)] * len(extra),
            out_specs=[ospec, ospec, aspec, aspec],
        ),
        out_shape=[jax.ShapeDtypeStruct((n, rows, hidden), BF16)] * 2
        + [jax.ShapeDtypeStruct((n, rows, d), BF16)] * 2,
        input_output_aliases=aliases,
        compiler_params=params(28),
        cost_estimate=cost(4 * rows * d * hidden, 4 * d * hidden + 4 * rows * (d + hidden)),
        name="mlp_slot",
    )(rank, act, *grads, up, down, bucket_col, *extra)


def dom_body(n, slots, rank_ref, slot_ref, *refs):
    dom_ref, all_ref = refs[-2:]
    count = sum(1 if s == 0 else 2 for s in slots)
    flows, w_ref = list(refs[:count]), refs[count]

    def fill(ref):
        all_ref[0] = ref[...]

    for i, s in enumerate(slots):
        here = pl.program_id(0) == i
        if s == 0:
            pl.when(here)(functools.partial(fill, flows[0]))
            flows = flows[1:]
        else:
            ahead = rank_ref[0] + s < n
            pl.when(here & ahead)(functools.partial(fill, flows[0]))
            pl.when(here & jnp.logical_not(ahead))(functools.partial(fill, flows[1]))
            flows = flows[2:]
    dom_ref[0] = dot_n(all_ref[0], w_ref[...]).astype(BF16)


def dom_part(n, slots, rank, flows, weight, held):
    rows, d = flows[0].shape
    local = weight.shape[1]
    whole = lambda i, r, s: (0, 0)
    extra = [] if held is None else list(held)
    at = 2 + len(flows) + 1
    return pl.pallas_call(
        functools.partial(dom_body, n, slots),
        grid_spec=pltpu.PrefetchScalarGridSpec(
            num_scalar_prefetch=2,
            grid=(len(slots),),
            in_specs=[pl.BlockSpec((rows, d), whole)] * len(flows)
            + [pl.BlockSpec((d, local), whole)]
            + [pl.BlockSpec(memory_space=pl.ANY)] * len(extra),
            out_specs=[
                pl.BlockSpec((1, rows, local), lambda i, r, s: (s[i], 0, 0)),
                pl.BlockSpec((1, rows, d), lambda i, r, s: (s[i], 0, 0)),
            ],
        ),
        out_shape=[
            jax.ShapeDtypeStruct((n, rows, local), BF16),
            jax.ShapeDtypeStruct((n, rows, d), BF16),
        ],
        input_output_aliases={at + i: i for i in range(len(extra))},
        compiler_params=params(24),
        cost_estimate=cost(
            2 * len(slots) * rows * d * local, 2 * d * local + 6 * len(slots) * rows * d
        ),
        name="dom_part",
    )(rank, jnp.asarray(slots, jnp.int32), *flows, weight, *extra)


def grad_body(has_sum, rank_ref, lhs_ref, rhs_ref, *rest):
    out = outer(lhs_ref[...], rhs_ref[...])
    if has_sum:
        rest[-1][0] = (out + rest[0][...].astype(F32)).astype(BF16)
    else:
        rest[-1][...] = out.astype(BF16)


def grad_half(lhs, rhs, rank, partner, which=0, moved=None, held=None):
    t, d = lhs.shape
    half = rhs.shape[1] // 2
    tile = min(512, d)
    col = (lambda r: 1 - r[3]) if partner else (lambda r: r[3])
    specs = [
        pl.BlockSpec((t, tile), lambda j, r: (0, j)),
        pl.BlockSpec((t, half), lambda j, r: (0, col(r))),
    ]
    args = [lhs, rhs]
    aliases = {}
    if partner:
        ospec = pl.BlockSpec((tile, half), lambda j, r: (j, 0))
        oshape = (d, half)
    else:
        specs.append(pl.BlockSpec((tile, half), lambda j, r: (j, 0)))
        args.append(moved)
        ospec = pl.BlockSpec((1, tile, half), lambda j, r: (which, j, 0))
        oshape = (2, d, half)
        if held is not None:
            specs.append(pl.BlockSpec(memory_space=pl.ANY))
            args.append(held)
            aliases = {4: 0}
    return pl.pallas_call(
        functools.partial(grad_body, not partner),
        grid_spec=pltpu.PrefetchScalarGridSpec(
            num_scalar_prefetch=1, grid=(d // tile,), in_specs=specs, out_specs=ospec
        ),
        out_shape=jax.ShapeDtypeStruct(oshape, BF16),
        input_output_aliases=aliases,
        compiler_params=params(28),
        cost_estimate=cost(1e6, 1e6),
        name="grad_half",
    )(rank, *args)


def attn_grad_body(partner, rank_ref, a_ref, s_ref, one_ref, key_ref, om_ref, *rest):
    out_ref = rest[-1]
    local = om_ref.shape[1]
    second = rank_ref[3] == (0 if partner else 1)
    act = a_ref[...]

    def put(cols, value):
        if not partner:
            value = value + rest[0][:, cols].astype(F32)
        out_ref[:, cols] = value.astype(BF16)

    put(slice(0, local), outer(act, one_ref[...]))

    @pl.when(second)
    def _():
        put(slice(local, 2 * local), outer(s_ref[...], om_ref[...]))

    @pl.when(jnp.logical_not(second))
    def _():
        put(slice(local, 2 * local), outer(act, key_ref[...]))


def attn_grads(act, states, dqkv, om, rank, moved=None):
    t, d = act.shape
    local = om.shape[1]
    tile = min(512, d)
    partner = moved is None
    pos = (lambda r: 1 - r[3]) if partner else (lambda r: r[3])
    col = pl.BlockSpec((t, tile), lambda j, r: (0, j))
    out = pl.BlockSpec((tile, 2 * local), lambda j, r: (j, 0))
    return pl.pallas_call(
        functools.partial(attn_grad_body, partner),
        grid_spec=pltpu.PrefetchScalarGridSpec(
            num_scalar_prefetch=1,
            grid=(d // tile,),
            in_specs=[
                col,
                col,
                pl.BlockSpec((t, local), lambda j, r: (0, 2 * pos(r))),
                pl.BlockSpec((t, local), lambda j, r: (0, 1)),
                pl.BlockSpec((t, local), lambda j, r: (0, 0)),
            ]
            + ([] if partner else [out]),
            out_specs=out,
        ),
        out_shape=jax.ShapeDtypeStruct((d, 2 * local), BF16),
        compiler_params=params(28),
        cost_estimate=cost(4 * t * d * local, 2 * t * (2 * d + 3 * local) + 8 * d * local),
        name="attn_grads",
    )(rank, act, states, dqkv, dqkv, om, *([] if partner else [moved]))


def join_body(slot, first, rank_ref, moved_ref, term_ref, out_ref):
    adds = rank_ref[0] < first if slot >= 0 else rank_ref[0] >= first

    @pl.when(adds)
    def _():
        out_ref[...] = (moved_ref[...].astype(F32) + term_ref[0].astype(F32)).astype(BF16)

    @pl.when(jnp.logical_not(adds))
    def _():
        out_ref[...] = moved_ref[...]


def join(rank, moved, terms, slot, first, right):
    rows, d = moved.shape
    tile = min(128, rows)
    row = pl.BlockSpec((tile, d), lambda i, r: (i, 0))
    return pl.pallas_call(
        functools.partial(join_body, 0 if right else -1, first),
        grid_spec=pltpu.PrefetchScalarGridSpec(
            num_scalar_prefetch=1,
            grid=(rows // tile,),
            in_specs=[row, pl.BlockSpec((1, tile, d), lambda i, r: (slot, i, 0))],
            out_specs=row,
        ),
        out_shape=jax.ShapeDtypeStruct((rows, d), BF16),
        compiler_params=params(8),
        cost_estimate=cost(rows * d, 6 * rows * d),
        name="join",
    )(rank, moved, terms)


def last_body(x_ref, gain_ref, term_ref, moved_ref, state_ref, out_ref):
    gain = gain_ref[...]
    _, normed, inverse = norm_forward(x_ref[...].astype(F32), gain, gain)
    back = norm_backward(term_ref[...].astype(F32) + moved_ref[...].astype(F32), normed, inverse, gain)
    out_ref[...] = (state_ref[...] + back).astype(BF16)


def last_step(x, gain, term, moved, state):
    rows, d = x.shape
    tile = min(64, rows)
    row = lambda w: pl.BlockSpec((tile, w), lambda i: (i, 0))
    return pl.pallas_call(
        last_body,
        grid=(rows // tile,),
        in_specs=[row(d), pl.BlockSpec((1, d), lambda i: (0, 0)), row(d), row(d), row(d)],
        out_specs=row(d),
        out_shape=jax.ShapeDtypeStruct((rows, d), BF16),
        compiler_params=params(12),
        cost_estimate=cost(15e9, 12 * rows * d),
        name="last_step",
    )(x, gain, term, moved, state)


def tie(values, *others):
    values = tuple(values)
    return lax.optimization_barrier(values + others)[: len(values)]


def sum_over(vec, axis, moves):
    return sum((lax.ppermute(vec, axis, pairs) for pairs in moves), vec)


def per_device(
    n,
    n_dp,
    tokens,
    mixed_grad,
    doc_ids,
    head_count,
    width_bucket,
    first_gain,
    first_shift,
    query_weight,
    key_weight,
    value_weight,
    output_weight,
    second_gain,
    second_shift,
    up_weight,
    down_weight,
):
    rank = lax.axis_index("mp")
    rows, d = tokens.shape[1:]
    half = d // 2
    local = query_weight.shape[1]
    local_heads = local // E
    hidden = up_weight.shape[1]
    length = n * rows
    own = tokens[0]
    send = lambda v, pairs: lax.ppermute(v, "mp", pairs)
    ring = [(i, (i - 1) % n) for i in range(n)]
    hop = lambda v: send(v, ring)
    right_line = [(i, i + 1) for i in range(n - 1)]
    left_line = [(i + 1, i) for i in range(n - 1)]

    def tick(k, right, left, terms):
        if k:
            right = join(where, right, terms, n - k, k, True)
            left = join(where, left, terms, k, n - k, False)
        return send(right, right_line), send(left, left_line)

    def owned(terms, right, left):
        return terms[0].astype(F32) + right.astype(F32) + left.astype(F32)

    low = lambda v: v.astype(BF16)
    flat = lambda v: v.reshape(length, v.shape[-1])
    add = lambda t, moved: (t.astype(F32) + moved.astype(F32)).astype(BF16)

    side = lax.rem(lax.axis_index("dp"), 2)
    where = jnp.stack([rank, rank * local_heads, rank * hidden, side]).astype(jnp.int32)
    swap = lambda v: lax.ppermute(v, "dp", [(i, i ^ 1) for i in range(n_dp)])
    sides = [list(range(c, n_dp, 2)) for c in range(2)]
    docs_col = doc_ids.reshape(n, rows, 1)
    docs_row = doc_ids.reshape(n, 1, rows)
    heads_col = head_count.reshape(n, rows, 1)
    bucket_col = width_bucket.reshape(n, rows, 1)
    cos, sin = (t.reshape(n, rows, E) for t in rotary_tables(length))
    gain1, shift1 = first_gain[None], first_shift[None]
    gain2, shift2 = second_gain[None], second_shift[None]

    held, block = None, [own[:, :half], own[:, half:]]
    for s in range(n):
        after = [None, None]
        for p in range(2):
            if s >= 1:
                block[p], *held = tie([block[p]] + list(held))
            if s < n - 1:
                after[p] = hop(block[p])
        held = qkv_slot(
            s, n, where, *block, gain1, shift1, query_weight, key_weight, value_weight, cos, sin, held
        )
        if s < n - 1:
            block = after
    first_all, query, keys, vals = held

    grad_own = mixed_grad[0]
    (right,) = tie([grad_own], block[0])
    left = right
    grads_r, grads_l = [right], [left]
    right, left = tick(0, right, left, None)
    masked = attend(where, query, keys, vals, docs_col, docs_row, heads_col)
    terms = low(dot_t(flat(masked), output_weight)).reshape(n, rows, d)
    for k in range(1, n):
        grads_r.append(right)
        grads_l.append(left)
        right, left = tick(k, right, left, terms)
    attn = owned(terms, right, left)
    x_rows = own.astype(F32)
    state = x_rows + attn
    second_out, normed_two, inverse_two = norm_forward(state, gain2, shift2)

    weights = jnp.concatenate([query_weight, key_weight, value_weight], axis=1)
    held, moved = None, None
    (block,) = tie([low(second_out)], weights)
    for s in range(n):
        if s >= 1:
            block, *held = tie([block] + list(held) + ([term0] if s == n - 1 else []))
            if s == n - 1:
                term0, held = held[-1], held[:-1]
        after = hop(block) if s < n - 1 else None
        held = mlp_slot(
            s, n, where, block, [grads_l[s], grads_r[n - s if s else 0]], up_weight, down_weight, bucket_col, held
        )
        if s >= 1:
            term = dot_t(held[1][s], up_weight)
            if s > 1:
                (term,) = tie([term])
            sent = low(term) if moved is None else add(term, moved)
            moved = hop(sent)
        else:
            term0 = dot_t(held[1][0], up_weight)
        block = after
    active, grad_upper, second_all, grad_all = held
    grad_all, active, second_all, grad_upper = tie([grad_all, active, second_all, grad_upper], sent)
    gifts = [
        grad_half(flat(grad_all), flat(active), where, True),
        grad_half(flat(second_all), flat(grad_upper), where, True),
    ]
    (moved,) = tie([moved], *gifts)
    down_gift, up_gift = (swap(v) for v in gifts)
    grad_second = term0 + moved.astype(F32)
    back_two = norm_backward(grad_second, normed_two, inverse_two, gain2)
    second_gain_part = jnp.sum(grad_second * normed_two, axis=0)
    second_shift_part = jnp.sum(grad_second, axis=0)
    grad_state = grad_own.astype(F32) + back_two

    start = low(grad_state)
    grad_all, active, second_all, grad_upper, start = tie([grad_all, active, second_all, grad_upper, start])
    right = left = start
    rights, lefts = [start], [start]
    right, left = tick(0, right, left, None)
    ffn = low(dot_t(flat(active), down_weight)).reshape(n, rows, d)
    pair = grad_half(flat(grad_all), flat(active), where, False, 0, down_gift)
    pair = grad_half(flat(second_all), flat(grad_upper), where, False, 1, up_gift, pair)
    wide_grad = lax.psum_scatter(pair, "dp", scatter_dimension=1, axis_index_groups=sides, tiled=True)
    right, left = tie([right, left], pair)
    for k in range(1, n):
        rights.append(right)
        lefts.append(left)
        right, left = tick(k, right, left, ffn)
    late = sorted({1, n - 1})
    early = [s for s in range(n) if s not in late]
    pick = lambda slots: sum(([start] if s == 0 else [lefts[s], rights[n - s]] for s in slots), [])
    held = dom_part(n, early, where, pick(early), output_weight, None)
    grad_masked, state_all = dom_part(n, late, where, pick(late), output_weight, held)
    dqkv = attend_back(
        where, query, keys, vals, grad_masked, docs_col, docs_row, heads_col, cos, sin
    )
    mixed = low(state + owned(ffn, right, left))

    (dqkv,) = tie([dqkv], right, left)
    tokens_of = lambda v: (flat(first_all), flat(state_all), flat(v), flat(masked), where)
    gift = attn_grads(*tokens_of(dqkv))
    (dqkv,) = tie([dqkv], gift)
    gift = swap(gift)
    sent = low(dot_t(dqkv[1], weights))
    (dqkv,) = tie([dqkv], sent)
    moved = hop(sent)
    attn_term = attn_grads(*tokens_of(dqkv), gift)
    (late,) = tie([attn_term], wide_grad)
    attn_grad = lax.psum_scatter(late, "dp", scatter_dimension=0, axis_index_groups=sides, tiled=True)
    (dqkv,) = tie([dqkv], attn_term)
    terms = {s: low(dot_t(dqkv[s], weights)) for s in range(1, n)}
    (dqkv,) = tie([dqkv], terms[n - 1])
    terms[0] = low(dot_t(dqkv[0], weights))
    sum_d = sum(jnp.sum(terms[s].astype(F32), axis=0) for s in range(n))
    sum_da = sum(jnp.sum(terms[s].astype(F32) * first_all[s].astype(F32), axis=0) for s in range(n))
    first_shift_part = sum_d
    first_gain_part = (sum_da - first_shift * sum_d) / first_gain

    lead = (rank == 0).astype(F32)
    bucket_part = lead * jnp.sum(
        (width_bucket[0][:, None] == jnp.arange(4, dtype=jnp.int32)[None, :]).astype(F32), axis=0
    )
    head_part = lead * jnp.sum(
        (head_count[0][:, None] == jnp.arange(1, HEADS + 1, dtype=jnp.int32)[None, :]).astype(F32),
        axis=0,
    )
    small = jnp.concatenate(
        [
            first_gain_part,
            first_shift_part,
            second_gain_part,
            second_shift_part,
            bucket_part,
            head_part,
            jnp.zeros((128 - 4 - HEADS,), F32),
        ]
    )
    small = sum_over(small, "dp", [[(i, i ^ 1) for i in range(n_dp)]])
    for s in range(2, n):
        sent = add(terms[s], moved)
        if s == 2:
            first_sent = sent
        moved = hop(sent)
    if n == 2:
        first_sent = sent

    planes = tie([send(small, [(i, (i + m) % n) for i in range(n)]) for m in range(1, n)], first_sent)
    small = small + sum(planes)
    others = [
        lax.ppermute(small, "dp", [(i, (i + 2 * m) % n_dp) for i in range(n_dp)])
        for m in range(1, n_dp // 2)
    ]
    input_grad = last_step(own, gain1, terms[0], moved, grad_state)
    small = small + sum(tie(others, input_grad))

    def whole(part):
        span = part.shape[-2] // 2
        mine = lax.dynamic_slice_in_dim(part, side * span, span, part.ndim - 2)
        got = swap(lax.dynamic_slice_in_dim(part, (1 - side) * span, span, part.ndim - 2))
        return jnp.where(side == 0, mine, got).astype(F32), jnp.where(side == 0, got, mine).astype(F32)

    wide = jnp.concatenate(whole(wide_grad), axis=2)
    query_key, value_out = whole(attn_grad)
    return (
        mixed[None],
        input_grad[None],
        small[:d],
        small[d : 2 * d],
        query_key[:, :local],
        query_key[:, local:],
        value_out[:, :local],
        value_out[:, local:],
        small[2 * d : 3 * d],
        small[3 * d : 4 * d],
        wide[1],
        wide[0],
        small[4 * d : 4 * d + 4].astype(jnp.int32),
        small[4 * d + 4 : 4 * d + 4 + HEADS].astype(jnp.int32),
    )


def solution(mesh):
    token, seq, copy, col = P("dp", "mp", None), P("dp", None), P(), P(None, "mp")
    grad = P("dp", "mp")
    return jax.shard_map(
        functools.partial(per_device, mesh.shape["mp"], mesh.shape["dp"]),
        mesh=mesh,
        in_specs=(token, token, seq, seq, seq, copy, copy, col, col, col, col, copy, copy, col, col),
        out_specs=(token, token, copy, copy, grad, grad, grad, grad, copy, copy, grad, grad, copy, copy),
        check_vma=False,
    )
```

```python
import functools
import jax
import jax.numpy as jnp
from jax import lax
from jax.experimental import pallas as pl
from jax.experimental.pallas import tpu as pltpu
from jax.sharding import PartitionSpec as P

HEADS = 16
E = 128
FF = 8192
EPS = 1e-05
DOC_MAX = 512
LOG2E = 1.4426950408889634
F32 = jnp.float32
BF16 = jnp.bfloat16


def params(mib):
    return pltpu.CompilerParams(vmem_limit_bytes=mib << 20)


def cost(flops, nbytes, trans=0):
    return pl.CostEstimate(flops=int(flops), bytes_accessed=int(nbytes), transcendentals=int(trans))


def norm_forward(values, gain, shift):
    mean = jnp.mean(values, axis=-1, keepdims=True)
    cent = values - mean
    inverse = lax.rsqrt(jnp.mean(cent * cent, axis=-1, keepdims=True) + EPS)
    normed = cent * inverse
    return (normed * gain + shift, normed, inverse)


def norm_backward(grad_out, normed, inverse, gain):
    scaled = grad_out * gain
    return inverse * (
        scaled
        - jnp.mean(scaled, axis=-1, keepdims=True)
        - normed * jnp.mean(scaled * normed, axis=-1, keepdims=True)
    )


def rotary_tables(length):
    half = E // 2
    freq = 10000.0 ** (-(jnp.arange(half, dtype=F32) * 2.0 / E))
    angle = jnp.arange(length, dtype=F32)[:, None] * freq[None, :]
    cos, sin = jnp.cos(angle), jnp.sin(angle)
    return jnp.concatenate([cos, cos], axis=1), jnp.concatenate([-sin, sin], axis=1)


def dot_t(left, right):
    return lax.dot_general(left, right, (((1,), (1,)), ((), ())), preferred_element_type=F32)


def dot_n(left, right):
    return lax.dot_general(left, right, (((1,), (0,)), ((), ())), preferred_element_type=F32)


def outer(left, right):
    return lax.dot_general(left, right, (((0,), (0,)), ((), ())), preferred_element_type=F32)


def qkv_body(rank_ref, xa_ref, xb_ref, gain_ref, shift_ref, wq_ref, wk_ref, wv_ref, cos_ref, sin_ref, *rest):
    a_ref, q_ref, k_ref, v_ref = rest[-4:]

    @pl.when(pl.program_id(0) == 0)
    def _():
        x = jnp.concatenate([xa_ref[...], xb_ref[...]], axis=1).astype(F32)
        out, _, _ = norm_forward(x, gain_ref[...], shift_ref[...])
        a_ref[0] = out.astype(BF16)

    act = a_ref[0]
    cos, sin = cos_ref[0], sin_ref[0]
    v_ref[0] = dot_n(act, wv_ref[...]).astype(BF16)
    for w_ref, o_ref in ((wq_ref, q_ref), (wk_ref, k_ref)):
        lin = dot_n(act, w_ref[...])
        for j in range(lin.shape[1] // E):
            part = lin[:, j * E : (j + 1) * E]
            turned = part * cos + pltpu.roll(part, E // 2, 1) * sin
            o_ref[0, :, j * E : (j + 1) * E] = turned.astype(BF16)


def qkv_slot(slot, n, rank, xa, xb, gain, shift, wq, wk, wv, cos, sin, held):
    rows, half = xa.shape
    d = 2 * half
    local = wq.shape[1]
    cb = min(512, local)
    whole = lambda j, r: (0, 0)
    wspec = pl.BlockSpec((d, cb), lambda j, r: (0, j))
    tspec = pl.BlockSpec((1, rows, E), lambda j, r: (lax.rem(r[0] + slot, n), 0, 0))
    in_specs = [
        pl.BlockSpec((rows, half), whole),
        pl.BlockSpec((rows, half), whole),
        pl.BlockSpec((1, d), whole),
        pl.BlockSpec((1, d), whole),
        wspec,
        wspec,
        wspec,
        tspec,
        tspec,
    ]
    extra = [] if held is None else list(held)
    aliases = {} if held is None else {10 + i: i for i in range(4)}
    ospec = pl.BlockSpec((1, rows, cb), lambda j, r: (slot, 0, j))
    return pl.pallas_call(
        qkv_body,
        grid_spec=pltpu.PrefetchScalarGridSpec(
            num_scalar_prefetch=1,
            grid=(local // cb,),
            in_specs=in_specs + [pl.BlockSpec(memory_space=pl.ANY)] * len(extra),
            out_specs=[pl.BlockSpec((1, rows, d), lambda j, r: (slot, 0, 0)), ospec, ospec, ospec],
        ),
        out_shape=[jax.ShapeDtypeStruct((n, rows, d), BF16)]
        + [jax.ShapeDtypeStruct((n, rows, local), BF16)] * 3,
        input_output_aliases=aliases,
        compiler_params=params(56),
        cost_estimate=cost(6 * rows * d * local, 6 * d * local + 4 * rows * d),
        name="qkv_slot",
    )(rank, xa, xb, gain, shift, wq, wk, wv, cos, sin, *extra)


def first_key(block, rows):
    return max(0, block - (DOC_MAX - 1 + rows - 1) // rows)


def attend_body(rank_ref, q_ref, k_ref, v_ref, dcol_ref, drow_ref, hc_ref, o_ref):
    n, rows, _ = q_ref.shape
    rank = rank_ref[0]
    head = rank_ref[1] + pl.program_id(0)
    slot = lambda b: lax.rem(b + n - rank, n)
    factor = E ** (-0.5) * LOG2E
    low = lax.broadcasted_iota(jnp.int32, (rows, rows), 0) >= lax.broadcasted_iota(
        jnp.int32, (rows, rows), 1
    )
    for b in range(n):
        q = q_ref[slot(b)]
        doc = dcol_ref[b]
        keys = range(first_key(b, rows), b + 1)
        scores = []
        for c in keys:
            s = dot_t(q, k_ref[slot(c)])
            ok = doc == drow_ref[c]
            if c == b:
                ok = ok & low
            scores.append(jnp.where(ok, s, -1e30))
        top = scores[0]
        for s in scores[1:]:
            top = jnp.maximum(top, s)
        top = jnp.max(top, axis=1, keepdims=True)
        total = None
        out = None
        for c, s in zip(keys, scores):
            p = jnp.exp2((s - top) * factor)
            total = p if total is None else total + p
            o = dot_n(p.astype(BF16), v_ref[slot(c)])
            out = o if out is None else out + o
        total = jnp.sum(total, axis=1, keepdims=True)
        gate = jnp.where(hc_ref[b] > head, 1.0, 0.0)
        o_ref[slot(b)] = (out * (gate / total)).astype(BF16)


def attend(rank, q, k, v, docs_col, docs_row, heads_col):
    n, rows, local = q.shape
    spec = pl.BlockSpec((n, rows, E), lambda h, r: (0, 0, h))
    col = pl.BlockSpec((n, rows, 1), lambda h, r: (0, 0, 0))
    row = pl.BlockSpec((n, 1, rows), lambda h, r: (0, 0, 0))
    t = n * rows
    return pl.pallas_call(
        attend_body,
        grid_spec=pltpu.PrefetchScalarGridSpec(
            num_scalar_prefetch=1,
            grid=(local // E,),
            in_specs=[spec, spec, spec, col, row, col],
            out_specs=spec,
        ),
        out_shape=jax.ShapeDtypeStruct((n, rows, local), BF16),
        compiler_params=params(16),
        cost_estimate=cost(4 * t * t * local, 8 * t * local, t * t * local // E),
        name="attend",
    )(rank, q, k, v, docs_col, docs_row, heads_col)


def attend_back_body(
    rank_ref, q_ref, k_ref, v_ref, do_ref, dcol_ref, drow_ref, hc_ref, cos_ref, sin_ref, out_ref, dk_ref, dv_ref
):
    n, rows, _ = q_ref.shape
    rank = rank_ref[0]
    head = rank_ref[1] + pl.program_id(0)
    slot = lambda b: lax.rem(b + n - rank, n)
    scale = E ** (-0.5)
    factor = scale * LOG2E
    low = lax.broadcasted_iota(jnp.int32, (rows, rows), 0) <= lax.broadcasted_iota(
        jnp.int32, (rows, rows), 1
    )
    local = out_ref.shape[2] // 3
    lanes = lambda i: pl.ds(pl.multiple_of(i * local + pl.program_id(0) * E, E), E)
    dk_ref[...] = jnp.zeros_like(dk_ref)
    dv_ref[...] = jnp.zeros_like(dv_ref)

    def unrotate(w, b):
        w = w * scale
        return (w * cos_ref[b] - pltpu.roll(w, E // 2, 1) * sin_ref[b]).astype(BF16)

    for b in range(n):
        q = q_ref[slot(b)]
        grad = jnp.where(hc_ref[b] > head, do_ref[slot(b)].astype(F32), 0.0).astype(BF16)
        keys = range(first_key(b, rows), b + 1)
        scores = []
        for c in keys:
            s = dot_t(k_ref[slot(c)], q)
            ok = dcol_ref[c] == drow_ref[b]
            if c == b:
                ok = ok & low
            scores.append(jnp.where(ok, s, -1e30))
        top = scores[0]
        for s in scores[1:]:
            top = jnp.maximum(top, s)
        top = jnp.max(top, axis=0, keepdims=True)
        probs = [jnp.exp2((s - top) * factor) for s in scores]
        total = probs[0]
        for p in probs[1:]:
            total = total + p
        inv = 1.0 / jnp.sum(total, axis=0, keepdims=True)
        probs = [p * inv for p in probs]
        dprobs = [dot_t(v_ref[slot(c)], grad) for c in keys]
        delta = None
        for p, g in zip(probs, dprobs):
            delta = p * g if delta is None else delta + p * g
        delta = jnp.sum(delta, axis=0, keepdims=True)
        dq = None
        for c, p, g in zip(keys, probs, dprobs):
            ds = (p * (g - delta)).astype(BF16)
            dk_ref[c] += dot_n(ds, q)
            dv_ref[c] += dot_n(p.astype(BF16), grad)
            part = outer(ds, k_ref[slot(c)])
            dq = part if dq is None else dq + part
        out_ref[slot(b), :, lanes(0)] = unrotate(dq, b)
    for b in range(n):
        out_ref[slot(b), :, lanes(1)] = unrotate(dk_ref[b], b)
        out_ref[slot(b), :, lanes(2)] = dv_ref[b].astype(BF16)


def attend_back(rank, q, k, v, do, docs_col, docs_row, heads_col, cos, sin):
    n, rows, local = q.shape
    spec = pl.BlockSpec((n, rows, E), lambda h, r: (0, 0, h))
    col = pl.BlockSpec((n, rows, 1), lambda h, r: (0, 0, 0))
    row = pl.BlockSpec((n, 1, rows), lambda h, r: (0, 0, 0))
    table = pl.BlockSpec((n, rows, E), lambda h, r: (0, 0, 0))
    t = n * rows
    return pl.pallas_call(
        attend_back_body,
        grid_spec=pltpu.PrefetchScalarGridSpec(
            num_scalar_prefetch=1,
            grid=(local // E,),
            in_specs=[spec, spec, spec, spec, col, row, col, table, table],
            out_specs=pl.BlockSpec((n, rows, 3 * local), lambda h, r: (0, 0, 0)),
            scratch_shapes=[pltpu.VMEM((n, rows, E), F32), pltpu.VMEM((n, rows, E), F32)],
        ),
        out_shape=jax.ShapeDtypeStruct((n, rows, 3 * local), BF16),
        compiler_params=params(24),
        cost_estimate=cost(108e9, 14 * t * local),
        name="attend_back",
    )(rank, q, k, v, do, docs_col, docs_row, heads_col, cos, sin)


def mlp_body(slot, n, rank_ref, a_ref, gl_ref, gr_ref, up_ref, down_ref, bucket_ref, *rest):
    r_ref, du_ref, aa_ref, ga_ref = rest[-4:]
    rows, cb = a_ref.shape[0], up_ref.shape[1]

    @pl.when(pl.program_id(0) == 0)
    def _():
        aa_ref[0] = a_ref[...]
        ahead = rank_ref[0] + slot < n


        @pl.when(ahead)
        def _():
            ga_ref[0] = gl_ref[...]

        @pl.when(jnp.logical_not(ahead))
        def _():
            ga_ref[0] = gr_ref[...]

    u = dot_n(a_ref[...], up_ref[...])
    dr = dot_n(ga_ref[0], down_ref[...]).astype(BF16).astype(F32)
    column = rank_ref[2] + pl.program_id(0) * cb + lax.broadcasted_iota(jnp.int32, (rows, cb), 1)
    lifted = jnp.where(column < (bucket_ref[0] + 1) * (FF // 4), jnp.maximum(u, 0.0), 0.0)
    r_ref[0] = (lifted * lifted).astype(BF16)
    du_ref[0] = (dr * (2.0 * lifted)).astype(BF16)


def mlp_slot(slot, n, rank, act, grads, up, down, bucket_col, held):
    rows, d = act.shape
    hidden = up.shape[1]
    cb = min(512, hidden)
    whole = lambda j, r: (0, 0)
    wspec = pl.BlockSpec((d, cb), lambda j, r: (0, j))
    extra = [] if held is None else list(held)
    aliases = {} if held is None else {7 + i: i for i in range(4)}
    ospec = pl.BlockSpec((1, rows, cb), lambda j, r: (slot, 0, j))
    aspec = pl.BlockSpec((1, rows, d), lambda j, r: (slot, 0, 0))
    return pl.pallas_call(
        functools.partial(mlp_body, slot, n),
        grid_spec=pltpu.PrefetchScalarGridSpec(
            num_scalar_prefetch=1,
            grid=(hidden // cb,),
            in_specs=[
                pl.BlockSpec((rows, d), whole),
            ]
            + [pl.BlockSpec((rows, d), whole)] * 2
            + [
                wspec,
                wspec,
                pl.BlockSpec((1, rows, 1), lambda j, r: (lax.rem(r[0] + slot, n), 0, 0)),
            ]
            + [pl.BlockSpec(memory_space=pl.ANY)] * len(extra),
            out_specs=[ospec, ospec, aspec, aspec],
        ),
        out_shape=[jax.ShapeDtypeStruct((n, rows, hidden), BF16)] * 2
        + [jax.ShapeDtypeStruct((n, rows, d), BF16)] * 2,
        input_output_aliases=aliases,
        compiler_params=params(28),
        cost_estimate=cost(4 * rows * d * hidden, 4 * d * hidden + 4 * rows * (d + hidden)),
        name="mlp_slot",
    )(rank, act, *grads, up, down, bucket_col, *extra)


def dom_body(n, slots, rank_ref, slot_ref, *refs):
    dom_ref, all_ref = refs[-2:]
    count = sum(1 if s == 0 else 2 for s in slots)
    flows, w_ref = list(refs[:count]), refs[count]

    def fill(ref):
        all_ref[0] = ref[...]

    for i, s in enumerate(slots):
        here = pl.program_id(0) == i
        if s == 0:
            pl.when(here)(functools.partial(fill, flows[0]))
            flows = flows[1:]
        else:
            ahead = rank_ref[0] + s < n
            pl.when(here & ahead)(functools.partial(fill, flows[0]))
            pl.when(here & jnp.logical_not(ahead))(functools.partial(fill, flows[1]))
            flows = flows[2:]
    dom_ref[0] = dot_n(all_ref[0], w_ref[...]).astype(BF16)


def dom_part(n, slots, rank, flows, weight, held):
    rows, d = flows[0].shape
    local = weight.shape[1]
    whole = lambda i, r, s: (0, 0)
    extra = [] if held is None else list(held)
    at = 2 + len(flows) + 1
    return pl.pallas_call(
        functools.partial(dom_body, n, slots),
        grid_spec=pltpu.PrefetchScalarGridSpec(
            num_scalar_prefetch=2,
            grid=(len(slots),),
            in_specs=[pl.BlockSpec((rows, d), whole)] * len(flows)
            + [pl.BlockSpec((d, local), whole)]
            + [pl.BlockSpec(memory_space=pl.ANY)] * len(extra),
            out_specs=[
                pl.BlockSpec((1, rows, local), lambda i, r, s: (s[i], 0, 0)),
                pl.BlockSpec((1, rows, d), lambda i, r, s: (s[i], 0, 0)),
            ],
        ),
        out_shape=[
            jax.ShapeDtypeStruct((n, rows, local), BF16),
            jax.ShapeDtypeStruct((n, rows, d), BF16),
        ],
        input_output_aliases={at + i: i for i in range(len(extra))},
        compiler_params=params(24),
        cost_estimate=cost(
            2 * len(slots) * rows * d * local, 2 * d * local + 6 * len(slots) * rows * d
        ),
        name="dom_part",
    )(rank, jnp.asarray(slots, jnp.int32), *flows, weight, *extra)


def grad_body(has_sum, rank_ref, lhs_ref, rhs_ref, *rest):
    out = outer(lhs_ref[...], rhs_ref[...])
    if has_sum:
        rest[-1][0] = (out + rest[0][...].astype(F32)).astype(BF16)
    else:
        rest[-1][...] = out.astype(BF16)


def grad_half(lhs, rhs, rank, partner, which=0, moved=None, held=None):
    t, d = lhs.shape
    half = rhs.shape[1] // 2
    tile = min(512, d)
    col = (lambda r: 1 - r[3]) if partner else (lambda r: r[3])
    specs = [
        pl.BlockSpec((t, tile), lambda j, r: (0, j)),
        pl.BlockSpec((t, half), lambda j, r: (0, col(r))),
    ]
    args = [lhs, rhs]
    aliases = {}
    if partner:
        ospec = pl.BlockSpec((tile, half), lambda j, r: (j, 0))
        oshape = (d, half)
    else:
        specs.append(pl.BlockSpec((tile, half), lambda j, r: (j, 0)))
        args.append(moved)
        ospec = pl.BlockSpec((1, tile, half), lambda j, r: (which, j, 0))
        oshape = (2, d, half)
        if held is not None:
            specs.append(pl.BlockSpec(memory_space=pl.ANY))
            args.append(held)
            aliases = {4: 0}
    return pl.pallas_call(
        functools.partial(grad_body, not partner),
        grid_spec=pltpu.PrefetchScalarGridSpec(
            num_scalar_prefetch=1, grid=(d // tile,), in_specs=specs, out_specs=ospec
        ),
        out_shape=jax.ShapeDtypeStruct(oshape, BF16),
        input_output_aliases=aliases,
        compiler_params=params(28),
        cost_estimate=cost(1e6, 1e6),
        name="grad_half",
    )(rank, *args)


def attn_grad_body(partner, rank_ref, a_ref, s_ref, one_ref, key_ref, om_ref, *rest):
    out_ref = rest[-1]
    local = om_ref.shape[1]
    second = rank_ref[3] == (0 if partner else 1)
    act = a_ref[...]

    def put(cols, value):
        if not partner:
            value = value + rest[0][:, cols].astype(F32)
        out_ref[:, cols] = value.astype(BF16)

    put(slice(0, local), outer(act, one_ref[...]))

    @pl.when(second)
    def _():
        put(slice(local, 2 * local), outer(s_ref[...], om_ref[...]))

    @pl.when(jnp.logical_not(second))
    def _():
        put(slice(local, 2 * local), outer(act, key_ref[...]))


def attn_grads(act, states, dqkv, om, rank, moved=None):
    t, d = act.shape
    local = om.shape[1]
    tile = min(512, d)
    partner = moved is None
    pos = (lambda r: 1 - r[3]) if partner else (lambda r: r[3])
    col = pl.BlockSpec((t, tile), lambda j, r: (0, j))
    out = pl.BlockSpec((tile, 2 * local), lambda j, r: (j, 0))
    return pl.pallas_call(
        functools.partial(attn_grad_body, partner),
        grid_spec=pltpu.PrefetchScalarGridSpec(
            num_scalar_prefetch=1,
            grid=(d // tile,),
            in_specs=[
                col,
                col,
                pl.BlockSpec((t, local), lambda j, r: (0, 2 * pos(r))),
                pl.BlockSpec((t, local), lambda j, r: (0, 1)),
                pl.BlockSpec((t, local), lambda j, r: (0, 0)),
            ]
            + ([] if partner else [out]),
            out_specs=out,
        ),
        out_shape=jax.ShapeDtypeStruct((d, 2 * local), BF16),
        compiler_params=params(28),
        cost_estimate=cost(1e6, 1e6),
        name="attn_grads",
    )(rank, act, states, dqkv, dqkv, om, *([] if partner else [moved]))


def join_body(slot, first, rank_ref, moved_ref, term_ref, out_ref):
    adds = rank_ref[0] < first if slot >= 0 else rank_ref[0] >= first

    @pl.when(adds)
    def _():
        out_ref[...] = (moved_ref[...].astype(F32) + term_ref[0].astype(F32)).astype(BF16)

    @pl.when(jnp.logical_not(adds))
    def _():
        out_ref[...] = moved_ref[...]


def join(rank, moved, terms, slot, first, right):
    rows, d = moved.shape
    tile = min(128, rows)
    row = pl.BlockSpec((tile, d), lambda i, r: (i, 0))
    return pl.pallas_call(
        functools.partial(join_body, 0 if right else -1, first),
        grid_spec=pltpu.PrefetchScalarGridSpec(
            num_scalar_prefetch=1,
            grid=(rows // tile,),
            in_specs=[row, pl.BlockSpec((1, tile, d), lambda i, r: (slot, i, 0))],
            out_specs=row,
        ),
        out_shape=jax.ShapeDtypeStruct((rows, d), BF16),
        compiler_params=params(8),
        cost_estimate=cost(rows * d, 6 * rows * d),
        name="join",
    )(rank, moved, terms)


def last_body(x_ref, gain_ref, term_ref, moved_ref, state_ref, out_ref):
    gain = gain_ref[...]
    _, normed, inverse = norm_forward(x_ref[...].astype(F32), gain, gain)
    back = norm_backward(term_ref[...].astype(F32) + moved_ref[...].astype(F32), normed, inverse, gain)
    out_ref[...] = (state_ref[...] + back).astype(BF16)


def last_step(x, gain, term, moved, state):
    rows, d = x.shape
    tile = min(64, rows)
    row = lambda w: pl.BlockSpec((tile, w), lambda i: (i, 0))
    return pl.pallas_call(
        last_body,
        grid=(rows // tile,),
        in_specs=[row(d), pl.BlockSpec((1, d), lambda i: (0, 0)), row(d), row(d), row(d)],
        out_specs=row(d),
        out_shape=jax.ShapeDtypeStruct((rows, d), BF16),
        compiler_params=params(12),
        cost_estimate=cost(22e9, 12 * rows * d),
        name="last_step",
    )(x, gain, term, moved, state)


def tie(values, *others):
    values = tuple(values)
    return lax.optimization_barrier(values + others)[: len(values)]


def sum_over(vec, axis, moves):
    return sum((lax.ppermute(vec, axis, pairs) for pairs in moves), vec)


def per_device(
    n,
    n_dp,
    tokens,
    mixed_grad,
    doc_ids,
    head_count,
    width_bucket,
    first_gain,
    first_shift,
    query_weight,
    key_weight,
    value_weight,
    output_weight,
    second_gain,
    second_shift,
    up_weight,
    down_weight,
):
    rank = lax.axis_index("mp")
    rows, d = tokens.shape[1:]
    half = d // 2
    local = query_weight.shape[1]
    local_heads = local // E
    hidden = up_weight.shape[1]
    length = n * rows
    own = tokens[0]
    send = lambda v, pairs: lax.ppermute(v, "mp", pairs)
    ring = [(i, (i - 1) % n) for i in range(n)]
    hop = lambda v: send(v, ring)
    right_line = [(i, i + 1) for i in range(n - 1)]
    left_line = [(i + 1, i) for i in range(n - 1)]

    def tick(k, right, left, terms):
        if k:
            right = join(where, right, terms, n - k, k, True)
            left = join(where, left, terms, k, n - k, False)
        return send(right, right_line), send(left, left_line), right, left

    def owned(terms, right, left):
        return terms[0].astype(F32) + right.astype(F32) + left.astype(F32)

    low = lambda v: v.astype(BF16)
    flat = lambda v: v.reshape(length, v.shape[-1])
    add = lambda t, moved: (t.astype(F32) + moved.astype(F32)).astype(BF16)

    side = lax.rem(lax.axis_index("dp"), 2)
    where = jnp.stack([rank, rank * local_heads, rank * hidden, side]).astype(jnp.int32)
    swap = lambda v: lax.ppermute(v, "dp", [(i, i ^ 1) for i in range(n_dp)])
    sides = [list(range(c, n_dp, 2)) for c in range(2)]
    docs_col = doc_ids.reshape(n, rows, 1)
    docs_row = doc_ids.reshape(n, 1, rows)
    heads_col = head_count.reshape(n, rows, 1)
    bucket_col = width_bucket.reshape(n, rows, 1)
    cos, sin = (t.reshape(n, rows, E) for t in rotary_tables(length))
    gain1, shift1 = first_gain[None], first_shift[None]
    gain2, shift2 = second_gain[None], second_shift[None]

    held, block = None, [own[:, :half], own[:, half:]]
    for s in range(n):
        after = [None, None]
        for p in range(2):
            if s >= 1:
                block[p], *held = tie([block[p]] + list(held))
            if s < n - 1:
                after[p] = hop(block[p])
        held = qkv_slot(
            s, n, where, *block, gain1, shift1, query_weight, key_weight, value_weight, cos, sin, held
        )
        if s < n - 1:
            block = after
    first_all, query, keys, vals = held

    grad_own = mixed_grad[0]
    (right,) = tie([grad_own], block[0])
    left = right
    grads_r, grads_l = [right], [left]
    right, left, _, _ = tick(0, right, left, None)
    masked = attend(where, query, keys, vals, docs_col, docs_row, heads_col)
    terms = low(dot_t(flat(masked), output_weight)).reshape(n, rows, d)
    for k in range(1, n):
        grads_r.append(right)
        grads_l.append(left)
        right, left, _, _ = tick(k, right, left, terms)
    attn = owned(terms, right, left)
    x_rows = own.astype(F32)
    state = x_rows + attn
    second_out, normed_two, inverse_two = norm_forward(state, gain2, shift2)

    weights = jnp.concatenate([query_weight, key_weight, value_weight], axis=1)
    held, moved = None, None
    (block,) = tie([low(second_out)], weights)
    for s in range(n):
        if s >= 1:
            block, *held = tie([block] + list(held) + ([term0] if s == n - 1 else []))
            if s == n - 1:
                term0, held = held[-1], held[:-1]
        after = hop(block) if s < n - 1 else None
        held = mlp_slot(
            s, n, where, block, [grads_l[s], grads_r[n - s if s else 0]], up_weight, down_weight, bucket_col, held
        )
        if s >= 1:
            term = dot_t(held[1][s], up_weight)
            if s > 1:
                (term,) = tie([term])
            sent = low(term) if moved is None else add(term, moved)
            moved = hop(sent)
        else:
            term0 = dot_t(held[1][0], up_weight)
        block = after
    active, grad_upper, second_all, grad_all = held
    grad_all, active, second_all, grad_upper = tie([grad_all, active, second_all, grad_upper], sent)
    gifts = [
        grad_half(flat(grad_all), flat(active), where, True),
        grad_half(flat(second_all), flat(grad_upper), where, True),
    ]
    (moved,) = tie([moved], *gifts)
    down_gift, up_gift = (swap(v) for v in gifts)
    grad_second = term0 + moved.astype(F32)
    back_two = norm_backward(grad_second, normed_two, inverse_two, gain2)
    second_gain_part = jnp.sum(grad_second * normed_two, axis=0)
    second_shift_part = jnp.sum(grad_second, axis=0)
    grad_state = grad_own.astype(F32) + back_two

    start = low(grad_state)
    grad_all, active, start = tie([grad_all, active, start])
    right = left = start
    rights, lefts = [start], [start]
    right, left, _, _ = tick(0, right, left, None)
    ffn = low(dot_t(flat(active), down_weight)).reshape(n, rows, d)
    pair = grad_half(flat(grad_all), flat(active), where, False, 0, down_gift)
    (right,) = tie([right], pair)
    (left,) = tie([left], pair)
    for k in range(1, n):
        rights.append(right)
        lefts.append(left)
        right, left, went_r, went_l = tick(k, right, left, ffn)
        if k == 1:
            second_all, grad_upper = tie([second_all, grad_upper], went_r, went_l)
            pair = grad_half(flat(second_all), flat(grad_upper), where, False, 1, up_gift, pair)
            wide_grad = lax.psum_scatter(pair, "dp", scatter_dimension=1, axis_index_groups=sides, tiled=True)
            (right,) = tie([right], pair)
            (left,) = tie([left], pair)
    late = sorted({1, n - 1})
    early = [s for s in range(n) if s not in late]
    pick = lambda slots: sum(([start] if s == 0 else [lefts[s], rights[n - s]] for s in slots), [])
    held = dom_part(n, early, where, pick(early), output_weight, None)
    grad_masked, state_all = dom_part(n, late, where, pick(late), output_weight, held)
    dqkv = attend_back(
        where, query, keys, vals, grad_masked, docs_col, docs_row, heads_col, cos, sin
    )
    mixed = low(state + owned(ffn, right, left))

    (dqkv,) = tie([dqkv], right, left)
    def whole(part):
        span = part.shape[-2] // 2
        mine = lax.dynamic_slice_in_dim(part, side * span, span, part.ndim - 2)
        got = swap(lax.dynamic_slice_in_dim(part, (1 - side) * span, span, part.ndim - 2))
        return jnp.where(side == 0, mine, got).astype(F32), jnp.where(side == 0, got, mine).astype(F32)

    tokens_of = lambda v: (flat(first_all), flat(state_all), flat(v), flat(masked), where)
    sent = low(dot_t(dqkv[1], weights))
    (dqkv,) = tie([dqkv], sent)
    moved = hop(sent)
    gift = attn_grads(*tokens_of(dqkv))
    (dqkv,) = tie([dqkv], gift)
    attn_term = attn_grads(*tokens_of(dqkv), swap(gift))
    (late,) = tie([attn_term], wide_grad)
    attn_grad = lax.psum_scatter(late, "dp", scatter_dimension=0, axis_index_groups=sides, tiled=True)
    terms = {1: sent}
    for s in range(2, n):
        (dqkv,) = tie([dqkv], attn_term)
        terms[s] = low(dot_t(dqkv[s], weights))
        (dqkv,) = tie([dqkv], terms[s])
        if s == 2:
            sent2 = sent = add(terms[2], moved)
            moved = hop(sent)
            (dqkv,) = tie([dqkv], sent)
    terms[0] = low(dot_t(dqkv[0], weights))
    held = tie([terms[s] for s in range(n)], sent2)
    sum_d = sum(jnp.sum(v.astype(F32), axis=0) for v in held)
    sum_da = sum(jnp.sum(v.astype(F32) * first_all[s].astype(F32), axis=0) for s, v in enumerate(held))
    first_shift_part = sum_d
    first_gain_part = (sum_da - first_shift * sum_d) / first_gain

    lead = (rank == 0).astype(F32)
    bucket_part = lead * jnp.sum(
        (width_bucket[0][:, None] == jnp.arange(4, dtype=jnp.int32)[None, :]).astype(F32), axis=0
    )
    head_part = lead * jnp.sum(
        (head_count[0][:, None] == jnp.arange(1, HEADS + 1, dtype=jnp.int32)[None, :]).astype(F32),
        axis=0,
    )
    small = jnp.concatenate(
        [
            first_gain_part,
            first_shift_part,
            second_gain_part,
            second_shift_part,
            bucket_part,
            head_part,
            jnp.zeros((128 - 4 - HEADS,), F32),
        ]
    )
    small = sum_over(small, "dp", [[(i, i ^ 1) for i in range(n_dp)]])
    wide = jnp.concatenate(whole(wide_grad), axis=2)
    for s in range(3, n):
        if s == 3:
            moved, wide = tie([moved, wide])
        sent = add(terms[s], moved)
        moved = hop(sent)

    planes = tie([send(small, [(i, (i + m) % n) for i in range(n)]) for m in range(1, n)], sent)
    small = small + sum(planes)
    others = [
        lax.ppermute(small, "dp", [(i, (i + 2 * m) % n_dp) for i in range(n_dp)])
        for m in range(1, n_dp // 2)
    ]
    input_grad = last_step(own, gain1, terms[0], moved, grad_state)
    small = small + sum(tie(others, input_grad))

    query_key, value_out = whole(attn_grad)
    return (
        mixed[None],
        input_grad[None],
        small[:d],
        small[d : 2 * d],
        query_key[:, :local],
        query_key[:, local:],
        value_out[:, :local],
        value_out[:, local:],
        small[2 * d : 3 * d],
        small[3 * d : 4 * d],
        wide[1],
        wide[0],
        small[4 * d : 4 * d + 4].astype(jnp.int32),
        small[4 * d + 4 : 4 * d + 4 + HEADS].astype(jnp.int32),
    )


def solution(mesh):
    token, seq, copy, col = P("dp", "mp", None), P("dp", None), P(), P(None, "mp")
    grad = P("dp", "mp")
    return jax.shard_map(
        functools.partial(per_device, mesh.shape["mp"], mesh.shape["dp"]),
        mesh=mesh,
        in_specs=(token, token, seq, seq, seq, copy, copy, col, col, col, col, copy, copy, col, col),
        out_specs=(token, token, copy, copy, grad, grad, grad, grad, copy, copy, grad, grad, copy, copy),
        check_vma=False,
    )
```

```python
import functools
import jax
import jax.numpy as jnp
from jax import lax
from jax.experimental import pallas as pl
from jax.experimental.pallas import tpu as pltpu
from jax.sharding import PartitionSpec as P

HEADS = 16
E = 128
FF = 8192
EPS = 1e-05
DOC_MAX = 512
LOG2E = 1.4426950408889634
F32 = jnp.float32
BF16 = jnp.bfloat16


def params(mib):
    return pltpu.CompilerParams(vmem_limit_bytes=mib << 20)


def cost(flops, nbytes, trans=0):
    return pl.CostEstimate(flops=int(flops), bytes_accessed=int(nbytes), transcendentals=int(trans))


def norm_forward(values, gain, shift):
    mean = jnp.mean(values, axis=-1, keepdims=True)
    cent = values - mean
    inverse = lax.rsqrt(jnp.mean(cent * cent, axis=-1, keepdims=True) + EPS)
    normed = cent * inverse
    return (normed * gain + shift, normed, inverse)


def norm_backward(grad_out, normed, inverse, gain):
    scaled = grad_out * gain
    return inverse * (
        scaled
        - jnp.mean(scaled, axis=-1, keepdims=True)
        - normed * jnp.mean(scaled * normed, axis=-1, keepdims=True)
    )


def rotary_tables(length):
    half = E // 2
    freq = 10000.0 ** (-(jnp.arange(half, dtype=F32) * 2.0 / E))
    angle = jnp.arange(length, dtype=F32)[:, None] * freq[None, :]
    cos, sin = jnp.cos(angle), jnp.sin(angle)
    return jnp.concatenate([cos, cos], axis=1), jnp.concatenate([-sin, sin], axis=1)


def dot_t(left, right):
    return lax.dot_general(left, right, (((1,), (1,)), ((), ())), preferred_element_type=F32)


def dot_n(left, right):
    return lax.dot_general(left, right, (((1,), (0,)), ((), ())), preferred_element_type=F32)


def outer(left, right):
    return lax.dot_general(left, right, (((0,), (0,)), ((), ())), preferred_element_type=F32)


def qkv_body(rank_ref, xa_ref, xb_ref, gain_ref, shift_ref, wq_ref, wk_ref, wv_ref, cos_ref, sin_ref, *rest):
    a_ref, q_ref, k_ref, v_ref = rest[-4:]

    @pl.when(pl.program_id(0) == 0)
    def _():
        x = jnp.concatenate([xa_ref[...], xb_ref[...]], axis=1).astype(F32)
        out, _, _ = norm_forward(x, gain_ref[...], shift_ref[...])
        a_ref[0] = out.astype(BF16)

    act = a_ref[0]
    cos, sin = cos_ref[0], sin_ref[0]
    v_ref[0] = dot_n(act, wv_ref[...]).astype(BF16)
    for w_ref, o_ref in ((wq_ref, q_ref), (wk_ref, k_ref)):
        lin = dot_n(act, w_ref[...])
        for j in range(lin.shape[1] // E):
            part = lin[:, j * E : (j + 1) * E]
            turned = part * cos + pltpu.roll(part, E // 2, 1) * sin
            o_ref[0, :, j * E : (j + 1) * E] = turned.astype(BF16)


def qkv_slot(slot, n, rank, xa, xb, gain, shift, wq, wk, wv, cos, sin, held):
    rows, half = xa.shape
    d = 2 * half
    local = wq.shape[1]
    cb = min(512, local)
    whole = lambda j, r: (0, 0)
    wspec = pl.BlockSpec((d, cb), lambda j, r: (0, j))
    tspec = pl.BlockSpec((1, rows, E), lambda j, r: (lax.rem(r[0] + slot, n), 0, 0))
    in_specs = [
        pl.BlockSpec((rows, half), whole),
        pl.BlockSpec((rows, half), whole),
        pl.BlockSpec((1, d), whole),
        pl.BlockSpec((1, d), whole),
        wspec,
        wspec,
        wspec,
        tspec,
        tspec,
    ]
    extra = [] if held is None else list(held)
    aliases = {} if held is None else {10 + i: i for i in range(4)}
    ospec = pl.BlockSpec((1, rows, cb), lambda j, r: (slot, 0, j))
    return pl.pallas_call(
        qkv_body,
        grid_spec=pltpu.PrefetchScalarGridSpec(
            num_scalar_prefetch=1,
            grid=(local // cb,),
            in_specs=in_specs + [pl.BlockSpec(memory_space=pl.ANY)] * len(extra),
            out_specs=[pl.BlockSpec((1, rows, d), lambda j, r: (slot, 0, 0)), ospec, ospec, ospec],
        ),
        out_shape=[jax.ShapeDtypeStruct((n, rows, d), BF16)]
        + [jax.ShapeDtypeStruct((n, rows, local), BF16)] * 3,
        input_output_aliases=aliases,
        compiler_params=params(56),
        cost_estimate=cost(6 * rows * d * local, 6 * d * local + 4 * rows * d),
        name="qkv_slot",
    )(rank, xa, xb, gain, shift, wq, wk, wv, cos, sin, *extra)


def first_key(block, rows):
    return max(0, block - (DOC_MAX - 1 + rows - 1) // rows)


def attend_body(rank_ref, q_ref, k_ref, v_ref, dcol_ref, drow_ref, hc_ref, o_ref):
    n, rows, _ = q_ref.shape
    rank = rank_ref[0]
    head = rank_ref[1] + pl.program_id(0)
    slot = lambda b: lax.rem(b + n - rank, n)
    factor = E ** (-0.5) * LOG2E
    low = lax.broadcasted_iota(jnp.int32, (rows, rows), 0) >= lax.broadcasted_iota(
        jnp.int32, (rows, rows), 1
    )
    for b in range(n):
        q = q_ref[slot(b)]
        doc = dcol_ref[b]
        keys = range(first_key(b, rows), b + 1)
        scores = []
        for c in keys:
            s = dot_t(q, k_ref[slot(c)])
            ok = doc == drow_ref[c]
            if c == b:
                ok = ok & low
            scores.append(jnp.where(ok, s, -1e30))
        top = scores[0]
        for s in scores[1:]:
            top = jnp.maximum(top, s)
        top = jnp.max(top, axis=1, keepdims=True)
        total = None
        out = None
        for c, s in zip(keys, scores):
            p = jnp.exp2((s - top) * factor)
            total = p if total is None else total + p
            o = dot_n(p.astype(BF16), v_ref[slot(c)])
            out = o if out is None else out + o
        total = jnp.sum(total, axis=1, keepdims=True)
        gate = jnp.where(hc_ref[b] > head, 1.0, 0.0)
        o_ref[slot(b)] = (out * (gate / total)).astype(BF16)


def attend(rank, q, k, v, docs_col, docs_row, heads_col):
    n, rows, local = q.shape
    spec = pl.BlockSpec((n, rows, E), lambda h, r: (0, 0, h))
    col = pl.BlockSpec((n, rows, 1), lambda h, r: (0, 0, 0))
    row = pl.BlockSpec((n, 1, rows), lambda h, r: (0, 0, 0))
    t = n * rows
    return pl.pallas_call(
        attend_body,
        grid_spec=pltpu.PrefetchScalarGridSpec(
            num_scalar_prefetch=1,
            grid=(local // E,),
            in_specs=[spec, spec, spec, col, row, col],
            out_specs=spec,
        ),
        out_shape=jax.ShapeDtypeStruct((n, rows, local), BF16),
        compiler_params=params(62),
        cost_estimate=cost(4 * t * t * local, 8 * t * local, t * t * local // E),
        name="attend",
    )(rank, q, k, v, docs_col, docs_row, heads_col)


def attend_back_body(
    rank_ref, q_ref, k_ref, v_ref, do_ref, dcol_ref, drow_ref, hc_ref, cos_ref, sin_ref, out_ref, dk_ref, dv_ref
):
    n, rows, _ = q_ref.shape
    rank = rank_ref[0]
    head = rank_ref[1] + pl.program_id(0)
    slot = lambda b: lax.rem(b + n - rank, n)
    scale = E ** (-0.5)
    factor = scale * LOG2E
    low = lax.broadcasted_iota(jnp.int32, (rows, rows), 0) <= lax.broadcasted_iota(
        jnp.int32, (rows, rows), 1
    )
    local = out_ref.shape[2] // 3
    lanes = lambda i: pl.ds(pl.multiple_of(i * local + pl.program_id(0) * E, E), E)
    dk_ref[...] = jnp.zeros_like(dk_ref)
    dv_ref[...] = jnp.zeros_like(dv_ref)

    def unrotate(w, b):
        w = w * scale
        return (w * cos_ref[b] - pltpu.roll(w, E // 2, 1) * sin_ref[b]).astype(BF16)

    for b in range(n):
        q = q_ref[slot(b)]
        grad = jnp.where(hc_ref[b] > head, do_ref[slot(b)].astype(F32), 0.0).astype(BF16)
        keys = range(first_key(b, rows), b + 1)
        scores = []
        for c in keys:
            s = dot_t(k_ref[slot(c)], q)
            ok = dcol_ref[c] == drow_ref[b]
            if c == b:
                ok = ok & low
            scores.append(jnp.where(ok, s, -1e30))
        top = scores[0]
        for s in scores[1:]:
            top = jnp.maximum(top, s)
        top = jnp.max(top, axis=0, keepdims=True)
        probs = [jnp.exp2((s - top) * factor) for s in scores]
        total = probs[0]
        for p in probs[1:]:
            total = total + p
        inv = 1.0 / jnp.sum(total, axis=0, keepdims=True)
        probs = [p * inv for p in probs]
        dprobs = [dot_t(v_ref[slot(c)], grad) for c in keys]
        delta = None
        for p, g in zip(probs, dprobs):
            delta = p * g if delta is None else delta + p * g
        delta = jnp.sum(delta, axis=0, keepdims=True)
        dq = None
        for c, p, g in zip(keys, probs, dprobs):
            ds = (p * (g - delta)).astype(BF16)
            dk_ref[c] += dot_n(ds, q)
            dv_ref[c] += dot_n(p.astype(BF16), grad)
            part = outer(ds, k_ref[slot(c)])
            dq = part if dq is None else dq + part
        out_ref[slot(b), :, lanes(0)] = unrotate(dq, b)
    for b in range(n):
        out_ref[slot(b), :, lanes(1)] = unrotate(dk_ref[b], b)
        out_ref[slot(b), :, lanes(2)] = dv_ref[b].astype(BF16)


def attend_back(rank, q, k, v, do, docs_col, docs_row, heads_col, cos, sin):
    n, rows, local = q.shape
    spec = pl.BlockSpec((n, rows, E), lambda h, r: (0, 0, h))
    col = pl.BlockSpec((n, rows, 1), lambda h, r: (0, 0, 0))
    row = pl.BlockSpec((n, 1, rows), lambda h, r: (0, 0, 0))
    table = pl.BlockSpec((n, rows, E), lambda h, r: (0, 0, 0))
    t = n * rows
    return pl.pallas_call(
        attend_back_body,
        grid_spec=pltpu.PrefetchScalarGridSpec(
            num_scalar_prefetch=1,
            grid=(local // E,),
            in_specs=[spec, spec, spec, spec, col, row, col, table, table],
            out_specs=pl.BlockSpec((n, rows, 3 * local), lambda h, r: (0, 0, 0)),
            scratch_shapes=[pltpu.VMEM((n, rows, E), F32), pltpu.VMEM((n, rows, E), F32)],
        ),
        out_shape=jax.ShapeDtypeStruct((n, rows, 3 * local), BF16),
        compiler_params=params(24),
        cost_estimate=cost(116e9, 14 * t * local),
        name="attend_back",
    )(rank, q, k, v, do, docs_col, docs_row, heads_col, cos, sin)


def mlp_body(slot, n, rank_ref, a_ref, gl_ref, gr_ref, up_ref, down_ref, bucket_ref, *rest):
    r_ref, du_ref, aa_ref, ga_ref = rest[-4:]
    rows, cb = a_ref.shape[0], up_ref.shape[1]

    @pl.when(pl.program_id(0) == 0)
    def _():
        aa_ref[0] = a_ref[...]
        ahead = rank_ref[0] + slot < n


        @pl.when(ahead)
        def _():
            ga_ref[0] = gl_ref[...]

        @pl.when(jnp.logical_not(ahead))
        def _():
            ga_ref[0] = gr_ref[...]

    u = dot_n(a_ref[...], up_ref[...])
    dr = dot_n(ga_ref[0], down_ref[...]).astype(BF16).astype(F32)
    column = rank_ref[2] + pl.program_id(0) * cb + lax.broadcasted_iota(jnp.int32, (rows, cb), 1)
    lifted = jnp.where(column < (bucket_ref[0] + 1) * (FF // 4), jnp.maximum(u, 0.0), 0.0)
    r_ref[0] = (lifted * lifted).astype(BF16)
    du_ref[0] = (dr * (2.0 * lifted)).astype(BF16)


def mlp_slot(slot, n, rank, act, grads, up, down, bucket_col, held):
    rows, d = act.shape
    hidden = up.shape[1]
    cb = min(512, hidden)
    whole = lambda j, r: (0, 0)
    wspec = pl.BlockSpec((d, cb), lambda j, r: (0, j))
    extra = [] if held is None else list(held)
    aliases = {} if held is None else {7 + i: i for i in range(4)}
    ospec = pl.BlockSpec((1, rows, cb), lambda j, r: (slot, 0, j))
    aspec = pl.BlockSpec((1, rows, d), lambda j, r: (slot, 0, 0))
    return pl.pallas_call(
        functools.partial(mlp_body, slot, n),
        grid_spec=pltpu.PrefetchScalarGridSpec(
            num_scalar_prefetch=1,
            grid=(hidden // cb,),
            in_specs=[
                pl.BlockSpec((rows, d), whole),
            ]
            + [pl.BlockSpec((rows, d), whole)] * 2
            + [
                wspec,
                wspec,
                pl.BlockSpec((1, rows, 1), lambda j, r: (lax.rem(r[0] + slot, n), 0, 0)),
            ]
            + [pl.BlockSpec(memory_space=pl.ANY)] * len(extra),
            out_specs=[ospec, ospec, aspec, aspec],
        ),
        out_shape=[jax.ShapeDtypeStruct((n, rows, hidden), BF16)] * 2
        + [jax.ShapeDtypeStruct((n, rows, d), BF16)] * 2,
        input_output_aliases=aliases,
        compiler_params=params(28),
        cost_estimate=cost(4 * rows * d * hidden, 4 * d * hidden + 4 * rows * (d + hidden)),
        name="mlp_slot",
    )(rank, act, *grads, up, down, bucket_col, *extra)


def dom_body(n, slots, rank_ref, slot_ref, *refs):
    dom_ref, all_ref = refs[-2:]
    count = sum(1 if s == 0 else 2 for s in slots)
    flows, w_ref = list(refs[:count]), refs[count]

    def fill(ref):
        all_ref[0] = ref[...]

    for i, s in enumerate(slots):
        here = pl.program_id(0) == i
        if s == 0:
            pl.when(here)(functools.partial(fill, flows[0]))
            flows = flows[1:]
        else:
            ahead = rank_ref[0] + s < n
            pl.when(here & ahead)(functools.partial(fill, flows[0]))
            pl.when(here & jnp.logical_not(ahead))(functools.partial(fill, flows[1]))
            flows = flows[2:]
    dom_ref[0] = dot_n(all_ref[0], w_ref[...]).astype(BF16)


def dom_part(n, slots, rank, flows, weight, held):
    rows, d = flows[0].shape
    local = weight.shape[1]
    whole = lambda i, r, s: (0, 0)
    extra = [] if held is None else list(held)
    at = 2 + len(flows) + 1
    return pl.pallas_call(
        functools.partial(dom_body, n, slots),
        grid_spec=pltpu.PrefetchScalarGridSpec(
            num_scalar_prefetch=2,
            grid=(len(slots),),
            in_specs=[pl.BlockSpec((rows, d), whole)] * len(flows)
            + [pl.BlockSpec((d, local), whole)]
            + [pl.BlockSpec(memory_space=pl.ANY)] * len(extra),
            out_specs=[
                pl.BlockSpec((1, rows, local), lambda i, r, s: (s[i], 0, 0)),
                pl.BlockSpec((1, rows, d), lambda i, r, s: (s[i], 0, 0)),
            ],
        ),
        out_shape=[
            jax.ShapeDtypeStruct((n, rows, local), BF16),
            jax.ShapeDtypeStruct((n, rows, d), BF16),
        ],
        input_output_aliases={at + i: i for i in range(len(extra))},
        compiler_params=params(24),
        cost_estimate=cost(
            2 * len(slots) * rows * d * local, 2 * d * local + 6 * len(slots) * rows * d
        ),
        name="dom_part",
    )(rank, jnp.asarray(slots, jnp.int32), *flows, weight, *extra)


def grad_body(has_sum, rank_ref, lhs_ref, rhs_ref, *rest):
    out = outer(lhs_ref[...], rhs_ref[...])
    if has_sum:
        rest[-1][0] = (out + rest[0][...].astype(F32)).astype(BF16)
    else:
        rest[-1][...] = out.astype(BF16)


def grad_half(lhs, rhs, rank, partner, which=0, moved=None, held=None):
    t, d = lhs.shape
    half = rhs.shape[1] // 2
    tile = min(512, d)
    col = (lambda r: 1 - r[3]) if partner else (lambda r: r[3])
    specs = [
        pl.BlockSpec((t, tile), lambda j, r: (0, j)),
        pl.BlockSpec((t, half), lambda j, r: (0, col(r))),
    ]
    args = [lhs, rhs]
    aliases = {}
    if partner:
        ospec = pl.BlockSpec((tile, half), lambda j, r: (j, 0))
        oshape = (d, half)
    else:
        specs.append(pl.BlockSpec((tile, half), lambda j, r: (j, 0)))
        args.append(moved)
        ospec = pl.BlockSpec((1, tile, half), lambda j, r: (which, j, 0))
        oshape = (2, d, half)
        if held is not None:
            specs.append(pl.BlockSpec(memory_space=pl.ANY))
            args.append(held)
            aliases = {4: 0}
    return pl.pallas_call(
        functools.partial(grad_body, not partner),
        grid_spec=pltpu.PrefetchScalarGridSpec(
            num_scalar_prefetch=1, grid=(d // tile,), in_specs=specs, out_specs=ospec
        ),
        out_shape=jax.ShapeDtypeStruct(oshape, BF16),
        input_output_aliases=aliases,
        compiler_params=params(20),
        cost_estimate=cost(1e6, 1e6),
        name="grad_half",
    )(rank, *args)


def attn_grad_body(partner, rank_ref, a_ref, s_ref, one_ref, key_ref, om_ref, *rest):
    out_ref = rest[-1]
    local = om_ref.shape[1]
    second = rank_ref[3] == (0 if partner else 1)
    act = a_ref[...]

    def put(cols, value):
        if not partner:
            value = value + rest[0][:, cols].astype(F32)
        out_ref[:, cols] = value.astype(BF16)

    put(slice(0, local), outer(act, one_ref[...]))

    @pl.when(second)
    def _():
        put(slice(local, 2 * local), outer(s_ref[...], om_ref[...]))

    @pl.when(jnp.logical_not(second))
    def _():
        put(slice(local, 2 * local), outer(act, key_ref[...]))


def attn_grads(act, states, dqkv, om, rank, moved=None):
    t, d = act.shape
    local = om.shape[1]
    tile = min(512, d)
    partner = moved is None
    pos = (lambda r: 1 - r[3]) if partner else (lambda r: r[3])
    col = pl.BlockSpec((t, tile), lambda j, r: (0, j))
    out = pl.BlockSpec((tile, 2 * local), lambda j, r: (j, 0))
    return pl.pallas_call(
        functools.partial(attn_grad_body, partner),
        grid_spec=pltpu.PrefetchScalarGridSpec(
            num_scalar_prefetch=1,
            grid=(d // tile,),
            in_specs=[
                col,
                col,
                pl.BlockSpec((t, local), lambda j, r: (0, 2 * pos(r))),
                pl.BlockSpec((t, local), lambda j, r: (0, 1)),
                pl.BlockSpec((t, local), lambda j, r: (0, 0)),
            ]
            + ([] if partner else [out]),
            out_specs=out,
        ),
        out_shape=jax.ShapeDtypeStruct((d, 2 * local), BF16),
        compiler_params=params(62),
        cost_estimate=cost(4e9 if partner else 1e6, 1e6),
        name="attn_grads",
    )(rank, act, states, dqkv, dqkv, om, *([] if partner else [moved]))


def term_body(x_ref, w_ref, *rest):
    out = dot_t(x_ref[0], w_ref[...])
    if len(rest) > 1:
        out = out + rest[0][...].astype(F32)
    rest[-1][...] = out.astype(BF16)


def block_term(acts, slot, weight, flops, moved=None):
    _, rows, k = acts.shape
    d = weight.shape[0]
    tile = min(512, d)
    out = pl.BlockSpec((rows, tile), lambda j: (0, j))
    return pl.pallas_call(
        term_body,
        grid=(d // tile,),
        in_specs=[
            pl.BlockSpec((1, rows, k), lambda j: (slot, 0, 0)),
            pl.BlockSpec((tile, k), lambda j: (j, 0)),
        ]
        + ([] if moved is None else [out]),
        out_specs=out,
        out_shape=jax.ShapeDtypeStruct((rows, d), BF16),
        compiler_params=params(16),
        cost_estimate=cost(flops, flops / 256),
        name="block_term",
    )(acts, weight, *([] if moved is None else [moved]))


def join_body(slot, first, rank_ref, moved_ref, term_ref, out_ref):
    adds = rank_ref[0] < first if slot >= 0 else rank_ref[0] >= first

    @pl.when(adds)
    def _():
        out_ref[...] = (moved_ref[...].astype(F32) + term_ref[0].astype(F32)).astype(BF16)

    @pl.when(jnp.logical_not(adds))
    def _():
        out_ref[...] = moved_ref[...]


def join(rank, moved, terms, slot, first, right):
    rows, d = moved.shape
    tile = min(128, rows)
    row = pl.BlockSpec((tile, d), lambda i, r: (i, 0))
    return pl.pallas_call(
        functools.partial(join_body, 0 if right else -1, first),
        grid_spec=pltpu.PrefetchScalarGridSpec(
            num_scalar_prefetch=1,
            grid=(rows // tile,),
            in_specs=[row, pl.BlockSpec((1, tile, d), lambda i, r: (slot, i, 0))],
            out_specs=row,
        ),
        out_shape=jax.ShapeDtypeStruct((rows, d), BF16),
        compiler_params=params(8),
        cost_estimate=cost(1e6, 1e6),
        name="join",
    )(rank, moved, terms)


def last_body(x_ref, gain_ref, term_ref, moved_ref, state_ref, out_ref):
    gain = gain_ref[...]
    _, normed, inverse = norm_forward(x_ref[...].astype(F32), gain, gain)
    back = norm_backward(term_ref[...].astype(F32) + moved_ref[...].astype(F32), normed, inverse, gain)
    out_ref[...] = (state_ref[...] + back).astype(BF16)


def last_step(x, gain, term, moved, state):
    rows, d = x.shape
    tile = min(64, rows)
    row = lambda w: pl.BlockSpec((tile, w), lambda i: (i, 0))
    return pl.pallas_call(
        last_body,
        grid=(rows // tile,),
        in_specs=[row(d), pl.BlockSpec((1, d), lambda i: (0, 0)), row(d), row(d), row(d)],
        out_specs=row(d),
        out_shape=jax.ShapeDtypeStruct((rows, d), BF16),
        compiler_params=params(12),
        cost_estimate=cost(30e9, 12 * rows * d),
        name="last_step",
    )(x, gain, term, moved, state)


def tie(values, *others):
    values = tuple(values)
    return lax.optimization_barrier(values + others)[: len(values)]


def sum_over(vec, axis, moves):
    return sum((lax.ppermute(vec, axis, pairs) for pairs in moves), vec)


def per_device(
    n,
    n_dp,
    tokens,
    mixed_grad,
    doc_ids,
    head_count,
    width_bucket,
    first_gain,
    first_shift,
    query_weight,
    key_weight,
    value_weight,
    output_weight,
    second_gain,
    second_shift,
    up_weight,
    down_weight,
):
    rank = lax.axis_index("mp")
    rows, d = tokens.shape[1:]
    half = d // 2
    local = query_weight.shape[1]
    local_heads = local // E
    hidden = up_weight.shape[1]
    length = n * rows
    own = tokens[0]
    send = lambda v, pairs: lax.ppermute(v, "mp", pairs)
    ring = [(i, (i - 1) % n) for i in range(n)]
    hop = lambda v: send(v, ring)
    right_line = [(i, i + 1) for i in range(n - 1)]
    left_line = [(i + 1, i) for i in range(n - 1)]

    def tick(k, right, left, terms):
        if k:
            right = join(where, right, terms, n - k, k, True)
            left = join(where, left, terms, k, n - k, False)
        return send(right, right_line), send(left, left_line), right, left

    def owned(terms, right, left):
        return terms[0].astype(F32) + right.astype(F32) + left.astype(F32)

    low = lambda v: v.astype(BF16)
    flat = lambda v: v.reshape(length, v.shape[-1])
    add = lambda t, moved: (t.astype(F32) + moved.astype(F32)).astype(BF16)

    side = lax.rem(lax.axis_index("dp"), 2)
    where = jnp.stack([rank, rank * local_heads, rank * hidden, side]).astype(jnp.int32)
    swap = lambda v: lax.ppermute(v, "dp", [(i, i ^ 1) for i in range(n_dp)])
    sides = [list(range(c, n_dp, 2)) for c in range(2)]
    docs_col = doc_ids.reshape(n, rows, 1)
    docs_row = doc_ids.reshape(n, 1, rows)
    heads_col = head_count.reshape(n, rows, 1)
    bucket_col = width_bucket.reshape(n, rows, 1)
    cos, sin = (t.reshape(n, rows, E) for t in rotary_tables(length))
    gain1, shift1 = first_gain[None], first_shift[None]
    gain2, shift2 = second_gain[None], second_shift[None]

    held, block = None, [own[:, :half], own[:, half:]]
    for s in range(n):
        after = [None, None]
        for p in range(2):
            if s >= 1:
                block[p], *held = tie([block[p]] + list(held))
            if s < n - 1:
                after[p] = hop(block[p])
        held = qkv_slot(
            s, n, where, *block, gain1, shift1, query_weight, key_weight, value_weight, cos, sin, held
        )
        if s < n - 1:
            block = after
    first_all, query, keys, vals = held

    grad_own = mixed_grad[0]
    (right,) = tie([grad_own], block[0])
    left = right
    grads_r, grads_l = [right], [left]
    right, left, _, _ = tick(0, right, left, None)
    masked = attend(where, query, keys, vals, docs_col, docs_row, heads_col)
    terms = low(dot_t(flat(masked), output_weight)).reshape(n, rows, d)
    for k in range(1, n):
        grads_r.append(right)
        grads_l.append(left)
        right, left, _, _ = tick(k, right, left, terms)
    attn = owned(terms, right, left)
    x_rows = own.astype(F32)
    state = x_rows + attn
    second_out, normed_two, inverse_two = norm_forward(state, gain2, shift2)

    weights = jnp.concatenate([query_weight, key_weight, value_weight], axis=1)
    held, moved = None, None
    (block,) = tie([low(second_out)], weights)
    for s in range(n):
        if s >= 1:
            block, *held = tie([block] + list(held), sent)
        after = hop(block) if s < n - 1 else None
        held = mlp_slot(
            s, n, where, block, [grads_l[s], grads_r[n - s if s else 0]], up_weight, down_weight, bucket_col, held
        )
        if s >= 1:
            fused = moved if s == n - 1 and s > 1 else None
            sent = block_term(held[1], s, up_weight, 2 * rows * d * hidden, fused)
            if s > 1 and fused is None:
                sent = add(sent, moved)
            moved = hop(sent)
        else:
            sent = term0 = block_term(held[1], 0, up_weight, 2 * rows * d * hidden)
        block = after
    active, grad_upper, second_all, grad_all = held
    grad_all, active, second_all, grad_upper = tie([grad_all, active, second_all, grad_upper], sent)
    gifts = [
        grad_half(flat(grad_all), flat(active), where, True),
        grad_half(flat(second_all), flat(grad_upper), where, True),
    ]
    (moved,) = tie([moved], *gifts)
    down_gift, up_gift = (swap(v) for v in gifts)
    grad_second = term0.astype(F32) + moved.astype(F32)
    back_two = norm_backward(grad_second, normed_two, inverse_two, gain2)
    second_gain_part = jnp.sum(grad_second * normed_two, axis=0)
    second_shift_part = jnp.sum(grad_second, axis=0)
    grad_state = grad_own.astype(F32) + back_two

    start = low(grad_state)
    grad_all, active, start = tie([grad_all, active, start])
    right = left = start
    rights, lefts = [start], [start]
    right, left, _, _ = tick(0, right, left, None)
    ffn = low(dot_t(flat(active), down_weight)).reshape(n, rows, d)
    pair = grad_half(flat(grad_all), flat(active), where, False, 0, down_gift)
    (right,) = tie([right], pair)
    (left,) = tie([left], pair)
    for k in range(1, n):
        rights.append(right)
        lefts.append(left)
        right, left, went_r, went_l = tick(k, right, left, ffn)
        if k == 1:
            second_all, grad_upper = tie([second_all, grad_upper], went_r, went_l)
            pair = grad_half(flat(second_all), flat(grad_upper), where, False, 1, up_gift, pair)
            wide_grad = lax.psum_scatter(pair, "dp", scatter_dimension=1, axis_index_groups=sides, tiled=True)
            (right,) = tie([right], pair)
            (left,) = tie([left], pair)
    late = sorted({1, n - 1})
    early = [s for s in range(n) if s not in late]
    pick = lambda slots: sum(([start] if s == 0 else [lefts[s], rights[n - s]] for s in slots), [])
    held = dom_part(n, early, where, pick(early), output_weight, None)
    grad_masked, state_all = dom_part(n, late, where, pick(late), output_weight, held)
    dqkv = attend_back(
        where, query, keys, vals, grad_masked, docs_col, docs_row, heads_col, cos, sin
    )
    mixed = low(state + owned(ffn, right, left))

    (dqkv,) = tie([dqkv], right, left)
    def whole(part):
        span = part.shape[-2] // 2
        mine = lax.dynamic_slice_in_dim(part, side * span, span, part.ndim - 2)
        got = swap(lax.dynamic_slice_in_dim(part, (1 - side) * span, span, part.ndim - 2))
        return jnp.where(side == 0, mine, got).astype(F32), jnp.where(side == 0, got, mine).astype(F32)

    tokens_of = lambda v: (flat(first_all), flat(state_all), flat(v), flat(masked), where)
    sent = block_term(dqkv, 1, weights, 1e6)
    (dqkv,) = tie([dqkv], sent)
    moved = hop(sent)
    gift = attn_grads(*tokens_of(dqkv))
    (dqkv,) = tie([dqkv], gift)
    terms = {1: sent, 2: block_term(dqkv, 2, weights, 1e6)}
    (dqkv,) = tie([dqkv], terms[2])
    attn_term = attn_grads(*tokens_of(dqkv), swap(gift))
    (late,) = tie([attn_term], wide_grad)
    attn_grad = lax.psum_scatter(late, "dp", scatter_dimension=0, axis_index_groups=sides, tiled=True)
    (moved,) = tie([moved], attn_term)
    sent2 = sent = add(terms[2], moved)
    moved = hop(sent)
    for s in range(3, n):
        (dqkv,) = tie([dqkv], sent)
        terms[s] = block_term(dqkv, s, weights, 1e6)
    (dqkv,) = tie([dqkv], terms[n - 1])
    terms[0] = block_term(dqkv, 0, weights, 1e6)
    held = tie([terms[s] for s in range(n)], sent2)
    sum_d = sum(jnp.sum(v.astype(F32), axis=0) for v in held)
    sum_da = sum(jnp.sum(v.astype(F32) * first_all[s].astype(F32), axis=0) for s, v in enumerate(held))
    first_shift_part = sum_d
    first_gain_part = (sum_da - first_shift * sum_d) / first_gain

    lead = (rank == 0).astype(F32)
    bucket_part = lead * jnp.sum(
        (width_bucket[0][:, None] == jnp.arange(4, dtype=jnp.int32)[None, :]).astype(F32), axis=0
    )
    head_part = lead * jnp.sum(
        (head_count[0][:, None] == jnp.arange(1, HEADS + 1, dtype=jnp.int32)[None, :]).astype(F32),
        axis=0,
    )
    small = jnp.concatenate(
        [
            first_gain_part,
            first_shift_part,
            second_gain_part,
            second_shift_part,
            bucket_part,
            head_part,
            jnp.zeros((128 - 4 - HEADS,), F32),
        ]
    )
    small = sum_over(small, "dp", [[(i, i ^ 1) for i in range(n_dp)]])
    wide = jnp.concatenate(whole(wide_grad), axis=2)
    for s in range(3, n):
        if s == 3:
            moved, wide = tie([moved, wide])
        sent = add(terms[s], moved)
        moved = hop(sent)

    planes = tie([send(small, [(i, (i + m) % n) for i in range(n)]) for m in range(1, n)], sent)
    small = small + sum(planes)
    others = [
        lax.ppermute(small, "dp", [(i, (i + 2 * m) % n_dp) for i in range(n_dp)])
        for m in range(1, n_dp // 2)
    ]
    input_grad = last_step(own, gain1, terms[0], moved, grad_state)
    small = small + sum(tie(others, input_grad))

    query_key, value_out = whole(attn_grad)
    return (
        mixed[None],
        input_grad[None],
        small[:d],
        small[d : 2 * d],
        query_key[:, :local],
        query_key[:, local:],
        value_out[:, :local],
        value_out[:, local:],
        small[2 * d : 3 * d],
        small[3 * d : 4 * d],
        wide[1],
        wide[0],
        small[4 * d : 4 * d + 4].astype(jnp.int32),
        small[4 * d + 4 : 4 * d + 4 + HEADS].astype(jnp.int32),
    )


def solution(mesh):
    token, seq, copy, col = P("dp", "mp", None), P("dp", None), P(), P(None, "mp")
    grad = P("dp", "mp")
    return jax.shard_map(
        functools.partial(per_device, mesh.shape["mp"], mesh.shape["dp"]),
        mesh=mesh,
        in_specs=(token, token, seq, seq, seq, copy, copy, col, col, col, col, copy, copy, col, col),
        out_specs=(token, token, copy, copy, grad, grad, grad, grad, copy, copy, grad, grad, copy, copy),
        check_vma=False,
    )
```

```python
import functools
import jax
import jax.numpy as jnp
from jax import lax
from jax.experimental import pallas as pl
from jax.experimental.pallas import tpu as pltpu
from jax.sharding import PartitionSpec as P

HEADS = 16
E = 128
FF = 8192
EPS = 1e-05
DOC_MAX = 512
LOG2E = 1.4426950408889634
F32 = jnp.float32
BF16 = jnp.bfloat16


def params(mib):
    return pltpu.CompilerParams(vmem_limit_bytes=mib << 20)


def cost(flops, nbytes, trans=0):
    return pl.CostEstimate(flops=int(flops), bytes_accessed=int(nbytes), transcendentals=int(trans))


def norm_forward(values, gain, shift):
    mean = jnp.mean(values, axis=-1, keepdims=True)
    cent = values - mean
    inverse = lax.rsqrt(jnp.mean(cent * cent, axis=-1, keepdims=True) + EPS)
    normed = cent * inverse
    return (normed * gain + shift, normed, inverse)


def norm_backward(grad_out, normed, inverse, gain):
    scaled = grad_out * gain
    return inverse * (
        scaled
        - jnp.mean(scaled, axis=-1, keepdims=True)
        - normed * jnp.mean(scaled * normed, axis=-1, keepdims=True)
    )


def rotary_tables(length):
    half = E // 2
    freq = 10000.0 ** (-(jnp.arange(half, dtype=F32) * 2.0 / E))
    angle = jnp.arange(length, dtype=F32)[:, None] * freq[None, :]
    cos, sin = jnp.cos(angle), jnp.sin(angle)
    return jnp.concatenate([cos, cos], axis=1), jnp.concatenate([-sin, sin], axis=1)


def dot_t(left, right):
    return lax.dot_general(left, right, (((1,), (1,)), ((), ())), preferred_element_type=F32)


def dot_n(left, right):
    return lax.dot_general(left, right, (((1,), (0,)), ((), ())), preferred_element_type=F32)


def outer(left, right):
    return lax.dot_general(left, right, (((0,), (0,)), ((), ())), preferred_element_type=F32)


def qkv_body(rank_ref, xa_ref, xb_ref, gain_ref, shift_ref, wq_ref, wk_ref, wv_ref, cos_ref, sin_ref, *rest):
    a_ref, q_ref, k_ref, v_ref = rest[-4:]

    @pl.when(pl.program_id(0) == 0)
    def _():
        x = jnp.concatenate([xa_ref[...], xb_ref[...]], axis=1).astype(F32)
        out, _, _ = norm_forward(x, gain_ref[...], shift_ref[...])
        a_ref[0] = out.astype(BF16)

    act = a_ref[0]
    cos, sin = cos_ref[0], sin_ref[0]
    v_ref[0] = dot_n(act, wv_ref[...]).astype(BF16)
    for w_ref, o_ref in ((wq_ref, q_ref), (wk_ref, k_ref)):
        lin = dot_n(act, w_ref[...])
        for j in range(lin.shape[1] // E):
            part = lin[:, j * E : (j + 1) * E]
            turned = part * cos + pltpu.roll(part, E // 2, 1) * sin
            o_ref[0, :, j * E : (j + 1) * E] = turned.astype(BF16)


def qkv_slot(slot, n, rank, xa, xb, gain, shift, wq, wk, wv, cos, sin, held):
    rows, half = xa.shape
    d = 2 * half
    local = wq.shape[1]
    cb = min(512, local)
    whole = lambda j, r: (0, 0)
    wspec = pl.BlockSpec((d, cb), lambda j, r: (0, j))
    tspec = pl.BlockSpec((1, rows, E), lambda j, r: (lax.rem(r[0] + slot, n), 0, 0))
    in_specs = [
        pl.BlockSpec((rows, half), whole),
        pl.BlockSpec((rows, half), whole),
        pl.BlockSpec((1, d), whole),
        pl.BlockSpec((1, d), whole),
        wspec,
        wspec,
        wspec,
        tspec,
        tspec,
    ]
    extra = [] if held is None else list(held)
    aliases = {} if held is None else {10 + i: i for i in range(4)}
    ospec = pl.BlockSpec((1, rows, cb), lambda j, r: (slot, 0, j))
    return pl.pallas_call(
        qkv_body,
        grid_spec=pltpu.PrefetchScalarGridSpec(
            num_scalar_prefetch=1,
            grid=(local // cb,),
            in_specs=in_specs + [pl.BlockSpec(memory_space=pl.ANY)] * len(extra),
            out_specs=[pl.BlockSpec((1, rows, d), lambda j, r: (slot, 0, 0)), ospec, ospec, ospec],
        ),
        out_shape=[jax.ShapeDtypeStruct((n, rows, d), BF16)]
        + [jax.ShapeDtypeStruct((n, rows, local), BF16)] * 3,
        input_output_aliases=aliases,
        compiler_params=params(56),
        cost_estimate=cost(6 * rows * d * local, 6 * d * local + 4 * rows * d),
        name="qkv_slot",
    )(rank, xa, xb, gain, shift, wq, wk, wv, cos, sin, *extra)


def first_key(block, rows):
    return max(0, block - (DOC_MAX - 1 + rows - 1) // rows)


def attend_body(rank_ref, q_ref, k_ref, v_ref, dcol_ref, drow_ref, hc_ref, o_ref):
    n, rows, _ = q_ref.shape
    rank = rank_ref[0]
    head = rank_ref[1] + pl.program_id(0)
    slot = lambda b: lax.rem(b + n - rank, n)
    factor = E ** (-0.5) * LOG2E
    low = lax.broadcasted_iota(jnp.int32, (rows, rows), 0) >= lax.broadcasted_iota(
        jnp.int32, (rows, rows), 1
    )
    for b in range(n):
        q = q_ref[slot(b)]
        doc = dcol_ref[b]
        keys = range(first_key(b, rows), b + 1)
        scores = []
        for c in keys:
            s = dot_t(q, k_ref[slot(c)])
            ok = doc == drow_ref[c]
            if c == b:
                ok = ok & low
            scores.append(jnp.where(ok, s, -1e30))
        top = scores[0]
        for s in scores[1:]:
            top = jnp.maximum(top, s)
        top = jnp.max(top, axis=1, keepdims=True)
        total = None
        out = None
        for c, s in zip(keys, scores):
            p = jnp.exp2((s - top) * factor)
            total = p if total is None else total + p
            o = dot_n(p.astype(BF16), v_ref[slot(c)])
            out = o if out is None else out + o
        total = jnp.sum(total, axis=1, keepdims=True)
        gate = jnp.where(hc_ref[b] > head, 1.0, 0.0)
        o_ref[slot(b)] = (out * (gate / total)).astype(BF16)


def attend(rank, q, k, v, docs_col, docs_row, heads_col):
    n, rows, local = q.shape
    spec = pl.BlockSpec((n, rows, E), lambda h, r: (0, 0, h))
    col = pl.BlockSpec((n, rows, 1), lambda h, r: (0, 0, 0))
    row = pl.BlockSpec((n, 1, rows), lambda h, r: (0, 0, 0))
    t = n * rows
    return pl.pallas_call(
        attend_body,
        grid_spec=pltpu.PrefetchScalarGridSpec(
            num_scalar_prefetch=1,
            grid=(local // E,),
            in_specs=[spec, spec, spec, col, row, col],
            out_specs=spec,
        ),
        out_shape=jax.ShapeDtypeStruct((n, rows, local), BF16),
        compiler_params=params(62),
        cost_estimate=cost(4 * t * t * local, 8 * t * local, t * t * local // E),
        name="attend",
    )(rank, q, k, v, docs_col, docs_row, heads_col)


def attend_back_body(
    rank_ref, q_ref, k_ref, v_ref, do_ref, dcol_ref, drow_ref, hc_ref, cos_ref, sin_ref, out_ref, dk_ref, dv_ref
):
    n, rows, _ = q_ref.shape
    rank = rank_ref[0]
    head = rank_ref[1] + pl.program_id(0)
    slot = lambda b: lax.rem(b + n - rank, n)
    scale = E ** (-0.5)
    factor = scale * LOG2E
    low = lax.broadcasted_iota(jnp.int32, (rows, rows), 0) <= lax.broadcasted_iota(
        jnp.int32, (rows, rows), 1
    )
    local = out_ref.shape[2] // 3
    lanes = lambda i: pl.ds(pl.multiple_of(i * local + pl.program_id(0) * E, E), E)
    dk_ref[...] = jnp.zeros_like(dk_ref)
    dv_ref[...] = jnp.zeros_like(dv_ref)

    def unrotate(w, b):
        w = w * scale
        return (w * cos_ref[b] - pltpu.roll(w, E // 2, 1) * sin_ref[b]).astype(BF16)

    for b in range(n):
        q = q_ref[slot(b)]
        grad = jnp.where(hc_ref[b] > head, do_ref[slot(b)].astype(F32), 0.0).astype(BF16)
        keys = range(first_key(b, rows), b + 1)
        scores = []
        for c in keys:
            s = dot_t(k_ref[slot(c)], q)
            ok = dcol_ref[c] == drow_ref[b]
            if c == b:
                ok = ok & low
            scores.append(jnp.where(ok, s, -1e30))
        top = scores[0]
        for s in scores[1:]:
            top = jnp.maximum(top, s)
        top = jnp.max(top, axis=0, keepdims=True)
        probs = [jnp.exp2((s - top) * factor) for s in scores]
        total = probs[0]
        for p in probs[1:]:
            total = total + p
        inv = 1.0 / jnp.sum(total, axis=0, keepdims=True)
        probs = [p * inv for p in probs]
        dprobs = [dot_t(v_ref[slot(c)], grad) for c in keys]
        delta = None
        for p, g in zip(probs, dprobs):
            delta = p * g if delta is None else delta + p * g
        delta = jnp.sum(delta, axis=0, keepdims=True)
        dq = None
        for c, p, g in zip(keys, probs, dprobs):
            ds = (p * (g - delta)).astype(BF16)
            dk_ref[c] += dot_n(ds, q)
            dv_ref[c] += dot_n(p.astype(BF16), grad)
            part = outer(ds, k_ref[slot(c)])
            dq = part if dq is None else dq + part
        out_ref[slot(b), :, lanes(0)] = unrotate(dq, b)
    for b in range(n):
        out_ref[slot(b), :, lanes(1)] = unrotate(dk_ref[b], b)
        out_ref[slot(b), :, lanes(2)] = dv_ref[b].astype(BF16)


def attend_back(rank, q, k, v, do, docs_col, docs_row, heads_col, cos, sin):
    n, rows, local = q.shape
    spec = pl.BlockSpec((n, rows, E), lambda h, r: (0, 0, h))
    col = pl.BlockSpec((n, rows, 1), lambda h, r: (0, 0, 0))
    row = pl.BlockSpec((n, 1, rows), lambda h, r: (0, 0, 0))
    table = pl.BlockSpec((n, rows, E), lambda h, r: (0, 0, 0))
    t = n * rows
    return pl.pallas_call(
        attend_back_body,
        grid_spec=pltpu.PrefetchScalarGridSpec(
            num_scalar_prefetch=1,
            grid=(local // E,),
            in_specs=[spec, spec, spec, spec, col, row, col, table, table],
            out_specs=pl.BlockSpec((n, rows, 3 * local), lambda h, r: (0, 0, 0)),
            scratch_shapes=[pltpu.VMEM((n, rows, E), F32), pltpu.VMEM((n, rows, E), F32)],
        ),
        out_shape=jax.ShapeDtypeStruct((n, rows, 3 * local), BF16),
        compiler_params=params(24),
        cost_estimate=cost(116e9, 14 * t * local),
        name="attend_back",
    )(rank, q, k, v, do, docs_col, docs_row, heads_col, cos, sin)


def mlp_body(slot, n, rank_ref, a_ref, gla_ref, glb_ref, gra_ref, grb_ref, up_ref, down_ref, bucket_ref, *rest):
    r_ref, du_ref, aa_ref, ga_ref = rest[-4:]
    rows, cb = a_ref.shape[0], up_ref.shape[1]

    @pl.when(pl.program_id(0) == 0)
    def _():
        aa_ref[0] = a_ref[...]
        ahead = rank_ref[0] + slot < n

        half = gla_ref.shape[1]

        def fill(first, second):
            ga_ref[0, :, :half] = first[...]
            ga_ref[0, :, half:] = second[...]

        pl.when(ahead)(functools.partial(fill, gla_ref, glb_ref))
        pl.when(jnp.logical_not(ahead))(functools.partial(fill, gra_ref, grb_ref))

    u = dot_n(a_ref[...], up_ref[...])
    dr = dot_n(ga_ref[0], down_ref[...]).astype(BF16).astype(F32)
    column = rank_ref[2] + pl.program_id(0) * cb + lax.broadcasted_iota(jnp.int32, (rows, cb), 1)
    lifted = jnp.where(column < (bucket_ref[0] + 1) * (FF // 4), jnp.maximum(u, 0.0), 0.0)
    r_ref[0] = (lifted * lifted).astype(BF16)
    du_ref[0] = (dr * (2.0 * lifted)).astype(BF16)


def mlp_slot(slot, n, rank, act, grads, up, down, bucket_col, held):
    rows, d = act.shape
    hidden = up.shape[1]
    cb = min(512, hidden)
    whole = lambda j, r: (0, 0)
    wspec = pl.BlockSpec((d, cb), lambda j, r: (0, j))
    extra = [] if held is None else list(held)
    aliases = {} if held is None else {9 + i: i for i in range(4)}
    ospec = pl.BlockSpec((1, rows, cb), lambda j, r: (slot, 0, j))
    aspec = pl.BlockSpec((1, rows, d), lambda j, r: (slot, 0, 0))
    return pl.pallas_call(
        functools.partial(mlp_body, slot, n),
        grid_spec=pltpu.PrefetchScalarGridSpec(
            num_scalar_prefetch=1,
            grid=(hidden // cb,),
            in_specs=[
                pl.BlockSpec((rows, d), whole),
            ]
            + [pl.BlockSpec((rows, d // 2), whole)] * 4
            + [
                wspec,
                wspec,
                pl.BlockSpec((1, rows, 1), lambda j, r: (lax.rem(r[0] + slot, n), 0, 0)),
            ]
            + [pl.BlockSpec(memory_space=pl.ANY)] * len(extra),
            out_specs=[ospec, ospec, aspec, aspec],
        ),
        out_shape=[jax.ShapeDtypeStruct((n, rows, hidden), BF16)] * 2
        + [jax.ShapeDtypeStruct((n, rows, d), BF16)] * 2,
        input_output_aliases=aliases,
        compiler_params=params(28),
        cost_estimate=cost(4 * rows * d * hidden, 4 * d * hidden + 4 * rows * (d + hidden)),
        name="mlp_slot",
    )(rank, act, *grads, up, down, bucket_col, *extra)


def dom_body(n, slots, rank_ref, slot_ref, *refs):
    dom_ref, all_ref = refs[-2:]
    count = sum(1 if s == 0 else 2 for s in slots)
    flows, w_ref = list(refs[:count]), refs[count]

    def fill(ref):
        all_ref[0] = ref[...]

    for i, s in enumerate(slots):
        here = pl.program_id(0) == i
        if s == 0:
            pl.when(here)(functools.partial(fill, flows[0]))
            flows = flows[1:]
        else:
            ahead = rank_ref[0] + s < n
            pl.when(here & ahead)(functools.partial(fill, flows[0]))
            pl.when(here & jnp.logical_not(ahead))(functools.partial(fill, flows[1]))
            flows = flows[2:]
    dom_ref[0] = dot_n(all_ref[0], w_ref[...]).astype(BF16)


def dom_part(n, slots, rank, flows, weight, held):
    rows, d = flows[0].shape
    local = weight.shape[1]
    whole = lambda i, r, s: (0, 0)
    extra = [] if held is None else list(held)
    at = 2 + len(flows) + 1
    return pl.pallas_call(
        functools.partial(dom_body, n, slots),
        grid_spec=pltpu.PrefetchScalarGridSpec(
            num_scalar_prefetch=2,
            grid=(len(slots),),
            in_specs=[pl.BlockSpec((rows, d), whole)] * len(flows)
            + [pl.BlockSpec((d, local), whole)]
            + [pl.BlockSpec(memory_space=pl.ANY)] * len(extra),
            out_specs=[
                pl.BlockSpec((1, rows, local), lambda i, r, s: (s[i], 0, 0)),
                pl.BlockSpec((1, rows, d), lambda i, r, s: (s[i], 0, 0)),
            ],
        ),
        out_shape=[
            jax.ShapeDtypeStruct((n, rows, local), BF16),
            jax.ShapeDtypeStruct((n, rows, d), BF16),
        ],
        input_output_aliases={at + i: i for i in range(len(extra))},
        compiler_params=params(24),
        cost_estimate=cost(
            2 * len(slots) * rows * d * local, 2 * d * local + 6 * len(slots) * rows * d
        ),
        name="dom_part",
    )(rank, jnp.asarray(slots, jnp.int32), *flows, weight, *extra)


def grad_body(has_sum, rank_ref, lhs_ref, rhs_ref, *rest):
    out = outer(lhs_ref[...], rhs_ref[...])
    if has_sum:
        rest[-1][0] = (out + rest[0][...].astype(F32)).astype(BF16)
    else:
        rest[-1][...] = out.astype(BF16)


def grad_half(lhs, rhs, rank, partner, which=0, moved=None, held=None):
    t, d = lhs.shape
    half = rhs.shape[1] // 2
    tile = min(512, d)
    col = (lambda r: 1 - r[3]) if partner else (lambda r: r[3])
    specs = [
        pl.BlockSpec((t, tile), lambda j, r: (0, j)),
        pl.BlockSpec((t, half), lambda j, r: (0, col(r))),
    ]
    args = [lhs, rhs]
    aliases = {}
    if partner:
        ospec = pl.BlockSpec((tile, half), lambda j, r: (j, 0))
        oshape = (d, half)
    else:
        specs.append(pl.BlockSpec((tile, half), lambda j, r: (j, 0)))
        args.append(moved)
        ospec = pl.BlockSpec((1, tile, half), lambda j, r: (which, j, 0))
        oshape = (2, d, half)
        if held is not None:
            specs.append(pl.BlockSpec(memory_space=pl.ANY))
            args.append(held)
            aliases = {4: 0}
    return pl.pallas_call(
        functools.partial(grad_body, not partner),
        grid_spec=pltpu.PrefetchScalarGridSpec(
            num_scalar_prefetch=1, grid=(d // tile,), in_specs=specs, out_specs=ospec
        ),
        out_shape=jax.ShapeDtypeStruct(oshape, BF16),
        input_output_aliases=aliases,
        compiler_params=params(20),
        cost_estimate=cost(1e6, 1e6),
        name="grad_half",
    )(rank, *args)


def attn_grad_body(partner, rank_ref, a_ref, s_ref, one_ref, key_ref, om_ref, *rest):
    out_ref = rest[-1]
    local = om_ref.shape[1]
    second = rank_ref[3] == (0 if partner else 1)
    act = a_ref[...]

    def put(cols, value):
        if not partner:
            value = value + rest[0][:, cols].astype(F32)
        out_ref[:, cols] = value.astype(BF16)

    put(slice(0, local), outer(act, one_ref[...]))

    @pl.when(second)
    def _():
        put(slice(local, 2 * local), outer(s_ref[...], om_ref[...]))

    @pl.when(jnp.logical_not(second))
    def _():
        put(slice(local, 2 * local), outer(act, key_ref[...]))


def attn_grads(act, states, dqkv, om, rank, moved=None):
    t, d = act.shape
    local = om.shape[1]
    tile = min(256, d)
    partner = moved is None
    pos = (lambda r: 1 - r[3]) if partner else (lambda r: r[3])
    col = pl.BlockSpec((t, tile), lambda j, r: (0, j))
    out = pl.BlockSpec((tile, 2 * local), lambda j, r: (j, 0))
    return pl.pallas_call(
        functools.partial(attn_grad_body, partner),
        grid_spec=pltpu.PrefetchScalarGridSpec(
            num_scalar_prefetch=1,
            grid=(d // tile,),
            in_specs=[
                col,
                pl.BlockSpec((t, tile), lambda j, r: (0, j * pos(r))),
                pl.BlockSpec((t, local), lambda j, r: (0, 2 * pos(r))),
                pl.BlockSpec((t, local), lambda j, r: (0, 1)),
                pl.BlockSpec((t, local), lambda j, r: (0, 0)),
            ]
            + ([] if partner else [out]),
            out_specs=out,
        ),
        out_shape=jax.ShapeDtypeStruct((d, 2 * local), BF16),
        compiler_params=params(62),
        cost_estimate=cost(4e9 if partner else 1e6, 1e6),
        name="attn_grads",
    )(rank, act, states, dqkv, dqkv, om, *([] if partner else [moved]))


def term_body(x_ref, w_ref, *rest):
    out = dot_t(x_ref[0], w_ref[...])
    if len(rest) > 1:
        out = out + rest[0][...].astype(F32)
    rest[-1][...] = out.astype(BF16)


def block_term(acts, slot, weight, flops, moved=None, mib=62):
    _, rows, k = acts.shape
    d = weight.shape[0]
    tile = min(512, d)
    out = pl.BlockSpec((rows, tile), lambda j: (0, j))
    return pl.pallas_call(
        term_body,
        grid=(d // tile,),
        in_specs=[
            pl.BlockSpec((1, rows, k), lambda j: (slot, 0, 0)),
            pl.BlockSpec((tile, k), lambda j: (j, 0)),
        ]
        + ([] if moved is None else [out]),
        out_specs=out,
        out_shape=jax.ShapeDtypeStruct((rows, d), BF16),
        compiler_params=params(mib),
        cost_estimate=cost(flops, flops / 256),
        name="block_term",
    )(acts, weight, *([] if moved is None else [moved]))


def join_body(slot, first, rank_ref, moved_ref, term_ref, out_ref):
    adds = rank_ref[0] < first if slot >= 0 else rank_ref[0] >= first

    @pl.when(adds)
    def _():
        out_ref[...] = (moved_ref[...].astype(F32) + term_ref[0].astype(F32)).astype(BF16)

    @pl.when(jnp.logical_not(adds))
    def _():
        out_ref[...] = moved_ref[...]


def join(rank, moved, terms, slot, first, right, part=0):
    rows, d = moved.shape
    tile = min(128, rows)
    row = pl.BlockSpec((tile, d), lambda i, r: (i, 0))
    return pl.pallas_call(
        functools.partial(join_body, 0 if right else -1, first),
        grid_spec=pltpu.PrefetchScalarGridSpec(
            num_scalar_prefetch=1,
            grid=(rows // tile,),
            in_specs=[row, pl.BlockSpec((1, tile, d), lambda i, r: (slot, i, part))],
            out_specs=row,
        ),
        out_shape=jax.ShapeDtypeStruct((rows, d), BF16),
        compiler_params=params(8),
        cost_estimate=cost(1e6, 1e6),
        name="join",
    )(rank, moved, terms)


def last_body(x_ref, gain_ref, term_ref, moved_ref, state_ref, out_ref):
    gain = gain_ref[...]
    _, normed, inverse = norm_forward(x_ref[...].astype(F32), gain, gain)
    back = norm_backward(term_ref[...].astype(F32) + moved_ref[...].astype(F32), normed, inverse, gain)
    out_ref[...] = (state_ref[...] + back).astype(BF16)


def last_step(x, gain, term, moved, state):
    rows, d = x.shape
    tile = min(64, rows)
    row = lambda w: pl.BlockSpec((tile, w), lambda i: (i, 0))
    return pl.pallas_call(
        last_body,
        grid=(rows // tile,),
        in_specs=[row(d), pl.BlockSpec((1, d), lambda i: (0, 0)), row(d), row(d), row(d)],
        out_specs=row(d),
        out_shape=jax.ShapeDtypeStruct((rows, d), BF16),
        compiler_params=params(12),
        cost_estimate=cost(30e9, 12 * rows * d),
        name="last_step",
    )(x, gain, term, moved, state)


def tie(values, *others):
    values = tuple(values)
    return lax.optimization_barrier(values + others)[: len(values)]


def sum_over(vec, axis, moves):
    return sum((lax.ppermute(vec, axis, pairs) for pairs in moves), vec)


def per_device(
    n,
    n_dp,
    tokens,
    mixed_grad,
    doc_ids,
    head_count,
    width_bucket,
    first_gain,
    first_shift,
    query_weight,
    key_weight,
    value_weight,
    output_weight,
    second_gain,
    second_shift,
    up_weight,
    down_weight,
):
    rank = lax.axis_index("mp")
    rows, d = tokens.shape[1:]
    half = d // 2
    local = query_weight.shape[1]
    local_heads = local // E
    hidden = up_weight.shape[1]
    length = n * rows
    own = tokens[0]
    send = lambda v, pairs: lax.ppermute(v, "mp", pairs)
    ring = [(i, (i - 1) % n) for i in range(n)]
    hop = lambda v: send(v, ring)
    right_line = [(i, i + 1) for i in range(n - 1)]
    left_line = [(i + 1, i) for i in range(n - 1)]

    def tick(k, right, left, terms):
        if k:
            right = join(where, right, terms, n - k, k, True)
            left = join(where, left, terms, k, n - k, False)
        return send(right, right_line), send(left, left_line), right, left

    def owned(terms, right, left):
        return terms[0].astype(F32) + right.astype(F32) + left.astype(F32)

    low = lambda v: v.astype(BF16)
    flat = lambda v: v.reshape(length, v.shape[-1])
    add = lambda t, moved: (t.astype(F32) + moved.astype(F32)).astype(BF16)

    side = lax.rem(lax.axis_index("dp"), 2)
    where = jnp.stack([rank, rank * local_heads, rank * hidden, side]).astype(jnp.int32)
    swap = lambda v: lax.ppermute(v, "dp", [(i, i ^ 1) for i in range(n_dp)])
    sides = [list(range(c, n_dp, 2)) for c in range(2)]
    docs_col = doc_ids.reshape(n, rows, 1)
    docs_row = doc_ids.reshape(n, 1, rows)
    heads_col = head_count.reshape(n, rows, 1)
    bucket_col = width_bucket.reshape(n, rows, 1)
    cos, sin = (t.reshape(n, rows, E) for t in rotary_tables(length))
    gain1, shift1 = first_gain[None], first_shift[None]
    gain2, shift2 = second_gain[None], second_shift[None]

    held, block = None, [own[:, :half], own[:, half:]]
    for s in range(n):
        after = [None, None]
        for p in range(2):
            if s >= 1:
                block[p], *held = tie([block[p]] + list(held))
            if s < n - 1:
                after[p] = hop(block[p])
        held = qkv_slot(
            s, n, where, *block, gain1, shift1, query_weight, key_weight, value_weight, cos, sin, held
        )
        if s < n - 1:
            block = after
    first_all, query, keys, vals = held

    grad_own = mixed_grad[0]
    (own_grad,) = tie([grad_own], block[0])
    right = [own_grad[:, :half], own_grad[:, half:]]
    left = list(right)
    grads_r, grads_l = [list(right)], [list(left)]

    def half_tick(k):
        for p in range(2):
            if k:
                right[p] = join(where, right[p], terms, n - k, k, True, p)
                left[p] = join(where, left[p], terms, k, n - k, False, p)
            right[p], left[p] = send(right[p], right_line), send(left[p], left_line)

    half_tick(0)
    masked = attend(where, query, keys, vals, docs_col, docs_row, heads_col)
    terms = low(dot_t(flat(masked), output_weight)).reshape(n, rows, d)
    for k in range(1, n):
        grads_r.append(list(right))
        grads_l.append(list(left))
        half_tick(k)
    right, left = (jnp.concatenate(v, axis=1) for v in (right, left))
    attn = owned(terms, right, left)
    x_rows = own.astype(F32)
    state = x_rows + attn
    second_out, normed_two, inverse_two = norm_forward(state, gain2, shift2)

    weights = jnp.concatenate([query_weight, key_weight, value_weight], axis=1)
    held, moved = None, None
    (block,) = tie([low(second_out)], weights)
    for s in range(n):
        if s >= 1:
            block, *held = tie([block] + list(held), sent)
        after = hop(block) if s < n - 1 else None
        held = mlp_slot(
            s, n, where, block, grads_l[s] + grads_r[n - s if s else 0], up_weight, down_weight, bucket_col, held
        )
        if s >= 1:
            fused = moved if s == n - 1 and s > 1 else None
            sent = block_term(held[1], s, up_weight, 2 * rows * d * hidden, fused, 16)
            if s > 1 and fused is None:
                sent = add(sent, moved)
            moved = hop(sent)
        else:
            sent = term0 = block_term(held[1], 0, up_weight, 2 * rows * d * hidden, None, 16)
        block = after
    active, grad_upper, second_all, grad_all = held
    grad_all, active, second_all, grad_upper = tie([grad_all, active, second_all, grad_upper], sent)
    gifts = [
        grad_half(flat(grad_all), flat(active), where, True),
        grad_half(flat(second_all), flat(grad_upper), where, True),
    ]
    (moved,) = tie([moved], *gifts)
    down_gift, up_gift = (swap(v) for v in gifts)
    grad_second = term0.astype(F32) + moved.astype(F32)
    back_two = norm_backward(grad_second, normed_two, inverse_two, gain2)
    second_gain_part = jnp.sum(grad_second * normed_two, axis=0)
    second_shift_part = jnp.sum(grad_second, axis=0)
    grad_state = grad_own.astype(F32) + back_two

    start = low(grad_state)
    grad_all, active, start = tie([grad_all, active, start])
    right = left = start
    rights, lefts = [start], [start]
    right, left, _, _ = tick(0, right, left, None)
    ffn = low(dot_t(flat(active), down_weight)).reshape(n, rows, d)
    pair = grad_half(flat(grad_all), flat(active), where, False, 0, down_gift)
    (right,) = tie([right], pair)
    (left,) = tie([left], pair)
    for k in range(1, n):
        rights.append(right)
        lefts.append(left)
        right, left, went_r, went_l = tick(k, right, left, ffn)
        if k == 1:
            second_all, grad_upper = tie([second_all, grad_upper], went_r, went_l)
            pair = grad_half(flat(second_all), flat(grad_upper), where, False, 1, up_gift, pair)
            wide_grad = lax.psum_scatter(pair, "dp", scatter_dimension=1, axis_index_groups=sides, tiled=True)
            (right,) = tie([right], pair)
            (left,) = tie([left], pair)
    late = sorted({1, n - 1})
    early = [s for s in range(n) if s not in late]
    pick = lambda slots: sum(([start] if s == 0 else [lefts[s], rights[n - s]] for s in slots), [])
    held = dom_part(n, early, where, pick(early), output_weight, None)
    grad_masked, state_all = dom_part(n, late, where, pick(late), output_weight, held)
    dqkv = attend_back(
        where, query, keys, vals, grad_masked, docs_col, docs_row, heads_col, cos, sin
    )
    mixed = low(state + owned(ffn, right, left))

    (dqkv,) = tie([dqkv], right, left)
    def whole(part):
        span = part.shape[-2] // 2
        mine = lax.dynamic_slice_in_dim(part, side * span, span, part.ndim - 2)
        got = swap(lax.dynamic_slice_in_dim(part, (1 - side) * span, span, part.ndim - 2))
        return jnp.where(side == 0, mine, got).astype(F32), jnp.where(side == 0, got, mine).astype(F32)

    tokens_of = lambda v: (flat(first_all), flat(state_all), flat(v), flat(masked), where)
    sent = block_term(dqkv, 1, weights, 1e6)
    (dqkv,) = tie([dqkv], sent)
    moved = hop(sent)
    gift = attn_grads(*tokens_of(dqkv))
    (dqkv,) = tie([dqkv], gift)
    terms = {1: sent, 2: block_term(dqkv, 2, weights, 1e6)}
    (dqkv,) = tie([dqkv], terms[2])
    attn_term = attn_grads(*tokens_of(dqkv), swap(gift))
    (late,) = tie([attn_term], wide_grad)
    attn_grad = lax.psum_scatter(late, "dp", scatter_dimension=0, axis_index_groups=sides, tiled=True)
    (moved,) = tie([moved], attn_term)
    sent2 = sent = add(terms[2], moved)
    moved = hop(sent)
    for s in range(3, n):
        (dqkv,) = tie([dqkv], sent)
        terms[s] = block_term(dqkv, s, weights, 1e6)
    (dqkv,) = tie([dqkv], terms[n - 1])
    terms[0] = block_term(dqkv, 0, weights, 1e6)
    held = tie([terms[s] for s in range(n)], sent2)
    sum_d = sum(jnp.sum(v.astype(F32), axis=0) for v in held)
    sum_da = sum(jnp.sum(v.astype(F32) * first_all[s].astype(F32), axis=0) for s, v in enumerate(held))
    first_shift_part = sum_d
    first_gain_part = (sum_da - first_shift * sum_d) / first_gain

    lead = (rank == 0).astype(F32)
    bucket_part = lead * jnp.sum(
        (width_bucket[0][:, None] == jnp.arange(4, dtype=jnp.int32)[None, :]).astype(F32), axis=0
    )
    head_part = lead * jnp.sum(
        (head_count[0][:, None] == jnp.arange(1, HEADS + 1, dtype=jnp.int32)[None, :]).astype(F32),
        axis=0,
    )
    small = jnp.concatenate(
        [
            first_gain_part,
            first_shift_part,
            second_gain_part,
            second_shift_part,
            bucket_part,
            head_part,
            jnp.zeros((128 - 4 - HEADS,), F32),
        ]
    )
    small = sum_over(small, "dp", [[(i, i ^ 1) for i in range(n_dp)]])
    wide = jnp.concatenate(whole(wide_grad), axis=2)
    for s in range(3, n):
        if s == 3:
            moved, wide = tie([moved, wide])
        sent = add(terms[s], moved)
        moved = hop(sent)

    planes = tie([send(small, [(i, (i + m) % n) for i in range(n)]) for m in range(1, n)], sent)
    small = small + sum(planes)
    others = [
        lax.ppermute(small, "dp", [(i, (i + 2 * m) % n_dp) for i in range(n_dp)])
        for m in range(1, n_dp // 2)
    ]
    input_grad = last_step(own, gain1, terms[0], moved, grad_state)
    small = small + sum(tie(others, input_grad))

    query_key, value_out = whole(attn_grad)
    return (
        mixed[None],
        input_grad[None],
        small[:d],
        small[d : 2 * d],
        query_key[:, :local],
        query_key[:, local:],
        value_out[:, :local],
        value_out[:, local:],
        small[2 * d : 3 * d],
        small[3 * d : 4 * d],
        wide[1],
        wide[0],
        small[4 * d : 4 * d + 4].astype(jnp.int32),
        small[4 * d + 4 : 4 * d + 4 + HEADS].astype(jnp.int32),
    )


def solution(mesh):
    token, seq, copy, col = P("dp", "mp", None), P("dp", None), P(), P(None, "mp")
    grad = P("dp", "mp")
    return jax.shard_map(
        functools.partial(per_device, mesh.shape["mp"], mesh.shape["dp"]),
        mesh=mesh,
        in_specs=(token, token, seq, seq, seq, copy, copy, col, col, col, col, copy, copy, col, col),
        out_specs=(token, token, copy, copy, grad, grad, grad, grad, copy, copy, grad, grad, copy, copy),
        check_vma=False,
    )
```

```python
import functools
import jax
import jax.numpy as jnp
from jax import lax
from jax.experimental import pallas as pl
from jax.experimental.pallas import tpu as pltpu
from jax.sharding import PartitionSpec as P

HEADS = 16
E = 128
FF = 8192
EPS = 1e-05
DOC_MAX = 512
LOG2E = 1.4426950408889634
F32 = jnp.float32
BF16 = jnp.bfloat16


def params(mib):
    return pltpu.CompilerParams(vmem_limit_bytes=mib << 20)


def cost(flops, nbytes, trans=0):
    return pl.CostEstimate(flops=int(flops), bytes_accessed=int(nbytes), transcendentals=int(trans))


def norm_forward(values, gain, shift):
    mean = jnp.mean(values, axis=-1, keepdims=True)
    cent = values - mean
    inverse = lax.rsqrt(jnp.mean(cent * cent, axis=-1, keepdims=True) + EPS)
    normed = cent * inverse
    return (normed * gain + shift, normed, inverse)


def norm_backward(grad_out, normed, inverse, gain):
    scaled = grad_out * gain
    return inverse * (
        scaled
        - jnp.mean(scaled, axis=-1, keepdims=True)
        - normed * jnp.mean(scaled * normed, axis=-1, keepdims=True)
    )


def rotary_tables(length):
    half = E // 2
    freq = 10000.0 ** (-(jnp.arange(half, dtype=F32) * 2.0 / E))
    angle = jnp.arange(length, dtype=F32)[:, None] * freq[None, :]
    cos, sin = jnp.cos(angle), jnp.sin(angle)
    return jnp.concatenate([cos, cos], axis=1), jnp.concatenate([-sin, sin], axis=1)


def dot_t(left, right):
    return lax.dot_general(left, right, (((1,), (1,)), ((), ())), preferred_element_type=F32)


def dot_n(left, right):
    return lax.dot_general(left, right, (((1,), (0,)), ((), ())), preferred_element_type=F32)


def outer(left, right):
    return lax.dot_general(left, right, (((0,), (0,)), ((), ())), preferred_element_type=F32)


def qkv_body(rank_ref, xa_ref, xb_ref, gain_ref, shift_ref, wq_ref, wk_ref, wv_ref, cos_ref, sin_ref, *rest):
    a_ref, q_ref, k_ref, v_ref = rest[-4:]

    @pl.when(pl.program_id(0) == 0)
    def _():
        x = jnp.concatenate([xa_ref[...], xb_ref[...]], axis=1).astype(F32)
        out, _, _ = norm_forward(x, gain_ref[...], shift_ref[...])
        a_ref[0] = out.astype(BF16)

    act = a_ref[0]
    cos, sin = cos_ref[0], sin_ref[0]
    v_ref[0] = dot_n(act, wv_ref[...]).astype(BF16)
    for w_ref, o_ref in ((wq_ref, q_ref), (wk_ref, k_ref)):
        lin = dot_n(act, w_ref[...])
        for j in range(lin.shape[1] // E):
            part = lin[:, j * E : (j + 1) * E]
            turned = part * cos + pltpu.roll(part, E // 2, 1) * sin
            o_ref[0, :, j * E : (j + 1) * E] = turned.astype(BF16)


def qkv_slot(slot, n, rank, xa, xb, gain, shift, wq, wk, wv, cos, sin, held):
    rows, half = xa.shape
    d = 2 * half
    local = wq.shape[1]
    cb = min(512, local)
    whole = lambda j, r: (0, 0)
    wspec = pl.BlockSpec((d, cb), lambda j, r: (0, j))
    tspec = pl.BlockSpec((1, rows, E), lambda j, r: (lax.rem(r[0] + slot, n), 0, 0))
    in_specs = [
        pl.BlockSpec((rows, half), whole),
        pl.BlockSpec((rows, half), whole),
        pl.BlockSpec((1, d), whole),
        pl.BlockSpec((1, d), whole),
        wspec,
        wspec,
        wspec,
        tspec,
        tspec,
    ]
    extra = [] if held is None else list(held)
    aliases = {} if held is None else {10 + i: i for i in range(4)}
    ospec = pl.BlockSpec((1, rows, cb), lambda j, r: (slot, 0, j))
    return pl.pallas_call(
        qkv_body,
        grid_spec=pltpu.PrefetchScalarGridSpec(
            num_scalar_prefetch=1,
            grid=(local // cb,),
            in_specs=in_specs + [pl.BlockSpec(memory_space=pl.ANY)] * len(extra),
            out_specs=[pl.BlockSpec((1, rows, d), lambda j, r: (slot, 0, 0)), ospec, ospec, ospec],
        ),
        out_shape=[jax.ShapeDtypeStruct((n, rows, d), BF16)]
        + [jax.ShapeDtypeStruct((n, rows, local), BF16)] * 3,
        input_output_aliases=aliases,
        compiler_params=params(56),
        cost_estimate=cost(6 * rows * d * local, 6 * d * local + 4 * rows * d),
        name="qkv_slot",
    )(rank, xa, xb, gain, shift, wq, wk, wv, cos, sin, *extra)


def first_key(block, rows):
    return max(0, block - (DOC_MAX - 1 + rows - 1) // rows)


def attend_body(rank_ref, q_ref, k_ref, v_ref, dcol_ref, drow_ref, hc_ref, o_ref):
    n, rows, _ = q_ref.shape
    rank = rank_ref[0]
    head = rank_ref[1] + pl.program_id(0)
    slot = lambda b: lax.rem(b + n - rank, n)
    factor = E ** (-0.5) * LOG2E
    low = lax.broadcasted_iota(jnp.int32, (rows, rows), 0) >= lax.broadcasted_iota(
        jnp.int32, (rows, rows), 1
    )
    for b in range(n):
        q = q_ref[slot(b)]
        doc = dcol_ref[b]
        keys = range(first_key(b, rows), b + 1)
        scores = []
        for c in keys:
            s = dot_t(q, k_ref[slot(c)])
            ok = doc == drow_ref[c]
            if c == b:
                ok = ok & low
            scores.append(jnp.where(ok, s, -1e30))
        top = scores[0]
        for s in scores[1:]:
            top = jnp.maximum(top, s)
        top = jnp.max(top, axis=1, keepdims=True)
        total = None
        out = None
        for c, s in zip(keys, scores):
            p = jnp.exp2((s - top) * factor)
            total = p if total is None else total + p
            o = dot_n(p.astype(BF16), v_ref[slot(c)])
            out = o if out is None else out + o
        total = jnp.sum(total, axis=1, keepdims=True)
        gate = jnp.where(hc_ref[b] > head, 1.0, 0.0)
        o_ref[slot(b)] = (out * (gate / total)).astype(BF16)


def attend(rank, q, k, v, docs_col, docs_row, heads_col):
    n, rows, local = q.shape
    spec = pl.BlockSpec((n, rows, E), lambda h, r: (0, 0, h))
    col = pl.BlockSpec((n, rows, 1), lambda h, r: (0, 0, 0))
    row = pl.BlockSpec((n, 1, rows), lambda h, r: (0, 0, 0))
    t = n * rows
    return pl.pallas_call(
        attend_body,
        grid_spec=pltpu.PrefetchScalarGridSpec(
            num_scalar_prefetch=1,
            grid=(local // E,),
            in_specs=[spec, spec, spec, col, row, col],
            out_specs=spec,
        ),
        out_shape=jax.ShapeDtypeStruct((n, rows, local), BF16),
        compiler_params=params(62),
        cost_estimate=cost(4 * t * t * local, 8 * t * local, t * t * local // E),
        name="attend",
    )(rank, q, k, v, docs_col, docs_row, heads_col)


def attend_back_body(
    rank_ref, q_ref, k_ref, v_ref, do_ref, dcol_ref, drow_ref, hc_ref, cos_ref, sin_ref, out_ref, dk_ref, dv_ref
):
    n, rows, _ = q_ref.shape
    rank = rank_ref[0]
    head = rank_ref[1] + pl.program_id(0)
    slot = lambda b: lax.rem(b + n - rank, n)
    scale = E ** (-0.5)
    factor = scale * LOG2E
    low = lax.broadcasted_iota(jnp.int32, (rows, rows), 0) <= lax.broadcasted_iota(
        jnp.int32, (rows, rows), 1
    )
    local = out_ref.shape[2] // 3
    lanes = lambda i: pl.ds(pl.multiple_of(i * local + pl.program_id(0) * E, E), E)
    dk_ref[...] = jnp.zeros_like(dk_ref)
    dv_ref[...] = jnp.zeros_like(dv_ref)

    def unrotate(w, b):
        w = w * scale
        return (w * cos_ref[b] - pltpu.roll(w, E // 2, 1) * sin_ref[b]).astype(BF16)

    for b in range(n):
        q = q_ref[slot(b)]
        grad = jnp.where(hc_ref[b] > head, do_ref[slot(b)].astype(F32), 0.0).astype(BF16)
        keys = range(first_key(b, rows), b + 1)
        scores = []
        for c in keys:
            s = dot_t(k_ref[slot(c)], q)
            ok = dcol_ref[c] == drow_ref[b]
            if c == b:
                ok = ok & low
            scores.append(jnp.where(ok, s, -1e30))
        top = scores[0]
        for s in scores[1:]:
            top = jnp.maximum(top, s)
        top = jnp.max(top, axis=0, keepdims=True)
        probs = [jnp.exp2((s - top) * factor) for s in scores]
        total = probs[0]
        for p in probs[1:]:
            total = total + p
        inv = 1.0 / jnp.sum(total, axis=0, keepdims=True)
        probs = [p * inv for p in probs]
        dprobs = [dot_t(v_ref[slot(c)], grad) for c in keys]
        delta = None
        for p, g in zip(probs, dprobs):
            delta = p * g if delta is None else delta + p * g
        delta = jnp.sum(delta, axis=0, keepdims=True)
        dq = None
        for c, p, g in zip(keys, probs, dprobs):
            ds = (p * (g - delta)).astype(BF16)
            dk_ref[c] += dot_n(ds, q)
            dv_ref[c] += dot_n(p.astype(BF16), grad)
            part = outer(ds, k_ref[slot(c)])
            dq = part if dq is None else dq + part
        out_ref[slot(b), :, lanes(0)] = unrotate(dq, b)
    for b in range(n):
        out_ref[slot(b), :, lanes(1)] = unrotate(dk_ref[b], b)
        out_ref[slot(b), :, lanes(2)] = dv_ref[b].astype(BF16)


def attend_back(rank, q, k, v, do, docs_col, docs_row, heads_col, cos, sin):
    n, rows, local = q.shape
    spec = pl.BlockSpec((n, rows, E), lambda h, r: (0, 0, h))
    col = pl.BlockSpec((n, rows, 1), lambda h, r: (0, 0, 0))
    row = pl.BlockSpec((n, 1, rows), lambda h, r: (0, 0, 0))
    table = pl.BlockSpec((n, rows, E), lambda h, r: (0, 0, 0))
    t = n * rows
    return pl.pallas_call(
        attend_back_body,
        grid_spec=pltpu.PrefetchScalarGridSpec(
            num_scalar_prefetch=1,
            grid=(local // E,),
            in_specs=[spec, spec, spec, spec, col, row, col, table, table],
            out_specs=pl.BlockSpec((n, rows, 3 * local), lambda h, r: (0, 0, 0)),
            scratch_shapes=[pltpu.VMEM((n, rows, E), F32), pltpu.VMEM((n, rows, E), F32)],
        ),
        out_shape=jax.ShapeDtypeStruct((n, rows, 3 * local), BF16),
        compiler_params=params(24),
        cost_estimate=cost(116e9, 14 * t * local),
        name="attend_back",
    )(rank, q, k, v, do, docs_col, docs_row, heads_col, cos, sin)


def mlp_body(slot, n, rank_ref, a_ref, gla_ref, glb_ref, gra_ref, grb_ref, up_ref, down_ref, bucket_ref, *rest):
    r_ref, du_ref, aa_ref, ga_ref = rest[-4:]
    rows, cb = a_ref.shape[0], up_ref.shape[1]

    @pl.when(pl.program_id(0) == 0)
    def _():
        aa_ref[0] = a_ref[...]
        ahead = rank_ref[0] + slot < n

        half = gla_ref.shape[1]

        def fill(first, second):
            ga_ref[0, :, :half] = first[...]
            ga_ref[0, :, half:] = second[...]

        pl.when(ahead)(functools.partial(fill, gla_ref, glb_ref))
        pl.when(jnp.logical_not(ahead))(functools.partial(fill, gra_ref, grb_ref))

    u = dot_n(a_ref[...], up_ref[...])
    dr = dot_n(ga_ref[0], down_ref[...]).astype(BF16).astype(F32)
    column = rank_ref[2] + pl.program_id(0) * cb + lax.broadcasted_iota(jnp.int32, (rows, cb), 1)
    lifted = jnp.where(column < (bucket_ref[0] + 1) * (FF // 4), jnp.maximum(u, 0.0), 0.0)
    r_ref[0] = (lifted * lifted).astype(BF16)
    du_ref[0] = (dr * (2.0 * lifted)).astype(BF16)


def mlp_slot(slot, n, rank, act, grads, up, down, bucket_col, held):
    rows, d = act.shape
    hidden = up.shape[1]
    cb = min(512, hidden)
    whole = lambda j, r: (0, 0)
    wspec = pl.BlockSpec((d, cb), lambda j, r: (0, j))
    extra = [] if held is None else list(held)
    aliases = {} if held is None else {9 + i: i for i in range(4)}
    ospec = pl.BlockSpec((1, rows, cb), lambda j, r: (slot, 0, j))
    aspec = pl.BlockSpec((1, rows, d), lambda j, r: (slot, 0, 0))
    return pl.pallas_call(
        functools.partial(mlp_body, slot, n),
        grid_spec=pltpu.PrefetchScalarGridSpec(
            num_scalar_prefetch=1,
            grid=(hidden // cb,),
            in_specs=[
                pl.BlockSpec((rows, d), whole),
            ]
            + [pl.BlockSpec((rows, d // 2), whole)] * 4
            + [
                wspec,
                wspec,
                pl.BlockSpec((1, rows, 1), lambda j, r: (lax.rem(r[0] + slot, n), 0, 0)),
            ]
            + [pl.BlockSpec(memory_space=pl.ANY)] * len(extra),
            out_specs=[ospec, ospec, aspec, aspec],
        ),
        out_shape=[jax.ShapeDtypeStruct((n, rows, hidden), BF16)] * 2
        + [jax.ShapeDtypeStruct((n, rows, d), BF16)] * 2,
        input_output_aliases=aliases,
        compiler_params=params(28),
        cost_estimate=cost(4 * rows * d * hidden, 4 * d * hidden + 4 * rows * (d + hidden)),
        name="mlp_slot",
    )(rank, act, *grads, up, down, bucket_col, *extra)


def dom_body(n, slots, rank_ref, slot_ref, *refs):
    dom_ref, all_ref = refs[-2:]
    count = sum(1 if s == 0 else 2 for s in slots)
    flows, w_ref = list(refs[:count]), refs[count]

    def fill(ref):
        all_ref[0] = ref[...]

    for i, s in enumerate(slots):
        here = pl.program_id(0) == i
        if s == 0:
            pl.when(here)(functools.partial(fill, flows[0]))
            flows = flows[1:]
        else:
            ahead = rank_ref[0] + s < n
            pl.when(here & ahead)(functools.partial(fill, flows[0]))
            pl.when(here & jnp.logical_not(ahead))(functools.partial(fill, flows[1]))
            flows = flows[2:]
    dom_ref[0] = dot_n(all_ref[0], w_ref[...]).astype(BF16)


def dom_part(n, slots, rank, flows, weight, held):
    rows, d = flows[0].shape
    local = weight.shape[1]
    whole = lambda i, r, s: (0, 0)
    extra = [] if held is None else list(held)
    at = 2 + len(flows) + 1
    return pl.pallas_call(
        functools.partial(dom_body, n, slots),
        grid_spec=pltpu.PrefetchScalarGridSpec(
            num_scalar_prefetch=2,
            grid=(len(slots),),
            in_specs=[pl.BlockSpec((rows, d), whole)] * len(flows)
            + [pl.BlockSpec((d, local), whole)]
            + [pl.BlockSpec(memory_space=pl.ANY)] * len(extra),
            out_specs=[
                pl.BlockSpec((1, rows, local), lambda i, r, s: (s[i], 0, 0)),
                pl.BlockSpec((1, rows, d), lambda i, r, s: (s[i], 0, 0)),
            ],
        ),
        out_shape=[
            jax.ShapeDtypeStruct((n, rows, local), BF16),
            jax.ShapeDtypeStruct((n, rows, d), BF16),
        ],
        input_output_aliases={at + i: i for i in range(len(extra))},
        compiler_params=params(24),
        cost_estimate=cost(
            2 * len(slots) * rows * d * local, 2 * d * local + 6 * len(slots) * rows * d
        ),
        name="dom_part",
    )(rank, jnp.asarray(slots, jnp.int32), *flows, weight, *extra)


def grad_body(has_sum, rank_ref, lhs_ref, rhs_ref, *rest):
    out = outer(lhs_ref[...], rhs_ref[...])
    if has_sum:
        rest[-1][0] = (out + rest[0][...].astype(F32)).astype(BF16)
    else:
        rest[-1][...] = out.astype(BF16)


def grad_half(lhs, rhs, rank, partner, which=0, moved=None, held=None):
    t, d = lhs.shape
    half = rhs.shape[1] // 2
    tile = min(512, d)
    col = (lambda r: 1 - r[3]) if partner else (lambda r: r[3])
    specs = [
        pl.BlockSpec((t, tile), lambda j, r: (0, j)),
        pl.BlockSpec((t, half), lambda j, r: (0, col(r))),
    ]
    args = [lhs, rhs]
    aliases = {}
    if partner:
        ospec = pl.BlockSpec((tile, half), lambda j, r: (j, 0))
        oshape = (d, half)
    else:
        specs.append(pl.BlockSpec((tile, half), lambda j, r: (j, 0)))
        args.append(moved)
        ospec = pl.BlockSpec((1, tile, half), lambda j, r: (which, j, 0))
        oshape = (2, d, half)
        if held is not None:
            specs.append(pl.BlockSpec(memory_space=pl.ANY))
            args.append(held)
            aliases = {4: 0}
    return pl.pallas_call(
        functools.partial(grad_body, not partner),
        grid_spec=pltpu.PrefetchScalarGridSpec(
            num_scalar_prefetch=1, grid=(d // tile,), in_specs=specs, out_specs=ospec
        ),
        out_shape=jax.ShapeDtypeStruct(oshape, BF16),
        input_output_aliases=aliases,
        compiler_params=params(20),
        cost_estimate=cost(1e6, 1e6),
        name="grad_half",
    )(rank, *args)


def attn_grad_body(partner, rank_ref, a_ref, s_ref, one_ref, key_ref, om_ref, *rest):
    out_ref = rest[-1]
    local = om_ref.shape[1]
    second = rank_ref[3] == (0 if partner else 1)
    act = a_ref[...]

    def put(cols, value):
        if not partner:
            value = value + rest[0][:, cols].astype(F32)
        out_ref[:, cols] = value.astype(BF16)

    put(slice(0, local), outer(act, one_ref[...]))

    @pl.when(second)
    def _():
        put(slice(local, 2 * local), outer(s_ref[...], om_ref[...]))

    @pl.when(jnp.logical_not(second))
    def _():
        put(slice(local, 2 * local), outer(act, key_ref[...]))


def attn_grads(act, states, dqkv, om, rank, moved=None):
    t, d = act.shape
    local = om.shape[1]
    tile = min(512, d)
    partner = moved is None
    pos = (lambda r: 1 - r[3]) if partner else (lambda r: r[3])
    col = pl.BlockSpec((t, tile), lambda j, r: (0, j))
    out = pl.BlockSpec((tile, 2 * local), lambda j, r: (j, 0))
    return pl.pallas_call(
        functools.partial(attn_grad_body, partner),
        grid_spec=pltpu.PrefetchScalarGridSpec(
            num_scalar_prefetch=1,
            grid=(d // tile,),
            in_specs=[
                col,
                pl.BlockSpec((t, tile), lambda j, r: (0, j * pos(r))),
                pl.BlockSpec((t, local), lambda j, r: (0, 2 * pos(r))),
                pl.BlockSpec((t, local), lambda j, r: (0, 1)),
                pl.BlockSpec((t, local), lambda j, r: (0, 0)),
            ]
            + ([] if partner else [out]),
            out_specs=out,
        ),
        out_shape=jax.ShapeDtypeStruct((d, 2 * local), BF16),
        compiler_params=params(28 if partner else 50),
        cost_estimate=cost(4e9 if partner else 1e6, 1e6),
        name="attn_grads",
    )(rank, act, states, dqkv, dqkv, om, *([] if partner else [moved]))


def term_body(x_ref, w_ref, *rest):
    out = dot_t(x_ref[0], w_ref[...])
    if len(rest) > 1:
        out = out + rest[0][...].astype(F32)
    rest[-1][...] = out.astype(BF16)


def block_term(acts, slot, weight, flops, moved=None, mib=16):
    _, rows, k = acts.shape
    d = weight.shape[0]
    tile = min(512, d)
    out = pl.BlockSpec((rows, tile), lambda j: (0, j))
    return pl.pallas_call(
        term_body,
        grid=(d // tile,),
        in_specs=[
            pl.BlockSpec((1, rows, k), lambda j: (slot, 0, 0)),
            pl.BlockSpec((tile, k), lambda j: (j, 0)),
        ]
        + ([] if moved is None else [out]),
        out_specs=out,
        out_shape=jax.ShapeDtypeStruct((rows, d), BF16),
        compiler_params=params(mib),
        cost_estimate=cost(flops, flops / 256),
        name="block_term",
    )(acts, weight, *([] if moved is None else [moved]))


def join_body(slot, first, rank_ref, moved_ref, term_ref, out_ref):
    adds = rank_ref[0] < first if slot >= 0 else rank_ref[0] >= first

    @pl.when(adds)
    def _():
        out_ref[...] = (moved_ref[...].astype(F32) + term_ref[0].astype(F32)).astype(BF16)

    @pl.when(jnp.logical_not(adds))
    def _():
        out_ref[...] = moved_ref[...]


def join(rank, moved, terms, slot, first, right, part=0):
    rows, d = moved.shape
    tile = min(128, rows)
    row = pl.BlockSpec((tile, d), lambda i, r: (i, 0))
    return pl.pallas_call(
        functools.partial(join_body, 0 if right else -1, first),
        grid_spec=pltpu.PrefetchScalarGridSpec(
            num_scalar_prefetch=1,
            grid=(rows // tile,),
            in_specs=[row, pl.BlockSpec((1, tile, d), lambda i, r: (slot, i, part))],
            out_specs=row,
        ),
        out_shape=jax.ShapeDtypeStruct((rows, d), BF16),
        compiler_params=params(8),
        cost_estimate=cost(1e6, 1e6),
        name="join",
    )(rank, moved, terms)


def last_body(x_ref, gain_ref, term_ref, moved_ref, state_ref, out_ref):
    gain = gain_ref[...]
    _, normed, inverse = norm_forward(x_ref[...].astype(F32), gain, gain)
    back = norm_backward(term_ref[...].astype(F32) + moved_ref[...].astype(F32), normed, inverse, gain)
    out_ref[...] = (state_ref[...] + back).astype(BF16)


def last_step(x, gain, term, moved, state):
    rows, d = x.shape
    tile = min(64, rows)
    row = lambda w: pl.BlockSpec((tile, w), lambda i: (i, 0))
    return pl.pallas_call(
        last_body,
        grid=(rows // tile,),
        in_specs=[row(d), pl.BlockSpec((1, d), lambda i: (0, 0)), row(d), row(d), row(d)],
        out_specs=row(d),
        out_shape=jax.ShapeDtypeStruct((rows, d), BF16),
        compiler_params=params(12),
        cost_estimate=cost(30e9, 12 * rows * d),
        name="last_step",
    )(x, gain, term, moved, state)


def tie(values, *others):
    values = tuple(values)
    return lax.optimization_barrier(values + others)[: len(values)]


def sum_over(vec, axis, moves):
    return sum((lax.ppermute(vec, axis, pairs) for pairs in moves), vec)


def per_device(
    n,
    n_dp,
    tokens,
    mixed_grad,
    doc_ids,
    head_count,
    width_bucket,
    first_gain,
    first_shift,
    query_weight,
    key_weight,
    value_weight,
    output_weight,
    second_gain,
    second_shift,
    up_weight,
    down_weight,
):
    rank = lax.axis_index("mp")
    rows, d = tokens.shape[1:]
    half = d // 2
    local = query_weight.shape[1]
    local_heads = local // E
    hidden = up_weight.shape[1]
    length = n * rows
    own = tokens[0]
    send = lambda v, pairs: lax.ppermute(v, "mp", pairs)
    ring = [(i, (i - 1) % n) for i in range(n)]
    hop = lambda v: send(v, ring)
    right_line = [(i, i + 1) for i in range(n - 1)]
    left_line = [(i + 1, i) for i in range(n - 1)]

    def tick(k, right, left, terms):
        if k:
            right = join(where, right, terms, n - k, k, True)
            left = join(where, left, terms, k, n - k, False)
        return send(right, right_line), send(left, left_line), right, left

    def owned(terms, right, left):
        return terms[0].astype(F32) + right.astype(F32) + left.astype(F32)

    low = lambda v: v.astype(BF16)
    flat = lambda v: v.reshape(length, v.shape[-1])
    add = lambda t, moved: (t.astype(F32) + moved.astype(F32)).astype(BF16)

    side = lax.rem(lax.axis_index("dp"), 2)
    where = jnp.stack([rank, rank * local_heads, rank * hidden, side]).astype(jnp.int32)
    swap = lambda v: lax.ppermute(v, "dp", [(i, i ^ 1) for i in range(n_dp)])
    sides = [list(range(c, n_dp, 2)) for c in range(2)]
    docs_col = doc_ids.reshape(n, rows, 1)
    docs_row = doc_ids.reshape(n, 1, rows)
    heads_col = head_count.reshape(n, rows, 1)
    bucket_col = width_bucket.reshape(n, rows, 1)
    cos, sin = (t.reshape(n, rows, E) for t in rotary_tables(length))
    gain1, shift1 = first_gain[None], first_shift[None]
    gain2, shift2 = second_gain[None], second_shift[None]

    held, block = None, [own[:, :half], own[:, half:]]
    for s in range(n):
        after = [None, None]
        for p in range(2):
            if s >= 1:
                block[p], *held = tie([block[p]] + list(held))
            if s < n - 1:
                after[p] = hop(block[p])
        held = qkv_slot(
            s, n, where, *block, gain1, shift1, query_weight, key_weight, value_weight, cos, sin, held
        )
        if s < n - 1:
            block = after
    first_all, query, keys, vals = held

    grad_own = mixed_grad[0]
    (own_grad,) = tie([grad_own], block[0])
    right = [own_grad[:, :half], own_grad[:, half:]]
    left = list(right)
    grads_r, grads_l = [list(right)], [list(left)]

    def half_tick(k):
        for p in range(2):
            if k:
                right[p] = join(where, right[p], terms, n - k, k, True, p)
                left[p] = join(where, left[p], terms, k, n - k, False, p)
            right[p], left[p] = send(right[p], right_line), send(left[p], left_line)

    half_tick(0)
    masked = attend(where, query, keys, vals, docs_col, docs_row, heads_col)
    terms = low(dot_t(flat(masked), output_weight)).reshape(n, rows, d)
    for k in range(1, n):
        grads_r.append(list(right))
        grads_l.append(list(left))
        half_tick(k)
    right, left = (jnp.concatenate(v, axis=1) for v in (right, left))
    attn = owned(terms, right, left)
    x_rows = own.astype(F32)
    state = x_rows + attn
    second_out, normed_two, inverse_two = norm_forward(state, gain2, shift2)

    weights = jnp.concatenate([query_weight, key_weight, value_weight], axis=1)
    held, moved = None, None
    (block,) = tie([low(second_out)], weights)
    for s in range(n):
        if s >= 1:
            block, *held = tie([block] + list(held), sent)
        after = hop(block) if s < n - 1 else None
        held = mlp_slot(
            s, n, where, block, grads_l[s] + grads_r[n - s if s else 0], up_weight, down_weight, bucket_col, held
        )
        if s >= 1:
            fused = moved if s == n - 1 and s > 1 else None
            sent = block_term(held[1], s, up_weight, 2 * rows * d * hidden, fused, 16)
            if s > 1 and fused is None:
                sent = add(sent, moved)
            moved = hop(sent)
        else:
            sent = term0 = block_term(held[1], 0, up_weight, 2 * rows * d * hidden, None, 16)
        block = after
    active, grad_upper, second_all, grad_all = held
    grad_all, active, second_all, grad_upper = tie([grad_all, active, second_all, grad_upper], sent)
    gifts = [
        grad_half(flat(grad_all), flat(active), where, True),
        grad_half(flat(second_all), flat(grad_upper), where, True),
    ]
    (moved,) = tie([moved], *gifts)
    down_gift, up_gift = (swap(v) for v in gifts)
    grad_second = term0.astype(F32) + moved.astype(F32)
    back_two = norm_backward(grad_second, normed_two, inverse_two, gain2)
    second_gain_part = jnp.sum(grad_second * normed_two, axis=0)
    second_shift_part = jnp.sum(grad_second, axis=0)
    grad_state = grad_own.astype(F32) + back_two

    start = low(grad_state)
    grad_all, active, start = tie([grad_all, active, start])
    right = left = start
    rights, lefts = [start], [start]
    right, left, _, _ = tick(0, right, left, None)
    ffn = low(dot_t(flat(active), down_weight)).reshape(n, rows, d)
    pair = grad_half(flat(grad_all), flat(active), where, False, 0, down_gift)
    (right,) = tie([right], pair)
    (left,) = tie([left], pair)
    for k in range(1, n):
        rights.append(right)
        lefts.append(left)
        right, left, went_r, went_l = tick(k, right, left, ffn)
        if k == 1:
            second_all, grad_upper = tie([second_all, grad_upper], went_r, went_l)
            pair = grad_half(flat(second_all), flat(grad_upper), where, False, 1, up_gift, pair)
            wide_grad = lax.psum_scatter(pair, "dp", scatter_dimension=1, axis_index_groups=sides, tiled=True)
            (right,) = tie([right], pair)
            (left,) = tie([left], pair)
    late = sorted({1, n - 1})
    early = [s for s in range(n) if s not in late]
    pick = lambda slots: sum(([start] if s == 0 else [lefts[s], rights[n - s]] for s in slots), [])
    held = dom_part(n, early, where, pick(early), output_weight, None)
    grad_masked, state_all = dom_part(n, late, where, pick(late), output_weight, held)
    dqkv = attend_back(
        where, query, keys, vals, grad_masked, docs_col, docs_row, heads_col, cos, sin
    )
    mixed = low(state + owned(ffn, right, left))

    (dqkv,) = tie([dqkv], right, left)
    def whole(part):
        span = part.shape[-2] // 2
        mine = lax.dynamic_slice_in_dim(part, side * span, span, part.ndim - 2)
        got = swap(lax.dynamic_slice_in_dim(part, (1 - side) * span, span, part.ndim - 2))
        return jnp.where(side == 0, mine, got).astype(F32), jnp.where(side == 0, got, mine).astype(F32)

    tokens_of = lambda v: (flat(first_all), flat(state_all), flat(v), flat(masked), where)
    sent = block_term(dqkv, 1, weights, 1e6)
    (dqkv,) = tie([dqkv], sent)
    moved = hop(sent)
    gift = attn_grads(*tokens_of(dqkv))
    (dqkv,) = tie([dqkv], gift)
    terms = {1: sent, 2: block_term(dqkv, 2, weights, 1e6)}
    (dqkv,) = tie([dqkv], terms[2])
    attn_term = attn_grads(*tokens_of(dqkv), swap(gift))
    (late,) = tie([attn_term], wide_grad)
    attn_grad = lax.psum_scatter(late, "dp", scatter_dimension=0, axis_index_groups=sides, tiled=True)
    (moved,) = tie([moved], attn_term)
    sent2 = sent = add(terms[2], moved)
    moved = hop(sent)
    for s in range(3, n):
        (dqkv,) = tie([dqkv], sent)
        terms[s] = block_term(dqkv, s, weights, 1e6)
    (dqkv,) = tie([dqkv], terms[n - 1])
    terms[0] = block_term(dqkv, 0, weights, 1e6)
    held = tie([terms[s] for s in range(n)], sent2)
    sum_d = sum(jnp.sum(v.astype(F32), axis=0) for v in held)
    sum_da = sum(jnp.sum(v.astype(F32) * first_all[s].astype(F32), axis=0) for s, v in enumerate(held))
    first_shift_part = sum_d
    first_gain_part = (sum_da - first_shift * sum_d) / first_gain

    lead = (rank == 0).astype(F32)
    bucket_part = lead * jnp.sum(
        (width_bucket[0][:, None] == jnp.arange(4, dtype=jnp.int32)[None, :]).astype(F32), axis=0
    )
    head_part = lead * jnp.sum(
        (head_count[0][:, None] == jnp.arange(1, HEADS + 1, dtype=jnp.int32)[None, :]).astype(F32),
        axis=0,
    )
    small = jnp.concatenate(
        [
            first_gain_part,
            first_shift_part,
            second_gain_part,
            second_shift_part,
            bucket_part,
            head_part,
            jnp.zeros((128 - 4 - HEADS,), F32),
        ]
    )
    small = sum_over(small, "dp", [[(i, i ^ 1) for i in range(n_dp)]])
    wide = jnp.concatenate(whole(wide_grad), axis=2)
    for s in range(3, n):
        if s == 3:
            moved, wide = tie([moved, wide])
        sent = add(terms[s], moved)
        moved = hop(sent)

    planes = tie([send(small, [(i, (i + m) % n) for i in range(n)]) for m in range(1, n)], sent)
    small = small + sum(planes)
    others = [
        lax.ppermute(small, "dp", [(i, (i + 2 * m) % n_dp) for i in range(n_dp)])
        for m in range(1, n_dp // 2)
    ]
    input_grad = last_step(own, gain1, terms[0], moved, grad_state)
    small = small + sum(tie(others, input_grad))

    query_key, value_out = whole(attn_grad)
    return (
        mixed[None],
        input_grad[None],
        small[:d],
        small[d : 2 * d],
        query_key[:, :local],
        query_key[:, local:],
        value_out[:, :local],
        value_out[:, local:],
        small[2 * d : 3 * d],
        small[3 * d : 4 * d],
        wide[1],
        wide[0],
        small[4 * d : 4 * d + 4].astype(jnp.int32),
        small[4 * d + 4 : 4 * d + 4 + HEADS].astype(jnp.int32),
    )


def solution(mesh):
    token, seq, copy, col = P("dp", "mp", None), P("dp", None), P(), P(None, "mp")
    grad = P("dp", "mp")
    return jax.shard_map(
        functools.partial(per_device, mesh.shape["mp"], mesh.shape["dp"]),
        mesh=mesh,
        in_specs=(token, token, seq, seq, seq, copy, copy, col, col, col, col, copy, copy, col, col),
        out_specs=(token, token, copy, copy, grad, grad, grad, grad, copy, copy, grad, grad, copy, copy),
        check_vma=False,
    )
```

```python
import functools
import jax
import jax.numpy as jnp
from jax import lax
from jax.experimental import pallas as pl
from jax.experimental.pallas import tpu as pltpu
from jax.sharding import PartitionSpec as P

HEADS = 16
E = 128
FF = 8192
EPS = 1e-05
DOC_MAX = 512
LOG2E = 1.4426950408889634
F32 = jnp.float32
BF16 = jnp.bfloat16


def params(mib):
    return pltpu.CompilerParams(vmem_limit_bytes=mib << 20)


def cost(flops, nbytes, trans=0):
    return pl.CostEstimate(flops=int(flops), bytes_accessed=int(nbytes), transcendentals=int(trans))


def norm_forward(values, gain, shift):
    mean = jnp.mean(values, axis=-1, keepdims=True)
    cent = values - mean
    inverse = lax.rsqrt(jnp.mean(cent * cent, axis=-1, keepdims=True) + EPS)
    normed = cent * inverse
    return (normed * gain + shift, normed, inverse)


def norm_backward(grad_out, normed, inverse, gain):
    scaled = grad_out * gain
    return inverse * (
        scaled
        - jnp.mean(scaled, axis=-1, keepdims=True)
        - normed * jnp.mean(scaled * normed, axis=-1, keepdims=True)
    )


def rotary_tables(length):
    half = E // 2
    freq = 10000.0 ** (-(jnp.arange(half, dtype=F32) * 2.0 / E))
    angle = jnp.arange(length, dtype=F32)[:, None] * freq[None, :]
    cos, sin = jnp.cos(angle), jnp.sin(angle)
    return jnp.concatenate([cos, cos], axis=1), jnp.concatenate([-sin, sin], axis=1)


def dot_t(left, right):
    return lax.dot_general(left, right, (((1,), (1,)), ((), ())), preferred_element_type=F32)


def dot_n(left, right):
    return lax.dot_general(left, right, (((1,), (0,)), ((), ())), preferred_element_type=F32)


def outer(left, right):
    return lax.dot_general(left, right, (((0,), (0,)), ((), ())), preferred_element_type=F32)


def qkv_body(rank_ref, xa_ref, xb_ref, gain_ref, shift_ref, wq_ref, wk_ref, wv_ref, cos_ref, sin_ref, *rest):
    a_ref, q_ref, k_ref, v_ref = rest[-4:]

    @pl.when(pl.program_id(0) == 0)
    def _():
        x = jnp.concatenate([xa_ref[...], xb_ref[...]], axis=1).astype(F32)
        out, _, _ = norm_forward(x, gain_ref[...], shift_ref[...])
        a_ref[0] = out.astype(BF16)

    act = a_ref[0]
    cos, sin = cos_ref[0], sin_ref[0]
    v_ref[0] = dot_n(act, wv_ref[...]).astype(BF16)
    for w_ref, o_ref in ((wq_ref, q_ref), (wk_ref, k_ref)):
        lin = dot_n(act, w_ref[...])
        for j in range(lin.shape[1] // E):
            part = lin[:, j * E : (j + 1) * E]
            turned = part * cos + pltpu.roll(part, E // 2, 1) * sin
            o_ref[0, :, j * E : (j + 1) * E] = turned.astype(BF16)


def qkv_slot(slot, n, rank, xa, xb, gain, shift, wq, wk, wv, cos, sin, held):
    rows, half = xa.shape
    d = 2 * half
    local = wq.shape[1]
    cb = min(512, local)
    whole = lambda j, r: (0, 0)
    wspec = pl.BlockSpec((d, cb), lambda j, r: (0, j))
    tspec = pl.BlockSpec((1, rows, E), lambda j, r: (lax.rem(r[0] + slot, n), 0, 0))
    in_specs = [
        pl.BlockSpec((rows, half), whole),
        pl.BlockSpec((rows, half), whole),
        pl.BlockSpec((1, d), whole),
        pl.BlockSpec((1, d), whole),
        wspec,
        wspec,
        wspec,
        tspec,
        tspec,
    ]
    extra = [] if held is None else list(held)
    aliases = {} if held is None else {10 + i: i for i in range(4)}
    ospec = pl.BlockSpec((1, rows, cb), lambda j, r: (slot, 0, j))
    return pl.pallas_call(
        qkv_body,
        grid_spec=pltpu.PrefetchScalarGridSpec(
            num_scalar_prefetch=1,
            grid=(local // cb,),
            in_specs=in_specs + [pl.BlockSpec(memory_space=pl.ANY)] * len(extra),
            out_specs=[pl.BlockSpec((1, rows, d), lambda j, r: (slot, 0, 0)), ospec, ospec, ospec],
        ),
        out_shape=[jax.ShapeDtypeStruct((n, rows, d), BF16)]
        + [jax.ShapeDtypeStruct((n, rows, local), BF16)] * 3,
        input_output_aliases=aliases,
        compiler_params=params(56),
        cost_estimate=cost(6 * rows * d * local, 6 * d * local + 4 * rows * d),
        name="qkv_slot",
    )(rank, xa, xb, gain, shift, wq, wk, wv, cos, sin, *extra)


def first_key(block, rows):
    return max(0, block - (DOC_MAX - 1 + rows - 1) // rows)


def attend_body(rank_ref, q_ref, k_ref, v_ref, dcol_ref, drow_ref, hc_ref, o_ref):
    n, rows, _ = q_ref.shape
    rank = rank_ref[0]
    head = rank_ref[1] + pl.program_id(0)
    slot = lambda b: lax.rem(b + n - rank, n)
    factor = E ** (-0.5) * LOG2E
    low = lax.broadcasted_iota(jnp.int32, (rows, rows), 0) >= lax.broadcasted_iota(
        jnp.int32, (rows, rows), 1
    )
    for b in range(n):
        q = q_ref[slot(b)]
        doc = dcol_ref[b]
        keys = range(first_key(b, rows), b + 1)
        scores = []
        for c in keys:
            s = dot_t(q, k_ref[slot(c)])
            ok = doc == drow_ref[c]
            if c == b:
                ok = ok & low
            scores.append(jnp.where(ok, s, -1e30))
        top = scores[0]
        for s in scores[1:]:
            top = jnp.maximum(top, s)
        top = jnp.max(top, axis=1, keepdims=True)
        total = None
        out = None
        for c, s in zip(keys, scores):
            p = jnp.exp2((s - top) * factor)
            total = p if total is None else total + p
            o = dot_n(p.astype(BF16), v_ref[slot(c)])
            out = o if out is None else out + o
        total = jnp.sum(total, axis=1, keepdims=True)
        gate = jnp.where(hc_ref[b] > head, 1.0, 0.0)
        o_ref[slot(b)] = (out * (gate / total)).astype(BF16)


def attend(rank, q, k, v, docs_col, docs_row, heads_col):
    n, rows, local = q.shape
    spec = pl.BlockSpec((n, rows, E), lambda h, r: (0, 0, h))
    col = pl.BlockSpec((n, rows, 1), lambda h, r: (0, 0, 0))
    row = pl.BlockSpec((n, 1, rows), lambda h, r: (0, 0, 0))
    t = n * rows
    return pl.pallas_call(
        attend_body,
        grid_spec=pltpu.PrefetchScalarGridSpec(
            num_scalar_prefetch=1,
            grid=(local // E,),
            in_specs=[spec, spec, spec, col, row, col],
            out_specs=spec,
        ),
        out_shape=jax.ShapeDtypeStruct((n, rows, local), BF16),
        compiler_params=params(62),
        cost_estimate=cost(4 * t * t * local, 8 * t * local, t * t * local // E),
        name="attend",
    )(rank, q, k, v, docs_col, docs_row, heads_col)


def attend_back_body(
    rank_ref, q_ref, k_ref, v_ref, do_ref, dcol_ref, drow_ref, hc_ref, cos_ref, sin_ref, out_ref, dk_ref, dv_ref
):
    n, rows, _ = q_ref.shape
    rank = rank_ref[0]
    head = rank_ref[1] + pl.program_id(0)
    slot = lambda b: lax.rem(b + n - rank, n)
    scale = E ** (-0.5)
    factor = scale * LOG2E
    low = lax.broadcasted_iota(jnp.int32, (rows, rows), 0) <= lax.broadcasted_iota(
        jnp.int32, (rows, rows), 1
    )
    local = out_ref.shape[2] // 3
    lanes = lambda i: pl.ds(pl.multiple_of(i * local + pl.program_id(0) * E, E), E)
    dk_ref[...] = jnp.zeros_like(dk_ref)
    dv_ref[...] = jnp.zeros_like(dv_ref)

    def unrotate(w, b):
        w = w * scale
        return (w * cos_ref[b] - pltpu.roll(w, E // 2, 1) * sin_ref[b]).astype(BF16)

    for b in range(n):
        q = q_ref[slot(b)]
        grad = jnp.where(hc_ref[b] > head, do_ref[slot(b)].astype(F32), 0.0).astype(BF16)
        keys = range(first_key(b, rows), b + 1)
        scores = []
        for c in keys:
            s = dot_t(k_ref[slot(c)], q)
            ok = dcol_ref[c] == drow_ref[b]
            if c == b:
                ok = ok & low
            scores.append(jnp.where(ok, s, -1e30))
        top = scores[0]
        for s in scores[1:]:
            top = jnp.maximum(top, s)
        top = jnp.max(top, axis=0, keepdims=True)
        probs = [jnp.exp2((s - top) * factor) for s in scores]
        total = probs[0]
        for p in probs[1:]:
            total = total + p
        inv = 1.0 / jnp.sum(total, axis=0, keepdims=True)
        probs = [p * inv for p in probs]
        dprobs = [dot_t(v_ref[slot(c)], grad) for c in keys]
        delta = None
        for p, g in zip(probs, dprobs):
            delta = p * g if delta is None else delta + p * g
        delta = jnp.sum(delta, axis=0, keepdims=True)
        dq = None
        for c, p, g in zip(keys, probs, dprobs):
            ds = (p * (g - delta)).astype(BF16)
            dk_ref[c] += dot_n(ds, q)
            dv_ref[c] += dot_n(p.astype(BF16), grad)
            part = outer(ds, k_ref[slot(c)])
            dq = part if dq is None else dq + part
        out_ref[slot(b), :, lanes(0)] = unrotate(dq, b)
    for b in range(n):
        out_ref[slot(b), :, lanes(1)] = unrotate(dk_ref[b], b)
        out_ref[slot(b), :, lanes(2)] = dv_ref[b].astype(BF16)


def attend_back(rank, q, k, v, do, docs_col, docs_row, heads_col, cos, sin):
    n, rows, local = q.shape
    spec = pl.BlockSpec((n, rows, E), lambda h, r: (0, 0, h))
    col = pl.BlockSpec((n, rows, 1), lambda h, r: (0, 0, 0))
    row = pl.BlockSpec((n, 1, rows), lambda h, r: (0, 0, 0))
    table = pl.BlockSpec((n, rows, E), lambda h, r: (0, 0, 0))
    t = n * rows
    return pl.pallas_call(
        attend_back_body,
        grid_spec=pltpu.PrefetchScalarGridSpec(
            num_scalar_prefetch=1,
            grid=(local // E,),
            in_specs=[spec, spec, spec, spec, col, row, col, table, table],
            out_specs=pl.BlockSpec((n, rows, 3 * local), lambda h, r: (0, 0, 0)),
            scratch_shapes=[pltpu.VMEM((n, rows, E), F32), pltpu.VMEM((n, rows, E), F32)],
        ),
        out_shape=jax.ShapeDtypeStruct((n, rows, 3 * local), BF16),
        compiler_params=params(24),
        cost_estimate=cost(116e9, 14 * t * local),
        name="attend_back",
    )(rank, q, k, v, do, docs_col, docs_row, heads_col, cos, sin)


def mlp_body(slot, n, rank_ref, a_ref, gla_ref, glb_ref, gra_ref, grb_ref, up_ref, down_ref, bucket_ref, *rest):
    r_ref, du_ref, aa_ref, ga_ref = rest[-4:]
    rows, cb = a_ref.shape[0], up_ref.shape[1]

    @pl.when(pl.program_id(0) == 0)
    def _():
        aa_ref[0] = a_ref[...]
        ahead = rank_ref[0] + slot < n

        half = gla_ref.shape[1]

        def fill(first, second):
            ga_ref[0, :, :half] = first[...]
            ga_ref[0, :, half:] = second[...]

        pl.when(ahead)(functools.partial(fill, gla_ref, glb_ref))
        pl.when(jnp.logical_not(ahead))(functools.partial(fill, gra_ref, grb_ref))

    u = dot_n(a_ref[...], up_ref[...])
    dr = dot_n(ga_ref[0], down_ref[...]).astype(BF16).astype(F32)
    column = rank_ref[2] + pl.program_id(0) * cb + lax.broadcasted_iota(jnp.int32, (rows, cb), 1)
    lifted = jnp.where(column < (bucket_ref[0] + 1) * (FF // 4), jnp.maximum(u, 0.0), 0.0)
    r_ref[0] = (lifted * lifted).astype(BF16)
    du_ref[0] = (dr * (2.0 * lifted)).astype(BF16)


def mlp_slot(slot, n, rank, act, grads, up, down, bucket_col, held):
    rows, d = act.shape
    hidden = up.shape[1]
    cb = min(512, hidden)
    whole = lambda j, r: (0, 0)
    wspec = pl.BlockSpec((d, cb), lambda j, r: (0, j))
    extra = [] if held is None else list(held)
    aliases = {} if held is None else {9 + i: i for i in range(4)}
    ospec = pl.BlockSpec((1, rows, cb), lambda j, r: (slot, 0, j))
    aspec = pl.BlockSpec((1, rows, d), lambda j, r: (slot, 0, 0))
    return pl.pallas_call(
        functools.partial(mlp_body, slot, n),
        grid_spec=pltpu.PrefetchScalarGridSpec(
            num_scalar_prefetch=1,
            grid=(hidden // cb,),
            in_specs=[
                pl.BlockSpec((rows, d), whole),
            ]
            + [pl.BlockSpec((rows, d // 2), whole)] * 4
            + [
                wspec,
                wspec,
                pl.BlockSpec((1, rows, 1), lambda j, r: (lax.rem(r[0] + slot, n), 0, 0)),
            ]
            + [pl.BlockSpec(memory_space=pl.ANY)] * len(extra),
            out_specs=[ospec, ospec, aspec, aspec],
        ),
        out_shape=[jax.ShapeDtypeStruct((n, rows, hidden), BF16)] * 2
        + [jax.ShapeDtypeStruct((n, rows, d), BF16)] * 2,
        input_output_aliases=aliases,
        compiler_params=params(28),
        cost_estimate=cost(4 * rows * d * hidden, 4 * d * hidden + 4 * rows * (d + hidden)),
        name="mlp_slot",
    )(rank, act, *grads, up, down, bucket_col, *extra)


def dom_body(n, slots, rank_ref, slot_ref, *refs):
    dom_ref, all_ref = refs[-2:]
    count = sum(1 if s == 0 else 2 for s in slots)
    flows, w_ref = list(refs[:count]), refs[count]

    def fill(ref):
        all_ref[0] = ref[...]

    for i, s in enumerate(slots):
        here = pl.program_id(0) == i
        if s == 0:
            pl.when(here)(functools.partial(fill, flows[0]))
            flows = flows[1:]
        else:
            ahead = rank_ref[0] + s < n
            pl.when(here & ahead)(functools.partial(fill, flows[0]))
            pl.when(here & jnp.logical_not(ahead))(functools.partial(fill, flows[1]))
            flows = flows[2:]
    dom_ref[0] = dot_n(all_ref[0], w_ref[...]).astype(BF16)


def dom_part(n, slots, rank, flows, weight, held):
    rows, d = flows[0].shape
    local = weight.shape[1]
    whole = lambda i, r, s: (0, 0)
    extra = [] if held is None else list(held)
    at = 2 + len(flows) + 1
    return pl.pallas_call(
        functools.partial(dom_body, n, slots),
        grid_spec=pltpu.PrefetchScalarGridSpec(
            num_scalar_prefetch=2,
            grid=(len(slots),),
            in_specs=[pl.BlockSpec((rows, d), whole)] * len(flows)
            + [pl.BlockSpec((d, local), whole)]
            + [pl.BlockSpec(memory_space=pl.ANY)] * len(extra),
            out_specs=[
                pl.BlockSpec((1, rows, local), lambda i, r, s: (s[i], 0, 0)),
                pl.BlockSpec((1, rows, d), lambda i, r, s: (s[i], 0, 0)),
            ],
        ),
        out_shape=[
            jax.ShapeDtypeStruct((n, rows, local), BF16),
            jax.ShapeDtypeStruct((n, rows, d), BF16),
        ],
        input_output_aliases={at + i: i for i in range(len(extra))},
        compiler_params=params(24),
        cost_estimate=cost(
            2 * len(slots) * rows * d * local, 2 * d * local + 6 * len(slots) * rows * d
        ),
        name="dom_part",
    )(rank, jnp.asarray(slots, jnp.int32), *flows, weight, *extra)


def grad_body(has_sum, rank_ref, lhs_ref, rhs_ref, *rest):
    out = outer(lhs_ref[...], rhs_ref[...])
    if has_sum:
        rest[-1][0] = (out + rest[0][...].astype(F32)).astype(BF16)
    else:
        rest[-1][...] = out.astype(BF16)


def grad_half(lhs, rhs, rank, partner, which=0, moved=None, held=None):
    t, d = lhs.shape
    half = rhs.shape[1] // 2
    tile = min(512, d)
    col = (lambda r: 1 - r[3]) if partner else (lambda r: r[3])
    specs = [
        pl.BlockSpec((t, tile), lambda j, r: (0, j)),
        pl.BlockSpec((t, half), lambda j, r: (0, col(r))),
    ]
    args = [lhs, rhs]
    aliases = {}
    if partner:
        ospec = pl.BlockSpec((tile, half), lambda j, r: (j, 0))
        oshape = (d, half)
    else:
        specs.append(pl.BlockSpec((tile, half), lambda j, r: (j, 0)))
        args.append(moved)
        ospec = pl.BlockSpec((1, tile, half), lambda j, r: (which, j, 0))
        oshape = (2, d, half)
        if held is not None:
            specs.append(pl.BlockSpec(memory_space=pl.ANY))
            args.append(held)
            aliases = {4: 0}
    return pl.pallas_call(
        functools.partial(grad_body, not partner),
        grid_spec=pltpu.PrefetchScalarGridSpec(
            num_scalar_prefetch=1, grid=(d // tile,), in_specs=specs, out_specs=ospec
        ),
        out_shape=jax.ShapeDtypeStruct(oshape, BF16),
        input_output_aliases=aliases,
        compiler_params=params(20),
        cost_estimate=cost(1e6, 1e6),
        name="grad_half",
    )(rank, *args)


def attn_grad_body(partner, rank_ref, a_ref, s_ref, one_ref, key_ref, om_ref, *rest):
    out_ref = rest[-1]
    local = om_ref.shape[1]
    second = rank_ref[3] == (0 if partner else 1)
    act = a_ref[...]

    def put(cols, value):
        if not partner:
            value = value + rest[0][:, cols].astype(F32)
        out_ref[:, cols] = value.astype(BF16)

    put(slice(0, local), outer(act, one_ref[...]))

    @pl.when(second)
    def _():
        put(slice(local, 2 * local), outer(s_ref[...], om_ref[...]))

    @pl.when(jnp.logical_not(second))
    def _():
        put(slice(local, 2 * local), outer(act, key_ref[...]))


def attn_grads(act, states, dqkv, om, rank, moved=None):
    t, d = act.shape
    local = om.shape[1]
    tile = min(512, d)
    partner = moved is None
    pos = (lambda r: 1 - r[3]) if partner else (lambda r: r[3])
    col = pl.BlockSpec((t, tile), lambda j, r: (0, j))
    out = pl.BlockSpec((tile, 2 * local), lambda j, r: (j, 0))
    return pl.pallas_call(
        functools.partial(attn_grad_body, partner),
        grid_spec=pltpu.PrefetchScalarGridSpec(
            num_scalar_prefetch=1,
            grid=(d // tile,),
            in_specs=[
                col,
                pl.BlockSpec((t, tile), lambda j, r: (0, j * pos(r))),
                pl.BlockSpec((t, local), lambda j, r: (0, 2 * pos(r))),
                pl.BlockSpec((t, local), lambda j, r: (0, 1)),
                pl.BlockSpec((t, local), lambda j, r: (0, 0)),
            ]
            + ([] if partner else [out]),
            out_specs=out,
        ),
        out_shape=jax.ShapeDtypeStruct((d, 2 * local), BF16),
        compiler_params=params(28 if partner else 50),
        cost_estimate=cost(1e6 if partner else 1e6, 1e6),
        name="attn_grads",
    )(rank, act, states, dqkv, dqkv, om, *([] if partner else [moved]))


def term_body(x_ref, w_ref, *rest):
    out = dot_t(x_ref[0], w_ref[...])
    if len(rest) > 1:
        out = out + rest[0][...].astype(F32)
    rest[-1][...] = out.astype(BF16)


def block_term(acts, slot, weight, flops, moved=None, mib=16):
    _, rows, k = acts.shape
    d = weight.shape[0]
    tile = min(512, d)
    out = pl.BlockSpec((rows, tile), lambda j: (0, j))
    return pl.pallas_call(
        term_body,
        grid=(d // tile,),
        in_specs=[
            pl.BlockSpec((1, rows, k), lambda j: (slot, 0, 0)),
            pl.BlockSpec((tile, k), lambda j: (j, 0)),
        ]
        + ([] if moved is None else [out]),
        out_specs=out,
        out_shape=jax.ShapeDtypeStruct((rows, d), BF16),
        compiler_params=params(mib),
        cost_estimate=cost(flops, flops / 256),
        name="block_term",
    )(acts, weight, *([] if moved is None else [moved]))


def join_body(slot, first, rank_ref, moved_ref, term_ref, out_ref):
    adds = rank_ref[0] < first if slot >= 0 else rank_ref[0] >= first

    @pl.when(adds)
    def _():
        out_ref[...] = (moved_ref[...].astype(F32) + term_ref[0].astype(F32)).astype(BF16)

    @pl.when(jnp.logical_not(adds))
    def _():
        out_ref[...] = moved_ref[...]


def join(rank, moved, terms, slot, first, right, part=0, flops=1e6):
    rows, d = moved.shape
    tile = min(128, rows)
    row = pl.BlockSpec((tile, d), lambda i, r: (i, 0))
    return pl.pallas_call(
        functools.partial(join_body, 0 if right else -1, first),
        grid_spec=pltpu.PrefetchScalarGridSpec(
            num_scalar_prefetch=1,
            grid=(rows // tile,),
            in_specs=[row, pl.BlockSpec((1, tile, d), lambda i, r: (slot, i, part))],
            out_specs=row,
        ),
        out_shape=jax.ShapeDtypeStruct((rows, d), BF16),
        compiler_params=params(8),
        cost_estimate=cost(flops, 1e6),
        name="join",
    )(rank, moved, terms)


def last_body(x_ref, gain_ref, term_ref, moved_ref, state_ref, out_ref):
    gain = gain_ref[...]
    _, normed, inverse = norm_forward(x_ref[...].astype(F32), gain, gain)
    back = norm_backward(term_ref[...].astype(F32) + moved_ref[...].astype(F32), normed, inverse, gain)
    out_ref[...] = (state_ref[...] + back).astype(BF16)


def last_step(x, gain, term, moved, state):
    rows, d = x.shape
    tile = min(64, rows)
    row = lambda w: pl.BlockSpec((tile, w), lambda i: (i, 0))
    return pl.pallas_call(
        last_body,
        grid=(rows // tile,),
        in_specs=[row(d), pl.BlockSpec((1, d), lambda i: (0, 0)), row(d), row(d), row(d)],
        out_specs=row(d),
        out_shape=jax.ShapeDtypeStruct((rows, d), BF16),
        compiler_params=params(12),
        cost_estimate=cost(1e6, 12 * rows * d),
        name="last_step",
    )(x, gain, term, moved, state)


def tie(values, *others):
    values = tuple(values)
    return lax.optimization_barrier(values + others)[: len(values)]


def sum_over(vec, axis, moves):
    return sum((lax.ppermute(vec, axis, pairs) for pairs in moves), vec)


def per_device(
    n,
    n_dp,
    tokens,
    mixed_grad,
    doc_ids,
    head_count,
    width_bucket,
    first_gain,
    first_shift,
    query_weight,
    key_weight,
    value_weight,
    output_weight,
    second_gain,
    second_shift,
    up_weight,
    down_weight,
):
    rank = lax.axis_index("mp")
    rows, d = tokens.shape[1:]
    half = d // 2
    local = query_weight.shape[1]
    local_heads = local // E
    hidden = up_weight.shape[1]
    length = n * rows
    own = tokens[0]
    send = lambda v, pairs: lax.ppermute(v, "mp", pairs)
    ring = [(i, (i - 1) % n) for i in range(n)]
    hop = lambda v: send(v, ring)
    right_line = [(i, i + 1) for i in range(n - 1)]
    left_line = [(i + 1, i) for i in range(n - 1)]

    def tick(k, right, left, terms):
        if k:
            right = join(where, right, terms, n - k, k, True)
            left = join(where, left, terms, k, n - k, False)
        return send(right, right_line), send(left, left_line), right, left

    def owned(terms, right, left):
        return terms[0].astype(F32) + right.astype(F32) + left.astype(F32)

    low = lambda v: v.astype(BF16)
    flat = lambda v: v.reshape(length, v.shape[-1])
    add = lambda t, moved: (t.astype(F32) + moved.astype(F32)).astype(BF16)

    side = lax.rem(lax.axis_index("dp"), 2)
    where = jnp.stack([rank, rank * local_heads, rank * hidden, side]).astype(jnp.int32)
    swap = lambda v: lax.ppermute(v, "dp", [(i, i ^ 1) for i in range(n_dp)])
    sides = [list(range(c, n_dp, 2)) for c in range(2)]
    docs_col = doc_ids.reshape(n, rows, 1)
    docs_row = doc_ids.reshape(n, 1, rows)
    heads_col = head_count.reshape(n, rows, 1)
    bucket_col = width_bucket.reshape(n, rows, 1)
    cos, sin = (t.reshape(n, rows, E) for t in rotary_tables(length))
    gain1, shift1 = first_gain[None], first_shift[None]
    gain2, shift2 = second_gain[None], second_shift[None]

    held, block = None, [own[:, :half], own[:, half:]]
    for s in range(n):
        after = [None, None]
        for p in range(2):
            if s >= 1:
                block[p], *held = tie([block[p]] + list(held))
            if s < n - 1:
                after[p] = hop(block[p])
        held = qkv_slot(
            s, n, where, *block, gain1, shift1, query_weight, key_weight, value_weight, cos, sin, held
        )
        if s < n - 1:
            block = after
    first_all, query, keys, vals = held

    grad_own = mixed_grad[0]
    (own_grad,) = tie([grad_own], block[0])
    right = [own_grad[:, :half], own_grad[:, half:]]
    left = list(right)
    grads_r, grads_l = [list(right)], [list(left)]

    def half_tick(k):
        for p in range(2):
            if k:
                right[p] = join(where, right[p], terms, n - k, k, True, p)
                left[p] = join(where, left[p], terms, k, n - k, False, p)
            right[p], left[p] = send(right[p], right_line), send(left[p], left_line)

    half_tick(0)
    masked = attend(where, query, keys, vals, docs_col, docs_row, heads_col)
    terms = low(dot_t(flat(masked), output_weight)).reshape(n, rows, d)
    for k in range(1, n):
        grads_r.append(list(right))
        grads_l.append(list(left))
        half_tick(k)
    right, left = (jnp.concatenate(v, axis=1) for v in (right, left))
    attn = owned(terms, right, left)
    x_rows = own.astype(F32)
    state = x_rows + attn
    second_out, normed_two, inverse_two = norm_forward(state, gain2, shift2)

    weights = jnp.concatenate([query_weight, key_weight, value_weight], axis=1)
    held, moved = None, None
    (block,) = tie([low(second_out)], weights)
    for s in range(n):
        if s >= 1:
            block, *held = tie([block] + list(held), sent)
        after = hop(block) if s < n - 1 else None
        held = mlp_slot(
            s, n, where, block, grads_l[s] + grads_r[n - s if s else 0], up_weight, down_weight, bucket_col, held
        )
        if s >= 1:
            fused = moved if s == n - 1 and s > 1 else None
            sent = block_term(held[1], s, up_weight, 2 * rows * d * hidden, fused, 16)
            if s > 1 and fused is None:
                sent = add(sent, moved)
            moved = hop(sent)
        else:
            sent = term0 = block_term(held[1], 0, up_weight, 2 * rows * d * hidden, None, 16)
        block = after
    active, grad_upper, second_all, grad_all = held
    grad_all, active, second_all, grad_upper = tie([grad_all, active, second_all, grad_upper], sent)
    gifts = [
        grad_half(flat(grad_all), flat(active), where, True),
        grad_half(flat(second_all), flat(grad_upper), where, True),
    ]
    (moved,) = tie([moved], *gifts)
    down_gift, up_gift = (swap(v) for v in gifts)
    grad_second = term0.astype(F32) + moved.astype(F32)
    back_two = norm_backward(grad_second, normed_two, inverse_two, gain2)
    second_gain_part = jnp.sum(grad_second * normed_two, axis=0)
    second_shift_part = jnp.sum(grad_second, axis=0)
    grad_state = grad_own.astype(F32) + back_two

    start = low(grad_state)
    grad_all, active, start = tie([grad_all, active, start])
    right = left = start
    rights, lefts = [start], [start]
    right, left, _, _ = tick(0, right, left, None)
    ffn = low(dot_t(flat(active), down_weight)).reshape(n, rows, d)
    pair = grad_half(flat(grad_all), flat(active), where, False, 0, down_gift)
    (right,) = tie([right], pair)
    (left,) = tie([left], pair)
    for k in range(1, n):
        rights.append(right)
        lefts.append(left)
        right, left, went_r, went_l = tick(k, right, left, ffn)
        if k == 1:
            second_all, grad_upper = tie([second_all, grad_upper], went_r, went_l)
            pair = grad_half(flat(second_all), flat(grad_upper), where, False, 1, up_gift, pair)
            wide_grad = lax.psum_scatter(pair, "dp", scatter_dimension=1, axis_index_groups=sides, tiled=True)
            (right,) = tie([right], pair)
            (left,) = tie([left], pair)
    late = sorted({1, n - 1})
    early = [s for s in range(n) if s not in late]
    pick = lambda slots: sum(([start] if s == 0 else [lefts[s], rights[n - s]] for s in slots), [])
    held = dom_part(n, early, where, pick(early), output_weight, None)
    grad_masked, state_all = dom_part(n, late, where, pick(late), output_weight, held)
    dqkv = attend_back(
        where, query, keys, vals, grad_masked, docs_col, docs_row, heads_col, cos, sin
    )
    mixed = low(state + owned(ffn, right, left))

    def whole(part):
        span = part.shape[-2] // 2
        mine = lax.dynamic_slice_in_dim(part, side * span, span, part.ndim - 2)
        got = swap(lax.dynamic_slice_in_dim(part, (1 - side) * span, span, part.ndim - 2))
        return jnp.where(side == 0, mine, got).astype(F32), jnp.where(side == 0, got, mine).astype(F32)

    tokens_of = lambda v: (flat(first_all), flat(state_all), flat(v), flat(masked), where)
    sent = block_term(dqkv, 1, weights, 1e6)
    (dqkv,) = tie([dqkv], sent, right, left)
    moved = hop(sent)
    gift = attn_grads(*tokens_of(dqkv))
    (dqkv,) = tie([dqkv], gift)
    terms = {1: sent, 2: block_term(dqkv, 2, weights, 1e6)}
    (dqkv,) = tie([dqkv], terms[2])
    attn_term = attn_grads(*tokens_of(dqkv), swap(gift))
    (late,) = tie([attn_term], wide_grad)
    attn_grad = lax.psum_scatter(late, "dp", scatter_dimension=0, axis_index_groups=sides, tiled=True)
    (moved,) = tie([moved], attn_term)
    sent2 = sent = join(where, moved, terms[2][None], 0, n + 1, True)
    moved = hop(sent)
    for s in range(3, n):
        (dqkv,) = tie([dqkv], sent)
        terms[s] = block_term(dqkv, s, weights, 1e6)
    (dqkv,) = tie([dqkv], terms[n - 1])
    terms[0] = block_term(dqkv, 0, weights, 1e6)
    held = tie([terms[s] for s in range(n)], sent2)
    sum_d = sum(jnp.sum(v.astype(F32), axis=0) for v in held)
    sum_da = sum(jnp.sum(v.astype(F32) * first_all[s].astype(F32), axis=0) for s, v in enumerate(held))
    first_shift_part = sum_d
    first_gain_part = (sum_da - first_shift * sum_d) / first_gain

    lead = (rank == 0).astype(F32)
    bucket_part = lead * jnp.sum(
        (width_bucket[0][:, None] == jnp.arange(4, dtype=jnp.int32)[None, :]).astype(F32), axis=0
    )
    head_part = lead * jnp.sum(
        (head_count[0][:, None] == jnp.arange(1, HEADS + 1, dtype=jnp.int32)[None, :]).astype(F32),
        axis=0,
    )
    small = jnp.concatenate(
        [
            first_gain_part,
            first_shift_part,
            second_gain_part,
            second_shift_part,
            bucket_part,
            head_part,
            jnp.zeros((128 - 4 - HEADS,), F32),
        ]
    )
    small = sum_over(small, "dp", [[(i, i ^ 1) for i in range(n_dp)]])
    wide = jnp.concatenate(whole(wide_grad), axis=2)
    for s in range(3, n):
        if s == 3:
            moved, wide = tie([moved, wide])
        sent = join(where, moved, terms[s][None], 0, n + 1, True, 0, 60e9)
        moved = hop(sent)

    planes = tie([send(small, [(i, (i + m) % n) for i in range(n)]) for m in range(1, n)], sent)
    small = small + sum(planes)
    others = [
        lax.ppermute(small, "dp", [(i, (i + 2 * m) % n_dp) for i in range(n_dp)])
        for m in range(1, n_dp // 2)
    ]
    query_key, value_out = whole(attn_grad)
    moved, query_key, value_out = tie([moved, query_key, value_out])
    input_grad = last_step(own, gain1, terms[0], moved, grad_state)
    small = small + sum(tie(others, input_grad))

    return (
        mixed[None],
        input_grad[None],
        small[:d],
        small[d : 2 * d],
        query_key[:, :local],
        query_key[:, local:],
        value_out[:, :local],
        value_out[:, local:],
        small[2 * d : 3 * d],
        small[3 * d : 4 * d],
        wide[1],
        wide[0],
        small[4 * d : 4 * d + 4].astype(jnp.int32),
        small[4 * d + 4 : 4 * d + 4 + HEADS].astype(jnp.int32),
    )


def solution(mesh):
    token, seq, copy, col = P("dp", "mp", None), P("dp", None), P(), P(None, "mp")
    grad = P("dp", "mp")
    return jax.shard_map(
        functools.partial(per_device, mesh.shape["mp"], mesh.shape["dp"]),
        mesh=mesh,
        in_specs=(token, token, seq, seq, seq, copy, copy, col, col, col, col, copy, copy, col, col),
        out_specs=(token, token, copy, copy, grad, grad, grad, grad, copy, copy, grad, grad, copy, copy),
        check_vma=False,
    )
```

```python
import functools
import jax
import jax.numpy as jnp
from jax import lax
from jax.experimental import pallas as pl
from jax.experimental.pallas import tpu as pltpu
from jax.sharding import PartitionSpec as P

HEADS = 16
E = 128
FF = 8192
EPS = 1e-05
DOC_MAX = 512
LOG2E = 1.4426950408889634
F32 = jnp.float32
BF16 = jnp.bfloat16


def params(mib):
    return pltpu.CompilerParams(vmem_limit_bytes=mib << 20)


def cost(flops, nbytes, trans=0):
    return pl.CostEstimate(flops=int(flops), bytes_accessed=int(nbytes), transcendentals=int(trans))


def norm_forward(values, gain, shift):
    mean = jnp.mean(values, axis=-1, keepdims=True)
    cent = values - mean
    inverse = lax.rsqrt(jnp.mean(cent * cent, axis=-1, keepdims=True) + EPS)
    normed = cent * inverse
    return (normed * gain + shift, normed, inverse)


def norm_backward(grad_out, normed, inverse, gain):
    scaled = grad_out * gain
    return inverse * (
        scaled
        - jnp.mean(scaled, axis=-1, keepdims=True)
        - normed * jnp.mean(scaled * normed, axis=-1, keepdims=True)
    )


def rotary_tables(length):
    half = E // 2
    freq = 10000.0 ** (-(jnp.arange(half, dtype=F32) * 2.0 / E))
    angle = jnp.arange(length, dtype=F32)[:, None] * freq[None, :]
    cos, sin = jnp.cos(angle), jnp.sin(angle)
    return jnp.concatenate([cos, cos], axis=1), jnp.concatenate([-sin, sin], axis=1)


def dot_t(left, right):
    return lax.dot_general(left, right, (((1,), (1,)), ((), ())), preferred_element_type=F32)


def dot_n(left, right):
    return lax.dot_general(left, right, (((1,), (0,)), ((), ())), preferred_element_type=F32)


def outer(left, right):
    return lax.dot_general(left, right, (((0,), (0,)), ((), ())), preferred_element_type=F32)


def qkv_body(rank_ref, xa_ref, xb_ref, gain_ref, shift_ref, wq_ref, wk_ref, wv_ref, cos_ref, sin_ref, *rest):
    a_ref, q_ref, k_ref, v_ref = rest[-4:]

    @pl.when(pl.program_id(0) == 0)
    def _():
        x = jnp.concatenate([xa_ref[...], xb_ref[...]], axis=1).astype(F32)
        out, _, _ = norm_forward(x, gain_ref[...], shift_ref[...])
        a_ref[0] = out.astype(BF16)

    act = a_ref[0]
    cos, sin = cos_ref[0], sin_ref[0]
    v_ref[0] = dot_n(act, wv_ref[...]).astype(BF16)
    for w_ref, o_ref in ((wq_ref, q_ref), (wk_ref, k_ref)):
        lin = dot_n(act, w_ref[...])
        for j in range(lin.shape[1] // E):
            part = lin[:, j * E : (j + 1) * E]
            turned = part * cos + pltpu.roll(part, E // 2, 1) * sin
            o_ref[0, :, j * E : (j + 1) * E] = turned.astype(BF16)


def qkv_slot(slot, n, rank, xa, xb, gain, shift, wq, wk, wv, cos, sin, held):
    rows, half = xa.shape
    d = 2 * half
    local = wq.shape[1]
    cb = min(512, local)
    whole = lambda j, r: (0, 0)
    wspec = pl.BlockSpec((d, cb), lambda j, r: (0, j))
    tspec = pl.BlockSpec((1, rows, E), lambda j, r: (lax.rem(r[0] + slot, n), 0, 0))
    in_specs = [
        pl.BlockSpec((rows, half), whole),
        pl.BlockSpec((rows, half), whole),
        pl.BlockSpec((1, d), whole),
        pl.BlockSpec((1, d), whole),
        wspec,
        wspec,
        wspec,
        tspec,
        tspec,
    ]
    extra = [] if held is None else list(held)
    aliases = {} if held is None else {10 + i: i for i in range(4)}
    ospec = pl.BlockSpec((1, rows, cb), lambda j, r: (slot, 0, j))
    return pl.pallas_call(
        qkv_body,
        grid_spec=pltpu.PrefetchScalarGridSpec(
            num_scalar_prefetch=1,
            grid=(local // cb,),
            in_specs=in_specs + [pl.BlockSpec(memory_space=pl.ANY)] * len(extra),
            out_specs=[pl.BlockSpec((1, rows, d), lambda j, r: (slot, 0, 0)), ospec, ospec, ospec],
        ),
        out_shape=[jax.ShapeDtypeStruct((n, rows, d), BF16)]
        + [jax.ShapeDtypeStruct((n, rows, local), BF16)] * 3,
        input_output_aliases=aliases,
        compiler_params=params(56),
        cost_estimate=cost(6 * rows * d * local, 6 * d * local + 4 * rows * d),
        name="qkv_slot",
    )(rank, xa, xb, gain, shift, wq, wk, wv, cos, sin, *extra)


def first_key(block, rows):
    return max(0, block - (DOC_MAX - 1 + rows - 1) // rows)


def attend_body(rank_ref, q_ref, k_ref, v_ref, dcol_ref, drow_ref, hc_ref, o_ref):
    n, rows, _ = q_ref.shape
    rank = rank_ref[0]
    head = rank_ref[1] + pl.program_id(0)
    slot = lambda b: lax.rem(b + n - rank, n)
    factor = E ** (-0.5) * LOG2E
    low = lax.broadcasted_iota(jnp.int32, (rows, rows), 0) >= lax.broadcasted_iota(
        jnp.int32, (rows, rows), 1
    )
    for b in range(n):
        q = q_ref[slot(b)]
        doc = dcol_ref[b]
        keys = range(first_key(b, rows), b + 1)
        scores = []
        for c in keys:
            s = dot_t(q, k_ref[slot(c)])
            ok = doc == drow_ref[c]
            if c == b:
                ok = ok & low
            scores.append(jnp.where(ok, s, -1e30))
        top = scores[0]
        for s in scores[1:]:
            top = jnp.maximum(top, s)
        top = jnp.max(top, axis=1, keepdims=True)
        total = None
        out = None
        for c, s in zip(keys, scores):
            p = jnp.exp2((s - top) * factor)
            total = p if total is None else total + p
            o = dot_n(p.astype(BF16), v_ref[slot(c)])
            out = o if out is None else out + o
        total = jnp.sum(total, axis=1, keepdims=True)
        gate = jnp.where(hc_ref[b] > head, 1.0, 0.0)
        o_ref[slot(b)] = (out * (gate / total)).astype(BF16)


def attend(rank, q, k, v, docs_col, docs_row, heads_col):
    n, rows, local = q.shape
    spec = pl.BlockSpec((n, rows, E), lambda h, r: (0, 0, h))
    col = pl.BlockSpec((n, rows, 1), lambda h, r: (0, 0, 0))
    row = pl.BlockSpec((n, 1, rows), lambda h, r: (0, 0, 0))
    t = n * rows
    return pl.pallas_call(
        attend_body,
        grid_spec=pltpu.PrefetchScalarGridSpec(
            num_scalar_prefetch=1,
            grid=(local // E,),
            in_specs=[spec, spec, spec, col, row, col],
            out_specs=spec,
        ),
        out_shape=jax.ShapeDtypeStruct((n, rows, local), BF16),
        compiler_params=params(62),
        cost_estimate=cost(4 * t * t * local, 8 * t * local, t * t * local // E),
        name="attend",
    )(rank, q, k, v, docs_col, docs_row, heads_col)


def attend_back_body(
    rank_ref, q_ref, k_ref, v_ref, do_ref, dcol_ref, drow_ref, hc_ref, cos_ref, sin_ref, out_ref, dk_ref, dv_ref
):
    n, rows, _ = q_ref.shape
    rank = rank_ref[0]
    head = rank_ref[1] + pl.program_id(0)
    slot = lambda b: lax.rem(b + n - rank, n)
    scale = E ** (-0.5)
    factor = scale * LOG2E
    low = lax.broadcasted_iota(jnp.int32, (rows, rows), 0) <= lax.broadcasted_iota(
        jnp.int32, (rows, rows), 1
    )
    local = out_ref.shape[2] // 3
    lanes = lambda i: pl.ds(pl.multiple_of(i * local + pl.program_id(0) * E, E), E)
    dk_ref[...] = jnp.zeros_like(dk_ref)
    dv_ref[...] = jnp.zeros_like(dv_ref)

    def unrotate(w, b):
        w = w * scale
        return (w * cos_ref[b] - pltpu.roll(w, E // 2, 1) * sin_ref[b]).astype(BF16)

    for b in range(n):
        q = q_ref[slot(b)]
        grad = jnp.where(hc_ref[b] > head, do_ref[slot(b)].astype(F32), 0.0).astype(BF16)
        keys = range(first_key(b, rows), b + 1)
        scores = []
        for c in keys:
            s = dot_t(k_ref[slot(c)], q)
            ok = dcol_ref[c] == drow_ref[b]
            if c == b:
                ok = ok & low
            scores.append(jnp.where(ok, s, -1e30))
        top = scores[0]
        for s in scores[1:]:
            top = jnp.maximum(top, s)
        top = jnp.max(top, axis=0, keepdims=True)
        probs = [jnp.exp2((s - top) * factor) for s in scores]
        total = probs[0]
        for p in probs[1:]:
            total = total + p
        inv = 1.0 / jnp.sum(total, axis=0, keepdims=True)
        probs = [p * inv for p in probs]
        dprobs = [dot_t(v_ref[slot(c)], grad) for c in keys]
        delta = None
        for p, g in zip(probs, dprobs):
            delta = p * g if delta is None else delta + p * g
        delta = jnp.sum(delta, axis=0, keepdims=True)
        dq = None
        for c, p, g in zip(keys, probs, dprobs):
            ds = (p * (g - delta)).astype(BF16)
            dk_ref[c] += dot_n(ds, q)
            dv_ref[c] += dot_n(p.astype(BF16), grad)
            part = outer(ds, k_ref[slot(c)])
            dq = part if dq is None else dq + part
        out_ref[slot(b), :, lanes(0)] = unrotate(dq, b)
    for b in range(n):
        out_ref[slot(b), :, lanes(1)] = unrotate(dk_ref[b], b)
        out_ref[slot(b), :, lanes(2)] = dv_ref[b].astype(BF16)


def attend_back(rank, q, k, v, do, docs_col, docs_row, heads_col, cos, sin):
    n, rows, local = q.shape
    spec = pl.BlockSpec((n, rows, E), lambda h, r: (0, 0, h))
    col = pl.BlockSpec((n, rows, 1), lambda h, r: (0, 0, 0))
    row = pl.BlockSpec((n, 1, rows), lambda h, r: (0, 0, 0))
    table = pl.BlockSpec((n, rows, E), lambda h, r: (0, 0, 0))
    t = n * rows
    return pl.pallas_call(
        attend_back_body,
        grid_spec=pltpu.PrefetchScalarGridSpec(
            num_scalar_prefetch=1,
            grid=(local // E,),
            in_specs=[spec, spec, spec, spec, col, row, col, table, table],
            out_specs=pl.BlockSpec((n, rows, 3 * local), lambda h, r: (0, 0, 0)),
            scratch_shapes=[pltpu.VMEM((n, rows, E), F32), pltpu.VMEM((n, rows, E), F32)],
        ),
        out_shape=jax.ShapeDtypeStruct((n, rows, 3 * local), BF16),
        compiler_params=params(24),
        cost_estimate=cost(116e9, 14 * t * local),
        name="attend_back",
    )(rank, q, k, v, do, docs_col, docs_row, heads_col, cos, sin)


def mlp_body(slot, n, rank_ref, a_ref, gla_ref, glb_ref, gra_ref, grb_ref, up_ref, down_ref, bucket_ref, *rest):
    r_ref, du_ref, aa_ref, ga_ref = rest[-4:]
    rows, cb = a_ref.shape[0], up_ref.shape[1]

    @pl.when(pl.program_id(0) == 0)
    def _():
        aa_ref[0] = a_ref[...]
        ahead = rank_ref[0] + slot < n

        half = gla_ref.shape[1]

        def fill(first, second):
            ga_ref[0, :, :half] = first[...]
            ga_ref[0, :, half:] = second[...]

        pl.when(ahead)(functools.partial(fill, gla_ref, glb_ref))
        pl.when(jnp.logical_not(ahead))(functools.partial(fill, gra_ref, grb_ref))

    u = dot_n(a_ref[...], up_ref[...])
    dr = dot_n(ga_ref[0], down_ref[...]).astype(BF16).astype(F32)
    column = rank_ref[2] + pl.program_id(0) * cb + lax.broadcasted_iota(jnp.int32, (rows, cb), 1)
    lifted = jnp.where(column < (bucket_ref[0] + 1) * (FF // 4), jnp.maximum(u, 0.0), 0.0)
    r_ref[0] = (lifted * lifted).astype(BF16)
    du_ref[0] = (dr * (2.0 * lifted)).astype(BF16)


def mlp_slot(slot, n, rank, act, grads, up, down, bucket_col, held):
    rows, d = act.shape
    hidden = up.shape[1]
    cb = min(512, hidden)
    whole = lambda j, r: (0, 0)
    wspec = pl.BlockSpec((d, cb), lambda j, r: (0, j))
    extra = [] if held is None else list(held)
    aliases = {} if held is None else {9 + i: i for i in range(4)}
    ospec = pl.BlockSpec((1, rows, cb), lambda j, r: (slot, 0, j))
    aspec = pl.BlockSpec((1, rows, d), lambda j, r: (slot, 0, 0))
    return pl.pallas_call(
        functools.partial(mlp_body, slot, n),
        grid_spec=pltpu.PrefetchScalarGridSpec(
            num_scalar_prefetch=1,
            grid=(hidden // cb,),
            in_specs=[
                pl.BlockSpec((rows, d), whole),
            ]
            + [pl.BlockSpec((rows, d // 2), whole)] * 4
            + [
                wspec,
                wspec,
                pl.BlockSpec((1, rows, 1), lambda j, r: (lax.rem(r[0] + slot, n), 0, 0)),
            ]
            + [pl.BlockSpec(memory_space=pl.ANY)] * len(extra),
            out_specs=[ospec, ospec, aspec, aspec],
        ),
        out_shape=[jax.ShapeDtypeStruct((n, rows, hidden), BF16)] * 2
        + [jax.ShapeDtypeStruct((n, rows, d), BF16)] * 2,
        input_output_aliases=aliases,
        compiler_params=params(28),
        cost_estimate=cost(4 * rows * d * hidden, 4 * d * hidden + 4 * rows * (d + hidden)),
        name="mlp_slot",
    )(rank, act, *grads, up, down, bucket_col, *extra)


def dom_body(n, slots, rank_ref, slot_ref, *refs):
    dom_ref, all_ref = refs[-2:]
    count = sum(1 if s == 0 else 2 for s in slots)
    flows, w_ref = list(refs[:count]), refs[count]

    def fill(ref):
        all_ref[0] = ref[...]

    for i, s in enumerate(slots):
        here = pl.program_id(0) == i
        if s == 0:
            pl.when(here)(functools.partial(fill, flows[0]))
            flows = flows[1:]
        else:
            ahead = rank_ref[0] + s < n
            pl.when(here & ahead)(functools.partial(fill, flows[0]))
            pl.when(here & jnp.logical_not(ahead))(functools.partial(fill, flows[1]))
            flows = flows[2:]
    dom_ref[0] = dot_n(all_ref[0], w_ref[...]).astype(BF16)


def dom_part(n, slots, rank, flows, weight, held):
    rows, d = flows[0].shape
    local = weight.shape[1]
    whole = lambda i, r, s: (0, 0)
    extra = [] if held is None else list(held)
    at = 2 + len(flows) + 1
    return pl.pallas_call(
        functools.partial(dom_body, n, slots),
        grid_spec=pltpu.PrefetchScalarGridSpec(
            num_scalar_prefetch=2,
            grid=(len(slots),),
            in_specs=[pl.BlockSpec((rows, d), whole)] * len(flows)
            + [pl.BlockSpec((d, local), whole)]
            + [pl.BlockSpec(memory_space=pl.ANY)] * len(extra),
            out_specs=[
                pl.BlockSpec((1, rows, local), lambda i, r, s: (s[i], 0, 0)),
                pl.BlockSpec((1, rows, d), lambda i, r, s: (s[i], 0, 0)),
            ],
        ),
        out_shape=[
            jax.ShapeDtypeStruct((n, rows, local), BF16),
            jax.ShapeDtypeStruct((n, rows, d), BF16),
        ],
        input_output_aliases={at + i: i for i in range(len(extra))},
        compiler_params=params(24),
        cost_estimate=cost(
            2 * len(slots) * rows * d * local, 2 * d * local + 6 * len(slots) * rows * d
        ),
        name="dom_part",
    )(rank, jnp.asarray(slots, jnp.int32), *flows, weight, *extra)


def grad_body(has_sum, rank_ref, lhs_ref, rhs_ref, *rest):
    out = outer(lhs_ref[...], rhs_ref[...])
    if has_sum:
        rest[-1][0] = (out + rest[0][...].astype(F32)).astype(BF16)
    else:
        rest[-1][...] = out.astype(BF16)


def grad_half(lhs, rhs, rank, partner, which=0, moved=None, held=None):
    t, d = lhs.shape
    half = rhs.shape[1] // 2
    tile = min(512, d)
    col = (lambda r: 1 - r[3]) if partner else (lambda r: r[3])
    specs = [
        pl.BlockSpec((t, tile), lambda j, r: (0, j)),
        pl.BlockSpec((t, half), lambda j, r: (0, col(r))),
    ]
    args = [lhs, rhs]
    aliases = {}
    if partner:
        ospec = pl.BlockSpec((tile, half), lambda j, r: (j, 0))
        oshape = (d, half)
    else:
        specs.append(pl.BlockSpec((tile, half), lambda j, r: (j, 0)))
        args.append(moved)
        ospec = pl.BlockSpec((1, tile, half), lambda j, r: (which, j, 0))
        oshape = (2, d, half)
        if held is not None:
            specs.append(pl.BlockSpec(memory_space=pl.ANY))
            args.append(held)
            aliases = {4: 0}
    return pl.pallas_call(
        functools.partial(grad_body, not partner),
        grid_spec=pltpu.PrefetchScalarGridSpec(
            num_scalar_prefetch=1, grid=(d // tile,), in_specs=specs, out_specs=ospec
        ),
        out_shape=jax.ShapeDtypeStruct(oshape, BF16),
        input_output_aliases=aliases,
        compiler_params=params(20),
        cost_estimate=cost(1e6, 1e6),
        name="grad_half",
    )(rank, *args)


def attn_grad_body(partner, rank_ref, a_ref, s_ref, one_ref, key_ref, om_ref, *rest):
    out_ref = rest[-1]
    local = om_ref.shape[1]
    second = rank_ref[3] == (0 if partner else 1)
    act = a_ref[...]

    def put(cols, value):
        if not partner:
            value = value + rest[0][:, cols].astype(F32)
        out_ref[:, cols] = value.astype(BF16)

    put(slice(0, local), outer(act, one_ref[...]))

    @pl.when(second)
    def _():
        put(slice(local, 2 * local), outer(s_ref[...], om_ref[...]))

    @pl.when(jnp.logical_not(second))
    def _():
        put(slice(local, 2 * local), outer(act, key_ref[...]))


def attn_grads(act, states, dqkv, om, rank, moved=None):
    t, d = act.shape
    local = om.shape[1]
    tile = min(512, d)
    partner = moved is None
    pos = (lambda r: 1 - r[3]) if partner else (lambda r: r[3])
    col = pl.BlockSpec((t, tile), lambda j, r: (0, j))
    out = pl.BlockSpec((tile, 2 * local), lambda j, r: (j, 0))
    return pl.pallas_call(
        functools.partial(attn_grad_body, partner),
        grid_spec=pltpu.PrefetchScalarGridSpec(
            num_scalar_prefetch=1,
            grid=(d // tile,),
            in_specs=[
                col,
                pl.BlockSpec((t, tile), lambda j, r: (0, j * pos(r))),
                pl.BlockSpec((t, local), lambda j, r: (0, 2 * pos(r))),
                pl.BlockSpec((t, local), lambda j, r: (0, 1)),
                pl.BlockSpec((t, local), lambda j, r: (0, 0)),
            ]
            + ([] if partner else [out]),
            out_specs=out,
        ),
        out_shape=jax.ShapeDtypeStruct((d, 2 * local), BF16),
        compiler_params=params(28 if partner else 50),
        cost_estimate=cost(4e9 if partner else 1e6, 1e6),
        name="attn_grads",
    )(rank, act, states, dqkv, dqkv, om, *([] if partner else [moved]))


def term_body(x_ref, w_ref, *rest):
    out = dot_t(x_ref[0], w_ref[...])
    if len(rest) > 1:
        out = out + rest[0][...].astype(F32)
    rest[-1][...] = out.astype(BF16)


def block_term(acts, slot, weight, flops, moved=None, mib=16):
    _, rows, k = acts.shape
    d = weight.shape[0]
    tile = min(512, d)
    out = pl.BlockSpec((rows, tile), lambda j: (0, j))
    return pl.pallas_call(
        term_body,
        grid=(d // tile,),
        in_specs=[
            pl.BlockSpec((1, rows, k), lambda j: (slot, 0, 0)),
            pl.BlockSpec((tile, k), lambda j: (j, 0)),
        ]
        + ([] if moved is None else [out]),
        out_specs=out,
        out_shape=jax.ShapeDtypeStruct((rows, d), BF16),
        compiler_params=params(mib),
        cost_estimate=cost(flops, flops / 256),
        name="block_term",
    )(acts, weight, *([] if moved is None else [moved]))


def join_body(slot, first, rank_ref, moved_ref, term_ref, out_ref):
    adds = rank_ref[0] < first if slot >= 0 else rank_ref[0] >= first

    @pl.when(adds)
    def _():
        out_ref[...] = (moved_ref[...].astype(F32) + term_ref[0].astype(F32)).astype(BF16)

    @pl.when(jnp.logical_not(adds))
    def _():
        out_ref[...] = moved_ref[...]


def join(rank, moved, terms, slot, first, right, part=0, flops=1e6):
    rows, d = moved.shape
    tile = min(128, rows)
    row = pl.BlockSpec((tile, d), lambda i, r: (i, 0))
    return pl.pallas_call(
        functools.partial(join_body, 0 if right else -1, first),
        grid_spec=pltpu.PrefetchScalarGridSpec(
            num_scalar_prefetch=1,
            grid=(rows // tile,),
            in_specs=[row, pl.BlockSpec((1, tile, d), lambda i, r: (slot, i, part))],
            out_specs=row,
        ),
        out_shape=jax.ShapeDtypeStruct((rows, d), BF16),
        compiler_params=params(8),
        cost_estimate=cost(flops, 1e6),
        name="join",
    )(rank, moved, terms)


def last_body(x_ref, gain_ref, term_ref, moved_ref, state_ref, out_ref):
    gain = gain_ref[...]
    _, normed, inverse = norm_forward(x_ref[...].astype(F32), gain, gain)
    back = norm_backward(term_ref[...].astype(F32) + moved_ref[...].astype(F32), normed, inverse, gain)
    out_ref[...] = (state_ref[...] + back).astype(BF16)


def last_step(x, gain, term, moved, state):
    rows, d = x.shape
    tile = min(64, rows)
    row = lambda w: pl.BlockSpec((tile, w), lambda i: (i, 0))
    return pl.pallas_call(
        last_body,
        grid=(rows // tile,),
        in_specs=[row(d), pl.BlockSpec((1, d), lambda i: (0, 0)), row(d), row(d), row(d)],
        out_specs=row(d),
        out_shape=jax.ShapeDtypeStruct((rows, d), BF16),
        compiler_params=params(12),
        cost_estimate=cost(1e6, 12 * rows * d),
        name="last_step",
    )(x, gain, term, moved, state)


def tie(values, *others):
    values = tuple(values)
    return lax.optimization_barrier(values + others)[: len(values)]


def sum_over(vec, axis, moves):
    return sum((lax.ppermute(vec, axis, pairs) for pairs in moves), vec)


def per_device(
    n,
    n_dp,
    tokens,
    mixed_grad,
    doc_ids,
    head_count,
    width_bucket,
    first_gain,
    first_shift,
    query_weight,
    key_weight,
    value_weight,
    output_weight,
    second_gain,
    second_shift,
    up_weight,
    down_weight,
):
    rank = lax.axis_index("mp")
    rows, d = tokens.shape[1:]
    half = d // 2
    local = query_weight.shape[1]
    local_heads = local // E
    hidden = up_weight.shape[1]
    length = n * rows
    own = tokens[0]
    send = lambda v, pairs: lax.ppermute(v, "mp", pairs)
    ring = [(i, (i - 1) % n) for i in range(n)]
    hop = lambda v: send(v, ring)
    right_line = [(i, i + 1) for i in range(n - 1)]
    left_line = [(i + 1, i) for i in range(n - 1)]

    def tick(k, right, left, terms):
        if k:
            right = join(where, right, terms, n - k, k, True, 0, 1e9)
            left = join(where, left, terms, k, n - k, False, 0, 1e6)
        return send(right, right_line), send(left, left_line), right, left

    def owned(terms, right, left):
        return terms[0].astype(F32) + right.astype(F32) + left.astype(F32)

    low = lambda v: v.astype(BF16)
    flat = lambda v: v.reshape(length, v.shape[-1])
    add = lambda t, moved: (t.astype(F32) + moved.astype(F32)).astype(BF16)

    side = lax.rem(lax.axis_index("dp"), 2)
    where = jnp.stack([rank, rank * local_heads, rank * hidden, side]).astype(jnp.int32)
    swap = lambda v: lax.ppermute(v, "dp", [(i, i ^ 1) for i in range(n_dp)])
    sides = [list(range(c, n_dp, 2)) for c in range(2)]
    docs_col = doc_ids.reshape(n, rows, 1)
    docs_row = doc_ids.reshape(n, 1, rows)
    heads_col = head_count.reshape(n, rows, 1)
    bucket_col = width_bucket.reshape(n, rows, 1)
    cos, sin = (t.reshape(n, rows, E) for t in rotary_tables(length))
    gain1, shift1 = first_gain[None], first_shift[None]
    gain2, shift2 = second_gain[None], second_shift[None]

    held, block = None, [own[:, :half], own[:, half:]]
    for s in range(n):
        after = [None, None]
        for p in range(2):
            if s >= 1:
                block[p], *held = tie([block[p]] + list(held))
            if s < n - 1:
                after[p] = hop(block[p])
        held = qkv_slot(
            s, n, where, *block, gain1, shift1, query_weight, key_weight, value_weight, cos, sin, held
        )
        if s < n - 1:
            block = after
    first_all, query, keys, vals = held

    grad_own = mixed_grad[0]
    (own_grad,) = tie([grad_own], block[0])
    right = [own_grad[:, :half], own_grad[:, half:]]
    left = list(right)
    grads_r, grads_l = [list(right)], [list(left)]

    def half_tick(k):
        for p in range(2):
            if k:
                right[p] = join(where, right[p], terms, n - k, k, True, p)
                left[p] = join(where, left[p], terms, k, n - k, False, p)
            right[p], left[p] = send(right[p], right_line), send(left[p], left_line)

    half_tick(0)
    masked = attend(where, query, keys, vals, docs_col, docs_row, heads_col)
    terms = low(dot_t(flat(masked), output_weight)).reshape(n, rows, d)
    for k in range(1, n):
        grads_r.append(list(right))
        grads_l.append(list(left))
        half_tick(k)
    right, left = (jnp.concatenate(v, axis=1) for v in (right, left))
    attn = owned(terms, right, left)
    x_rows = own.astype(F32)
    state = x_rows + attn
    second_out, normed_two, inverse_two = norm_forward(state, gain2, shift2)

    weights = jnp.concatenate([query_weight, key_weight, value_weight], axis=1)
    held, moved = None, None
    (block,) = tie([low(second_out)], weights)
    for s in range(n):
        if s >= 1:
            block, *held = tie([block] + list(held), sent)
        after = hop(block) if s < n - 1 else None
        held = mlp_slot(
            s, n, where, block, grads_l[s] + grads_r[n - s if s else 0], up_weight, down_weight, bucket_col, held
        )
        if s >= 1:
            fused = moved if s == n - 1 and s > 1 else None
            sent = block_term(held[1], s, up_weight, 2 * rows * d * hidden, fused, 16)
            if s > 1 and fused is None:
                sent = add(sent, moved)
            moved = hop(sent)
        else:
            sent = term0 = block_term(held[1], 0, up_weight, 2 * rows * d * hidden, None, 16)
        block = after
    active, grad_upper, second_all, grad_all = held
    grad_all, active, second_all, grad_upper = tie([grad_all, active, second_all, grad_upper], sent)
    gifts = [
        grad_half(flat(grad_all), flat(active), where, True),
        grad_half(flat(second_all), flat(grad_upper), where, True),
    ]
    (moved,) = tie([moved], *gifts)
    down_gift, up_gift = (swap(v) for v in gifts)
    grad_second = term0.astype(F32) + moved.astype(F32)
    back_two = norm_backward(grad_second, normed_two, inverse_two, gain2)
    second_gain_part = jnp.sum(grad_second * normed_two, axis=0)
    second_shift_part = jnp.sum(grad_second, axis=0)
    grad_state = grad_own.astype(F32) + back_two

    start = low(grad_state)
    grad_all, active, start = tie([grad_all, active, start])
    right = left = start
    rights, lefts = [start], [start]
    right, left, _, _ = tick(0, right, left, None)
    ffn = low(dot_t(flat(active), down_weight)).reshape(n, rows, d)
    pair = grad_half(flat(grad_all), flat(active), where, False, 0, down_gift)
    (right,) = tie([right], pair)
    (left,) = tie([left], pair)
    for k in range(1, n):
        rights.append(right)
        lefts.append(left)
        right, left, went_r, went_l = tick(k, right, left, ffn)
        if k == 1:
            second_all, grad_upper = tie([second_all, grad_upper], went_r, went_l)
            pair = grad_half(flat(second_all), flat(grad_upper), where, False, 1, up_gift, pair)
            wide_grad = lax.psum_scatter(pair, "dp", scatter_dimension=1, axis_index_groups=sides, tiled=True)
            (right,) = tie([right], pair)
            (left,) = tie([left], pair)
    late = sorted({1, n - 1})
    early = [s for s in range(n) if s not in late]
    pick = lambda slots: sum(([start] if s == 0 else [lefts[s], rights[n - s]] for s in slots), [])
    held = dom_part(n, early, where, pick(early), output_weight, None)
    grad_masked, state_all = dom_part(n, late, where, pick(late), output_weight, held)
    dqkv = attend_back(
        where, query, keys, vals, grad_masked, docs_col, docs_row, heads_col, cos, sin
    )
    mixed = low(state + owned(ffn, right, left))

    def whole(part):
        span = part.shape[-2] // 2
        mine = lax.dynamic_slice_in_dim(part, side * span, span, part.ndim - 2)
        got = swap(lax.dynamic_slice_in_dim(part, (1 - side) * span, span, part.ndim - 2))
        return jnp.where(side == 0, mine, got).astype(F32), jnp.where(side == 0, got, mine).astype(F32)

    tokens_of = lambda v: (flat(first_all), flat(state_all), flat(v), flat(masked), where)
    sent = block_term(dqkv, 1, weights, 1e6)
    (dqkv,) = tie([dqkv], sent, right, left)
    moved = hop(sent)
    gift = attn_grads(*tokens_of(dqkv))
    (dqkv,) = tie([dqkv], gift)
    terms = {1: sent, 2: block_term(dqkv, 2, weights, 1e6)}
    (dqkv,) = tie([dqkv], terms[2])
    attn_term = attn_grads(*tokens_of(dqkv), swap(gift))
    (late,) = tie([attn_term], wide_grad)
    attn_grad = lax.psum_scatter(late, "dp", scatter_dimension=0, axis_index_groups=sides, tiled=True)
    (moved,) = tie([moved], attn_term)
    sent2 = sent = join(where, moved, terms[2][None], 0, n + 1, True)
    moved = hop(sent)
    for s in range(3, n):
        (dqkv,) = tie([dqkv], sent)
        terms[s] = block_term(dqkv, s, weights, 1e6)
    (dqkv,) = tie([dqkv], terms[n - 1])
    terms[0] = block_term(dqkv, 0, weights, 1e6)
    held = tie([terms[s] for s in range(n)], sent2)
    sum_d = sum(jnp.sum(v.astype(F32), axis=0) for v in held)
    sum_da = sum(jnp.sum(v.astype(F32) * first_all[s].astype(F32), axis=0) for s, v in enumerate(held))
    first_shift_part = sum_d
    first_gain_part = (sum_da - first_shift * sum_d) / first_gain

    lead = (rank == 0).astype(F32)
    bucket_part = lead * jnp.sum(
        (width_bucket[0][:, None] == jnp.arange(4, dtype=jnp.int32)[None, :]).astype(F32), axis=0
    )
    head_part = lead * jnp.sum(
        (head_count[0][:, None] == jnp.arange(1, HEADS + 1, dtype=jnp.int32)[None, :]).astype(F32),
        axis=0,
    )
    small = jnp.concatenate(
        [
            first_gain_part,
            first_shift_part,
            second_gain_part,
            second_shift_part,
            bucket_part,
            head_part,
            jnp.zeros((128 - 4 - HEADS,), F32),
        ]
    )
    small = sum_over(small, "dp", [[(i, i ^ 1) for i in range(n_dp)]])
    wide = jnp.concatenate(whole(wide_grad), axis=2)
    for s in range(3, n):
        if s == 3:
            moved, wide = tie([moved, wide])
        sent = join(where, moved, terms[s][None], 0, n + 1, True, 0, 60e9)
        moved = hop(sent)

    planes = tie([send(small, [(i, (i + m) % n) for i in range(n)]) for m in range(1, n)], sent)
    small = small + sum(planes)
    others = [
        lax.ppermute(small, "dp", [(i, (i + 2 * m) % n_dp) for i in range(n_dp)])
        for m in range(1, n_dp // 2)
    ]
    query_key, value_out = whole(attn_grad)
    moved, query_key, value_out = tie([moved, query_key, value_out])
    input_grad = last_step(own, gain1, terms[0], moved, grad_state)
    small = small + sum(tie(others, input_grad))

    return (
        mixed[None],
        input_grad[None],
        small[:d],
        small[d : 2 * d],
        query_key[:, :local],
        query_key[:, local:],
        value_out[:, :local],
        value_out[:, local:],
        small[2 * d : 3 * d],
        small[3 * d : 4 * d],
        wide[1],
        wide[0],
        small[4 * d : 4 * d + 4].astype(jnp.int32),
        small[4 * d + 4 : 4 * d + 4 + HEADS].astype(jnp.int32),
    )


def solution(mesh):
    token, seq, copy, col = P("dp", "mp", None), P("dp", None), P(), P(None, "mp")
    grad = P("dp", "mp")
    return jax.shard_map(
        functools.partial(per_device, mesh.shape["mp"], mesh.shape["dp"]),
        mesh=mesh,
        in_specs=(token, token, seq, seq, seq, copy, copy, col, col, col, col, copy, copy, col, col),
        out_specs=(token, token, copy, copy, grad, grad, grad, grad, copy, copy, grad, grad, copy, copy),
        check_vma=False,
    )
```

```python
import functools
import jax
import jax.numpy as jnp
from jax import lax
from jax.experimental import pallas as pl
from jax.experimental.pallas import tpu as pltpu
from jax.sharding import PartitionSpec as P

HEADS = 16
E = 128
FF = 8192
EPS = 1e-05
DOC_MAX = 512
LOG2E = 1.4426950408889634
F32 = jnp.float32
BF16 = jnp.bfloat16


def params(mib):
    return pltpu.CompilerParams(vmem_limit_bytes=mib << 20)


def cost(flops, nbytes, trans=0):
    return pl.CostEstimate(flops=int(flops), bytes_accessed=int(nbytes), transcendentals=int(trans))


def norm_forward(values, gain, shift):
    mean = jnp.mean(values, axis=-1, keepdims=True)
    cent = values - mean
    inverse = lax.rsqrt(jnp.mean(cent * cent, axis=-1, keepdims=True) + EPS)
    normed = cent * inverse
    return (normed * gain + shift, normed, inverse)


def norm_backward(grad_out, normed, inverse, gain):
    scaled = grad_out * gain
    return inverse * (
        scaled
        - jnp.mean(scaled, axis=-1, keepdims=True)
        - normed * jnp.mean(scaled * normed, axis=-1, keepdims=True)
    )


def rotary_tables(length):
    half = E // 2
    freq = 10000.0 ** (-(jnp.arange(half, dtype=F32) * 2.0 / E))
    angle = jnp.arange(length, dtype=F32)[:, None] * freq[None, :]
    cos, sin = jnp.cos(angle), jnp.sin(angle)
    return jnp.concatenate([cos, cos], axis=1), jnp.concatenate([-sin, sin], axis=1)


def dot_t(left, right):
    return lax.dot_general(left, right, (((1,), (1,)), ((), ())), preferred_element_type=F32)


def dot_n(left, right):
    return lax.dot_general(left, right, (((1,), (0,)), ((), ())), preferred_element_type=F32)


def outer(left, right):
    return lax.dot_general(left, right, (((0,), (0,)), ((), ())), preferred_element_type=F32)


def qkv_body(rank_ref, xa_ref, xb_ref, gain_ref, shift_ref, wq_ref, wk_ref, wv_ref, cos_ref, sin_ref, *rest):
    a_ref, q_ref, k_ref, v_ref = rest[-4:]

    @pl.when(pl.program_id(0) == 0)
    def _():
        x = jnp.concatenate([xa_ref[...], xb_ref[...]], axis=1).astype(F32)
        out, _, _ = norm_forward(x, gain_ref[...], shift_ref[...])
        a_ref[0] = out.astype(BF16)

    act = a_ref[0]
    cos, sin = cos_ref[0], sin_ref[0]
    v_ref[0] = dot_n(act, wv_ref[...]).astype(BF16)
    for w_ref, o_ref in ((wq_ref, q_ref), (wk_ref, k_ref)):
        lin = dot_n(act, w_ref[...])
        for j in range(lin.shape[1] // E):
            part = lin[:, j * E : (j + 1) * E]
            turned = part * cos + pltpu.roll(part, E // 2, 1) * sin
            o_ref[0, :, j * E : (j + 1) * E] = turned.astype(BF16)


def qkv_slot(slot, n, rank, xa, xb, gain, shift, wq, wk, wv, cos, sin, held):
    rows, half = xa.shape
    d = 2 * half
    local = wq.shape[1]
    cb = min(512, local)
    whole = lambda j, r: (0, 0)
    wspec = pl.BlockSpec((d, cb), lambda j, r: (0, j))
    tspec = pl.BlockSpec((1, rows, E), lambda j, r: (lax.rem(r[0] + slot, n), 0, 0))
    in_specs = [
        pl.BlockSpec((rows, half), whole),
        pl.BlockSpec((rows, half), whole),
        pl.BlockSpec((1, d), whole),
        pl.BlockSpec((1, d), whole),
        wspec,
        wspec,
        wspec,
        tspec,
        tspec,
    ]
    extra = [] if held is None else list(held)
    aliases = {} if held is None else {10 + i: i for i in range(4)}
    ospec = pl.BlockSpec((1, rows, cb), lambda j, r: (slot, 0, j))
    return pl.pallas_call(
        qkv_body,
        grid_spec=pltpu.PrefetchScalarGridSpec(
            num_scalar_prefetch=1,
            grid=(local // cb,),
            in_specs=in_specs + [pl.BlockSpec(memory_space=pl.ANY)] * len(extra),
            out_specs=[pl.BlockSpec((1, rows, d), lambda j, r: (slot, 0, 0)), ospec, ospec, ospec],
        ),
        out_shape=[jax.ShapeDtypeStruct((n, rows, d), BF16)]
        + [jax.ShapeDtypeStruct((n, rows, local), BF16)] * 3,
        input_output_aliases=aliases,
        compiler_params=params(56),
        cost_estimate=cost(6 * rows * d * local, 6 * d * local + 4 * rows * d),
        name="qkv_slot",
    )(rank, xa, xb, gain, shift, wq, wk, wv, cos, sin, *extra)


def first_key(block, rows):
    return max(0, block - (DOC_MAX - 1 + rows - 1) // rows)


def attend_body(rank_ref, q_ref, k_ref, v_ref, dcol_ref, drow_ref, hc_ref, o_ref):
    n, rows, _ = q_ref.shape
    rank = rank_ref[0]
    head = rank_ref[1] + pl.program_id(0)
    slot = lambda b: lax.rem(b + n - rank, n)
    factor = E ** (-0.5) * LOG2E
    low = lax.broadcasted_iota(jnp.int32, (rows, rows), 0) >= lax.broadcasted_iota(
        jnp.int32, (rows, rows), 1
    )
    for b in range(n):
        q = q_ref[slot(b)]
        doc = dcol_ref[b]
        keys = range(first_key(b, rows), b + 1)
        scores = []
        for c in keys:
            s = dot_t(q, k_ref[slot(c)])
            ok = doc == drow_ref[c]
            if c == b:
                ok = ok & low
            scores.append(jnp.where(ok, s, -1e30))
        top = scores[0]
        for s in scores[1:]:
            top = jnp.maximum(top, s)
        top = jnp.max(top, axis=1, keepdims=True)
        total = None
        out = None
        for c, s in zip(keys, scores):
            p = jnp.exp2((s - top) * factor)
            total = p if total is None else total + p
            o = dot_n(p.astype(BF16), v_ref[slot(c)])
            out = o if out is None else out + o
        total = jnp.sum(total, axis=1, keepdims=True)
        gate = jnp.where(hc_ref[b] > head, 1.0, 0.0)
        o_ref[slot(b)] = (out * (gate / total)).astype(BF16)


def attend(rank, q, k, v, docs_col, docs_row, heads_col):
    n, rows, local = q.shape
    spec = pl.BlockSpec((n, rows, E), lambda h, r: (0, 0, h))
    col = pl.BlockSpec((n, rows, 1), lambda h, r: (0, 0, 0))
    row = pl.BlockSpec((n, 1, rows), lambda h, r: (0, 0, 0))
    t = n * rows
    return pl.pallas_call(
        attend_body,
        grid_spec=pltpu.PrefetchScalarGridSpec(
            num_scalar_prefetch=1,
            grid=(local // E,),
            in_specs=[spec, spec, spec, col, row, col],
            out_specs=spec,
        ),
        out_shape=jax.ShapeDtypeStruct((n, rows, local), BF16),
        compiler_params=params(62),
        cost_estimate=cost(4 * t * t * local, 8 * t * local, t * t * local // E),
        name="attend",
    )(rank, q, k, v, docs_col, docs_row, heads_col)


def attend_back_body(
    rank_ref, q_ref, k_ref, v_ref, do_ref, dcol_ref, drow_ref, hc_ref, cos_ref, sin_ref, out_ref, dk_ref, dv_ref
):
    n, rows, _ = q_ref.shape
    rank = rank_ref[0]
    head = rank_ref[1] + pl.program_id(0)
    slot = lambda b: lax.rem(b + n - rank, n)
    scale = E ** (-0.5)
    factor = scale * LOG2E
    low = lax.broadcasted_iota(jnp.int32, (rows, rows), 0) <= lax.broadcasted_iota(
        jnp.int32, (rows, rows), 1
    )
    local = out_ref.shape[2] // 3
    lanes = lambda i: pl.ds(pl.multiple_of(i * local + pl.program_id(0) * E, E), E)
    dk_ref[...] = jnp.zeros_like(dk_ref)
    dv_ref[...] = jnp.zeros_like(dv_ref)

    def unrotate(w, b):
        w = w * scale
        return (w * cos_ref[b] - pltpu.roll(w, E // 2, 1) * sin_ref[b]).astype(BF16)

    for b in range(n):
        q = q_ref[slot(b)]
        grad = jnp.where(hc_ref[b] > head, do_ref[slot(b)].astype(F32), 0.0).astype(BF16)
        keys = range(first_key(b, rows), b + 1)
        scores = []
        for c in keys:
            s = dot_t(k_ref[slot(c)], q)
            ok = dcol_ref[c] == drow_ref[b]
            if c == b:
                ok = ok & low
            scores.append(jnp.where(ok, s, -1e30))
        top = scores[0]
        for s in scores[1:]:
            top = jnp.maximum(top, s)
        top = jnp.max(top, axis=0, keepdims=True)
        probs = [jnp.exp2((s - top) * factor) for s in scores]
        total = probs[0]
        for p in probs[1:]:
            total = total + p
        inv = 1.0 / jnp.sum(total, axis=0, keepdims=True)
        probs = [p * inv for p in probs]
        dprobs = [dot_t(v_ref[slot(c)], grad) for c in keys]
        delta = None
        for p, g in zip(probs, dprobs):
            delta = p * g if delta is None else delta + p * g
        delta = jnp.sum(delta, axis=0, keepdims=True)
        dq = None
        for c, p, g in zip(keys, probs, dprobs):
            ds = (p * (g - delta)).astype(BF16)
            dk_ref[c] += dot_n(ds, q)
            dv_ref[c] += dot_n(p.astype(BF16), grad)
            part = outer(ds, k_ref[slot(c)])
            dq = part if dq is None else dq + part
        out_ref[slot(b), :, lanes(0)] = unrotate(dq, b)
    for b in range(n):
        out_ref[slot(b), :, lanes(1)] = unrotate(dk_ref[b], b)
        out_ref[slot(b), :, lanes(2)] = dv_ref[b].astype(BF16)


def attend_back(rank, q, k, v, do, docs_col, docs_row, heads_col, cos, sin):
    n, rows, local = q.shape
    spec = pl.BlockSpec((n, rows, E), lambda h, r: (0, 0, h))
    col = pl.BlockSpec((n, rows, 1), lambda h, r: (0, 0, 0))
    row = pl.BlockSpec((n, 1, rows), lambda h, r: (0, 0, 0))
    table = pl.BlockSpec((n, rows, E), lambda h, r: (0, 0, 0))
    t = n * rows
    return pl.pallas_call(
        attend_back_body,
        grid_spec=pltpu.PrefetchScalarGridSpec(
            num_scalar_prefetch=1,
            grid=(local // E,),
            in_specs=[spec, spec, spec, spec, col, row, col, table, table],
            out_specs=pl.BlockSpec((n, rows, 3 * local), lambda h, r: (0, 0, 0)),
            scratch_shapes=[pltpu.VMEM((n, rows, E), F32), pltpu.VMEM((n, rows, E), F32)],
        ),
        out_shape=jax.ShapeDtypeStruct((n, rows, 3 * local), BF16),
        compiler_params=params(24),
        cost_estimate=cost(116e9, 14 * t * local),
        name="attend_back",
    )(rank, q, k, v, do, docs_col, docs_row, heads_col, cos, sin)


def mlp_body(slot, n, rank_ref, a_ref, gla_ref, glb_ref, gra_ref, grb_ref, up_ref, down_ref, bucket_ref, *rest):
    r_ref, du_ref, aa_ref, ga_ref = rest[-4:]
    rows, cb = a_ref.shape[0], up_ref.shape[1]

    @pl.when(pl.program_id(0) == 0)
    def _():
        aa_ref[0] = a_ref[...]
        ahead = rank_ref[0] + slot < n

        half = gla_ref.shape[1]

        def fill(first, second):
            ga_ref[0, :, :half] = first[...]
            ga_ref[0, :, half:] = second[...]

        pl.when(ahead)(functools.partial(fill, gla_ref, glb_ref))
        pl.when(jnp.logical_not(ahead))(functools.partial(fill, gra_ref, grb_ref))

    u = dot_n(a_ref[...], up_ref[...])
    dr = dot_n(ga_ref[0], down_ref[...]).astype(BF16).astype(F32)
    column = rank_ref[2] + pl.program_id(0) * cb + lax.broadcasted_iota(jnp.int32, (rows, cb), 1)
    lifted = jnp.where(column < (bucket_ref[0] + 1) * (FF // 4), jnp.maximum(u, 0.0), 0.0)
    r_ref[0] = (lifted * lifted).astype(BF16)
    du_ref[0] = (dr * (2.0 * lifted)).astype(BF16)


def mlp_slot(slot, n, rank, act, grads, up, down, bucket_col, held):
    rows, d = act.shape
    hidden = up.shape[1]
    cb = min(512, hidden)
    whole = lambda j, r: (0, 0)
    wspec = pl.BlockSpec((d, cb), lambda j, r: (0, j))
    extra = [] if held is None else list(held)
    aliases = {} if held is None else {9 + i: i for i in range(4)}
    ospec = pl.BlockSpec((1, rows, cb), lambda j, r: (slot, 0, j))
    aspec = pl.BlockSpec((1, rows, d), lambda j, r: (slot, 0, 0))
    return pl.pallas_call(
        functools.partial(mlp_body, slot, n),
        grid_spec=pltpu.PrefetchScalarGridSpec(
            num_scalar_prefetch=1,
            grid=(hidden // cb,),
            in_specs=[
                pl.BlockSpec((rows, d), whole),
            ]
            + [pl.BlockSpec((rows, d // 2), whole)] * 4
            + [
                wspec,
                wspec,
                pl.BlockSpec((1, rows, 1), lambda j, r: (lax.rem(r[0] + slot, n), 0, 0)),
            ]
            + [pl.BlockSpec(memory_space=pl.ANY)] * len(extra),
            out_specs=[ospec, ospec, aspec, aspec],
        ),
        out_shape=[jax.ShapeDtypeStruct((n, rows, hidden), BF16)] * 2
        + [jax.ShapeDtypeStruct((n, rows, d), BF16)] * 2,
        input_output_aliases=aliases,
        compiler_params=params(28),
        cost_estimate=cost(4 * rows * d * hidden, 4 * d * hidden + 4 * rows * (d + hidden)),
        name="mlp_slot",
    )(rank, act, *grads, up, down, bucket_col, *extra)


def dom_body(n, slots, rank_ref, slot_ref, *refs):
    dom_ref, all_ref = refs[-2:]
    count = sum(1 if s == 0 else 2 for s in slots)
    flows, w_ref = list(refs[:count]), refs[count]

    def fill(ref):
        all_ref[0] = ref[...]

    for i, s in enumerate(slots):
        here = pl.program_id(0) == i
        if s == 0:
            pl.when(here)(functools.partial(fill, flows[0]))
            flows = flows[1:]
        else:
            ahead = rank_ref[0] + s < n
            pl.when(here & ahead)(functools.partial(fill, flows[0]))
            pl.when(here & jnp.logical_not(ahead))(functools.partial(fill, flows[1]))
            flows = flows[2:]
    dom_ref[0] = dot_n(all_ref[0], w_ref[...]).astype(BF16)


def dom_part(n, slots, rank, flows, weight, held):
    rows, d = flows[0].shape
    local = weight.shape[1]
    whole = lambda i, r, s: (0, 0)
    extra = [] if held is None else list(held)
    at = 2 + len(flows) + 1
    return pl.pallas_call(
        functools.partial(dom_body, n, slots),
        grid_spec=pltpu.PrefetchScalarGridSpec(
            num_scalar_prefetch=2,
            grid=(len(slots),),
            in_specs=[pl.BlockSpec((rows, d), whole)] * len(flows)
            + [pl.BlockSpec((d, local), whole)]
            + [pl.BlockSpec(memory_space=pl.ANY)] * len(extra),
            out_specs=[
                pl.BlockSpec((1, rows, local), lambda i, r, s: (s[i], 0, 0)),
                pl.BlockSpec((1, rows, d), lambda i, r, s: (s[i], 0, 0)),
            ],
        ),
        out_shape=[
            jax.ShapeDtypeStruct((n, rows, local), BF16),
            jax.ShapeDtypeStruct((n, rows, d), BF16),
        ],
        input_output_aliases={at + i: i for i in range(len(extra))},
        compiler_params=params(24),
        cost_estimate=cost(
            2 * len(slots) * rows * d * local, 2 * d * local + 6 * len(slots) * rows * d
        ),
        name="dom_part",
    )(rank, jnp.asarray(slots, jnp.int32), *flows, weight, *extra)


def grad_body(has_sum, rank_ref, lhs_ref, rhs_ref, *rest):
    out = outer(lhs_ref[...], rhs_ref[...])
    if has_sum:
        rest[-1][0] = (out + rest[0][...].astype(F32)).astype(BF16)
    else:
        rest[-1][...] = out.astype(BF16)


def grad_half(lhs, rhs, rank, partner, which=0, moved=None, held=None):
    t, d = lhs.shape
    half = rhs.shape[1] // 2
    tile = min(512, d)
    col = (lambda r: 1 - r[3]) if partner else (lambda r: r[3])
    specs = [
        pl.BlockSpec((t, tile), lambda j, r: (0, j)),
        pl.BlockSpec((t, half), lambda j, r: (0, col(r))),
    ]
    args = [lhs, rhs]
    aliases = {}
    if partner:
        ospec = pl.BlockSpec((tile, half), lambda j, r: (j, 0))
        oshape = (d, half)
    else:
        specs.append(pl.BlockSpec((tile, half), lambda j, r: (j, 0)))
        args.append(moved)
        ospec = pl.BlockSpec((1, tile, half), lambda j, r: (which, j, 0))
        oshape = (2, d, half)
        if held is not None:
            specs.append(pl.BlockSpec(memory_space=pl.ANY))
            args.append(held)
            aliases = {4: 0}
    return pl.pallas_call(
        functools.partial(grad_body, not partner),
        grid_spec=pltpu.PrefetchScalarGridSpec(
            num_scalar_prefetch=1, grid=(d // tile,), in_specs=specs, out_specs=ospec
        ),
        out_shape=jax.ShapeDtypeStruct(oshape, BF16),
        input_output_aliases=aliases,
        compiler_params=params(20),
        cost_estimate=cost(1e6, 1e6),
        name="grad_half",
    )(rank, *args)


def attn_grad_body(partner, rank_ref, a_ref, s_ref, one_ref, key_ref, om_ref, *rest):
    out_ref = rest[-1]
    local = om_ref.shape[1]
    second = rank_ref[3] == (0 if partner else 1)
    act = a_ref[...]

    def put(cols, value):
        if not partner:
            value = value + rest[0][:, cols].astype(F32)
        out_ref[:, cols] = value.astype(BF16)

    put(slice(0, local), outer(act, one_ref[...]))

    @pl.when(second)
    def _():
        put(slice(local, 2 * local), outer(s_ref[...], om_ref[...]))

    @pl.when(jnp.logical_not(second))
    def _():
        put(slice(local, 2 * local), outer(act, key_ref[...]))


def attn_grads(act, states, dqkv, om, rank, moved=None):
    t, d = act.shape
    local = om.shape[1]
    tile = min(512, d)
    partner = moved is None
    pos = (lambda r: 1 - r[3]) if partner else (lambda r: r[3])
    col = pl.BlockSpec((t, tile), lambda j, r: (0, j))
    out = pl.BlockSpec((tile, 2 * local), lambda j, r: (j, 0))
    return pl.pallas_call(
        functools.partial(attn_grad_body, partner),
        grid_spec=pltpu.PrefetchScalarGridSpec(
            num_scalar_prefetch=1,
            grid=(d // tile,),
            in_specs=[
                col,
                pl.BlockSpec((t, tile), lambda j, r: (0, j * pos(r))),
                pl.BlockSpec((t, local), lambda j, r: (0, 2 * pos(r))),
                pl.BlockSpec((t, local), lambda j, r: (0, 1)),
                pl.BlockSpec((t, local), lambda j, r: (0, 0)),
            ]
            + ([] if partner else [out]),
            out_specs=out,
        ),
        out_shape=jax.ShapeDtypeStruct((d, 2 * local), BF16),
        compiler_params=params(28 if partner else 50),
        cost_estimate=cost(4e9 if partner else 1e6, 1e6),
        name="attn_grads",
    )(rank, act, states, dqkv, dqkv, om, *([] if partner else [moved]))


def term_body(x_ref, w_ref, *rest):
    out = dot_t(x_ref[0], w_ref[...])
    if len(rest) > 1:
        out = out + rest[0][...].astype(F32)
    rest[-1][...] = out.astype(BF16)


def block_term(acts, slot, weight, flops, moved=None, mib=16):
    _, rows, k = acts.shape
    d = weight.shape[0]
    tile = min(512, d)
    out = pl.BlockSpec((rows, tile), lambda j: (0, j))
    return pl.pallas_call(
        term_body,
        grid=(d // tile,),
        in_specs=[
            pl.BlockSpec((1, rows, k), lambda j: (slot, 0, 0)),
            pl.BlockSpec((tile, k), lambda j: (j, 0)),
        ]
        + ([] if moved is None else [out]),
        out_specs=out,
        out_shape=jax.ShapeDtypeStruct((rows, d), BF16),
        compiler_params=params(mib),
        cost_estimate=cost(flops, flops / 256),
        name="block_term",
    )(acts, weight, *([] if moved is None else [moved]))


def join_body(slot, first, rank_ref, moved_ref, term_ref, out_ref):
    adds = rank_ref[0] < first if slot >= 0 else rank_ref[0] >= first

    @pl.when(adds)
    def _():
        out_ref[...] = (moved_ref[...].astype(F32) + term_ref[0].astype(F32)).astype(BF16)

    @pl.when(jnp.logical_not(adds))
    def _():
        out_ref[...] = moved_ref[...]


def join(rank, moved, terms, slot, first, right, part=0, flops=1e6):
    rows, d = moved.shape
    tile = min(128, rows)
    row = pl.BlockSpec((tile, d), lambda i, r: (i, 0))
    return pl.pallas_call(
        functools.partial(join_body, 0 if right else -1, first),
        grid_spec=pltpu.PrefetchScalarGridSpec(
            num_scalar_prefetch=1,
            grid=(rows // tile,),
            in_specs=[row, pl.BlockSpec((1, tile, d), lambda i, r: (slot, i, part))],
            out_specs=row,
        ),
        out_shape=jax.ShapeDtypeStruct((rows, d), BF16),
        compiler_params=params(8),
        cost_estimate=cost(flops, 1e6),
        name="join",
    )(rank, moved, terms)


def last_body(x_ref, gain_ref, term_ref, moved_ref, state_ref, out_ref):
    gain = gain_ref[...]
    _, normed, inverse = norm_forward(x_ref[...].astype(F32), gain, gain)
    back = norm_backward(term_ref[...].astype(F32) + moved_ref[...].astype(F32), normed, inverse, gain)
    out_ref[...] = (state_ref[...] + back).astype(BF16)


def last_step(x, gain, term, moved, state):
    rows, d = x.shape
    tile = min(64, rows)
    row = lambda w: pl.BlockSpec((tile, w), lambda i: (i, 0))
    return pl.pallas_call(
        last_body,
        grid=(rows // tile,),
        in_specs=[row(d), pl.BlockSpec((1, d), lambda i: (0, 0)), row(d), row(d), row(d)],
        out_specs=row(d),
        out_shape=jax.ShapeDtypeStruct((rows, d), BF16),
        compiler_params=params(12),
        cost_estimate=cost(1e6, 12 * rows * d),
        name="last_step",
    )(x, gain, term, moved, state)


def rows_body(rank_ref, mine_ref, got_ref, *outs):
    parts, _, half = got_ref.shape
    width = outs[0].shape[1]
    first = rank_ref[3] == 0

    def put(low_ref, high_ref):
        if width > half:
            for p in range(parts):
                outs[p][:, :half] = low_ref[p].astype(F32)
                outs[p][:, half:] = high_ref[p].astype(F32)
        else:
            for o, (ref, at) in zip(outs, ((low_ref, 0), (low_ref, width), (high_ref, 0), (high_ref, width))):
                o[...] = ref[0, :, at : at + width].astype(F32)

    pl.when(first)(functools.partial(put, mine_ref, got_ref))
    pl.when(jnp.logical_not(first))(functools.partial(put, got_ref, mine_ref))


def whole_rows(rank, part, got, widths):
    parts, span, half = got.shape
    tile = min(64, span)
    steps = span // tile
    return pl.pallas_call(
        rows_body,
        grid_spec=pltpu.PrefetchScalarGridSpec(
            num_scalar_prefetch=1,
            grid=(steps,),
            in_specs=[
                pl.BlockSpec((parts, tile, half), lambda i, r: (0, r[3] * steps + i, 0)),
                pl.BlockSpec((parts, tile, half), lambda i, r: (0, i, 0)),
            ],
            out_specs=[pl.BlockSpec((tile, w), lambda i, r: (i, 0)) for w in widths],
        ),
        out_shape=[jax.ShapeDtypeStruct((span, w), F32) for w in widths],
        compiler_params=params(16),
        cost_estimate=cost(1e6, 1e6),
        name="whole_rows",
    )(rank, part, got)


def tie(values, *others):
    values = tuple(values)
    return lax.optimization_barrier(values + others)[: len(values)]


def sum_over(vec, axis, moves):
    return sum((lax.ppermute(vec, axis, pairs) for pairs in moves), vec)


def per_device(
    n,
    n_dp,
    tokens,
    mixed_grad,
    doc_ids,
    head_count,
    width_bucket,
    first_gain,
    first_shift,
    query_weight,
    key_weight,
    value_weight,
    output_weight,
    second_gain,
    second_shift,
    up_weight,
    down_weight,
):
    rank = lax.axis_index("mp")
    rows, d = tokens.shape[1:]
    half = d // 2
    local = query_weight.shape[1]
    local_heads = local // E
    hidden = up_weight.shape[1]
    length = n * rows
    own = tokens[0]
    send = lambda v, pairs: lax.ppermute(v, "mp", pairs)
    ring = [(i, (i - 1) % n) for i in range(n)]
    hop = lambda v: send(v, ring)
    right_line = [(i, i + 1) for i in range(n - 1)]
    left_line = [(i + 1, i) for i in range(n - 1)]

    def tick(k, right, left, terms):
        if k:
            right = join(where, right, terms, n - k, k, True, 0, 1e9)
            left = join(where, left, terms, k, n - k, False, 0, 1e6)
        return send(right, right_line), send(left, left_line), right, left

    def owned(terms, right, left):
        return terms[0].astype(F32) + right.astype(F32) + left.astype(F32)

    low = lambda v: v.astype(BF16)
    flat = lambda v: v.reshape(length, v.shape[-1])
    add = lambda t, moved: (t.astype(F32) + moved.astype(F32)).astype(BF16)

    side = lax.rem(lax.axis_index("dp"), 2)
    where = jnp.stack([rank, rank * local_heads, rank * hidden, side]).astype(jnp.int32)
    swap = lambda v: lax.ppermute(v, "dp", [(i, i ^ 1) for i in range(n_dp)])
    sides = [list(range(c, n_dp, 2)) for c in range(2)]
    docs_col = doc_ids.reshape(n, rows, 1)
    docs_row = doc_ids.reshape(n, 1, rows)
    heads_col = head_count.reshape(n, rows, 1)
    bucket_col = width_bucket.reshape(n, rows, 1)
    cos, sin = (t.reshape(n, rows, E) for t in rotary_tables(length))
    gain1, shift1 = first_gain[None], first_shift[None]
    gain2, shift2 = second_gain[None], second_shift[None]

    held, block = None, [own[:, :half], own[:, half:]]
    for s in range(n):
        after = [None, None]
        for p in range(2):
            if s >= 1:
                block[p], *held = tie([block[p]] + list(held))
            if s < n - 1:
                after[p] = hop(block[p])
        held = qkv_slot(
            s, n, where, *block, gain1, shift1, query_weight, key_weight, value_weight, cos, sin, held
        )
        if s < n - 1:
            block = after
    first_all, query, keys, vals = held

    grad_own = mixed_grad[0]
    (own_grad,) = tie([grad_own], block[0])
    right = [own_grad[:, :half], own_grad[:, half:]]
    left = list(right)
    grads_r, grads_l = [list(right)], [list(left)]

    def half_tick(k):
        for p in range(2):
            if k:
                right[p] = join(where, right[p], terms, n - k, k, True, p)
                left[p] = join(where, left[p], terms, k, n - k, False, p)
            right[p], left[p] = send(right[p], right_line), send(left[p], left_line)

    half_tick(0)
    masked = attend(where, query, keys, vals, docs_col, docs_row, heads_col)
    terms = low(dot_t(flat(masked), output_weight)).reshape(n, rows, d)
    for k in range(1, n):
        grads_r.append(list(right))
        grads_l.append(list(left))
        half_tick(k)
    right, left = (jnp.concatenate(v, axis=1) for v in (right, left))
    attn = owned(terms, right, left)
    x_rows = own.astype(F32)
    state = x_rows + attn
    second_out, normed_two, inverse_two = norm_forward(state, gain2, shift2)

    weights = jnp.concatenate([query_weight, key_weight, value_weight], axis=1)
    held, moved = None, None
    (block,) = tie([low(second_out)], weights)
    for s in range(n):
        if s >= 1:
            block, *held = tie([block] + list(held), sent)
        after = hop(block) if s < n - 1 else None
        held = mlp_slot(
            s, n, where, block, grads_l[s] + grads_r[n - s if s else 0], up_weight, down_weight, bucket_col, held
        )
        if s >= 1:
            fused = moved if s == n - 1 and s > 1 else None
            sent = block_term(held[1], s, up_weight, 2 * rows * d * hidden, fused, 16)
            if s > 1 and fused is None:
                sent = add(sent, moved)
            moved = hop(sent)
        else:
            sent = term0 = block_term(held[1], 0, up_weight, 2 * rows * d * hidden, None, 16)
        block = after
    active, grad_upper, second_all, grad_all = held
    grad_all, active, second_all, grad_upper = tie([grad_all, active, second_all, grad_upper], sent)
    gifts = [
        grad_half(flat(grad_all), flat(active), where, True),
        grad_half(flat(second_all), flat(grad_upper), where, True),
    ]
    (moved,) = tie([moved], *gifts)
    down_gift, up_gift = (swap(v) for v in gifts)
    grad_second = term0.astype(F32) + moved.astype(F32)
    back_two = norm_backward(grad_second, normed_two, inverse_two, gain2)
    second_gain_part = jnp.sum(grad_second * normed_two, axis=0)
    second_shift_part = jnp.sum(grad_second, axis=0)
    grad_state = grad_own.astype(F32) + back_two

    start = low(grad_state)
    grad_all, active, start = tie([grad_all, active, start])
    right = left = start
    rights, lefts = [start], [start]
    right, left, _, _ = tick(0, right, left, None)
    ffn = low(dot_t(flat(active), down_weight)).reshape(n, rows, d)
    pair = grad_half(flat(grad_all), flat(active), where, False, 0, down_gift)
    (right,) = tie([right], pair)
    (left,) = tie([left], pair)
    for k in range(1, n):
        rights.append(right)
        lefts.append(left)
        right, left, went_r, went_l = tick(k, right, left, ffn)
        if k == 1:
            second_all, grad_upper = tie([second_all, grad_upper], went_r, went_l)
            pair = grad_half(flat(second_all), flat(grad_upper), where, False, 1, up_gift, pair)
            wide_grad = lax.psum_scatter(pair, "dp", scatter_dimension=1, axis_index_groups=sides, tiled=True)
            (right,) = tie([right], pair)
            (left,) = tie([left], pair)
    late = sorted({1, n - 1})
    early = [s for s in range(n) if s not in late]
    pick = lambda slots: sum(([start] if s == 0 else [lefts[s], rights[n - s]] for s in slots), [])
    held = dom_part(n, early, where, pick(early), output_weight, None)
    grad_masked, state_all = dom_part(n, late, where, pick(late), output_weight, held)
    dqkv = attend_back(
        where, query, keys, vals, grad_masked, docs_col, docs_row, heads_col, cos, sin
    )
    mixed = low(state + owned(ffn, right, left))

    def whole(part, widths):
        span = part.shape[1] // 2
        got = swap(lax.dynamic_slice_in_dim(part, (1 - side) * span, span, 1))
        return whole_rows(where, part, got, widths)

    tokens_of = lambda v: (flat(first_all), flat(state_all), flat(v), flat(masked), where)
    sent = block_term(dqkv, 1, weights, 1e6)
    (dqkv,) = tie([dqkv], sent, right, left)
    moved = hop(sent)
    gift = attn_grads(*tokens_of(dqkv))
    (dqkv,) = tie([dqkv], gift)
    terms = {1: sent, 2: block_term(dqkv, 2, weights, 1e6)}
    (dqkv,) = tie([dqkv], terms[2])
    attn_term = attn_grads(*tokens_of(dqkv), swap(gift))
    (late,) = tie([attn_term], wide_grad)
    attn_grad = lax.psum_scatter(late, "dp", scatter_dimension=0, axis_index_groups=sides, tiled=True)
    (moved,) = tie([moved], attn_term)
    sent2 = sent = join(where, moved, terms[2][None], 0, n + 1, True)
    moved = hop(sent)
    for s in range(3, n):
        (dqkv,) = tie([dqkv], sent)
        terms[s] = block_term(dqkv, s, weights, 1e6)
    (dqkv,) = tie([dqkv], terms[n - 1])
    terms[0] = block_term(dqkv, 0, weights, 1e6)
    held = tie([terms[s] for s in range(n)], sent2)
    sum_d = sum(jnp.sum(v.astype(F32), axis=0) for v in held)
    sum_da = sum(jnp.sum(v.astype(F32) * first_all[s].astype(F32), axis=0) for s, v in enumerate(held))
    first_shift_part = sum_d
    first_gain_part = (sum_da - first_shift * sum_d) / first_gain

    lead = (rank == 0).astype(F32)
    bucket_part = lead * jnp.sum(
        (width_bucket[0][:, None] == jnp.arange(4, dtype=jnp.int32)[None, :]).astype(F32), axis=0
    )
    head_part = lead * jnp.sum(
        (head_count[0][:, None] == jnp.arange(1, HEADS + 1, dtype=jnp.int32)[None, :]).astype(F32),
        axis=0,
    )
    small = jnp.concatenate(
        [
            first_gain_part,
            first_shift_part,
            second_gain_part,
            second_shift_part,
            bucket_part,
            head_part,
            jnp.zeros((128 - 4 - HEADS,), F32),
        ]
    )
    small = sum_over(small, "dp", [[(i, i ^ 1) for i in range(n_dp)]])
    for s in range(3, n):
        sent = join(where, moved, terms[s][None], 0, n + 1, True, 0, 64e9)
        moved = hop(sent)

    planes = tie([send(small, [(i, (i + m) % n) for i in range(n)]) for m in range(1, n)], sent)
    small = small + sum(planes)
    others = [
        lax.ppermute(small, "dp", [(i, (i + 2 * m) % n_dp) for i in range(n_dp)])
        for m in range(1, n_dp // 2)
    ]
    wide = whole(wide_grad, [hidden] * 2)
    weight_grads = whole(attn_grad[None], [local] * 4)
    moved, *outs = tie([moved, *wide, *weight_grads])
    wide, weight_grads = outs[:2], outs[2:]
    input_grad = last_step(own, gain1, terms[0], moved, grad_state)
    small = small + sum(tie(others, input_grad))

    return (
        mixed[None],
        input_grad[None],
        small[:d],
        small[d : 2 * d],
        *weight_grads,
        small[2 * d : 3 * d],
        small[3 * d : 4 * d],
        wide[1],
        wide[0],
        small[4 * d : 4 * d + 4].astype(jnp.int32),
        small[4 * d + 4 : 4 * d + 4 + HEADS].astype(jnp.int32),
    )


def solution(mesh):
    token, seq, copy, col = P("dp", "mp", None), P("dp", None), P(), P(None, "mp")
    grad = P("dp", "mp")
    return jax.shard_map(
        functools.partial(per_device, mesh.shape["mp"], mesh.shape["dp"]),
        mesh=mesh,
        in_specs=(token, token, seq, seq, seq, copy, copy, col, col, col, col, copy, copy, col, col),
        out_specs=(token, token, copy, copy, grad, grad, grad, grad, copy, copy, grad, grad, copy, copy),
        check_vma=False,
    )
```

```python
import functools
import jax
import jax.numpy as jnp
from jax import lax
from jax.experimental import pallas as pl
from jax.experimental.pallas import tpu as pltpu
from jax.sharding import PartitionSpec as P

HEADS = 16
E = 128
FF = 8192
EPS = 1e-05
DOC_MAX = 512
LOG2E = 1.4426950408889634
F32 = jnp.float32
BF16 = jnp.bfloat16


def params(mib):
    return pltpu.CompilerParams(vmem_limit_bytes=mib << 20)


def cost(flops, nbytes, trans=0):
    return pl.CostEstimate(flops=int(flops), bytes_accessed=int(nbytes), transcendentals=int(trans))


def norm_forward(values, gain, shift):
    mean = jnp.mean(values, axis=-1, keepdims=True)
    cent = values - mean
    inverse = lax.rsqrt(jnp.mean(cent * cent, axis=-1, keepdims=True) + EPS)
    normed = cent * inverse
    return (normed * gain + shift, normed, inverse)


def norm_backward(grad_out, normed, inverse, gain):
    scaled = grad_out * gain
    return inverse * (
        scaled
        - jnp.mean(scaled, axis=-1, keepdims=True)
        - normed * jnp.mean(scaled * normed, axis=-1, keepdims=True)
    )


def rotary_tables(length):
    half = E // 2
    freq = 10000.0 ** (-(jnp.arange(half, dtype=F32) * 2.0 / E))
    angle = jnp.arange(length, dtype=F32)[:, None] * freq[None, :]
    cos, sin = jnp.cos(angle), jnp.sin(angle)
    return jnp.concatenate([cos, cos], axis=1), jnp.concatenate([-sin, sin], axis=1)


def dot_t(left, right):
    return lax.dot_general(left, right, (((1,), (1,)), ((), ())), preferred_element_type=F32)


def dot_n(left, right):
    return lax.dot_general(left, right, (((1,), (0,)), ((), ())), preferred_element_type=F32)


def outer(left, right):
    return lax.dot_general(left, right, (((0,), (0,)), ((), ())), preferred_element_type=F32)


def qkv_body(rank_ref, xa_ref, xb_ref, gain_ref, shift_ref, wq_ref, wk_ref, wv_ref, cos_ref, sin_ref, *rest):
    a_ref, q_ref, k_ref, v_ref = rest[-4:]

    @pl.when(pl.program_id(0) == 0)
    def _():
        x = jnp.concatenate([xa_ref[...], xb_ref[...]], axis=1).astype(F32)
        out, _, _ = norm_forward(x, gain_ref[...], shift_ref[...])
        a_ref[0] = out.astype(BF16)

    act = a_ref[0]
    cos, sin = cos_ref[0], sin_ref[0]
    v_ref[0] = dot_n(act, wv_ref[...]).astype(BF16)
    for w_ref, o_ref in ((wq_ref, q_ref), (wk_ref, k_ref)):
        lin = dot_n(act, w_ref[...])
        for j in range(lin.shape[1] // E):
            part = lin[:, j * E : (j + 1) * E]
            turned = part * cos + pltpu.roll(part, E // 2, 1) * sin
            o_ref[0, :, j * E : (j + 1) * E] = turned.astype(BF16)


def qkv_slot(slot, n, rank, xa, xb, gain, shift, wq, wk, wv, cos, sin, held):
    rows, half = xa.shape
    d = 2 * half
    local = wq.shape[1]
    cb = min(512, local)
    whole = lambda j, r: (0, 0)
    wspec = pl.BlockSpec((d, cb), lambda j, r: (0, j))
    tspec = pl.BlockSpec((1, rows, E), lambda j, r: (lax.rem(r[0] + slot, n), 0, 0))
    in_specs = [
        pl.BlockSpec((rows, half), whole),
        pl.BlockSpec((rows, half), whole),
        pl.BlockSpec((1, d), whole),
        pl.BlockSpec((1, d), whole),
        wspec,
        wspec,
        wspec,
        tspec,
        tspec,
    ]
    extra = [] if held is None else list(held)
    aliases = {} if held is None else {10 + i: i for i in range(4)}
    ospec = pl.BlockSpec((1, rows, cb), lambda j, r: (slot, 0, j))
    return pl.pallas_call(
        qkv_body,
        grid_spec=pltpu.PrefetchScalarGridSpec(
            num_scalar_prefetch=1,
            grid=(local // cb,),
            in_specs=in_specs + [pl.BlockSpec(memory_space=pl.ANY)] * len(extra),
            out_specs=[pl.BlockSpec((1, rows, d), lambda j, r: (slot, 0, 0)), ospec, ospec, ospec],
        ),
        out_shape=[jax.ShapeDtypeStruct((n, rows, d), BF16)]
        + [jax.ShapeDtypeStruct((n, rows, local), BF16)] * 3,
        input_output_aliases=aliases,
        compiler_params=params(56),
        cost_estimate=cost(6 * rows * d * local, 6 * d * local + 4 * rows * d),
        name="qkv_slot",
    )(rank, xa, xb, gain, shift, wq, wk, wv, cos, sin, *extra)


def first_key(block, rows):
    return max(0, block - (DOC_MAX - 1 + rows - 1) // rows)


def attend_body(rank_ref, q_ref, k_ref, v_ref, dcol_ref, drow_ref, hc_ref, o_ref):
    n, rows, _ = q_ref.shape
    rank = rank_ref[0]
    head = rank_ref[1] + pl.program_id(0)
    slot = lambda b: lax.rem(b + n - rank, n)
    factor = E ** (-0.5) * LOG2E
    low = lax.broadcasted_iota(jnp.int32, (rows, rows), 0) >= lax.broadcasted_iota(
        jnp.int32, (rows, rows), 1
    )
    for b in range(n):
        q = q_ref[slot(b)]
        doc = dcol_ref[b]
        keys = range(first_key(b, rows), b + 1)
        scores = []
        for c in keys:
            s = dot_t(q, k_ref[slot(c)])
            ok = doc == drow_ref[c]
            if c == b:
                ok = ok & low
            scores.append(jnp.where(ok, s, -1e30))
        top = scores[0]
        for s in scores[1:]:
            top = jnp.maximum(top, s)
        top = jnp.max(top, axis=1, keepdims=True)
        total = None
        out = None
        for c, s in zip(keys, scores):
            p = jnp.exp2((s - top) * factor)
            total = p if total is None else total + p
            o = dot_n(p.astype(BF16), v_ref[slot(c)])
            out = o if out is None else out + o
        total = jnp.sum(total, axis=1, keepdims=True)
        gate = jnp.where(hc_ref[b] > head, 1.0, 0.0)
        o_ref[slot(b)] = (out * (gate / total)).astype(BF16)


def attend(rank, q, k, v, docs_col, docs_row, heads_col):
    n, rows, local = q.shape
    spec = pl.BlockSpec((n, rows, E), lambda h, r: (0, 0, h))
    col = pl.BlockSpec((n, rows, 1), lambda h, r: (0, 0, 0))
    row = pl.BlockSpec((n, 1, rows), lambda h, r: (0, 0, 0))
    t = n * rows
    return pl.pallas_call(
        attend_body,
        grid_spec=pltpu.PrefetchScalarGridSpec(
            num_scalar_prefetch=1,
            grid=(local // E,),
            in_specs=[spec, spec, spec, col, row, col],
            out_specs=spec,
        ),
        out_shape=jax.ShapeDtypeStruct((n, rows, local), BF16),
        compiler_params=params(62),
        cost_estimate=cost(4 * t * t * local, 8 * t * local, t * t * local // E),
        name="attend",
    )(rank, q, k, v, docs_col, docs_row, heads_col)


def attend_back_body(
    rank_ref, q_ref, k_ref, v_ref, do_ref, dcol_ref, drow_ref, hc_ref, cos_ref, sin_ref, out_ref, dk_ref, dv_ref
):
    n, rows, _ = q_ref.shape
    rank = rank_ref[0]
    head = rank_ref[1] + pl.program_id(0)
    slot = lambda b: lax.rem(b + n - rank, n)
    scale = E ** (-0.5)
    factor = scale * LOG2E
    low = lax.broadcasted_iota(jnp.int32, (rows, rows), 0) <= lax.broadcasted_iota(
        jnp.int32, (rows, rows), 1
    )
    local = out_ref.shape[2] // 3
    lanes = lambda i: pl.ds(pl.multiple_of(i * local + pl.program_id(0) * E, E), E)
    dk_ref[...] = jnp.zeros_like(dk_ref)
    dv_ref[...] = jnp.zeros_like(dv_ref)

    def unrotate(w, b):
        w = w * scale
        return (w * cos_ref[b] - pltpu.roll(w, E // 2, 1) * sin_ref[b]).astype(BF16)

    for b in range(n):
        q = q_ref[slot(b)]
        grad = jnp.where(hc_ref[b] > head, do_ref[slot(b)].astype(F32), 0.0).astype(BF16)
        keys = range(first_key(b, rows), b + 1)
        scores = []
        for c in keys:
            s = dot_t(k_ref[slot(c)], q)
            ok = dcol_ref[c] == drow_ref[b]
            if c == b:
                ok = ok & low
            scores.append(jnp.where(ok, s, -1e30))
        top = scores[0]
        for s in scores[1:]:
            top = jnp.maximum(top, s)
        top = jnp.max(top, axis=0, keepdims=True)
        probs = [jnp.exp2((s - top) * factor) for s in scores]
        total = probs[0]
        for p in probs[1:]:
            total = total + p
        inv = 1.0 / jnp.sum(total, axis=0, keepdims=True)
        probs = [p * inv for p in probs]
        dprobs = [dot_t(v_ref[slot(c)], grad) for c in keys]
        delta = None
        for p, g in zip(probs, dprobs):
            delta = p * g if delta is None else delta + p * g
        delta = jnp.sum(delta, axis=0, keepdims=True)
        dq = None
        for c, p, g in zip(keys, probs, dprobs):
            ds = (p * (g - delta)).astype(BF16)
            dk_ref[c] += dot_n(ds, q)
            dv_ref[c] += dot_n(p.astype(BF16), grad)
            part = outer(ds, k_ref[slot(c)])
            dq = part if dq is None else dq + part
        out_ref[slot(b), :, lanes(0)] = unrotate(dq, b)
    for b in range(n):
        out_ref[slot(b), :, lanes(1)] = unrotate(dk_ref[b], b)
        out_ref[slot(b), :, lanes(2)] = dv_ref[b].astype(BF16)


def attend_back(rank, q, k, v, do, docs_col, docs_row, heads_col, cos, sin):
    n, rows, local = q.shape
    spec = pl.BlockSpec((n, rows, E), lambda h, r: (0, 0, h))
    col = pl.BlockSpec((n, rows, 1), lambda h, r: (0, 0, 0))
    row = pl.BlockSpec((n, 1, rows), lambda h, r: (0, 0, 0))
    table = pl.BlockSpec((n, rows, E), lambda h, r: (0, 0, 0))
    t = n * rows
    return pl.pallas_call(
        attend_back_body,
        grid_spec=pltpu.PrefetchScalarGridSpec(
            num_scalar_prefetch=1,
            grid=(local // E,),
            in_specs=[spec, spec, spec, spec, col, row, col, table, table],
            out_specs=pl.BlockSpec((n, rows, 3 * local), lambda h, r: (0, 0, 0)),
            scratch_shapes=[pltpu.VMEM((n, rows, E), F32), pltpu.VMEM((n, rows, E), F32)],
        ),
        out_shape=jax.ShapeDtypeStruct((n, rows, 3 * local), BF16),
        compiler_params=params(24),
        cost_estimate=cost(116e9, 14 * t * local),
        name="attend_back",
    )(rank, q, k, v, do, docs_col, docs_row, heads_col, cos, sin)


def mlp_body(slot, n, rank_ref, a_ref, gla_ref, glb_ref, gra_ref, grb_ref, up_ref, down_ref, bucket_ref, *rest):
    r_ref, du_ref, aa_ref, ga_ref = rest[-4:]
    rows, cb = a_ref.shape[0], up_ref.shape[1]

    @pl.when(pl.program_id(0) == 0)
    def _():
        aa_ref[0] = a_ref[...]
        ahead = rank_ref[0] + slot < n

        half = gla_ref.shape[1]

        def fill(first, second):
            ga_ref[0, :, :half] = first[...]
            ga_ref[0, :, half:] = second[...]

        pl.when(ahead)(functools.partial(fill, gla_ref, glb_ref))
        pl.when(jnp.logical_not(ahead))(functools.partial(fill, gra_ref, grb_ref))

    u = dot_n(a_ref[...], up_ref[...])
    dr = dot_n(ga_ref[0], down_ref[...]).astype(BF16).astype(F32)
    column = rank_ref[2] + pl.program_id(0) * cb + lax.broadcasted_iota(jnp.int32, (rows, cb), 1)
    lifted = jnp.where(column < (bucket_ref[0] + 1) * (FF // 4), jnp.maximum(u, 0.0), 0.0)
    r_ref[0] = (lifted * lifted).astype(BF16)
    du_ref[0] = (dr * (2.0 * lifted)).astype(BF16)


def mlp_slot(slot, n, rank, act, grads, up, down, bucket_col, held):
    rows, d = act.shape
    hidden = up.shape[1]
    cb = min(512, hidden)
    whole = lambda j, r: (0, 0)
    wspec = pl.BlockSpec((d, cb), lambda j, r: (0, j))
    extra = [] if held is None else list(held)
    aliases = {} if held is None else {9 + i: i for i in range(4)}
    ospec = pl.BlockSpec((1, rows, cb), lambda j, r: (slot, 0, j))
    aspec = pl.BlockSpec((1, rows, d), lambda j, r: (slot, 0, 0))
    return pl.pallas_call(
        functools.partial(mlp_body, slot, n),
        grid_spec=pltpu.PrefetchScalarGridSpec(
            num_scalar_prefetch=1,
            grid=(hidden // cb,),
            in_specs=[
                pl.BlockSpec((rows, d), whole),
            ]
            + [pl.BlockSpec((rows, d // 2), whole)] * 4
            + [
                wspec,
                wspec,
                pl.BlockSpec((1, rows, 1), lambda j, r: (lax.rem(r[0] + slot, n), 0, 0)),
            ]
            + [pl.BlockSpec(memory_space=pl.ANY)] * len(extra),
            out_specs=[ospec, ospec, aspec, aspec],
        ),
        out_shape=[jax.ShapeDtypeStruct((n, rows, hidden), BF16)] * 2
        + [jax.ShapeDtypeStruct((n, rows, d), BF16)] * 2,
        input_output_aliases=aliases,
        compiler_params=params(28),
        cost_estimate=cost(4 * rows * d * hidden, 4 * d * hidden + 4 * rows * (d + hidden)),
        name="mlp_slot",
    )(rank, act, *grads, up, down, bucket_col, *extra)


def dom_body(n, slots, rank_ref, slot_ref, *refs):
    dom_ref, all_ref = refs[-2:]
    count = sum(1 if s == 0 else 2 for s in slots)
    flows, w_ref = list(refs[:count]), refs[count]

    def fill(ref):
        all_ref[0] = ref[...]

    for i, s in enumerate(slots):
        here = pl.program_id(0) == i
        if s == 0:
            pl.when(here)(functools.partial(fill, flows[0]))
            flows = flows[1:]
        else:
            ahead = rank_ref[0] + s < n
            pl.when(here & ahead)(functools.partial(fill, flows[0]))
            pl.when(here & jnp.logical_not(ahead))(functools.partial(fill, flows[1]))
            flows = flows[2:]
    dom_ref[0] = dot_n(all_ref[0], w_ref[...]).astype(BF16)


def dom_part(n, slots, rank, flows, weight, held):
    rows, d = flows[0].shape
    local = weight.shape[1]
    whole = lambda i, r, s: (0, 0)
    extra = [] if held is None else list(held)
    at = 2 + len(flows) + 1
    return pl.pallas_call(
        functools.partial(dom_body, n, slots),
        grid_spec=pltpu.PrefetchScalarGridSpec(
            num_scalar_prefetch=2,
            grid=(len(slots),),
            in_specs=[pl.BlockSpec((rows, d), whole)] * len(flows)
            + [pl.BlockSpec((d, local), whole)]
            + [pl.BlockSpec(memory_space=pl.ANY)] * len(extra),
            out_specs=[
                pl.BlockSpec((1, rows, local), lambda i, r, s: (s[i], 0, 0)),
                pl.BlockSpec((1, rows, d), lambda i, r, s: (s[i], 0, 0)),
            ],
        ),
        out_shape=[
            jax.ShapeDtypeStruct((n, rows, local), BF16),
            jax.ShapeDtypeStruct((n, rows, d), BF16),
        ],
        input_output_aliases={at + i: i for i in range(len(extra))},
        compiler_params=params(24),
        cost_estimate=cost(
            2 * len(slots) * rows * d * local, 2 * d * local + 6 * len(slots) * rows * d
        ),
        name="dom_part",
    )(rank, jnp.asarray(slots, jnp.int32), *flows, weight, *extra)


def grad_body(has_sum, rank_ref, lhs_ref, rhs_ref, *rest):
    out = outer(lhs_ref[...], rhs_ref[...])
    if has_sum:
        rest[-1][0] = (out + rest[0][...].astype(F32)).astype(BF16)
    else:
        rest[-1][...] = out.astype(BF16)


def grad_half(lhs, rhs, rank, partner, which=0, moved=None, held=None):
    t, d = lhs.shape
    half = rhs.shape[1] // 2
    tile = min(512, d)
    col = (lambda r: 1 - r[3]) if partner else (lambda r: r[3])
    specs = [
        pl.BlockSpec((t, tile), lambda j, r: (0, j)),
        pl.BlockSpec((t, half), lambda j, r: (0, col(r))),
    ]
    args = [lhs, rhs]
    aliases = {}
    if partner:
        ospec = pl.BlockSpec((tile, half), lambda j, r: (j, 0))
        oshape = (d, half)
    else:
        specs.append(pl.BlockSpec((tile, half), lambda j, r: (j, 0)))
        args.append(moved)
        ospec = pl.BlockSpec((1, tile, half), lambda j, r: (which, j, 0))
        oshape = (2, d, half)
        if held is not None:
            specs.append(pl.BlockSpec(memory_space=pl.ANY))
            args.append(held)
            aliases = {4: 0}
    return pl.pallas_call(
        functools.partial(grad_body, not partner),
        grid_spec=pltpu.PrefetchScalarGridSpec(
            num_scalar_prefetch=1, grid=(d // tile,), in_specs=specs, out_specs=ospec
        ),
        out_shape=jax.ShapeDtypeStruct(oshape, BF16),
        input_output_aliases=aliases,
        compiler_params=params(20),
        cost_estimate=cost(1e6, 1e6),
        name="grad_half",
    )(rank, *args)


def attn_grad_body(partner, rank_ref, a_ref, s_ref, one_ref, key_ref, om_ref, *rest):
    out_ref = rest[-1]
    local = om_ref.shape[1]
    second = rank_ref[3] == (0 if partner else 1)
    act = a_ref[...]

    def put(cols, value):
        if not partner:
            value = value + rest[0][:, cols].astype(F32)
        out_ref[:, cols] = value.astype(BF16)

    put(slice(0, local), outer(act, one_ref[...]))

    @pl.when(second)
    def _():
        put(slice(local, 2 * local), outer(s_ref[...], om_ref[...]))

    @pl.when(jnp.logical_not(second))
    def _():
        put(slice(local, 2 * local), outer(act, key_ref[...]))


def attn_grads(act, states, dqkv, om, rank, moved=None):
    t, d = act.shape
    local = om.shape[1]
    tile = min(512, d)
    partner = moved is None
    pos = (lambda r: 1 - r[3]) if partner else (lambda r: r[3])
    col = pl.BlockSpec((t, tile), lambda j, r: (0, j))
    out = pl.BlockSpec((tile, 2 * local), lambda j, r: (j, 0))
    return pl.pallas_call(
        functools.partial(attn_grad_body, partner),
        grid_spec=pltpu.PrefetchScalarGridSpec(
            num_scalar_prefetch=1,
            grid=(d // tile,),
            in_specs=[
                col,
                pl.BlockSpec((t, tile), lambda j, r: (0, j * pos(r))),
                pl.BlockSpec((t, local), lambda j, r: (0, 2 * pos(r))),
                pl.BlockSpec((t, local), lambda j, r: (0, 1)),
                pl.BlockSpec((t, local), lambda j, r: (0, 0)),
            ]
            + ([] if partner else [out]),
            out_specs=out,
        ),
        out_shape=jax.ShapeDtypeStruct((d, 2 * local), BF16),
        compiler_params=params(28 if partner else 50),
        cost_estimate=cost(4e9 if partner else 1e6, 1e6),
        name="attn_grads",
    )(rank, act, states, dqkv, dqkv, om, *([] if partner else [moved]))


def term_body(x_ref, w_ref, *rest):
    out = dot_t(x_ref[0], w_ref[...])
    if len(rest) > 1:
        out = out + rest[0][...].astype(F32)
    rest[-1][...] = out.astype(BF16)


def block_term(acts, slot, weight, flops, moved=None, mib=16):
    _, rows, k = acts.shape
    d = weight.shape[0]
    tile = min(512, d)
    out = pl.BlockSpec((rows, tile), lambda j: (0, j))
    return pl.pallas_call(
        term_body,
        grid=(d // tile,),
        in_specs=[
            pl.BlockSpec((1, rows, k), lambda j: (slot, 0, 0)),
            pl.BlockSpec((tile, k), lambda j: (j, 0)),
        ]
        + ([] if moved is None else [out]),
        out_specs=out,
        out_shape=jax.ShapeDtypeStruct((rows, d), BF16),
        compiler_params=params(mib),
        cost_estimate=cost(flops, flops / 256),
        name="block_term",
    )(acts, weight, *([] if moved is None else [moved]))


def join_body(slot, first, rank_ref, moved_ref, term_ref, out_ref):
    adds = rank_ref[0] < first if slot >= 0 else rank_ref[0] >= first

    @pl.when(adds)
    def _():
        out_ref[...] = (moved_ref[...].astype(F32) + term_ref[0].astype(F32)).astype(BF16)

    @pl.when(jnp.logical_not(adds))
    def _():
        out_ref[...] = moved_ref[...]


def join(rank, moved, terms, slot, first, right, part=0, flops=1e6):
    rows, d = moved.shape
    tile = min(128, rows)
    row = pl.BlockSpec((tile, d), lambda i, r: (i, 0))
    return pl.pallas_call(
        functools.partial(join_body, 0 if right else -1, first),
        grid_spec=pltpu.PrefetchScalarGridSpec(
            num_scalar_prefetch=1,
            grid=(rows // tile,),
            in_specs=[row, pl.BlockSpec((1, tile, d), lambda i, r: (slot, i, part))],
            out_specs=row,
        ),
        out_shape=jax.ShapeDtypeStruct((rows, d), BF16),
        compiler_params=params(8),
        cost_estimate=cost(flops, 1e6),
        name="join",
    )(rank, moved, terms)


def last_body(x_ref, gain_ref, term_ref, moved_ref, state_ref, out_ref):
    gain = gain_ref[...]
    _, normed, inverse = norm_forward(x_ref[...].astype(F32), gain, gain)
    back = norm_backward(term_ref[...].astype(F32) + moved_ref[...].astype(F32), normed, inverse, gain)
    out_ref[...] = (state_ref[...] + back).astype(BF16)


def last_step(x, gain, term, moved, state):
    rows, d = x.shape
    tile = min(64, rows)
    row = lambda w: pl.BlockSpec((tile, w), lambda i: (i, 0))
    return pl.pallas_call(
        last_body,
        grid=(rows // tile,),
        in_specs=[row(d), pl.BlockSpec((1, d), lambda i: (0, 0)), row(d), row(d), row(d)],
        out_specs=row(d),
        out_shape=jax.ShapeDtypeStruct((rows, d), BF16),
        compiler_params=params(12),
        cost_estimate=cost(1e6, 12 * rows * d),
        name="last_step",
    )(x, gain, term, moved, state)


def rows_body(rank_ref, mine_ref, got_ref, *outs):
    parts, _, half = got_ref.shape
    width = outs[0].shape[1]
    first = rank_ref[3] == 0

    def put(low_ref, high_ref):
        if width > half:
            for p in range(parts):
                outs[p][:, :half] = low_ref[p].astype(F32)
                outs[p][:, half:] = high_ref[p].astype(F32)
        else:
            for o, (ref, at) in zip(outs, ((low_ref, 0), (low_ref, width), (high_ref, 0), (high_ref, width))):
                o[...] = ref[0, :, at : at + width].astype(F32)

    pl.when(first)(functools.partial(put, mine_ref, got_ref))
    pl.when(jnp.logical_not(first))(functools.partial(put, got_ref, mine_ref))


def whole_rows(rank, part, got, widths):
    parts, span, half = got.shape
    tile = min(64, span)
    steps = span // tile
    return pl.pallas_call(
        rows_body,
        grid_spec=pltpu.PrefetchScalarGridSpec(
            num_scalar_prefetch=1,
            grid=(steps,),
            in_specs=[
                pl.BlockSpec((parts, tile, half), lambda i, r: (0, r[3] * steps + i, 0)),
                pl.BlockSpec((parts, tile, half), lambda i, r: (0, i, 0)),
            ],
            out_specs=[pl.BlockSpec((tile, w), lambda i, r: (i, 0)) for w in widths],
        ),
        out_shape=[jax.ShapeDtypeStruct((span, w), F32) for w in widths],
        compiler_params=params(16),
        cost_estimate=cost(1e6, 1e6),
        name="whole_rows",
    )(rank, part, got)


def tie(values, *others):
    values = tuple(values)
    return lax.optimization_barrier(values + others)[: len(values)]


def sum_over(vec, axis, moves):
    return sum((lax.ppermute(vec, axis, pairs) for pairs in moves), vec)


def per_device(
    n,
    n_dp,
    tokens,
    mixed_grad,
    doc_ids,
    head_count,
    width_bucket,
    first_gain,
    first_shift,
    query_weight,
    key_weight,
    value_weight,
    output_weight,
    second_gain,
    second_shift,
    up_weight,
    down_weight,
):
    rank = lax.axis_index("mp")
    rows, d = tokens.shape[1:]
    half = d // 2
    local = query_weight.shape[1]
    local_heads = local // E
    hidden = up_weight.shape[1]
    length = n * rows
    own = tokens[0]
    send = lambda v, pairs: lax.ppermute(v, "mp", pairs)
    ring = [(i, (i - 1) % n) for i in range(n)]
    hop = lambda v: send(v, ring)
    right_line = [(i, i + 1) for i in range(n - 1)]
    left_line = [(i + 1, i) for i in range(n - 1)]

    def tick(k, right, left, terms):
        if k:
            right = join(where, right, terms, n - k, k, True, 0, 1e9)
            left = join(where, left, terms, k, n - k, False, 0, 1e6)
        return send(right, right_line), send(left, left_line), right, left

    def owned(terms, right, left):
        return terms[0].astype(F32) + right.astype(F32) + left.astype(F32)

    low = lambda v: v.astype(BF16)
    flat = lambda v: v.reshape(length, v.shape[-1])
    add = lambda t, moved: (t.astype(F32) + moved.astype(F32)).astype(BF16)

    side = lax.rem(lax.axis_index("dp"), 2)
    where = jnp.stack([rank, rank * local_heads, rank * hidden, side]).astype(jnp.int32)
    swap = lambda v: lax.ppermute(v, "dp", [(i, i ^ 1) for i in range(n_dp)])
    sides = [list(range(c, n_dp, 2)) for c in range(2)]
    docs_col = doc_ids.reshape(n, rows, 1)
    docs_row = doc_ids.reshape(n, 1, rows)
    heads_col = head_count.reshape(n, rows, 1)
    bucket_col = width_bucket.reshape(n, rows, 1)
    cos, sin = (t.reshape(n, rows, E) for t in rotary_tables(length))
    gain1, shift1 = first_gain[None], first_shift[None]
    gain2, shift2 = second_gain[None], second_shift[None]

    held, block = None, [own[:, :half], own[:, half:]]
    for s in range(n):
        after = [None, None]
        for p in range(2):
            if s >= 1:
                block[p], *held = tie([block[p]] + list(held))
            if s < n - 1:
                after[p] = hop(block[p])
        held = qkv_slot(
            s, n, where, *block, gain1, shift1, query_weight, key_weight, value_weight, cos, sin, held
        )
        if s < n - 1:
            block = after
    first_all, query, keys, vals = held

    grad_own = mixed_grad[0]
    (own_grad,) = tie([grad_own], block[0])
    right = [own_grad[:, :half], own_grad[:, half:]]
    left = list(right)
    grads_r, grads_l = [list(right)], [list(left)]

    def half_tick(k):
        for p in range(2):
            if k:
                right[p] = join(where, right[p], terms, n - k, k, True, p)
                left[p] = join(where, left[p], terms, k, n - k, False, p)
            right[p], left[p] = send(right[p], right_line), send(left[p], left_line)

    half_tick(0)
    masked = attend(where, query, keys, vals, docs_col, docs_row, heads_col)
    terms = low(dot_t(flat(masked), output_weight)).reshape(n, rows, d)
    for k in range(1, n):
        grads_r.append(list(right))
        grads_l.append(list(left))
        half_tick(k)
    right, left = (jnp.concatenate(v, axis=1) for v in (right, left))
    attn = owned(terms, right, left)
    x_rows = own.astype(F32)
    state = x_rows + attn
    second_out, normed_two, inverse_two = norm_forward(state, gain2, shift2)

    weights = jnp.concatenate([query_weight, key_weight, value_weight], axis=1)
    held, moved = None, None
    (block,) = tie([low(second_out)], weights)
    for s in range(n):
        if s >= 1:
            block, *held = tie([block] + list(held), sent)
        after = hop(block) if s < n - 1 else None
        held = mlp_slot(
            s, n, where, block, grads_l[s] + grads_r[n - s if s else 0], up_weight, down_weight, bucket_col, held
        )
        if s >= 1:
            fused = moved if s == n - 1 and s > 1 else None
            sent = block_term(held[1], s, up_weight, 2 * rows * d * hidden, fused, 16)
            if s > 1 and fused is None:
                sent = add(sent, moved)
            moved = hop(sent)
        else:
            sent = term0 = block_term(held[1], 0, up_weight, 2 * rows * d * hidden, None, 16)
        block = after
    active, grad_upper, second_all, grad_all = held
    grad_all, active, second_all, grad_upper = tie([grad_all, active, second_all, grad_upper], sent)
    gifts = [
        grad_half(flat(grad_all), flat(active), where, True),
        grad_half(flat(second_all), flat(grad_upper), where, True),
    ]
    (moved,) = tie([moved], *gifts)
    down_gift, up_gift = (swap(v) for v in gifts)
    grad_second = term0.astype(F32) + moved.astype(F32)
    back_two = norm_backward(grad_second, normed_two, inverse_two, gain2)
    second_gain_part = jnp.sum(grad_second * normed_two, axis=0)
    second_shift_part = jnp.sum(grad_second, axis=0)
    grad_state = grad_own.astype(F32) + back_two

    start = low(grad_state)
    grad_all, active, start = tie([grad_all, active, start])
    right = left = start
    rights, lefts = [start], [start]
    right, left, _, _ = tick(0, right, left, None)
    ffn = low(dot_t(flat(active), down_weight)).reshape(n, rows, d)
    pair = grad_half(flat(grad_all), flat(active), where, False, 0, down_gift)
    (right,) = tie([right], pair)
    (left,) = tie([left], pair)
    for k in range(1, n):
        rights.append(right)
        lefts.append(left)
        right, left, went_r, went_l = tick(k, right, left, ffn)
        if k == 1:
            second_all, grad_upper = tie([second_all, grad_upper], went_r, went_l)
            pair = grad_half(flat(second_all), flat(grad_upper), where, False, 1, up_gift, pair)
            wide_grad = lax.psum_scatter(pair, "dp", scatter_dimension=1, axis_index_groups=sides, tiled=True)
            (right,) = tie([right], pair)
            (left,) = tie([left], pair)
    late = sorted({1, n - 1})
    early = [s for s in range(n) if s not in late]
    pick = lambda slots: sum(([start] if s == 0 else [lefts[s], rights[n - s]] for s in slots), [])
    held = dom_part(n, early, where, pick(early), output_weight, None)
    grad_masked, state_all = dom_part(n, late, where, pick(late), output_weight, held)
    dqkv = attend_back(
        where, query, keys, vals, grad_masked, docs_col, docs_row, heads_col, cos, sin
    )
    mixed = low(state + owned(ffn, right, left))

    def whole(part, widths):
        span = part.shape[1] // 2
        got = swap(lax.dynamic_slice_in_dim(part, (1 - side) * span, span, 1))
        return whole_rows(where, part, got, widths)

    tokens_of = lambda v: (flat(first_all), flat(state_all), flat(v), flat(masked), where)
    sent = block_term(dqkv, 1, weights, 1e6)
    (dqkv,) = tie([dqkv], sent, right, left)
    moved = hop(sent)
    gift = attn_grads(*tokens_of(dqkv))
    (dqkv,) = tie([dqkv], gift)
    terms = {1: sent, 2: block_term(dqkv, 2, weights, 1e6)}
    (dqkv,) = tie([dqkv], terms[2])
    attn_term = attn_grads(*tokens_of(dqkv), swap(gift))
    (late,) = tie([attn_term], wide_grad)
    attn_grad = lax.psum_scatter(late, "dp", scatter_dimension=0, axis_index_groups=sides, tiled=True)
    (moved,) = tie([moved], attn_term)
    sent2 = sent = join(where, moved, terms[2][None], 0, n + 1, True)
    moved = hop(sent)
    for s in range(3, n):
        (dqkv,) = tie([dqkv], sent)
        terms[s] = block_term(dqkv, s, weights, 1e6)
    (dqkv,) = tie([dqkv], terms[n - 1])
    terms[0] = block_term(dqkv, 0, weights, 1e6)
    held = tie([terms[s] for s in range(n)], sent2)
    sum_d = sum(jnp.sum(v.astype(F32), axis=0) for v in held)
    sum_da = sum(jnp.sum(v.astype(F32) * first_all[s].astype(F32), axis=0) for s, v in enumerate(held))
    first_shift_part = sum_d
    first_gain_part = (sum_da - first_shift * sum_d) / first_gain

    lead = (rank == 0).astype(F32)
    bucket_part = lead * jnp.sum(
        (width_bucket[0][:, None] == jnp.arange(4, dtype=jnp.int32)[None, :]).astype(F32), axis=0
    )
    head_part = lead * jnp.sum(
        (head_count[0][:, None] == jnp.arange(1, HEADS + 1, dtype=jnp.int32)[None, :]).astype(F32),
        axis=0,
    )
    small = jnp.concatenate(
        [
            first_gain_part,
            first_shift_part,
            second_gain_part,
            second_shift_part,
            bucket_part,
            head_part,
            jnp.zeros((128 - 4 - HEADS,), F32),
        ]
    )
    small = sum_over(small, "dp", [[(i, i ^ 1) for i in range(n_dp)]])
    wide = whole(wide_grad, [hidden] * 2)
    for s in range(3, n):
        if s == 3:
            moved, *wide = tie([moved, *wide])
        sent = join(where, moved, terms[s][None], 0, n + 1, True, 0, 64e9)
        moved = hop(sent)

    planes = tie([send(small, [(i, (i + m) % n) for i in range(n)]) for m in range(1, n)], sent)
    small = small + sum(planes)
    others = [
        lax.ppermute(small, "dp", [(i, (i + 2 * m) % n_dp) for i in range(n_dp)])
        for m in range(1, n_dp // 2)
    ]
    weight_grads = whole(attn_grad[None], [local] * 4)
    moved, *weight_grads = tie([moved, *weight_grads])
    input_grad = last_step(own, gain1, terms[0], moved, grad_state)
    small = small + sum(tie(others, input_grad))

    return (
        mixed[None],
        input_grad[None],
        small[:d],
        small[d : 2 * d],
        *weight_grads,
        small[2 * d : 3 * d],
        small[3 * d : 4 * d],
        wide[1],
        wide[0],
        small[4 * d : 4 * d + 4].astype(jnp.int32),
        small[4 * d + 4 : 4 * d + 4 + HEADS].astype(jnp.int32),
    )


def solution(mesh):
    token, seq, copy, col = P("dp", "mp", None), P("dp", None), P(), P(None, "mp")
    grad = P("dp", "mp")
    return jax.shard_map(
        functools.partial(per_device, mesh.shape["mp"], mesh.shape["dp"]),
        mesh=mesh,
        in_specs=(token, token, seq, seq, seq, copy, copy, col, col, col, col, copy, copy, col, col),
        out_specs=(token, token, copy, copy, grad, grad, grad, grad, copy, copy, grad, grad, copy, copy),
        check_vma=False,
    )
```

```python
import functools
import jax
import jax.numpy as jnp
from jax import lax
from jax.experimental import pallas as pl
from jax.experimental.pallas import tpu as pltpu
from jax.sharding import PartitionSpec as P

HEADS = 16
E = 128
FF = 8192
EPS = 1e-05
DOC_MAX = 512
LOG2E = 1.4426950408889634
F32 = jnp.float32
BF16 = jnp.bfloat16


def params(mib):
    return pltpu.CompilerParams(vmem_limit_bytes=mib << 20)


def cost(flops, nbytes, trans=0):
    return pl.CostEstimate(flops=int(flops), bytes_accessed=int(nbytes), transcendentals=int(trans))


def norm_forward(values, gain, shift):
    mean = jnp.mean(values, axis=-1, keepdims=True)
    cent = values - mean
    inverse = lax.rsqrt(jnp.mean(cent * cent, axis=-1, keepdims=True) + EPS)
    normed = cent * inverse
    return (normed * gain + shift, normed, inverse)


def norm_backward(grad_out, normed, inverse, gain):
    scaled = grad_out * gain
    return inverse * (
        scaled
        - jnp.mean(scaled, axis=-1, keepdims=True)
        - normed * jnp.mean(scaled * normed, axis=-1, keepdims=True)
    )


def rotary_tables(length):
    half = E // 2
    freq = 10000.0 ** (-(jnp.arange(half, dtype=F32) * 2.0 / E))
    angle = jnp.arange(length, dtype=F32)[:, None] * freq[None, :]
    cos, sin = jnp.cos(angle), jnp.sin(angle)
    return jnp.concatenate([cos, cos], axis=1), jnp.concatenate([-sin, sin], axis=1)


def dot_t(left, right):
    return lax.dot_general(left, right, (((1,), (1,)), ((), ())), preferred_element_type=F32)


def dot_n(left, right):
    return lax.dot_general(left, right, (((1,), (0,)), ((), ())), preferred_element_type=F32)


def outer(left, right):
    return lax.dot_general(left, right, (((0,), (0,)), ((), ())), preferred_element_type=F32)


def qkv_body(rank_ref, xa_ref, xb_ref, gain_ref, shift_ref, wq_ref, wk_ref, wv_ref, cos_ref, sin_ref, *rest):
    a_ref, q_ref, k_ref, v_ref = rest[-4:]

    @pl.when(pl.program_id(0) == 0)
    def _():
        x = jnp.concatenate([xa_ref[...], xb_ref[...]], axis=1).astype(F32)
        out, _, _ = norm_forward(x, gain_ref[...], shift_ref[...])
        a_ref[0] = out.astype(BF16)

    act = a_ref[0]
    cos, sin = cos_ref[0], sin_ref[0]
    v_ref[0] = dot_n(act, wv_ref[...]).astype(BF16)
    for w_ref, o_ref in ((wq_ref, q_ref), (wk_ref, k_ref)):
        lin = dot_n(act, w_ref[...])
        for j in range(lin.shape[1] // E):
            part = lin[:, j * E : (j + 1) * E]
            turned = part * cos + pltpu.roll(part, E // 2, 1) * sin
            o_ref[0, :, j * E : (j + 1) * E] = turned.astype(BF16)


def qkv_slot(slot, n, rank, xa, xb, gain, shift, wq, wk, wv, cos, sin, held):
    rows, half = xa.shape
    d = 2 * half
    local = wq.shape[1]
    cb = min(512, local)
    whole = lambda j, r: (0, 0)
    wspec = pl.BlockSpec((d, cb), lambda j, r: (0, j))
    tspec = pl.BlockSpec((1, rows, E), lambda j, r: (lax.rem(r[0] + slot, n), 0, 0))
    in_specs = [
        pl.BlockSpec((rows, half), whole),
        pl.BlockSpec((rows, half), whole),
        pl.BlockSpec((1, d), whole),
        pl.BlockSpec((1, d), whole),
        wspec,
        wspec,
        wspec,
        tspec,
        tspec,
    ]
    extra = [] if held is None else list(held)
    aliases = {} if held is None else {10 + i: i for i in range(4)}
    ospec = pl.BlockSpec((1, rows, cb), lambda j, r: (slot, 0, j))
    return pl.pallas_call(
        qkv_body,
        grid_spec=pltpu.PrefetchScalarGridSpec(
            num_scalar_prefetch=1,
            grid=(local // cb,),
            in_specs=in_specs + [pl.BlockSpec(memory_space=pl.ANY)] * len(extra),
            out_specs=[pl.BlockSpec((1, rows, d), lambda j, r: (slot, 0, 0)), ospec, ospec, ospec],
        ),
        out_shape=[jax.ShapeDtypeStruct((n, rows, d), BF16)]
        + [jax.ShapeDtypeStruct((n, rows, local), BF16)] * 3,
        input_output_aliases=aliases,
        compiler_params=params(56),
        cost_estimate=cost(6 * rows * d * local, 6 * d * local + 4 * rows * d),
        name="qkv_slot",
    )(rank, xa, xb, gain, shift, wq, wk, wv, cos, sin, *extra)


def by_reach(n, rows, edge_ref, block):
    for b in range(n):
        keys = list(range(first_key(b, rows), b + 1))
        if len(keys) <= 2:
            block(b, keys)
        else:
            far = edge_ref[n + b - 2] == edge_ref[b]
            pl.when(far)(functools.partial(block, b, keys))
            pl.when(jnp.logical_not(far))(functools.partial(block, b, keys[-2:]))


def first_key(block, rows):
    return max(0, block - (DOC_MAX - 1 + rows - 1) // rows)


def attend_body(rank_ref, edge_ref, q_ref, k_ref, v_ref, dcol_ref, drow_ref, hc_ref, o_ref):
    n, rows, _ = q_ref.shape
    rank = rank_ref[0]
    head = rank_ref[1] + pl.program_id(0)
    slot = lambda b: lax.rem(b + n - rank, n)
    factor = E ** (-0.5) * LOG2E
    low = lax.broadcasted_iota(jnp.int32, (rows, rows), 0) >= lax.broadcasted_iota(
        jnp.int32, (rows, rows), 1
    )

    def block(b, keys):
        q = q_ref[slot(b)]
        doc = dcol_ref[b]
        scores = []
        for c in keys:
            s = dot_t(q, k_ref[slot(c)])
            ok = doc == drow_ref[c]
            if c == b:
                ok = ok & low
            scores.append(jnp.where(ok, s, -1e30))
        top = scores[0]
        for s in scores[1:]:
            top = jnp.maximum(top, s)
        top = jnp.max(top, axis=1, keepdims=True)
        total = None
        out = None
        for c, s in zip(keys, scores):
            p = jnp.exp2((s - top) * factor)
            total = p if total is None else total + p
            o = dot_n(p.astype(BF16), v_ref[slot(c)])
            out = o if out is None else out + o
        total = jnp.sum(total, axis=1, keepdims=True)
        gate = jnp.where(hc_ref[b] > head, 1.0, 0.0)
        o_ref[slot(b)] = (out * (gate / total)).astype(BF16)

    by_reach(n, rows, edge_ref, block)


def attend(rank, edges, q, k, v, docs_col, docs_row, heads_col):
    n, rows, local = q.shape
    spec = pl.BlockSpec((n, rows, E), lambda h, r, e: (0, 0, h))
    col = pl.BlockSpec((n, rows, 1), lambda h, r, e: (0, 0, 0))
    row = pl.BlockSpec((n, 1, rows), lambda h, r, e: (0, 0, 0))
    t = n * rows
    return pl.pallas_call(
        attend_body,
        grid_spec=pltpu.PrefetchScalarGridSpec(
            num_scalar_prefetch=2,
            grid=(local // E,),
            in_specs=[spec, spec, spec, col, row, col],
            out_specs=spec,
        ),
        out_shape=jax.ShapeDtypeStruct((n, rows, local), BF16),
        compiler_params=params(62),
        cost_estimate=cost(4 * t * t * local, 8 * t * local, t * t * local // E),
        name="attend",
    )(rank, edges, q, k, v, docs_col, docs_row, heads_col)


def attend_back_body(
    rank_ref, edge_ref, q_ref, k_ref, v_ref, do_ref, dcol_ref, drow_ref, hc_ref, cos_ref, sin_ref, out_ref, dk_ref, dv_ref
):
    n, rows, _ = q_ref.shape
    rank = rank_ref[0]
    head = rank_ref[1] + pl.program_id(0)
    slot = lambda b: lax.rem(b + n - rank, n)
    scale = E ** (-0.5)
    factor = scale * LOG2E
    low = lax.broadcasted_iota(jnp.int32, (rows, rows), 0) <= lax.broadcasted_iota(
        jnp.int32, (rows, rows), 1
    )
    local = out_ref.shape[2] // 3
    lanes = lambda i: pl.ds(pl.multiple_of(i * local + pl.program_id(0) * E, E), E)
    dk_ref[...] = jnp.zeros_like(dk_ref)
    dv_ref[...] = jnp.zeros_like(dv_ref)

    def unrotate(w, b):
        w = w * scale
        return (w * cos_ref[b] - pltpu.roll(w, E // 2, 1) * sin_ref[b]).astype(BF16)

    def block(b, keys):
        q = q_ref[slot(b)]
        grad = jnp.where(hc_ref[b] > head, do_ref[slot(b)].astype(F32), 0.0).astype(BF16)
        scores = []
        for c in keys:
            s = dot_t(k_ref[slot(c)], q)
            ok = dcol_ref[c] == drow_ref[b]
            if c == b:
                ok = ok & low
            scores.append(jnp.where(ok, s, -1e30))
        top = scores[0]
        for s in scores[1:]:
            top = jnp.maximum(top, s)
        top = jnp.max(top, axis=0, keepdims=True)
        probs = [jnp.exp2((s - top) * factor) for s in scores]
        total = probs[0]
        for p in probs[1:]:
            total = total + p
        inv = 1.0 / jnp.sum(total, axis=0, keepdims=True)
        probs = [p * inv for p in probs]
        dprobs = [dot_t(v_ref[slot(c)], grad) for c in keys]
        delta = None
        for p, g in zip(probs, dprobs):
            delta = p * g if delta is None else delta + p * g
        delta = jnp.sum(delta, axis=0, keepdims=True)
        dq = None
        for c, p, g in zip(keys, probs, dprobs):
            ds = (p * (g - delta)).astype(BF16)
            dk_ref[c] += dot_n(ds, q)
            dv_ref[c] += dot_n(p.astype(BF16), grad)
            part = outer(ds, k_ref[slot(c)])
            dq = part if dq is None else dq + part
        out_ref[slot(b), :, lanes(0)] = unrotate(dq, b)

    by_reach(n, rows, edge_ref, block)
    for b in range(n):
        out_ref[slot(b), :, lanes(1)] = unrotate(dk_ref[b], b)
        out_ref[slot(b), :, lanes(2)] = dv_ref[b].astype(BF16)


def attend_back(rank, edges, q, k, v, do, docs_col, docs_row, heads_col, cos, sin):
    n, rows, local = q.shape
    spec = pl.BlockSpec((n, rows, E), lambda h, r, e: (0, 0, h))
    col = pl.BlockSpec((n, rows, 1), lambda h, r, e: (0, 0, 0))
    row = pl.BlockSpec((n, 1, rows), lambda h, r, e: (0, 0, 0))
    table = pl.BlockSpec((n, rows, E), lambda h, r, e: (0, 0, 0))
    t = n * rows
    return pl.pallas_call(
        attend_back_body,
        grid_spec=pltpu.PrefetchScalarGridSpec(
            num_scalar_prefetch=2,
            grid=(local // E,),
            in_specs=[spec, spec, spec, spec, col, row, col, table, table],
            out_specs=pl.BlockSpec((n, rows, 3 * local), lambda h, r, e: (0, 0, 0)),
            scratch_shapes=[pltpu.VMEM((n, rows, E), F32), pltpu.VMEM((n, rows, E), F32)],
        ),
        out_shape=jax.ShapeDtypeStruct((n, rows, 3 * local), BF16),
        compiler_params=params(24),
        cost_estimate=cost(116e9, 14 * t * local),
        name="attend_back",
    )(rank, edges, q, k, v, do, docs_col, docs_row, heads_col, cos, sin)


def mlp_body(slot, n, rank_ref, a_ref, gla_ref, glb_ref, gra_ref, grb_ref, up_ref, down_ref, bucket_ref, *rest):
    r_ref, du_ref, aa_ref, ga_ref = rest[-4:]
    rows, cb = a_ref.shape[0], up_ref.shape[1]

    @pl.when(pl.program_id(0) == 0)
    def _():
        aa_ref[0] = a_ref[...]
        ahead = rank_ref[0] + slot < n

        half = gla_ref.shape[1]

        def fill(first, second):
            ga_ref[0, :, :half] = first[...]
            ga_ref[0, :, half:] = second[...]

        pl.when(ahead)(functools.partial(fill, gla_ref, glb_ref))
        pl.when(jnp.logical_not(ahead))(functools.partial(fill, gra_ref, grb_ref))

    u = dot_n(a_ref[...], up_ref[...])
    dr = dot_n(ga_ref[0], down_ref[...]).astype(BF16).astype(F32)
    column = rank_ref[2] + pl.program_id(0) * cb + lax.broadcasted_iota(jnp.int32, (rows, cb), 1)
    lifted = jnp.where(column < (bucket_ref[0] + 1) * (FF // 4), jnp.maximum(u, 0.0), 0.0)
    r_ref[0] = (lifted * lifted).astype(BF16)
    du_ref[0] = (dr * (2.0 * lifted)).astype(BF16)


def mlp_slot(slot, n, rank, act, grads, up, down, bucket_col, held):
    rows, d = act.shape
    hidden = up.shape[1]
    cb = min(512, hidden)
    whole = lambda j, r: (0, 0)
    wspec = pl.BlockSpec((d, cb), lambda j, r: (0, j))
    extra = [] if held is None else list(held)
    aliases = {} if held is None else {9 + i: i for i in range(4)}
    ospec = pl.BlockSpec((1, rows, cb), lambda j, r: (slot, 0, j))
    aspec = pl.BlockSpec((1, rows, d), lambda j, r: (slot, 0, 0))
    return pl.pallas_call(
        functools.partial(mlp_body, slot, n),
        grid_spec=pltpu.PrefetchScalarGridSpec(
            num_scalar_prefetch=1,
            grid=(hidden // cb,),
            in_specs=[
                pl.BlockSpec((rows, d), whole),
            ]
            + [pl.BlockSpec((rows, d // 2), whole)] * 4
            + [
                wspec,
                wspec,
                pl.BlockSpec((1, rows, 1), lambda j, r: (lax.rem(r[0] + slot, n), 0, 0)),
            ]
            + [pl.BlockSpec(memory_space=pl.ANY)] * len(extra),
            out_specs=[ospec, ospec, aspec, aspec],
        ),
        out_shape=[jax.ShapeDtypeStruct((n, rows, hidden), BF16)] * 2
        + [jax.ShapeDtypeStruct((n, rows, d), BF16)] * 2,
        input_output_aliases=aliases,
        compiler_params=params(28),
        cost_estimate=cost(4 * rows * d * hidden, 4 * d * hidden + 4 * rows * (d + hidden)),
        name="mlp_slot",
    )(rank, act, *grads, up, down, bucket_col, *extra)


def dom_body(n, slots, rank_ref, slot_ref, *refs):
    dom_ref, all_ref = refs[-2:]
    count = sum(1 if s == 0 else 2 for s in slots)
    flows, w_ref = list(refs[:count]), refs[count]

    def fill(ref):
        all_ref[0] = ref[...]

    for i, s in enumerate(slots):
        here = pl.program_id(0) == i
        if s == 0:
            pl.when(here)(functools.partial(fill, flows[0]))
            flows = flows[1:]
        else:
            ahead = rank_ref[0] + s < n
            pl.when(here & ahead)(functools.partial(fill, flows[0]))
            pl.when(here & jnp.logical_not(ahead))(functools.partial(fill, flows[1]))
            flows = flows[2:]
    dom_ref[0] = dot_n(all_ref[0], w_ref[...]).astype(BF16)


def dom_part(n, slots, rank, flows, weight, held):
    rows, d = flows[0].shape
    local = weight.shape[1]
    whole = lambda i, r, s: (0, 0)
    extra = [] if held is None else list(held)
    at = 2 + len(flows) + 1
    return pl.pallas_call(
        functools.partial(dom_body, n, slots),
        grid_spec=pltpu.PrefetchScalarGridSpec(
            num_scalar_prefetch=2,
            grid=(len(slots),),
            in_specs=[pl.BlockSpec((rows, d), whole)] * len(flows)
            + [pl.BlockSpec((d, local), whole)]
            + [pl.BlockSpec(memory_space=pl.ANY)] * len(extra),
            out_specs=[
                pl.BlockSpec((1, rows, local), lambda i, r, s: (s[i], 0, 0)),
                pl.BlockSpec((1, rows, d), lambda i, r, s: (s[i], 0, 0)),
            ],
        ),
        out_shape=[
            jax.ShapeDtypeStruct((n, rows, local), BF16),
            jax.ShapeDtypeStruct((n, rows, d), BF16),
        ],
        input_output_aliases={at + i: i for i in range(len(extra))},
        compiler_params=params(24),
        cost_estimate=cost(
            2 * len(slots) * rows * d * local, 2 * d * local + 6 * len(slots) * rows * d
        ),
        name="dom_part",
    )(rank, jnp.asarray(slots, jnp.int32), *flows, weight, *extra)


def grad_body(has_sum, rank_ref, lhs_ref, rhs_ref, *rest):
    out = outer(lhs_ref[...], rhs_ref[...])
    if has_sum:
        rest[-1][0] = (out + rest[0][...].astype(F32)).astype(BF16)
    else:
        rest[-1][...] = out.astype(BF16)


def grad_half(lhs, rhs, rank, partner, which=0, moved=None, held=None):
    t, d = lhs.shape
    half = rhs.shape[1] // 2
    tile = min(512, d)
    col = (lambda r: 1 - r[3]) if partner else (lambda r: r[3])
    specs = [
        pl.BlockSpec((t, tile), lambda j, r: (0, j)),
        pl.BlockSpec((t, half), lambda j, r: (0, col(r))),
    ]
    args = [lhs, rhs]
    aliases = {}
    if partner:
        ospec = pl.BlockSpec((tile, half), lambda j, r: (j, 0))
        oshape = (d, half)
    else:
        specs.append(pl.BlockSpec((tile, half), lambda j, r: (j, 0)))
        args.append(moved)
        ospec = pl.BlockSpec((1, tile, half), lambda j, r: (which, j, 0))
        oshape = (2, d, half)
        if held is not None:
            specs.append(pl.BlockSpec(memory_space=pl.ANY))
            args.append(held)
            aliases = {4: 0}
    return pl.pallas_call(
        functools.partial(grad_body, not partner),
        grid_spec=pltpu.PrefetchScalarGridSpec(
            num_scalar_prefetch=1, grid=(d // tile,), in_specs=specs, out_specs=ospec
        ),
        out_shape=jax.ShapeDtypeStruct(oshape, BF16),
        input_output_aliases=aliases,
        compiler_params=params(20),
        cost_estimate=cost(1e6, 1e6),
        name="grad_half",
    )(rank, *args)


def attn_grad_body(partner, rank_ref, a_ref, s_ref, one_ref, key_ref, om_ref, *rest):
    out_ref = rest[-1]
    local = om_ref.shape[1]
    second = rank_ref[3] == (0 if partner else 1)
    act = a_ref[...]

    def put(cols, value):
        if not partner:
            value = value + rest[0][:, cols].astype(F32)
        out_ref[:, cols] = value.astype(BF16)

    put(slice(0, local), outer(act, one_ref[...]))

    @pl.when(second)
    def _():
        put(slice(local, 2 * local), outer(s_ref[...], om_ref[...]))

    @pl.when(jnp.logical_not(second))
    def _():
        put(slice(local, 2 * local), outer(act, key_ref[...]))


def attn_grads(act, states, dqkv, om, rank, moved=None):
    t, d = act.shape
    local = om.shape[1]
    tile = min(512, d)
    partner = moved is None
    pos = (lambda r: 1 - r[3]) if partner else (lambda r: r[3])
    col = pl.BlockSpec((t, tile), lambda j, r: (0, j))
    out = pl.BlockSpec((tile, 2 * local), lambda j, r: (j, 0))
    return pl.pallas_call(
        functools.partial(attn_grad_body, partner),
        grid_spec=pltpu.PrefetchScalarGridSpec(
            num_scalar_prefetch=1,
            grid=(d // tile,),
            in_specs=[
                col,
                pl.BlockSpec((t, tile), lambda j, r: (0, j * pos(r))),
                pl.BlockSpec((t, local), lambda j, r: (0, 2 * pos(r))),
                pl.BlockSpec((t, local), lambda j, r: (0, 1)),
                pl.BlockSpec((t, local), lambda j, r: (0, 0)),
            ]
            + ([] if partner else [out]),
            out_specs=out,
        ),
        out_shape=jax.ShapeDtypeStruct((d, 2 * local), BF16),
        compiler_params=params(28 if partner else 50),
        cost_estimate=cost(4e9 if partner else 1e6, 1e6),
        name="attn_grads",
    )(rank, act, states, dqkv, dqkv, om, *([] if partner else [moved]))


def term_body(x_ref, w_ref, *rest):
    out = dot_t(x_ref[0], w_ref[...])
    if len(rest) > 1:
        out = out + rest[0][...].astype(F32)
    rest[-1][...] = out.astype(BF16)


def block_term(acts, slot, weight, flops, moved=None, mib=16):
    _, rows, k = acts.shape
    d = weight.shape[0]
    tile = min(512, d)
    out = pl.BlockSpec((rows, tile), lambda j: (0, j))
    return pl.pallas_call(
        term_body,
        grid=(d // tile,),
        in_specs=[
            pl.BlockSpec((1, rows, k), lambda j: (slot, 0, 0)),
            pl.BlockSpec((tile, k), lambda j: (j, 0)),
        ]
        + ([] if moved is None else [out]),
        out_specs=out,
        out_shape=jax.ShapeDtypeStruct((rows, d), BF16),
        compiler_params=params(mib),
        cost_estimate=cost(flops, flops / 256),
        name="block_term",
    )(acts, weight, *([] if moved is None else [moved]))


def join_body(slot, first, rank_ref, moved_ref, term_ref, out_ref):
    adds = rank_ref[0] < first if slot >= 0 else rank_ref[0] >= first

    @pl.when(adds)
    def _():
        out_ref[...] = (moved_ref[...].astype(F32) + term_ref[0].astype(F32)).astype(BF16)

    @pl.when(jnp.logical_not(adds))
    def _():
        out_ref[...] = moved_ref[...]


def join(rank, moved, terms, slot, first, right, part=0, flops=1e6):
    rows, d = moved.shape
    tile = min(128, rows)
    row = pl.BlockSpec((tile, d), lambda i, r: (i, 0))
    return pl.pallas_call(
        functools.partial(join_body, 0 if right else -1, first),
        grid_spec=pltpu.PrefetchScalarGridSpec(
            num_scalar_prefetch=1,
            grid=(rows // tile,),
            in_specs=[row, pl.BlockSpec((1, tile, d), lambda i, r: (slot, i, part))],
            out_specs=row,
        ),
        out_shape=jax.ShapeDtypeStruct((rows, d), BF16),
        compiler_params=params(8),
        cost_estimate=cost(flops, 1e6),
        name="join",
    )(rank, moved, terms)


def last_body(x_ref, gain_ref, term_ref, moved_ref, state_ref, out_ref):
    gain = gain_ref[...]
    _, normed, inverse = norm_forward(x_ref[...].astype(F32), gain, gain)
    back = norm_backward(term_ref[...].astype(F32) + moved_ref[...].astype(F32), normed, inverse, gain)
    out_ref[...] = (state_ref[...] + back).astype(BF16)


def last_step(x, gain, term, moved, state):
    rows, d = x.shape
    tile = min(64, rows)
    row = lambda w: pl.BlockSpec((tile, w), lambda i: (i, 0))
    return pl.pallas_call(
        last_body,
        grid=(rows // tile,),
        in_specs=[row(d), pl.BlockSpec((1, d), lambda i: (0, 0)), row(d), row(d), row(d)],
        out_specs=row(d),
        out_shape=jax.ShapeDtypeStruct((rows, d), BF16),
        compiler_params=params(12),
        cost_estimate=cost(1e6, 12 * rows * d),
        name="last_step",
    )(x, gain, term, moved, state)


def rows_body(rank_ref, mine_ref, got_ref, *outs):
    parts, _, half = got_ref.shape
    width = outs[0].shape[1]
    first = rank_ref[3] == 0

    def put(low_ref, high_ref):
        if width > half:
            for p in range(parts):
                outs[p][:, :half] = low_ref[p].astype(F32)
                outs[p][:, half:] = high_ref[p].astype(F32)
        else:
            for o, (ref, at) in zip(outs, ((low_ref, 0), (low_ref, width), (high_ref, 0), (high_ref, width))):
                o[...] = ref[0, :, at : at + width].astype(F32)

    pl.when(first)(functools.partial(put, mine_ref, got_ref))
    pl.when(jnp.logical_not(first))(functools.partial(put, got_ref, mine_ref))


def whole_rows(rank, part, got, widths):
    parts, span, half = got.shape
    tile = min(64, span)
    steps = span // tile
    return pl.pallas_call(
        rows_body,
        grid_spec=pltpu.PrefetchScalarGridSpec(
            num_scalar_prefetch=1,
            grid=(steps,),
            in_specs=[
                pl.BlockSpec((parts, tile, half), lambda i, r: (0, r[3] * steps + i, 0)),
                pl.BlockSpec((parts, tile, half), lambda i, r: (0, i, 0)),
            ],
            out_specs=[pl.BlockSpec((tile, w), lambda i, r: (i, 0)) for w in widths],
        ),
        out_shape=[jax.ShapeDtypeStruct((span, w), F32) for w in widths],
        compiler_params=params(16),
        cost_estimate=cost(1e6, 1e6),
        name="whole_rows",
    )(rank, part, got)


def tie(values, *others):
    values = tuple(values)
    return lax.optimization_barrier(values + others)[: len(values)]


def sum_over(vec, axis, moves):
    return sum((lax.ppermute(vec, axis, pairs) for pairs in moves), vec)


def per_device(
    n,
    n_dp,
    tokens,
    mixed_grad,
    doc_ids,
    head_count,
    width_bucket,
    first_gain,
    first_shift,
    query_weight,
    key_weight,
    value_weight,
    output_weight,
    second_gain,
    second_shift,
    up_weight,
    down_weight,
):
    rank = lax.axis_index("mp")
    rows, d = tokens.shape[1:]
    half = d // 2
    local = query_weight.shape[1]
    local_heads = local // E
    hidden = up_weight.shape[1]
    length = n * rows
    own = tokens[0]
    send = lambda v, pairs: lax.ppermute(v, "mp", pairs)
    ring = [(i, (i - 1) % n) for i in range(n)]
    hop = lambda v: send(v, ring)
    right_line = [(i, i + 1) for i in range(n - 1)]
    left_line = [(i + 1, i) for i in range(n - 1)]

    def tick(k, right, left, terms):
        if k:
            right = join(where, right, terms, n - k, k, True, 0, 1e9)
            left = join(where, left, terms, k, n - k, False, 0, 1e6)
        return send(right, right_line), send(left, left_line), right, left

    def owned(terms, right, left):
        return terms[0].astype(F32) + right.astype(F32) + left.astype(F32)

    low = lambda v: v.astype(BF16)
    flat = lambda v: v.reshape(length, v.shape[-1])
    add = lambda t, moved: (t.astype(F32) + moved.astype(F32)).astype(BF16)

    side = lax.rem(lax.axis_index("dp"), 2)
    where = jnp.stack([rank, rank * local_heads, rank * hidden, side]).astype(jnp.int32)
    swap = lambda v: lax.ppermute(v, "dp", [(i, i ^ 1) for i in range(n_dp)])
    sides = [list(range(c, n_dp, 2)) for c in range(2)]
    docs_col = doc_ids.reshape(n, rows, 1)
    edges = jnp.concatenate([doc_ids[0, ::rows], doc_ids[0, rows - 1 :: rows]])
    docs_row = doc_ids.reshape(n, 1, rows)
    heads_col = head_count.reshape(n, rows, 1)
    bucket_col = width_bucket.reshape(n, rows, 1)
    cos, sin = (t.reshape(n, rows, E) for t in rotary_tables(length))
    gain1, shift1 = first_gain[None], first_shift[None]
    gain2, shift2 = second_gain[None], second_shift[None]

    held, block = None, [own[:, :half], own[:, half:]]
    for s in range(n):
        after = [None, None]
        for p in range(2):
            if s >= 1:
                block[p], *held = tie([block[p]] + list(held))
            if s < n - 1:
                after[p] = hop(block[p])
        held = qkv_slot(
            s, n, where, *block, gain1, shift1, query_weight, key_weight, value_weight, cos, sin, held
        )
        if s < n - 1:
            block = after
    first_all, query, keys, vals = held

    grad_own = mixed_grad[0]
    (own_grad,) = tie([grad_own], block[0])
    right = [own_grad[:, :half], own_grad[:, half:]]
    left = list(right)
    grads_r, grads_l = [list(right)], [list(left)]

    def half_tick(k):
        for p in range(2):
            if k:
                right[p] = join(where, right[p], terms, n - k, k, True, p)
                left[p] = join(where, left[p], terms, k, n - k, False, p)
            right[p], left[p] = send(right[p], right_line), send(left[p], left_line)

    half_tick(0)
    masked = attend(where, edges, query, keys, vals, docs_col, docs_row, heads_col)
    terms = low(dot_t(flat(masked), output_weight)).reshape(n, rows, d)
    for k in range(1, n):
        grads_r.append(list(right))
        grads_l.append(list(left))
        half_tick(k)
    right, left = (jnp.concatenate(v, axis=1) for v in (right, left))
    attn = owned(terms, right, left)
    x_rows = own.astype(F32)
    state = x_rows + attn
    second_out, normed_two, inverse_two = norm_forward(state, gain2, shift2)

    weights = jnp.concatenate([query_weight, key_weight, value_weight], axis=1)
    held, moved = None, None
    (block,) = tie([low(second_out)], weights)
    for s in range(n):
        if s >= 1:
            block, *held = tie([block] + list(held), sent)
        after = hop(block) if s < n - 1 else None
        held = mlp_slot(
            s, n, where, block, grads_l[s] + grads_r[n - s if s else 0], up_weight, down_weight, bucket_col, held
        )
        if s >= 1:
            fused = moved if s == n - 1 and s > 1 else None
            sent = block_term(held[1], s, up_weight, 2 * rows * d * hidden, fused, 16)
            if s > 1 and fused is None:
                sent = add(sent, moved)
            moved = hop(sent)
        else:
            sent = term0 = block_term(held[1], 0, up_weight, 2 * rows * d * hidden, None, 16)
        block = after
    active, grad_upper, second_all, grad_all = held
    grad_all, active, second_all, grad_upper = tie([grad_all, active, second_all, grad_upper], sent)
    gifts = [
        grad_half(flat(grad_all), flat(active), where, True),
        grad_half(flat(second_all), flat(grad_upper), where, True),
    ]
    (moved,) = tie([moved], *gifts)
    down_gift, up_gift = (swap(v) for v in gifts)
    grad_second = term0.astype(F32) + moved.astype(F32)
    back_two = norm_backward(grad_second, normed_two, inverse_two, gain2)
    second_gain_part = jnp.sum(grad_second * normed_two, axis=0)
    second_shift_part = jnp.sum(grad_second, axis=0)
    grad_state = grad_own.astype(F32) + back_two

    start = low(grad_state)
    grad_all, active, start = tie([grad_all, active, start])
    right = left = start
    rights, lefts = [start], [start]
    right, left, _, _ = tick(0, right, left, None)
    ffn = low(dot_t(flat(active), down_weight)).reshape(n, rows, d)
    pair = grad_half(flat(grad_all), flat(active), where, False, 0, down_gift)
    (right,) = tie([right], pair)
    (left,) = tie([left], pair)
    for k in range(1, n):
        rights.append(right)
        lefts.append(left)
        right, left, went_r, went_l = tick(k, right, left, ffn)
        if k == 1:
            second_all, grad_upper = tie([second_all, grad_upper], went_r, went_l)
            pair = grad_half(flat(second_all), flat(grad_upper), where, False, 1, up_gift, pair)
            wide_grad = lax.psum_scatter(pair, "dp", scatter_dimension=1, axis_index_groups=sides, tiled=True)
            (right,) = tie([right], pair)
            (left,) = tie([left], pair)
    late = sorted({1, n - 1})
    early = [s for s in range(n) if s not in late]
    pick = lambda slots: sum(([start] if s == 0 else [lefts[s], rights[n - s]] for s in slots), [])
    held = dom_part(n, early, where, pick(early), output_weight, None)
    grad_masked, state_all = dom_part(n, late, where, pick(late), output_weight, held)
    dqkv = attend_back(
        where, edges, query, keys, vals, grad_masked, docs_col, docs_row, heads_col, cos, sin
    )
    mixed = low(state + owned(ffn, right, left))

    def whole(part, widths):
        span = part.shape[1] // 2
        got = swap(lax.dynamic_slice_in_dim(part, (1 - side) * span, span, 1))
        return whole_rows(where, part, got, widths)

    tokens_of = lambda v: (flat(first_all), flat(state_all), flat(v), flat(masked), where)
    sent = block_term(dqkv, 1, weights, 1e6)
    (dqkv,) = tie([dqkv], sent, right, left)
    moved = hop(sent)
    gift = attn_grads(*tokens_of(dqkv))
    (dqkv,) = tie([dqkv], gift)
    terms = {1: sent, 2: block_term(dqkv, 2, weights, 1e6)}
    (dqkv,) = tie([dqkv], terms[2])
    attn_term = attn_grads(*tokens_of(dqkv), swap(gift))
    (late,) = tie([attn_term], wide_grad)
    attn_grad = lax.psum_scatter(late, "dp", scatter_dimension=0, axis_index_groups=sides, tiled=True)
    (moved,) = tie([moved], attn_term)
    sent2 = sent = join(where, moved, terms[2][None], 0, n + 1, True)
    moved = hop(sent)
    for s in range(3, n):
        (dqkv,) = tie([dqkv], sent)
        terms[s] = block_term(dqkv, s, weights, 1e6)
    (dqkv,) = tie([dqkv], terms[n - 1])
    terms[0] = block_term(dqkv, 0, weights, 1e6)
    held = tie([terms[s] for s in range(n)], sent2)
    sum_d = sum(jnp.sum(v.astype(F32), axis=0) for v in held)
    sum_da = sum(jnp.sum(v.astype(F32) * first_all[s].astype(F32), axis=0) for s, v in enumerate(held))
    first_shift_part = sum_d
    first_gain_part = (sum_da - first_shift * sum_d) / first_gain

    lead = (rank == 0).astype(F32)
    bucket_part = lead * jnp.sum(
        (width_bucket[0][:, None] == jnp.arange(4, dtype=jnp.int32)[None, :]).astype(F32), axis=0
    )
    head_part = lead * jnp.sum(
        (head_count[0][:, None] == jnp.arange(1, HEADS + 1, dtype=jnp.int32)[None, :]).astype(F32),
        axis=0,
    )
    small = jnp.concatenate(
        [
            first_gain_part,
            first_shift_part,
            second_gain_part,
            second_shift_part,
            bucket_part,
            head_part,
            jnp.zeros((128 - 4 - HEADS,), F32),
        ]
    )
    small = sum_over(small, "dp", [[(i, i ^ 1) for i in range(n_dp)]])
    wide = whole(wide_grad, [hidden] * 2)
    for s in range(3, n):
        if s == 3:
            moved, *wide = tie([moved, *wide])
        sent = join(where, moved, terms[s][None], 0, n + 1, True, 0, 64e9)
        moved = hop(sent)

    planes = tie([send(small, [(i, (i + m) % n) for i in range(n)]) for m in range(1, n)], sent)
    small = small + sum(planes)
    others = [
        lax.ppermute(small, "dp", [(i, (i + 2 * m) % n_dp) for i in range(n_dp)])
        for m in range(1, n_dp // 2)
    ]
    weight_grads = whole(attn_grad[None], [local] * 4)
    moved, *weight_grads = tie([moved, *weight_grads])
    input_grad = last_step(own, gain1, terms[0], moved, grad_state)
    small = small + sum(tie(others, input_grad))

    return (
        mixed[None],
        input_grad[None],
        small[:d],
        small[d : 2 * d],
        *weight_grads,
        small[2 * d : 3 * d],
        small[3 * d : 4 * d],
        wide[1],
        wide[0],
        small[4 * d : 4 * d + 4].astype(jnp.int32),
        small[4 * d + 4 : 4 * d + 4 + HEADS].astype(jnp.int32),
    )


def solution(mesh):
    token, seq, copy, col = P("dp", "mp", None), P("dp", None), P(), P(None, "mp")
    grad = P("dp", "mp")
    return jax.shard_map(
        functools.partial(per_device, mesh.shape["mp"], mesh.shape["dp"]),
        mesh=mesh,
        in_specs=(token, token, seq, seq, seq, copy, copy, col, col, col, col, copy, copy, col, col),
        out_specs=(token, token, copy, copy, grad, grad, grad, grad, copy, copy, grad, grad, copy, copy),
        check_vma=False,
    )
```

```python
import functools
import jax
import jax.numpy as jnp
from jax import lax
from jax.experimental import pallas as pl
from jax.experimental.pallas import tpu as pltpu
from jax.sharding import PartitionSpec as P

HEADS = 16
E = 128
FF = 8192
EPS = 1e-05
DOC_MAX = 512
LOG2E = 1.4426950408889634
F32 = jnp.float32
BF16 = jnp.bfloat16


def params(mib):
    return pltpu.CompilerParams(vmem_limit_bytes=mib << 20)


def cost(flops, nbytes, trans=0):
    return pl.CostEstimate(flops=int(flops), bytes_accessed=int(nbytes), transcendentals=int(trans))


def norm_forward(values, gain, shift):
    mean = jnp.mean(values, axis=-1, keepdims=True)
    cent = values - mean
    inverse = lax.rsqrt(jnp.mean(cent * cent, axis=-1, keepdims=True) + EPS)
    normed = cent * inverse
    return (normed * gain + shift, normed, inverse)


def norm_backward(grad_out, normed, inverse, gain):
    scaled = grad_out * gain
    return inverse * (
        scaled
        - jnp.mean(scaled, axis=-1, keepdims=True)
        - normed * jnp.mean(scaled * normed, axis=-1, keepdims=True)
    )


def rotary_tables(length):
    half = E // 2
    freq = 10000.0 ** (-(jnp.arange(half, dtype=F32) * 2.0 / E))
    angle = jnp.arange(length, dtype=F32)[:, None] * freq[None, :]
    cos, sin = jnp.cos(angle), jnp.sin(angle)
    return jnp.concatenate([cos, cos], axis=1), jnp.concatenate([-sin, sin], axis=1)


def dot_t(left, right):
    return lax.dot_general(left, right, (((1,), (1,)), ((), ())), preferred_element_type=F32)


def dot_n(left, right):
    return lax.dot_general(left, right, (((1,), (0,)), ((), ())), preferred_element_type=F32)


def outer(left, right):
    return lax.dot_general(left, right, (((0,), (0,)), ((), ())), preferred_element_type=F32)


def qkv_body(rank_ref, xa_ref, xb_ref, gain_ref, shift_ref, wq_ref, wk_ref, wv_ref, cos_ref, sin_ref, *rest):
    a_ref, q_ref, k_ref, v_ref = rest[-4:]

    @pl.when(pl.program_id(0) == 0)
    def _():
        x = jnp.concatenate([xa_ref[...], xb_ref[...]], axis=1).astype(F32)
        out, _, _ = norm_forward(x, gain_ref[...], shift_ref[...])
        a_ref[0] = out.astype(BF16)

    act = a_ref[0]
    cos, sin = cos_ref[0], sin_ref[0]
    v_ref[0] = dot_n(act, wv_ref[...]).astype(BF16)
    for w_ref, o_ref in ((wq_ref, q_ref), (wk_ref, k_ref)):
        lin = dot_n(act, w_ref[...])
        for j in range(lin.shape[1] // E):
            part = lin[:, j * E : (j + 1) * E]
            turned = part * cos + pltpu.roll(part, E // 2, 1) * sin
            o_ref[0, :, j * E : (j + 1) * E] = turned.astype(BF16)


def qkv_slot(slot, n, rank, xa, xb, gain, shift, wq, wk, wv, cos, sin, held):
    rows, half = xa.shape
    d = 2 * half
    local = wq.shape[1]
    cb = min(512, local)
    whole = lambda j, r: (0, 0)
    wspec = pl.BlockSpec((d, cb), lambda j, r: (0, j))
    tspec = pl.BlockSpec((1, rows, E), lambda j, r: (lax.rem(r[0] + slot, n), 0, 0))
    in_specs = [
        pl.BlockSpec((rows, half), whole),
        pl.BlockSpec((rows, half), whole),
        pl.BlockSpec((1, d), whole),
        pl.BlockSpec((1, d), whole),
        wspec,
        wspec,
        wspec,
        tspec,
        tspec,
    ]
    extra = [] if held is None else list(held)
    aliases = {} if held is None else {10 + i: i for i in range(4)}
    ospec = pl.BlockSpec((1, rows, cb), lambda j, r: (slot, 0, j))
    return pl.pallas_call(
        qkv_body,
        grid_spec=pltpu.PrefetchScalarGridSpec(
            num_scalar_prefetch=1,
            grid=(local // cb,),
            in_specs=in_specs + [pl.BlockSpec(memory_space=pl.ANY)] * len(extra),
            out_specs=[pl.BlockSpec((1, rows, d), lambda j, r: (slot, 0, 0)), ospec, ospec, ospec],
        ),
        out_shape=[jax.ShapeDtypeStruct((n, rows, d), BF16)]
        + [jax.ShapeDtypeStruct((n, rows, local), BF16)] * 3,
        input_output_aliases=aliases,
        compiler_params=params(56),
        cost_estimate=cost(6 * rows * d * local, 6 * d * local + 4 * rows * d),
        name="qkv_slot",
    )(rank, xa, xb, gain, shift, wq, wk, wv, cos, sin, *extra)


def first_key(block, rows):
    return max(0, block - (DOC_MAX - 1 + rows - 1) // rows)


def attend_body(rank_ref, q_ref, k_ref, v_ref, dcol_ref, drow_ref, hc_ref, o_ref):
    n, rows, _ = q_ref.shape
    rank = rank_ref[0]
    head = rank_ref[1] + pl.program_id(0)
    slot = lambda b: lax.rem(b + n - rank, n)
    factor = E ** (-0.5) * LOG2E
    low = lax.broadcasted_iota(jnp.int32, (rows, rows), 0) >= lax.broadcasted_iota(
        jnp.int32, (rows, rows), 1
    )
    for b in range(n):
        q = q_ref[slot(b)]
        doc = dcol_ref[b]
        keys = range(first_key(b, rows), b + 1)
        scores = []
        for c in keys:
            s = dot_t(q, k_ref[slot(c)])
            ok = doc == drow_ref[c]
            if c == b:
                ok = ok & low
            scores.append(jnp.where(ok, s, -1e30))
        top = scores[0]
        for s in scores[1:]:
            top = jnp.maximum(top, s)
        top = jnp.max(top, axis=1, keepdims=True)
        total = None
        out = None
        for c, s in zip(keys, scores):
            p = jnp.exp2((s - top) * factor)
            total = p if total is None else total + p
            o = dot_n(p.astype(BF16), v_ref[slot(c)])
            out = o if out is None else out + o
        total = jnp.sum(total, axis=1, keepdims=True)
        gate = jnp.where(hc_ref[b] > head, 1.0, 0.0)
        o_ref[slot(b)] = (out * (gate / total)).astype(BF16)


def attend(rank, q, k, v, docs_col, docs_row, heads_col):
    n, rows, local = q.shape
    spec = pl.BlockSpec((n, rows, E), lambda h, r: (0, 0, h))
    col = pl.BlockSpec((n, rows, 1), lambda h, r: (0, 0, 0))
    row = pl.BlockSpec((n, 1, rows), lambda h, r: (0, 0, 0))
    t = n * rows
    return pl.pallas_call(
        attend_body,
        grid_spec=pltpu.PrefetchScalarGridSpec(
            num_scalar_prefetch=1,
            grid=(local // E,),
            in_specs=[spec, spec, spec, col, row, col],
            out_specs=spec,
        ),
        out_shape=jax.ShapeDtypeStruct((n, rows, local), BF16),
        compiler_params=params(62),
        cost_estimate=cost(4 * t * t * local, 8 * t * local, t * t * local // E),
        name="attend",
    )(rank, q, k, v, docs_col, docs_row, heads_col)


def attend_back_body(
    rank_ref, q_ref, k_ref, v_ref, do_ref, dcol_ref, drow_ref, hc_ref, cos_ref, sin_ref, out_ref, dk_ref, dv_ref
):
    n, rows, _ = q_ref.shape
    rank = rank_ref[0]
    head = rank_ref[1] + pl.program_id(0)
    slot = lambda b: lax.rem(b + n - rank, n)
    scale = E ** (-0.5)
    factor = scale * LOG2E
    low = lax.broadcasted_iota(jnp.int32, (rows, rows), 0) <= lax.broadcasted_iota(
        jnp.int32, (rows, rows), 1
    )
    local = out_ref.shape[2] // 3
    lanes = lambda i: pl.ds(pl.multiple_of(i * local + pl.program_id(0) * E, E), E)
    dk_ref[...] = jnp.zeros_like(dk_ref)
    dv_ref[...] = jnp.zeros_like(dv_ref)

    def unrotate(w, b):
        w = w * scale
        return (w * cos_ref[b] - pltpu.roll(w, E // 2, 1) * sin_ref[b]).astype(BF16)

    for b in range(n):
        q = q_ref[slot(b)]
        grad = jnp.where(hc_ref[b] > head, do_ref[slot(b)].astype(F32), 0.0).astype(BF16)
        keys = range(first_key(b, rows), b + 1)
        scores = []
        for c in keys:
            s = dot_t(k_ref[slot(c)], q)
            ok = dcol_ref[c] == drow_ref[b]
            if c == b:
                ok = ok & low
            scores.append(jnp.where(ok, s, -1e30))
        top = scores[0]
        for s in scores[1:]:
            top = jnp.maximum(top, s)
        top = jnp.max(top, axis=0, keepdims=True)
        probs = [jnp.exp2((s - top) * factor) for s in scores]
        total = probs[0]
        for p in probs[1:]:
            total = total + p
        inv = 1.0 / jnp.sum(total, axis=0, keepdims=True)
        probs = [p * inv for p in probs]
        dprobs = [dot_t(v_ref[slot(c)], grad) for c in keys]
        delta = None
        for p, g in zip(probs, dprobs):
            delta = p * g if delta is None else delta + p * g
        delta = jnp.sum(delta, axis=0, keepdims=True)
        dq = None
        for c, p, g in zip(keys, probs, dprobs):
            ds = (p * (g - delta)).astype(BF16)
            dk_ref[c] += dot_n(ds, q)
            dv_ref[c] += dot_n(p.astype(BF16), grad)
            part = outer(ds, k_ref[slot(c)])
            dq = part if dq is None else dq + part
        out_ref[slot(b), :, lanes(0)] = unrotate(dq, b)
    for b in range(n):
        out_ref[slot(b), :, lanes(1)] = unrotate(dk_ref[b], b)
        out_ref[slot(b), :, lanes(2)] = dv_ref[b].astype(BF16)


def attend_back(rank, q, k, v, do, docs_col, docs_row, heads_col, cos, sin):
    n, rows, local = q.shape
    spec = pl.BlockSpec((n, rows, E), lambda h, r: (0, 0, h))
    col = pl.BlockSpec((n, rows, 1), lambda h, r: (0, 0, 0))
    row = pl.BlockSpec((n, 1, rows), lambda h, r: (0, 0, 0))
    table = pl.BlockSpec((n, rows, E), lambda h, r: (0, 0, 0))
    t = n * rows
    return pl.pallas_call(
        attend_back_body,
        grid_spec=pltpu.PrefetchScalarGridSpec(
            num_scalar_prefetch=1,
            grid=(local // E,),
            in_specs=[spec, spec, spec, spec, col, row, col, table, table],
            out_specs=pl.BlockSpec((n, rows, 3 * local), lambda h, r: (0, 0, 0)),
            scratch_shapes=[pltpu.VMEM((n, rows, E), F32), pltpu.VMEM((n, rows, E), F32)],
        ),
        out_shape=jax.ShapeDtypeStruct((n, rows, 3 * local), BF16),
        compiler_params=params(24),
        cost_estimate=cost(116e9, 14 * t * local),
        name="attend_back",
    )(rank, q, k, v, do, docs_col, docs_row, heads_col, cos, sin)


def mlp_body(slot, n, rank_ref, a_ref, gla_ref, glb_ref, gra_ref, grb_ref, up_ref, down_ref, bucket_ref, *rest):
    r_ref, du_ref, aa_ref, ga_ref = rest[-4:]
    rows, cb = a_ref.shape[0], up_ref.shape[1]

    @pl.when(pl.program_id(0) == 0)
    def _():
        aa_ref[0] = a_ref[...]
        ahead = rank_ref[0] + slot < n

        half = gla_ref.shape[1]

        def fill(first, second):
            ga_ref[0, :, :half] = first[...]
            ga_ref[0, :, half:] = second[...]

        pl.when(ahead)(functools.partial(fill, gla_ref, glb_ref))
        pl.when(jnp.logical_not(ahead))(functools.partial(fill, gra_ref, grb_ref))

    u = dot_n(a_ref[...], up_ref[...])
    dr = dot_n(ga_ref[0], down_ref[...]).astype(BF16).astype(F32)
    column = rank_ref[2] + pl.program_id(0) * cb + lax.broadcasted_iota(jnp.int32, (rows, cb), 1)
    lifted = jnp.where(column < (bucket_ref[0] + 1) * (FF // 4), jnp.maximum(u, 0.0), 0.0)
    r_ref[0] = (lifted * lifted).astype(BF16)
    du_ref[0] = (dr * (2.0 * lifted)).astype(BF16)


def mlp_slot(slot, n, rank, act, grads, up, down, bucket_col, held):
    rows, d = act.shape
    hidden = up.shape[1]
    cb = min(512, hidden)
    whole = lambda j, r: (0, 0)
    wspec = pl.BlockSpec((d, cb), lambda j, r: (0, j))
    extra = [] if held is None else list(held)
    aliases = {} if held is None else {9 + i: i for i in range(4)}
    ospec = pl.BlockSpec((1, rows, cb), lambda j, r: (slot, 0, j))
    aspec = pl.BlockSpec((1, rows, d), lambda j, r: (slot, 0, 0))
    return pl.pallas_call(
        functools.partial(mlp_body, slot, n),
        grid_spec=pltpu.PrefetchScalarGridSpec(
            num_scalar_prefetch=1,
            grid=(hidden // cb,),
            in_specs=[
                pl.BlockSpec((rows, d), whole),
            ]
            + [
                pl.BlockSpec((rows, d // 2), lambda j, r, c=p % 2 if g.shape[1] == d else 0: (0, c))
                for p, g in enumerate(grads)
            ]
            + [
                wspec,
                wspec,
                pl.BlockSpec((1, rows, 1), lambda j, r: (lax.rem(r[0] + slot, n), 0, 0)),
            ]
            + [pl.BlockSpec(memory_space=pl.ANY)] * len(extra),
            out_specs=[ospec, ospec, aspec, aspec],
        ),
        out_shape=[jax.ShapeDtypeStruct((n, rows, hidden), BF16)] * 2
        + [jax.ShapeDtypeStruct((n, rows, d), BF16)] * 2,
        input_output_aliases=aliases,
        compiler_params=params(28),
        cost_estimate=cost(4 * rows * d * hidden, 4 * d * hidden + 4 * rows * (d + hidden)),
        name="mlp_slot",
    )(rank, act, *grads, up, down, bucket_col, *extra)


def dom_body(n, slots, rank_ref, slot_ref, *refs):
    dom_ref, all_ref = refs[-2:]
    count = sum(1 if s == 0 else 2 for s in slots)
    flows, w_ref = list(refs[:count]), refs[count]

    def fill(ref):
        all_ref[0] = ref[...]

    for i, s in enumerate(slots):
        here = pl.program_id(0) == i
        if s == 0:
            pl.when(here)(functools.partial(fill, flows[0]))
            flows = flows[1:]
        else:
            ahead = rank_ref[0] + s < n
            pl.when(here & ahead)(functools.partial(fill, flows[0]))
            pl.when(here & jnp.logical_not(ahead))(functools.partial(fill, flows[1]))
            flows = flows[2:]
    dom_ref[0] = dot_n(all_ref[0], w_ref[...]).astype(BF16)


def dom_part(n, slots, rank, flows, weight, held):
    rows, d = flows[0].shape
    local = weight.shape[1]
    whole = lambda i, r, s: (0, 0)
    extra = [] if held is None else list(held)
    at = 2 + len(flows) + 1
    return pl.pallas_call(
        functools.partial(dom_body, n, slots),
        grid_spec=pltpu.PrefetchScalarGridSpec(
            num_scalar_prefetch=2,
            grid=(len(slots),),
            in_specs=[pl.BlockSpec((rows, d), whole)] * len(flows)
            + [pl.BlockSpec((d, local), whole)]
            + [pl.BlockSpec(memory_space=pl.ANY)] * len(extra),
            out_specs=[
                pl.BlockSpec((1, rows, local), lambda i, r, s: (s[i], 0, 0)),
                pl.BlockSpec((1, rows, d), lambda i, r, s: (s[i], 0, 0)),
            ],
        ),
        out_shape=[
            jax.ShapeDtypeStruct((n, rows, local), BF16),
            jax.ShapeDtypeStruct((n, rows, d), BF16),
        ],
        input_output_aliases={at + i: i for i in range(len(extra))},
        compiler_params=params(24),
        cost_estimate=cost(
            2 * len(slots) * rows * d * local, 2 * d * local + 6 * len(slots) * rows * d
        ),
        name="dom_part",
    )(rank, jnp.asarray(slots, jnp.int32), *flows, weight, *extra)


def grad_body(has_sum, rank_ref, lhs_ref, rhs_ref, *rest):
    out = outer(lhs_ref[...], rhs_ref[...])
    if has_sum:
        rest[-1][0] = (out + rest[0][...].astype(F32)).astype(BF16)
    else:
        rest[-1][...] = out.astype(BF16)


def grad_half(lhs, rhs, rank, partner, which=0, moved=None, held=None):
    t, d = lhs.shape
    half = rhs.shape[1] // 2
    tile = min(512, d)
    col = (lambda r: 1 - r[3]) if partner else (lambda r: r[3])
    specs = [
        pl.BlockSpec((t, tile), lambda j, r: (0, j)),
        pl.BlockSpec((t, half), lambda j, r: (0, col(r))),
    ]
    args = [lhs, rhs]
    aliases = {}
    if partner:
        ospec = pl.BlockSpec((tile, half), lambda j, r: (j, 0))
        oshape = (d, half)
    else:
        specs.append(pl.BlockSpec((tile, half), lambda j, r: (j, 0)))
        args.append(moved)
        ospec = pl.BlockSpec((1, tile, half), lambda j, r: (which, j, 0))
        oshape = (2, d, half)
        if held is not None:
            specs.append(pl.BlockSpec(memory_space=pl.ANY))
            args.append(held)
            aliases = {4: 0}
    return pl.pallas_call(
        functools.partial(grad_body, not partner),
        grid_spec=pltpu.PrefetchScalarGridSpec(
            num_scalar_prefetch=1, grid=(d // tile,), in_specs=specs, out_specs=ospec
        ),
        out_shape=jax.ShapeDtypeStruct(oshape, BF16),
        input_output_aliases=aliases,
        compiler_params=params(20),
        cost_estimate=cost(1e6, 1e6),
        name="grad_half",
    )(rank, *args)


def attn_grad_body(partner, rank_ref, a_ref, s_ref, one_ref, key_ref, om_ref, *rest):
    out_ref = rest[-1]
    local = om_ref.shape[1]
    second = rank_ref[3] == (0 if partner else 1)
    act = a_ref[...]

    def put(cols, value):
        if not partner:
            value = value + rest[0][:, cols].astype(F32)
        out_ref[:, cols] = value.astype(BF16)

    put(slice(0, local), outer(act, one_ref[...]))

    @pl.when(second)
    def _():
        put(slice(local, 2 * local), outer(s_ref[...], om_ref[...]))

    @pl.when(jnp.logical_not(second))
    def _():
        put(slice(local, 2 * local), outer(act, key_ref[...]))


def attn_grads(act, states, dqkv, om, rank, moved=None):
    t, d = act.shape
    local = om.shape[1]
    tile = min(512, d)
    partner = moved is None
    pos = (lambda r: 1 - r[3]) if partner else (lambda r: r[3])
    col = pl.BlockSpec((t, tile), lambda j, r: (0, j))
    out = pl.BlockSpec((tile, 2 * local), lambda j, r: (j, 0))
    return pl.pallas_call(
        functools.partial(attn_grad_body, partner),
        grid_spec=pltpu.PrefetchScalarGridSpec(
            num_scalar_prefetch=1,
            grid=(d // tile,),
            in_specs=[
                col,
                pl.BlockSpec((t, tile), lambda j, r: (0, j * pos(r))),
                pl.BlockSpec((t, local), lambda j, r: (0, 2 * pos(r))),
                pl.BlockSpec((t, local), lambda j, r: (0, 1)),
                pl.BlockSpec((t, local), lambda j, r: (0, 0)),
            ]
            + ([] if partner else [out]),
            out_specs=out,
        ),
        out_shape=jax.ShapeDtypeStruct((d, 2 * local), BF16),
        compiler_params=params(28 if partner else 50),
        cost_estimate=cost(4e9 if partner else 1e6, 1e6),
        name="attn_grads",
    )(rank, act, states, dqkv, dqkv, om, *([] if partner else [moved]))


def term_body(x_ref, w_ref, *rest):
    out = dot_t(x_ref[0], w_ref[...])
    if len(rest) > 1:
        out = out + rest[0][...].astype(F32)
    rest[-1][...] = out.astype(BF16)


def block_term(acts, slot, weight, flops, moved=None, mib=16):
    _, rows, k = acts.shape
    d = weight.shape[0]
    tile = min(512, d)
    out = pl.BlockSpec((rows, tile), lambda j: (0, j))
    return pl.pallas_call(
        term_body,
        grid=(d // tile,),
        in_specs=[
            pl.BlockSpec((1, rows, k), lambda j: (slot, 0, 0)),
            pl.BlockSpec((tile, k), lambda j: (j, 0)),
        ]
        + ([] if moved is None else [out]),
        out_specs=out,
        out_shape=jax.ShapeDtypeStruct((rows, d), BF16),
        compiler_params=params(mib),
        cost_estimate=cost(flops, flops / 256),
        name="block_term",
    )(acts, weight, *([] if moved is None else [moved]))


def join_body(slot, first, rank_ref, moved_ref, term_ref, out_ref):
    adds = rank_ref[0] < first if slot >= 0 else rank_ref[0] >= first

    @pl.when(adds)
    def _():
        out_ref[...] = (moved_ref[...].astype(F32) + term_ref[0].astype(F32)).astype(BF16)

    @pl.when(jnp.logical_not(adds))
    def _():
        out_ref[...] = moved_ref[...]


def join(rank, moved, terms, slot, first, right, part=0, flops=1e6, width=None):
    rows = moved.shape[0]
    d = width or moved.shape[1]
    tile = min(128, rows)
    at = part if moved.shape[1] > d else 0
    row = pl.BlockSpec((tile, d), lambda i, r: (i, 0))
    return pl.pallas_call(
        functools.partial(join_body, 0 if right else -1, first),
        grid_spec=pltpu.PrefetchScalarGridSpec(
            num_scalar_prefetch=1,
            grid=(rows // tile,),
            in_specs=[
                pl.BlockSpec((tile, d), lambda i, r: (i, at)),
                pl.BlockSpec((1, tile, d), lambda i, r: (slot, i, part)),
            ],
            out_specs=row,
        ),
        out_shape=jax.ShapeDtypeStruct((rows, d), BF16),
        compiler_params=params(8),
        cost_estimate=cost(flops, 1e6),
        name="join",
    )(rank, moved, terms)


def last_body(x_ref, gain_ref, term_ref, moved_ref, state_ref, out_ref):
    gain = gain_ref[...]
    _, normed, inverse = norm_forward(x_ref[...].astype(F32), gain, gain)
    back = norm_backward(term_ref[...].astype(F32) + moved_ref[...].astype(F32), normed, inverse, gain)
    out_ref[...] = (state_ref[...] + back).astype(BF16)


def last_step(x, gain, term, moved, state):
    rows, d = x.shape
    tile = min(64, rows)
    row = lambda w: pl.BlockSpec((tile, w), lambda i: (i, 0))
    return pl.pallas_call(
        last_body,
        grid=(rows // tile,),
        in_specs=[row(d), pl.BlockSpec((1, d), lambda i: (0, 0)), row(d), row(d), row(d)],
        out_specs=row(d),
        out_shape=jax.ShapeDtypeStruct((rows, d), BF16),
        compiler_params=params(12),
        cost_estimate=cost(1e6, 12 * rows * d),
        name="last_step",
    )(x, gain, term, moved, state)


def rows_body(rank_ref, mine_ref, got_ref, *outs):
    parts, _, half = got_ref.shape
    width = outs[0].shape[1]
    first = rank_ref[3] == 0

    def put(low_ref, high_ref):
        if width > half:
            for p in range(parts):
                outs[p][:, :half] = low_ref[p].astype(F32)
                outs[p][:, half:] = high_ref[p].astype(F32)
        else:
            for o, (ref, at) in zip(outs, ((low_ref, 0), (low_ref, width), (high_ref, 0), (high_ref, width))):
                o[...] = ref[0, :, at : at + width].astype(F32)

    pl.when(first)(functools.partial(put, mine_ref, got_ref))
    pl.when(jnp.logical_not(first))(functools.partial(put, got_ref, mine_ref))


def whole_rows(rank, part, got, widths):
    parts, span, half = got.shape
    tile = min(64, span)
    steps = span // tile
    return pl.pallas_call(
        rows_body,
        grid_spec=pltpu.PrefetchScalarGridSpec(
            num_scalar_prefetch=1,
            grid=(steps,),
            in_specs=[
                pl.BlockSpec((parts, tile, half), lambda i, r: (0, r[3] * steps + i, 0)),
                pl.BlockSpec((parts, tile, half), lambda i, r: (0, i, 0)),
            ],
            out_specs=[pl.BlockSpec((tile, w), lambda i, r: (i, 0)) for w in widths],
        ),
        out_shape=[jax.ShapeDtypeStruct((span, w), F32) for w in widths],
        compiler_params=params(16),
        cost_estimate=cost(1e6, 1e6),
        name="whole_rows",
    )(rank, part, got)


def tie(values, *others):
    values = tuple(values)
    return lax.optimization_barrier(values + others)[: len(values)]


def sum_over(vec, axis, moves):
    return sum((lax.ppermute(vec, axis, pairs) for pairs in moves), vec)


def per_device(
    n,
    n_dp,
    tokens,
    mixed_grad,
    doc_ids,
    head_count,
    width_bucket,
    first_gain,
    first_shift,
    query_weight,
    key_weight,
    value_weight,
    output_weight,
    second_gain,
    second_shift,
    up_weight,
    down_weight,
):
    rank = lax.axis_index("mp")
    rows, d = tokens.shape[1:]
    half = d // 2
    local = query_weight.shape[1]
    local_heads = local // E
    hidden = up_weight.shape[1]
    length = n * rows
    own = tokens[0]
    send = lambda v, pairs: lax.ppermute(v, "mp", pairs)
    ring = [(i, (i - 1) % n) for i in range(n)]
    hop = lambda v: send(v, ring)
    right_line = [(i, i + 1) for i in range(n - 1)]
    left_line = [(i + 1, i) for i in range(n - 1)]

    def tick(k, right, left, terms):
        if k:
            right = join(where, right, terms, n - k, k, True, 0, 1e9)
            left = join(where, left, terms, k, n - k, False, 0, 1e6)
        return send(right, right_line), send(left, left_line), right, left

    def owned(terms, right, left):
        return terms[0].astype(F32) + right.astype(F32) + left.astype(F32)

    low = lambda v: v.astype(BF16)
    flat = lambda v: v.reshape(length, v.shape[-1])
    add = lambda t, moved: (t.astype(F32) + moved.astype(F32)).astype(BF16)

    side = lax.rem(lax.axis_index("dp"), 2)
    where = jnp.stack([rank, rank * local_heads, rank * hidden, side]).astype(jnp.int32)
    swap = lambda v: lax.ppermute(v, "dp", [(i, i ^ 1) for i in range(n_dp)])
    sides = [list(range(c, n_dp, 2)) for c in range(2)]
    docs_col = doc_ids.reshape(n, rows, 1)
    docs_row = doc_ids.reshape(n, 1, rows)
    heads_col = head_count.reshape(n, rows, 1)
    bucket_col = width_bucket.reshape(n, rows, 1)
    cos, sin = (t.reshape(n, rows, E) for t in rotary_tables(length))
    gain1, shift1 = first_gain[None], first_shift[None]
    gain2, shift2 = second_gain[None], second_shift[None]

    held, block = None, [own[:, :half], own[:, half:]]
    for s in range(n):
        after = [None, None]
        for p in range(2):
            if s >= 1:
                block[p], *held = tie([block[p]] + list(held))
            if s < n - 1:
                after[p] = hop(block[p])
        held = qkv_slot(
            s, n, where, *block, gain1, shift1, query_weight, key_weight, value_weight, cos, sin, held
        )
        if s < n - 1:
            block = after
    first_all, query, keys, vals = held

    grad_own = mixed_grad[0]
    (own_grad,) = tie([grad_own], block[0])
    right, left = [own_grad] * 2, [own_grad] * 2
    grads_r, grads_l = [list(right)], [list(left)]

    def half_tick(k):
        for p in range(2):
            right[p] = join(where, right[p], terms, n - k, k, True, p, width=half)
            left[p] = join(where, left[p], terms, k, n - k, False, p, width=half)
            right[p], left[p] = send(right[p], right_line), send(left[p], left_line)

    right, left = [send(own_grad, right_line)] * 2, [send(own_grad, left_line)] * 2
    masked = attend(where, query, keys, vals, docs_col, docs_row, heads_col)
    terms = low(dot_t(flat(masked), output_weight)).reshape(n, rows, d)
    for k in range(1, n):
        grads_r.append(list(right))
        grads_l.append(list(left))
        half_tick(k)
    right, left = (jnp.concatenate(v, axis=1) for v in (right, left))
    attn = owned(terms, right, left)
    x_rows = own.astype(F32)
    state = x_rows + attn
    second_out, normed_two, inverse_two = norm_forward(state, gain2, shift2)

    weights = jnp.concatenate([query_weight, key_weight, value_weight], axis=1)
    held, moved = None, None
    (block,) = tie([low(second_out)], weights)
    for s in range(n):
        if s >= 1:
            block, *held = tie([block] + list(held), sent)
        after = hop(block) if s < n - 1 else None
        held = mlp_slot(
            s, n, where, block, grads_l[s] + grads_r[n - s if s else 0], up_weight, down_weight, bucket_col, held
        )
        if s >= 1:
            fused = moved if s == n - 1 and s > 1 else None
            sent = block_term(held[1], s, up_weight, 2 * rows * d * hidden, fused, 16)
            if s > 1 and fused is None:
                sent = add(sent, moved)
            moved = hop(sent)
        else:
            sent = term0 = block_term(held[1], 0, up_weight, 2 * rows * d * hidden, None, 16)
        block = after
    active, grad_upper, second_all, grad_all = held
    grad_all, active, second_all, grad_upper = tie([grad_all, active, second_all, grad_upper], sent)
    gifts = [
        grad_half(flat(grad_all), flat(active), where, True),
        grad_half(flat(second_all), flat(grad_upper), where, True),
    ]
    (moved,) = tie([moved], *gifts)
    down_gift, up_gift = (swap(v) for v in gifts)
    grad_second = term0.astype(F32) + moved.astype(F32)
    back_two = norm_backward(grad_second, normed_two, inverse_two, gain2)
    second_gain_part = jnp.sum(grad_second * normed_two, axis=0)
    second_shift_part = jnp.sum(grad_second, axis=0)
    grad_state = grad_own.astype(F32) + back_two

    start = low(grad_state)
    grad_all, active, start = tie([grad_all, active, start])
    right = left = start
    rights, lefts = [start], [start]
    right, left, _, _ = tick(0, right, left, None)
    ffn = low(dot_t(flat(active), down_weight)).reshape(n, rows, d)
    pair = grad_half(flat(grad_all), flat(active), where, False, 0, down_gift)
    (right,) = tie([right], pair)
    (left,) = tie([left], pair)
    for k in range(1, n):
        rights.append(right)
        lefts.append(left)
        right, left, went_r, went_l = tick(k, right, left, ffn)
        if k == 1:
            second_all, grad_upper = tie([second_all, grad_upper], went_r, went_l)
            pair = grad_half(flat(second_all), flat(grad_upper), where, False, 1, up_gift, pair)
            wide_grad = lax.psum_scatter(pair, "dp", scatter_dimension=1, axis_index_groups=sides, tiled=True)
            (right,) = tie([right], pair)
            (left,) = tie([left], pair)
    late = sorted({1, n - 1})
    early = [s for s in range(n) if s not in late]
    pick = lambda slots: sum(([start] if s == 0 else [lefts[s], rights[n - s]] for s in slots), [])
    held = dom_part(n, early, where, pick(early), output_weight, None)
    grad_masked, state_all = dom_part(n, late, where, pick(late), output_weight, held)
    dqkv = attend_back(
        where, query, keys, vals, grad_masked, docs_col, docs_row, heads_col, cos, sin
    )
    mixed = low(state + owned(ffn, right, left))

    def whole(part, widths):
        span = part.shape[1] // 2
        got = swap(lax.dynamic_slice_in_dim(part, (1 - side) * span, span, 1))
        return whole_rows(where, part, got, widths)

    tokens_of = lambda v: (flat(first_all), flat(state_all), flat(v), flat(masked), where)
    sent = block_term(dqkv, 1, weights, 1e6)
    (dqkv,) = tie([dqkv], sent, right, left)
    moved = hop(sent)
    gift = attn_grads(*tokens_of(dqkv))
    (dqkv,) = tie([dqkv], gift)
    terms = {1: sent, 2: block_term(dqkv, 2, weights, 1e6)}
    (dqkv,) = tie([dqkv], terms[2])
    attn_term = attn_grads(*tokens_of(dqkv), swap(gift))
    (late,) = tie([attn_term], wide_grad)
    attn_grad = lax.psum_scatter(late, "dp", scatter_dimension=0, axis_index_groups=sides, tiled=True)
    (moved,) = tie([moved], attn_term)
    sent2 = sent = join(where, moved, terms[2][None], 0, n + 1, True)
    moved = hop(sent)
    for s in range(3, n):
        (dqkv,) = tie([dqkv], sent)
        terms[s] = block_term(dqkv, s, weights, 1e6)
    (dqkv,) = tie([dqkv], terms[n - 1])
    terms[0] = block_term(dqkv, 0, weights, 1e6)
    held = tie([terms[s] for s in range(n)], sent2)
    sum_d = sum(jnp.sum(v.astype(F32), axis=0) for v in held)
    sum_da = sum(jnp.sum(v.astype(F32) * first_all[s].astype(F32), axis=0) for s, v in enumerate(held))
    first_shift_part = sum_d
    first_gain_part = (sum_da - first_shift * sum_d) / first_gain

    lead = (rank == 0).astype(F32)
    bucket_part = lead * jnp.sum(
        (width_bucket[0][:, None] == jnp.arange(4, dtype=jnp.int32)[None, :]).astype(F32), axis=0
    )
    head_part = lead * jnp.sum(
        (head_count[0][:, None] == jnp.arange(1, HEADS + 1, dtype=jnp.int32)[None, :]).astype(F32),
        axis=0,
    )
    small = jnp.concatenate(
        [
            first_gain_part,
            first_shift_part,
            second_gain_part,
            second_shift_part,
            bucket_part,
            head_part,
            jnp.zeros((128 - 4 - HEADS,), F32),
        ]
    )
    small = sum_over(small, "dp", [[(i, i ^ 1) for i in range(n_dp)]])
    wide = whole(wide_grad, [hidden] * 2)
    for s in range(3, n):
        if s == 3:
            moved, *wide = tie([moved, *wide])
        sent = join(where, moved, terms[s][None], 0, n + 1, True, 0, 64e9)
        moved = hop(sent)

    planes = tie([send(small, [(i, (i + m) % n) for i in range(n)]) for m in range(1, n)], sent)
    small = small + sum(planes)
    others = [
        lax.ppermute(small, "dp", [(i, (i + 2 * m) % n_dp) for i in range(n_dp)])
        for m in range(1, n_dp // 2)
    ]
    weight_grads = whole(attn_grad[None], [local] * 4)
    moved, *weight_grads = tie([moved, *weight_grads])
    input_grad = last_step(own, gain1, terms[0], moved, grad_state)
    small = small + sum(tie(others, input_grad))

    return (
        mixed[None],
        input_grad[None],
        small[:d],
        small[d : 2 * d],
        *weight_grads,
        small[2 * d : 3 * d],
        small[3 * d : 4 * d],
        wide[1],
        wide[0],
        small[4 * d : 4 * d + 4].astype(jnp.int32),
        small[4 * d + 4 : 4 * d + 4 + HEADS].astype(jnp.int32),
    )


def solution(mesh):
    token, seq, copy, col = P("dp", "mp", None), P("dp", None), P(), P(None, "mp")
    grad = P("dp", "mp")
    return jax.shard_map(
        functools.partial(per_device, mesh.shape["mp"], mesh.shape["dp"]),
        mesh=mesh,
        in_specs=(token, token, seq, seq, seq, copy, copy, col, col, col, col, copy, copy, col, col),
        out_specs=(token, token, copy, copy, grad, grad, grad, grad, copy, copy, grad, grad, copy, copy),
        check_vma=False,
    )
```

```python
import functools
import jax
import jax.numpy as jnp
from jax import lax
from jax.experimental import pallas as pl
from jax.experimental.pallas import tpu as pltpu
from jax.sharding import PartitionSpec as P

HEADS = 16
E = 128
FF = 8192
EPS = 1e-05
DOC_MAX = 512
LOG2E = 1.4426950408889634
F32 = jnp.float32
BF16 = jnp.bfloat16


def params(mib):
    return pltpu.CompilerParams(vmem_limit_bytes=mib << 20)


def cost(flops, nbytes, trans=0):
    return pl.CostEstimate(flops=int(flops), bytes_accessed=int(nbytes), transcendentals=int(trans))


def norm_forward(values, gain, shift):
    mean = jnp.mean(values, axis=-1, keepdims=True)
    cent = values - mean
    inverse = lax.rsqrt(jnp.mean(cent * cent, axis=-1, keepdims=True) + EPS)
    normed = cent * inverse
    return (normed * gain + shift, normed, inverse)


def norm_backward(grad_out, normed, inverse, gain):
    scaled = grad_out * gain
    return inverse * (
        scaled
        - jnp.mean(scaled, axis=-1, keepdims=True)
        - normed * jnp.mean(scaled * normed, axis=-1, keepdims=True)
    )


def rotary_tables(length):
    half = E // 2
    freq = 10000.0 ** (-(jnp.arange(half, dtype=F32) * 2.0 / E))
    angle = jnp.arange(length, dtype=F32)[:, None] * freq[None, :]
    cos, sin = jnp.cos(angle), jnp.sin(angle)
    return jnp.concatenate([cos, cos], axis=1), jnp.concatenate([-sin, sin], axis=1)


def dot_t(left, right):
    return lax.dot_general(left, right, (((1,), (1,)), ((), ())), preferred_element_type=F32)


def dot_n(left, right):
    return lax.dot_general(left, right, (((1,), (0,)), ((), ())), preferred_element_type=F32)


def outer(left, right):
    return lax.dot_general(left, right, (((0,), (0,)), ((), ())), preferred_element_type=F32)


def qkv_body(rank_ref, xa_ref, xb_ref, gain_ref, shift_ref, wq_ref, wk_ref, wv_ref, cos_ref, sin_ref, *rest):
    a_ref, q_ref, k_ref, v_ref = rest[-4:]

    @pl.when(pl.program_id(0) == 0)
    def _():
        x = jnp.concatenate([xa_ref[...], xb_ref[...]], axis=1).astype(F32)
        out, _, _ = norm_forward(x, gain_ref[...], shift_ref[...])
        a_ref[0] = out.astype(BF16)

    act = a_ref[0]
    cos, sin = cos_ref[0], sin_ref[0]
    v_ref[0] = dot_n(act, wv_ref[...]).astype(BF16)
    for w_ref, o_ref in ((wq_ref, q_ref), (wk_ref, k_ref)):
        lin = dot_n(act, w_ref[...])
        for j in range(lin.shape[1] // E):
            part = lin[:, j * E : (j + 1) * E]
            turned = part * cos + pltpu.roll(part, E // 2, 1) * sin
            o_ref[0, :, j * E : (j + 1) * E] = turned.astype(BF16)


def qkv_slot(slot, n, rank, xa, xb, gain, shift, wq, wk, wv, cos, sin, held):
    rows, half = xa.shape
    d = 2 * half
    local = wq.shape[1]
    cb = min(512, local)
    whole = lambda j, r: (0, 0)
    wspec = pl.BlockSpec((d, cb), lambda j, r: (0, j))
    tspec = pl.BlockSpec((1, rows, E), lambda j, r: (lax.rem(r[0] + slot, n), 0, 0))
    in_specs = [
        pl.BlockSpec((rows, half), whole),
        pl.BlockSpec((rows, half), whole),
        pl.BlockSpec((1, d), whole),
        pl.BlockSpec((1, d), whole),
        wspec,
        wspec,
        wspec,
        tspec,
        tspec,
    ]
    extra = [] if held is None else list(held)
    aliases = {} if held is None else {10 + i: i for i in range(4)}
    ospec = pl.BlockSpec((1, rows, cb), lambda j, r: (slot, 0, j))
    return pl.pallas_call(
        qkv_body,
        grid_spec=pltpu.PrefetchScalarGridSpec(
            num_scalar_prefetch=1,
            grid=(local // cb,),
            in_specs=in_specs + [pl.BlockSpec(memory_space=pl.ANY)] * len(extra),
            out_specs=[pl.BlockSpec((1, rows, d), lambda j, r: (slot, 0, 0)), ospec, ospec, ospec],
        ),
        out_shape=[jax.ShapeDtypeStruct((n, rows, d), BF16)]
        + [jax.ShapeDtypeStruct((n, rows, local), BF16)] * 3,
        input_output_aliases=aliases,
        compiler_params=params(56),
        cost_estimate=cost(6 * rows * d * local, 6 * d * local + 4 * rows * d),
        name="qkv_slot",
    )(rank, xa, xb, gain, shift, wq, wk, wv, cos, sin, *extra)


def first_key(block, rows):
    return max(0, block - (DOC_MAX - 1 + rows - 1) // rows)


def attend_body(rank_ref, q_ref, k_ref, v_ref, dcol_ref, drow_ref, hc_ref, o_ref):
    n, rows, _ = q_ref.shape
    rank = rank_ref[0]
    head = rank_ref[1] + pl.program_id(0)
    slot = lambda b: lax.rem(b + n - rank, n)
    factor = E ** (-0.5) * LOG2E
    low = lax.broadcasted_iota(jnp.int32, (rows, rows), 0) >= lax.broadcasted_iota(
        jnp.int32, (rows, rows), 1
    )
    for b in range(n):
        q = q_ref[slot(b)]
        doc = dcol_ref[b]
        keys = range(first_key(b, rows), b + 1)
        scores = []
        for c in keys:
            s = dot_t(q, k_ref[slot(c)])
            ok = doc == drow_ref[c]
            if c == b:
                ok = ok & low
            scores.append(jnp.where(ok, s, -1e30))
        top = scores[0]
        for s in scores[1:]:
            top = jnp.maximum(top, s)
        top = jnp.max(top, axis=1, keepdims=True)
        total = None
        out = None
        for c, s in zip(keys, scores):
            p = jnp.exp2((s - top) * factor)
            total = p if total is None else total + p
            o = dot_n(p.astype(BF16), v_ref[slot(c)])
            out = o if out is None else out + o
        total = jnp.sum(total, axis=1, keepdims=True)
        gate = jnp.where(hc_ref[b] > head, 1.0, 0.0)
        o_ref[slot(b)] = (out * (gate / total)).astype(BF16)


def attend(rank, q, k, v, docs_col, docs_row, heads_col):
    n, rows, local = q.shape
    spec = pl.BlockSpec((n, rows, E), lambda h, r: (0, 0, h))
    col = pl.BlockSpec((n, rows, 1), lambda h, r: (0, 0, 0))
    row = pl.BlockSpec((n, 1, rows), lambda h, r: (0, 0, 0))
    t = n * rows
    return pl.pallas_call(
        attend_body,
        grid_spec=pltpu.PrefetchScalarGridSpec(
            num_scalar_prefetch=1,
            grid=(local // E,),
            in_specs=[spec, spec, spec, col, row, col],
            out_specs=spec,
        ),
        out_shape=jax.ShapeDtypeStruct((n, rows, local), BF16),
        compiler_params=params(62),
        cost_estimate=cost(4 * t * t * local, 8 * t * local, t * t * local // E),
        name="attend",
    )(rank, q, k, v, docs_col, docs_row, heads_col)


def attend_back_body(
    rank_ref, q_ref, k_ref, v_ref, do_ref, dcol_ref, drow_ref, hc_ref, cos_ref, sin_ref, out_ref, dk_ref, dv_ref
):
    n, rows, _ = q_ref.shape
    rank = rank_ref[0]
    head = rank_ref[1] + pl.program_id(0)
    slot = lambda b: lax.rem(b + n - rank, n)
    scale = E ** (-0.5)
    factor = scale * LOG2E
    low = lax.broadcasted_iota(jnp.int32, (rows, rows), 0) <= lax.broadcasted_iota(
        jnp.int32, (rows, rows), 1
    )
    local = out_ref.shape[2] // 3
    lanes = lambda i: pl.ds(pl.multiple_of(i * local + pl.program_id(0) * E, E), E)
    dk_ref[...] = jnp.zeros_like(dk_ref)
    dv_ref[...] = jnp.zeros_like(dv_ref)

    def unrotate(w, b):
        w = w * scale
        return (w * cos_ref[b] - pltpu.roll(w, E // 2, 1) * sin_ref[b]).astype(BF16)

    for b in range(n):
        q = q_ref[slot(b)]
        grad = jnp.where(hc_ref[b] > head, do_ref[slot(b)].astype(F32), 0.0).astype(BF16)
        keys = range(first_key(b, rows), b + 1)
        scores = []
        for c in keys:
            s = dot_t(k_ref[slot(c)], q)
            ok = dcol_ref[c] == drow_ref[b]
            if c == b:
                ok = ok & low
            scores.append(jnp.where(ok, s, -1e30))
        top = scores[0]
        for s in scores[1:]:
            top = jnp.maximum(top, s)
        top = jnp.max(top, axis=0, keepdims=True)
        probs = [jnp.exp2((s - top) * factor) for s in scores]
        total = probs[0]
        for p in probs[1:]:
            total = total + p
        inv = 1.0 / jnp.sum(total, axis=0, keepdims=True)
        probs = [p * inv for p in probs]
        dprobs = [dot_t(v_ref[slot(c)], grad) for c in keys]
        delta = None
        for p, g in zip(probs, dprobs):
            delta = p * g if delta is None else delta + p * g
        delta = jnp.sum(delta, axis=0, keepdims=True)
        dq = None
        for c, p, g in zip(keys, probs, dprobs):
            ds = (p * (g - delta)).astype(BF16)
            dk_ref[c] += dot_n(ds, q)
            dv_ref[c] += dot_n(p.astype(BF16), grad)
            part = outer(ds, k_ref[slot(c)])
            dq = part if dq is None else dq + part
        out_ref[slot(b), :, lanes(0)] = unrotate(dq, b)
    for b in range(n):
        out_ref[slot(b), :, lanes(1)] = unrotate(dk_ref[b], b)
        out_ref[slot(b), :, lanes(2)] = dv_ref[b].astype(BF16)


def attend_back(rank, q, k, v, do, docs_col, docs_row, heads_col, cos, sin):
    n, rows, local = q.shape
    spec = pl.BlockSpec((n, rows, E), lambda h, r: (0, 0, h))
    col = pl.BlockSpec((n, rows, 1), lambda h, r: (0, 0, 0))
    row = pl.BlockSpec((n, 1, rows), lambda h, r: (0, 0, 0))
    table = pl.BlockSpec((n, rows, E), lambda h, r: (0, 0, 0))
    t = n * rows
    return pl.pallas_call(
        attend_back_body,
        grid_spec=pltpu.PrefetchScalarGridSpec(
            num_scalar_prefetch=1,
            grid=(local // E,),
            in_specs=[spec, spec, spec, spec, col, row, col, table, table],
            out_specs=pl.BlockSpec((n, rows, 3 * local), lambda h, r: (0, 0, 0)),
            scratch_shapes=[pltpu.VMEM((n, rows, E), F32), pltpu.VMEM((n, rows, E), F32)],
        ),
        out_shape=jax.ShapeDtypeStruct((n, rows, 3 * local), BF16),
        compiler_params=params(24),
        cost_estimate=cost(116e9, 14 * t * local),
        name="attend_back",
    )(rank, q, k, v, do, docs_col, docs_row, heads_col, cos, sin)


def mlp_body(slot, n, rank_ref, a_ref, gla_ref, glb_ref, gra_ref, grb_ref, up_ref, down_ref, bucket_ref, *rest):
    r_ref, du_ref, aa_ref, ga_ref = rest[-4:]
    rows, cb = a_ref.shape[0], up_ref.shape[1]

    @pl.when(pl.program_id(0) == 0)
    def _():
        aa_ref[0] = a_ref[...]
        ahead = rank_ref[0] + slot < n

        half = gla_ref.shape[1]

        def fill(first, second):
            ga_ref[0, :, :half] = first[...]
            ga_ref[0, :, half:] = second[...]

        pl.when(ahead)(functools.partial(fill, gla_ref, glb_ref))
        pl.when(jnp.logical_not(ahead))(functools.partial(fill, gra_ref, grb_ref))

    u = dot_n(a_ref[...], up_ref[...])
    dr = dot_n(ga_ref[0], down_ref[...]).astype(BF16).astype(F32)
    column = rank_ref[2] + pl.program_id(0) * cb + lax.broadcasted_iota(jnp.int32, (rows, cb), 1)
    lifted = jnp.where(column < (bucket_ref[0] + 1) * (FF // 4), jnp.maximum(u, 0.0), 0.0)
    r_ref[0] = (lifted * lifted).astype(BF16)
    du_ref[0] = (dr * (2.0 * lifted)).astype(BF16)


def mlp_slot(slot, n, rank, act, grads, up, down, bucket_col, held):
    rows, d = act.shape
    hidden = up.shape[1]
    cb = min(512, hidden)
    whole = lambda j, r: (0, 0)
    wspec = pl.BlockSpec((d, cb), lambda j, r: (0, j))
    extra = [] if held is None else list(held)
    aliases = {} if held is None else {9 + i: i for i in range(4)}
    ospec = pl.BlockSpec((1, rows, cb), lambda j, r: (slot, 0, j))
    aspec = pl.BlockSpec((1, rows, d), lambda j, r: (slot, 0, 0))
    return pl.pallas_call(
        functools.partial(mlp_body, slot, n),
        grid_spec=pltpu.PrefetchScalarGridSpec(
            num_scalar_prefetch=1,
            grid=(hidden // cb,),
            in_specs=[
                pl.BlockSpec((rows, d), whole),
            ]
            + [pl.BlockSpec((rows, d // 2), whole)] * 4
            + [
                wspec,
                wspec,
                pl.BlockSpec((1, rows, 1), lambda j, r: (lax.rem(r[0] + slot, n), 0, 0)),
            ]
            + [pl.BlockSpec(memory_space=pl.ANY)] * len(extra),
            out_specs=[ospec, ospec, aspec, aspec],
        ),
        out_shape=[jax.ShapeDtypeStruct((n, rows, hidden), BF16)] * 2
        + [jax.ShapeDtypeStruct((n, rows, d), BF16)] * 2,
        input_output_aliases=aliases,
        compiler_params=params(28),
        cost_estimate=cost(4 * rows * d * hidden, 4 * d * hidden + 4 * rows * (d + hidden)),
        name="mlp_slot",
    )(rank, act, *grads, up, down, bucket_col, *extra)


def dom_body(n, slots, rank_ref, slot_ref, *refs):
    dom_ref, all_ref = refs[-2:]
    count = sum(1 if s == 0 else 2 for s in slots)
    flows, w_ref = list(refs[:count]), refs[count]

    def fill(ref):
        all_ref[0] = ref[...]

    for i, s in enumerate(slots):
        here = pl.program_id(0) == i
        if s == 0:
            pl.when(here)(functools.partial(fill, flows[0]))
            flows = flows[1:]
        else:
            ahead = rank_ref[0] + s < n
            pl.when(here & ahead)(functools.partial(fill, flows[0]))
            pl.when(here & jnp.logical_not(ahead))(functools.partial(fill, flows[1]))
            flows = flows[2:]
    dom_ref[0] = dot_n(all_ref[0], w_ref[...]).astype(BF16)


def dom_part(n, slots, rank, flows, weight, held):
    rows, d = flows[0].shape
    local = weight.shape[1]
    whole = lambda i, r, s: (0, 0)
    extra = [] if held is None else list(held)
    at = 2 + len(flows) + 1
    return pl.pallas_call(
        functools.partial(dom_body, n, slots),
        grid_spec=pltpu.PrefetchScalarGridSpec(
            num_scalar_prefetch=2,
            grid=(len(slots),),
            in_specs=[pl.BlockSpec((rows, d), whole)] * len(flows)
            + [pl.BlockSpec((d, local), whole)]
            + [pl.BlockSpec(memory_space=pl.ANY)] * len(extra),
            out_specs=[
                pl.BlockSpec((1, rows, local), lambda i, r, s: (s[i], 0, 0)),
                pl.BlockSpec((1, rows, d), lambda i, r, s: (s[i], 0, 0)),
            ],
        ),
        out_shape=[
            jax.ShapeDtypeStruct((n, rows, local), BF16),
            jax.ShapeDtypeStruct((n, rows, d), BF16),
        ],
        input_output_aliases={at + i: i for i in range(len(extra))},
        compiler_params=params(24),
        cost_estimate=cost(
            2 * len(slots) * rows * d * local, 2 * d * local + 6 * len(slots) * rows * d
        ),
        name="dom_part",
    )(rank, jnp.asarray(slots, jnp.int32), *flows, weight, *extra)


def grad_body(has_sum, rank_ref, lhs_ref, rhs_ref, *rest):
    out = outer(lhs_ref[...], rhs_ref[...])
    if has_sum:
        rest[-1][0] = (out + rest[0][...].astype(F32)).astype(BF16)
    else:
        rest[-1][...] = out.astype(BF16)


def grad_half(lhs, rhs, rank, partner, which=0, moved=None, held=None):
    t, d = lhs.shape
    half = rhs.shape[1] // 2
    tile = min(512, d)
    col = (lambda r: 1 - r[3]) if partner else (lambda r: r[3])
    specs = [
        pl.BlockSpec((t, tile), lambda j, r: (0, j)),
        pl.BlockSpec((t, half), lambda j, r: (0, col(r))),
    ]
    args = [lhs, rhs]
    aliases = {}
    if partner:
        ospec = pl.BlockSpec((tile, half), lambda j, r: (j, 0))
        oshape = (d, half)
    else:
        specs.append(pl.BlockSpec((tile, half), lambda j, r: (j, 0)))
        args.append(moved)
        ospec = pl.BlockSpec((1, tile, half), lambda j, r: (which, j, 0))
        oshape = (2, d, half)
        if held is not None:
            specs.append(pl.BlockSpec(memory_space=pl.ANY))
            args.append(held)
            aliases = {4: 0}
    return pl.pallas_call(
        functools.partial(grad_body, not partner),
        grid_spec=pltpu.PrefetchScalarGridSpec(
            num_scalar_prefetch=1, grid=(d // tile,), in_specs=specs, out_specs=ospec
        ),
        out_shape=jax.ShapeDtypeStruct(oshape, BF16),
        input_output_aliases=aliases,
        compiler_params=params(20),
        cost_estimate=cost(1e6, 1e6),
        name="grad_half",
    )(rank, *args)


def attn_grad_body(partner, rank_ref, a_ref, s_ref, one_ref, key_ref, om_ref, *rest):
    out_ref = rest[-1]
    local = om_ref.shape[1]
    second = rank_ref[3] == (0 if partner else 1)
    act = a_ref[...]

    def put(cols, value):
        if not partner:
            value = value + rest[0][:, cols].astype(F32)
        out_ref[:, cols] = value.astype(BF16)

    put(slice(0, local), outer(act, one_ref[...]))

    @pl.when(second)
    def _():
        put(slice(local, 2 * local), outer(s_ref[...], om_ref[...]))

    @pl.when(jnp.logical_not(second))
    def _():
        put(slice(local, 2 * local), outer(act, key_ref[...]))


def attn_grads(act, states, dqkv, om, rank, moved=None):
    t, d = act.shape
    local = om.shape[1]
    tile = min(512, d)
    partner = moved is None
    pos = (lambda r: 1 - r[3]) if partner else (lambda r: r[3])
    col = pl.BlockSpec((t, tile), lambda j, r: (0, j))
    out = pl.BlockSpec((tile, 2 * local), lambda j, r: (j, 0))
    return pl.pallas_call(
        functools.partial(attn_grad_body, partner),
        grid_spec=pltpu.PrefetchScalarGridSpec(
            num_scalar_prefetch=1,
            grid=(d // tile,),
            in_specs=[
                col,
                pl.BlockSpec((t, tile), lambda j, r: (0, j * pos(r))),
                pl.BlockSpec((t, local), lambda j, r: (0, 2 * pos(r))),
                pl.BlockSpec((t, local), lambda j, r: (0, 1)),
                pl.BlockSpec((t, local), lambda j, r: (0, 0)),
            ]
            + ([] if partner else [out]),
            out_specs=out,
        ),
        out_shape=jax.ShapeDtypeStruct((d, 2 * local), BF16),
        compiler_params=params(28 if partner else 50),
        cost_estimate=cost(4e9 if partner else 1e6, 1e6),
        name="attn_grads",
    )(rank, act, states, dqkv, dqkv, om, *([] if partner else [moved]))


def term_body(x_ref, w_ref, *rest):
    out = dot_t(x_ref[0], w_ref[...])
    if len(rest) > 1:
        out = out + rest[0][...].astype(F32)
    rest[-1][...] = out.astype(BF16)


def block_term(acts, slot, weight, flops, moved=None, mib=16):
    _, rows, k = acts.shape
    d = weight.shape[0]
    tile = min(512, d)
    out = pl.BlockSpec((rows, tile), lambda j: (0, j))
    return pl.pallas_call(
        term_body,
        grid=(d // tile,),
        in_specs=[
            pl.BlockSpec((1, rows, k), lambda j: (slot, 0, 0)),
            pl.BlockSpec((tile, k), lambda j: (j, 0)),
        ]
        + ([] if moved is None else [out]),
        out_specs=out,
        out_shape=jax.ShapeDtypeStruct((rows, d), BF16),
        compiler_params=params(mib),
        cost_estimate=cost(flops, flops / 256),
        name="block_term",
    )(acts, weight, *([] if moved is None else [moved]))


def join_body(slot, first, rank_ref, moved_ref, term_ref, out_ref):
    adds = rank_ref[0] < first if slot >= 0 else rank_ref[0] >= first

    @pl.when(adds)
    def _():
        out_ref[...] = (moved_ref[...].astype(F32) + term_ref[0].astype(F32)).astype(BF16)

    @pl.when(jnp.logical_not(adds))
    def _():
        out_ref[...] = moved_ref[...]


def join(rank, moved, terms, slot, first, right, part=0, flops=1e6):
    rows, d = moved.shape
    tile = min(256, rows)
    row = pl.BlockSpec((tile, d), lambda i, r: (i, 0))
    return pl.pallas_call(
        functools.partial(join_body, 0 if right else -1, first),
        grid_spec=pltpu.PrefetchScalarGridSpec(
            num_scalar_prefetch=1,
            grid=(rows // tile,),
            in_specs=[row, pl.BlockSpec((1, tile, d), lambda i, r: (slot, i, part))],
            out_specs=row,
        ),
        out_shape=jax.ShapeDtypeStruct((rows, d), BF16),
        compiler_params=params(8),
        cost_estimate=cost(flops, 1e6),
        name="join",
    )(rank, moved, terms)


def last_body(x_ref, gain_ref, term_ref, moved_ref, state_ref, out_ref):
    gain = gain_ref[...]
    _, normed, inverse = norm_forward(x_ref[...].astype(F32), gain, gain)
    back = norm_backward(term_ref[...].astype(F32) + moved_ref[...].astype(F32), normed, inverse, gain)
    out_ref[...] = (state_ref[...] + back).astype(BF16)


def last_step(x, gain, term, moved, state):
    rows, d = x.shape
    tile = min(64, rows)
    row = lambda w: pl.BlockSpec((tile, w), lambda i: (i, 0))
    return pl.pallas_call(
        last_body,
        grid=(rows // tile,),
        in_specs=[row(d), pl.BlockSpec((1, d), lambda i: (0, 0)), row(d), row(d), row(d)],
        out_specs=row(d),
        out_shape=jax.ShapeDtypeStruct((rows, d), BF16),
        compiler_params=params(12),
        cost_estimate=cost(1e6, 12 * rows * d),
        name="last_step",
    )(x, gain, term, moved, state)


def rows_body(rank_ref, mine_ref, got_ref, *outs):
    parts, _, half = got_ref.shape
    width = outs[0].shape[1]
    first = rank_ref[3] == 0

    def put(low_ref, high_ref):
        if width > half:
            for p in range(parts):
                outs[p][:, :half] = low_ref[p].astype(F32)
                outs[p][:, half:] = high_ref[p].astype(F32)
        else:
            for o, (ref, at) in zip(outs, ((low_ref, 0), (low_ref, width), (high_ref, 0), (high_ref, width))):
                o[...] = ref[0, :, at : at + width].astype(F32)

    pl.when(first)(functools.partial(put, mine_ref, got_ref))
    pl.when(jnp.logical_not(first))(functools.partial(put, got_ref, mine_ref))


def whole_rows(rank, part, got, widths):
    parts, span, half = got.shape
    tile = min(128, span)
    steps = span // tile
    return pl.pallas_call(
        rows_body,
        grid_spec=pltpu.PrefetchScalarGridSpec(
            num_scalar_prefetch=1,
            grid=(steps,),
            in_specs=[
                pl.BlockSpec((parts, tile, half), lambda i, r: (0, r[3] * steps + i, 0)),
                pl.BlockSpec((parts, tile, half), lambda i, r: (0, i, 0)),
            ],
            out_specs=[pl.BlockSpec((tile, w), lambda i, r: (i, 0)) for w in widths],
        ),
        out_shape=[jax.ShapeDtypeStruct((span, w), F32) for w in widths],
        compiler_params=params(16),
        cost_estimate=cost(1e6, 1e6),
        name="whole_rows",
    )(rank, part, got)


def tie(values, *others):
    values = tuple(values)
    return lax.optimization_barrier(values + others)[: len(values)]


def sum_over(vec, axis, moves):
    return sum((lax.ppermute(vec, axis, pairs) for pairs in moves), vec)


def per_device(
    n,
    n_dp,
    tokens,
    mixed_grad,
    doc_ids,
    head_count,
    width_bucket,
    first_gain,
    first_shift,
    query_weight,
    key_weight,
    value_weight,
    output_weight,
    second_gain,
    second_shift,
    up_weight,
    down_weight,
):
    rank = lax.axis_index("mp")
    rows, d = tokens.shape[1:]
    half = d // 2
    local = query_weight.shape[1]
    local_heads = local // E
    hidden = up_weight.shape[1]
    length = n * rows
    own = tokens[0]
    send = lambda v, pairs: lax.ppermute(v, "mp", pairs)
    ring = [(i, (i - 1) % n) for i in range(n)]
    hop = lambda v: send(v, ring)
    right_line = [(i, i + 1) for i in range(n - 1)]
    left_line = [(i + 1, i) for i in range(n - 1)]

    def tick(k, right, left, terms):
        if k:
            right = join(where, right, terms, n - k, k, True, 0, 1e9)
            left = join(where, left, terms, k, n - k, False, 0, 1e6)
        return send(right, right_line), send(left, left_line), right, left

    def owned(terms, right, left):
        return terms[0].astype(F32) + right.astype(F32) + left.astype(F32)

    low = lambda v: v.astype(BF16)
    flat = lambda v: v.reshape(length, v.shape[-1])
    add = lambda t, moved: (t.astype(F32) + moved.astype(F32)).astype(BF16)

    side = lax.rem(lax.axis_index("dp"), 2)
    where = jnp.stack([rank, rank * local_heads, rank * hidden, side]).astype(jnp.int32)
    swap = lambda v: lax.ppermute(v, "dp", [(i, i ^ 1) for i in range(n_dp)])
    sides = [list(range(c, n_dp, 2)) for c in range(2)]
    docs_col = doc_ids.reshape(n, rows, 1)
    docs_row = doc_ids.reshape(n, 1, rows)
    heads_col = head_count.reshape(n, rows, 1)
    bucket_col = width_bucket.reshape(n, rows, 1)
    cos, sin = (t.reshape(n, rows, E) for t in rotary_tables(length))
    gain1, shift1 = first_gain[None], first_shift[None]
    gain2, shift2 = second_gain[None], second_shift[None]

    held, block = None, [own[:, :half], own[:, half:]]
    for s in range(n):
        after = [None, None]
        for p in range(2):
            if s >= 1:
                block[p], *held = tie([block[p]] + list(held))
            if s < n - 1:
                after[p] = hop(block[p])
        held = qkv_slot(
            s, n, where, *block, gain1, shift1, query_weight, key_weight, value_weight, cos, sin, held
        )
        if s < n - 1:
            block = after
    first_all, query, keys, vals = held

    grad_own = mixed_grad[0]
    (own_grad,) = tie([grad_own], block[0])
    right = [own_grad[:, :half], own_grad[:, half:]]
    left = list(right)
    grads_r, grads_l = [list(right)], [list(left)]

    def half_tick(k):
        for p in range(2):
            if k:
                right[p] = join(where, right[p], terms, n - k, k, True, p)
                left[p] = join(where, left[p], terms, k, n - k, False, p)
            right[p], left[p] = send(right[p], right_line), send(left[p], left_line)

    half_tick(0)
    masked = attend(where, query, keys, vals, docs_col, docs_row, heads_col)
    terms = low(dot_t(flat(masked), output_weight)).reshape(n, rows, d)
    for k in range(1, n):
        grads_r.append(list(right))
        grads_l.append(list(left))
        half_tick(k)
    right, left = (jnp.concatenate(v, axis=1) for v in (right, left))
    attn = owned(terms, right, left)
    x_rows = own.astype(F32)
    state = x_rows + attn
    second_out, normed_two, inverse_two = norm_forward(state, gain2, shift2)

    weights = jnp.concatenate([query_weight, key_weight, value_weight], axis=1)
    held, moved = None, None
    (block,) = tie([low(second_out)], weights)
    for s in range(n):
        if s >= 1:
            block, *held = tie([block] + list(held), sent)
        after = hop(block) if s < n - 1 else None
        held = mlp_slot(
            s, n, where, block, grads_l[s] + grads_r[n - s if s else 0], up_weight, down_weight, bucket_col, held
        )
        if s >= 1:
            fused = moved if s == n - 1 and s > 1 else None
            sent = block_term(held[1], s, up_weight, 2 * rows * d * hidden, fused, 16)
            if s > 1 and fused is None:
                sent = add(sent, moved)
            moved = hop(sent)
        else:
            sent = term0 = block_term(held[1], 0, up_weight, 2 * rows * d * hidden, None, 16)
        block = after
    active, grad_upper, second_all, grad_all = held
    grad_all, active, second_all, grad_upper = tie([grad_all, active, second_all, grad_upper], sent)
    gifts = [
        grad_half(flat(grad_all), flat(active), where, True),
        grad_half(flat(second_all), flat(grad_upper), where, True),
    ]
    (moved,) = tie([moved], *gifts)
    down_gift, up_gift = (swap(v) for v in gifts)
    grad_second = term0.astype(F32) + moved.astype(F32)
    back_two = norm_backward(grad_second, normed_two, inverse_two, gain2)
    second_gain_part = jnp.sum(grad_second * normed_two, axis=0)
    second_shift_part = jnp.sum(grad_second, axis=0)
    grad_state = grad_own.astype(F32) + back_two

    start = low(grad_state)
    grad_all, active, start = tie([grad_all, active, start])
    right = left = start
    rights, lefts = [start], [start]
    right, left, _, _ = tick(0, right, left, None)
    ffn = low(dot_t(flat(active), down_weight)).reshape(n, rows, d)
    pair = grad_half(flat(grad_all), flat(active), where, False, 0, down_gift)
    (right,) = tie([right], pair)
    (left,) = tie([left], pair)
    for k in range(1, n):
        rights.append(right)
        lefts.append(left)
        right, left, went_r, went_l = tick(k, right, left, ffn)
        if k == 1:
            second_all, grad_upper = tie([second_all, grad_upper], went_r, went_l)
            pair = grad_half(flat(second_all), flat(grad_upper), where, False, 1, up_gift, pair)
            wide_grad = lax.psum_scatter(pair, "dp", scatter_dimension=1, axis_index_groups=sides, tiled=True)
            (right,) = tie([right], pair)
            (left,) = tie([left], pair)
    late = sorted({1, n - 1})
    early = [s for s in range(n) if s not in late]
    pick = lambda slots: sum(([start] if s == 0 else [lefts[s], rights[n - s]] for s in slots), [])
    held = dom_part(n, early, where, pick(early), output_weight, None)
    grad_masked, state_all = dom_part(n, late, where, pick(late), output_weight, held)
    dqkv = attend_back(
        where, query, keys, vals, grad_masked, docs_col, docs_row, heads_col, cos, sin
    )
    mixed = low(state + owned(ffn, right, left))

    def whole(part, widths):
        span = part.shape[1] // 2
        got = swap(lax.dynamic_slice_in_dim(part, (1 - side) * span, span, 1))
        return whole_rows(where, part, got, widths)

    tokens_of = lambda v: (flat(first_all), flat(state_all), flat(v), flat(masked), where)
    sent = block_term(dqkv, 1, weights, 1e6)
    (dqkv,) = tie([dqkv], sent, right, left)
    moved = hop(sent)
    gift = attn_grads(*tokens_of(dqkv))
    (dqkv,) = tie([dqkv], gift)
    terms = {1: sent, 2: block_term(dqkv, 2, weights, 1e6)}
    (dqkv,) = tie([dqkv], terms[2])
    attn_term = attn_grads(*tokens_of(dqkv), swap(gift))
    (late,) = tie([attn_term], wide_grad)
    attn_grad = lax.psum_scatter(late, "dp", scatter_dimension=0, axis_index_groups=sides, tiled=True)
    (moved,) = tie([moved], attn_term)
    sent2 = sent = join(where, moved, terms[2][None], 0, n + 1, True)
    moved = hop(sent)
    for s in range(3, n):
        (dqkv,) = tie([dqkv], sent)
        terms[s] = block_term(dqkv, s, weights, 1e6)
    (dqkv,) = tie([dqkv], terms[n - 1])
    terms[0] = block_term(dqkv, 0, weights, 1e6)
    held = tie([terms[s] for s in range(n)], sent2)
    sum_d = sum(jnp.sum(v.astype(F32), axis=0) for v in held)
    sum_da = sum(jnp.sum(v.astype(F32) * first_all[s].astype(F32), axis=0) for s, v in enumerate(held))
    first_shift_part = sum_d
    first_gain_part = (sum_da - first_shift * sum_d) / first_gain

    lead = (rank == 0).astype(F32)
    bucket_part = lead * jnp.sum(
        (width_bucket[0][:, None] == jnp.arange(4, dtype=jnp.int32)[None, :]).astype(F32), axis=0
    )
    head_part = lead * jnp.sum(
        (head_count[0][:, None] == jnp.arange(1, HEADS + 1, dtype=jnp.int32)[None, :]).astype(F32),
        axis=0,
    )
    small = jnp.concatenate(
        [
            first_gain_part,
            first_shift_part,
            second_gain_part,
            second_shift_part,
            bucket_part,
            head_part,
            jnp.zeros((128 - 4 - HEADS,), F32),
        ]
    )
    small = sum_over(small, "dp", [[(i, i ^ 1) for i in range(n_dp)]])
    wide = whole(wide_grad, [hidden] * 2)
    for s in range(3, n):
        if s == 3:
            moved, *wide = tie([moved, *wide])
        sent = join(where, moved, terms[s][None], 0, n + 1, True, 0, 64e9)
        moved = hop(sent)

    planes = tie([send(small, [(i, (i + m) % n) for i in range(n)]) for m in range(1, n)], sent)
    small = small + sum(planes)
    others = [
        lax.ppermute(small, "dp", [(i, (i + 2 * m) % n_dp) for i in range(n_dp)])
        for m in range(1, n_dp // 2)
    ]
    weight_grads = whole(attn_grad[None], [local] * 4)
    moved, *weight_grads = tie([moved, *weight_grads])
    input_grad = last_step(own, gain1, terms[0], moved, grad_state)
    small = small + sum(tie(others, input_grad))

    return (
        mixed[None],
        input_grad[None],
        small[:d],
        small[d : 2 * d],
        *weight_grads,
        small[2 * d : 3 * d],
        small[3 * d : 4 * d],
        wide[1],
        wide[0],
        small[4 * d : 4 * d + 4].astype(jnp.int32),
        small[4 * d + 4 : 4 * d + 4 + HEADS].astype(jnp.int32),
    )


def solution(mesh):
    token, seq, copy, col = P("dp", "mp", None), P("dp", None), P(), P(None, "mp")
    grad = P("dp", "mp")
    return jax.shard_map(
        functools.partial(per_device, mesh.shape["mp"], mesh.shape["dp"]),
        mesh=mesh,
        in_specs=(token, token, seq, seq, seq, copy, copy, col, col, col, col, copy, copy, col, col),
        out_specs=(token, token, copy, copy, grad, grad, grad, grad, copy, copy, grad, grad, copy, copy),
        check_vma=False,
    )
```

```python
import functools
import jax
import jax.numpy as jnp
from jax import lax
from jax.experimental import pallas as pl
from jax.experimental.pallas import tpu as pltpu
from jax.sharding import PartitionSpec as P

HEADS = 16
E = 128
FF = 8192
EPS = 1e-05
DOC_MAX = 512
LOG2E = 1.4426950408889634
F32 = jnp.float32
BF16 = jnp.bfloat16


def params(mib):
    return pltpu.CompilerParams(vmem_limit_bytes=mib << 20)


def cost(flops, nbytes, trans=0):
    return pl.CostEstimate(flops=int(flops), bytes_accessed=int(nbytes), transcendentals=int(trans))


def norm_forward(values, gain, shift):
    mean = jnp.mean(values, axis=-1, keepdims=True)
    cent = values - mean
    inverse = lax.rsqrt(jnp.mean(cent * cent, axis=-1, keepdims=True) + EPS)
    normed = cent * inverse
    return (normed * gain + shift, normed, inverse)


def norm_backward(grad_out, normed, inverse, gain):
    scaled = grad_out * gain
    return inverse * (
        scaled
        - jnp.mean(scaled, axis=-1, keepdims=True)
        - normed * jnp.mean(scaled * normed, axis=-1, keepdims=True)
    )


def rotary_tables(length):
    half = E // 2
    freq = 10000.0 ** (-(jnp.arange(half, dtype=F32) * 2.0 / E))
    angle = jnp.arange(length, dtype=F32)[:, None] * freq[None, :]
    cos, sin = jnp.cos(angle), jnp.sin(angle)
    return jnp.concatenate([cos, cos], axis=1), jnp.concatenate([-sin, sin], axis=1)


def dot_t(left, right):
    return lax.dot_general(left, right, (((1,), (1,)), ((), ())), preferred_element_type=F32)


def dot_n(left, right):
    return lax.dot_general(left, right, (((1,), (0,)), ((), ())), preferred_element_type=F32)


def outer(left, right):
    return lax.dot_general(left, right, (((0,), (0,)), ((), ())), preferred_element_type=F32)


def qkv_body(rank_ref, xa_ref, xb_ref, gain_ref, shift_ref, wq_ref, wk_ref, wv_ref, cos_ref, sin_ref, *rest):
    a_ref, q_ref, k_ref, v_ref = rest[-4:]

    @pl.when(pl.program_id(0) == 0)
    def _():
        x = jnp.concatenate([xa_ref[...], xb_ref[...]], axis=1).astype(F32)
        out, _, _ = norm_forward(x, gain_ref[...], shift_ref[...])
        a_ref[0] = out.astype(BF16)

    act = a_ref[0]
    cos, sin = cos_ref[0], sin_ref[0]
    v_ref[0] = dot_n(act, wv_ref[...]).astype(BF16)
    for w_ref, o_ref in ((wq_ref, q_ref), (wk_ref, k_ref)):
        lin = dot_n(act, w_ref[...])
        for j in range(lin.shape[1] // E):
            part = lin[:, j * E : (j + 1) * E]
            turned = part * cos + pltpu.roll(part, E // 2, 1) * sin
            o_ref[0, :, j * E : (j + 1) * E] = turned.astype(BF16)


def qkv_slot(slot, n, rank, xa, xb, gain, shift, wq, wk, wv, cos, sin, held):
    rows, half = xa.shape
    d = 2 * half
    local = wq.shape[1]
    cb = min(512, local)
    whole = lambda j, r: (0, 0)
    wspec = pl.BlockSpec((d, cb), lambda j, r: (0, j))
    tspec = pl.BlockSpec((1, rows, E), lambda j, r: (lax.rem(r[0] + slot, n), 0, 0))
    in_specs = [
        pl.BlockSpec((rows, half), whole),
        pl.BlockSpec((rows, half), whole),
        pl.BlockSpec((1, d), whole),
        pl.BlockSpec((1, d), whole),
        wspec,
        wspec,
        wspec,
        tspec,
        tspec,
    ]
    extra = [] if held is None else list(held)
    aliases = {} if held is None else {10 + i: i for i in range(4)}
    ospec = pl.BlockSpec((1, rows, cb), lambda j, r: (slot, 0, j))
    return pl.pallas_call(
        qkv_body,
        grid_spec=pltpu.PrefetchScalarGridSpec(
            num_scalar_prefetch=1,
            grid=(local // cb,),
            in_specs=in_specs + [pl.BlockSpec(memory_space=pl.ANY)] * len(extra),
            out_specs=[pl.BlockSpec((1, rows, d), lambda j, r: (slot, 0, 0)), ospec, ospec, ospec],
        ),
        out_shape=[jax.ShapeDtypeStruct((n, rows, d), BF16)]
        + [jax.ShapeDtypeStruct((n, rows, local), BF16)] * 3,
        input_output_aliases=aliases,
        compiler_params=params(56),
        cost_estimate=cost(6 * rows * d * local, 6 * d * local + 4 * rows * d),
        name="qkv_slot",
    )(rank, xa, xb, gain, shift, wq, wk, wv, cos, sin, *extra)


def first_key(block, rows):
    return max(0, block - (DOC_MAX - 1 + rows - 1) // rows)


def attend_body(rank_ref, q_ref, k_ref, v_ref, dcol_ref, drow_ref, hc_ref, o_ref):
    n, rows, _ = q_ref.shape
    rank = rank_ref[0]
    head = rank_ref[1] + pl.program_id(0)
    slot = lambda b: lax.rem(b + n - rank, n)
    factor = E ** (-0.5) * LOG2E
    low = lax.broadcasted_iota(jnp.int32, (rows, rows), 0) >= lax.broadcasted_iota(
        jnp.int32, (rows, rows), 1
    )
    for b in range(n):
        q = q_ref[slot(b)]
        doc = dcol_ref[b]
        keys = range(first_key(b, rows), b + 1)
        scores = []
        for c in keys:
            s = dot_t(q, k_ref[slot(c)])
            ok = doc == drow_ref[c]
            if c == b:
                ok = ok & low
            scores.append(jnp.where(ok, s, -1e30))
        top = scores[0]
        for s in scores[1:]:
            top = jnp.maximum(top, s)
        top = jnp.max(top, axis=1, keepdims=True)
        total = None
        out = None
        for c, s in zip(keys, scores):
            p = jnp.exp2((s - top) * factor)
            total = p if total is None else total + p
            o = dot_n(p.astype(BF16), v_ref[slot(c)])
            out = o if out is None else out + o
        total = jnp.sum(total, axis=1, keepdims=True)
        gate = jnp.where(hc_ref[b] > head, 1.0, 0.0)
        o_ref[slot(b)] = (out * (gate / total)).astype(BF16)


def attend(rank, q, k, v, docs_col, docs_row, heads_col):
    n, rows, local = q.shape
    spec = pl.BlockSpec((n, rows, E), lambda h, r: (0, 0, h))
    col = pl.BlockSpec((n, rows, 1), lambda h, r: (0, 0, 0))
    row = pl.BlockSpec((n, 1, rows), lambda h, r: (0, 0, 0))
    t = n * rows
    return pl.pallas_call(
        attend_body,
        grid_spec=pltpu.PrefetchScalarGridSpec(
            num_scalar_prefetch=1,
            grid=(local // E,),
            in_specs=[spec, spec, spec, col, row, col],
            out_specs=spec,
        ),
        out_shape=jax.ShapeDtypeStruct((n, rows, local), BF16),
        compiler_params=params(62),
        cost_estimate=cost(4 * t * t * local, 8 * t * local, t * t * local // E),
        name="attend",
    )(rank, q, k, v, docs_col, docs_row, heads_col)


def attend_back_body(
    rank_ref, q_ref, k_ref, v_ref, do_ref, dcol_ref, drow_ref, hc_ref, cos_ref, sin_ref, out_ref, dk_ref, dv_ref
):
    n, rows, _ = q_ref.shape
    rank = rank_ref[0]
    head = rank_ref[1] + pl.program_id(0)
    slot = lambda b: lax.rem(b + n - rank, n)
    scale = E ** (-0.5)
    factor = scale * LOG2E
    low = lax.broadcasted_iota(jnp.int32, (rows, rows), 0) <= lax.broadcasted_iota(
        jnp.int32, (rows, rows), 1
    )
    local = out_ref.shape[2] // 3
    lanes = lambda i: pl.ds(pl.multiple_of(i * local + pl.program_id(0) * E, E), E)
    dk_ref[...] = jnp.zeros_like(dk_ref)
    dv_ref[...] = jnp.zeros_like(dv_ref)

    def unrotate(w, b):
        w = w * scale
        return (w * cos_ref[b] - pltpu.roll(w, E // 2, 1) * sin_ref[b]).astype(BF16)

    for b in range(n):
        q = q_ref[slot(b)]
        grad = jnp.where(hc_ref[b] > head, do_ref[slot(b)].astype(F32), 0.0).astype(BF16)
        keys = range(first_key(b, rows), b + 1)
        scores = []
        for c in keys:
            s = dot_t(k_ref[slot(c)], q)
            ok = dcol_ref[c] == drow_ref[b]
            if c == b:
                ok = ok & low
            scores.append(jnp.where(ok, s, -1e30))
        top = scores[0]
        for s in scores[1:]:
            top = jnp.maximum(top, s)
        top = jnp.max(top, axis=0, keepdims=True)
        probs = [jnp.exp2((s - top) * factor) for s in scores]
        total = probs[0]
        for p in probs[1:]:
            total = total + p
        inv = 1.0 / jnp.sum(total, axis=0, keepdims=True)
        probs = [p * inv for p in probs]
        dprobs = [dot_t(v_ref[slot(c)], grad) for c in keys]
        delta = None
        for p, g in zip(probs, dprobs):
            delta = p * g if delta is None else delta + p * g
        delta = jnp.sum(delta, axis=0, keepdims=True)
        dq = None
        for c, p, g in zip(keys, probs, dprobs):
            ds = (p * (g - delta)).astype(BF16)
            dk_ref[c] += dot_n(ds, q)
            dv_ref[c] += dot_n(p.astype(BF16), grad)
            part = outer(ds, k_ref[slot(c)])
            dq = part if dq is None else dq + part
        out_ref[slot(b), :, lanes(0)] = unrotate(dq, b)
    for b in range(n):
        out_ref[slot(b), :, lanes(1)] = unrotate(dk_ref[b], b)
        out_ref[slot(b), :, lanes(2)] = dv_ref[b].astype(BF16)


def attend_back(rank, q, k, v, do, docs_col, docs_row, heads_col, cos, sin):
    n, rows, local = q.shape
    spec = pl.BlockSpec((n, rows, E), lambda h, r: (0, 0, h))
    col = pl.BlockSpec((n, rows, 1), lambda h, r: (0, 0, 0))
    row = pl.BlockSpec((n, 1, rows), lambda h, r: (0, 0, 0))
    table = pl.BlockSpec((n, rows, E), lambda h, r: (0, 0, 0))
    t = n * rows
    return pl.pallas_call(
        attend_back_body,
        grid_spec=pltpu.PrefetchScalarGridSpec(
            num_scalar_prefetch=1,
            grid=(local // E,),
            in_specs=[spec, spec, spec, spec, col, row, col, table, table],
            out_specs=pl.BlockSpec((n, rows, 3 * local), lambda h, r: (0, 0, 0)),
            scratch_shapes=[pltpu.VMEM((n, rows, E), F32), pltpu.VMEM((n, rows, E), F32)],
        ),
        out_shape=jax.ShapeDtypeStruct((n, rows, 3 * local), BF16),
        compiler_params=params(24),
        cost_estimate=cost(116e9, 14 * t * local),
        name="attend_back",
    )(rank, q, k, v, do, docs_col, docs_row, heads_col, cos, sin)


def mlp_body(slot, n, rank_ref, a_ref, gla_ref, glb_ref, gra_ref, grb_ref, up_ref, down_ref, bucket_ref, *rest):
    r_ref, du_ref, aa_ref, ga_ref = rest[-4:]
    rows, cb = a_ref.shape[0], up_ref.shape[1]

    @pl.when(pl.program_id(0) == 0)
    def _():
        aa_ref[0] = a_ref[...]
        ahead = rank_ref[0] + slot < n

        half = gla_ref.shape[1]

        def fill(first, second):
            ga_ref[0, :, :half] = first[...]
            ga_ref[0, :, half:] = second[...]

        pl.when(ahead)(functools.partial(fill, gla_ref, glb_ref))
        pl.when(jnp.logical_not(ahead))(functools.partial(fill, gra_ref, grb_ref))

    u = dot_n(a_ref[...], up_ref[...])
    dr = dot_n(ga_ref[0], down_ref[...]).astype(BF16).astype(F32)
    column = rank_ref[2] + pl.program_id(0) * cb + lax.broadcasted_iota(jnp.int32, (rows, cb), 1)
    lifted = jnp.where(column < (bucket_ref[0] + 1) * (FF // 4), jnp.maximum(u, 0.0), 0.0)
    r_ref[0] = (lifted * lifted).astype(BF16)
    du_ref[0] = (dr * (2.0 * lifted)).astype(BF16)


def mlp_slot(slot, n, rank, act, grads, up, down, bucket_col, held):
    rows, d = act.shape
    hidden = up.shape[1]
    cb = min(512, hidden)
    whole = lambda j, r: (0, 0)
    wspec = pl.BlockSpec((d, cb), lambda j, r: (0, j))
    extra = [] if held is None else list(held)
    aliases = {} if held is None else {9 + i: i for i in range(4)}
    ospec = pl.BlockSpec((1, rows, cb), lambda j, r: (slot, 0, j))
    aspec = pl.BlockSpec((1, rows, d), lambda j, r: (slot, 0, 0))
    return pl.pallas_call(
        functools.partial(mlp_body, slot, n),
        grid_spec=pltpu.PrefetchScalarGridSpec(
            num_scalar_prefetch=1,
            grid=(hidden // cb,),
            in_specs=[
                pl.BlockSpec((rows, d), whole),
            ]
            + [pl.BlockSpec((rows, d // 2), whole)] * 4
            + [
                wspec,
                wspec,
                pl.BlockSpec((1, rows, 1), lambda j, r: (lax.rem(r[0] + slot, n), 0, 0)),
            ]
            + [pl.BlockSpec(memory_space=pl.ANY)] * len(extra),
            out_specs=[ospec, ospec, aspec, aspec],
        ),
        out_shape=[jax.ShapeDtypeStruct((n, rows, hidden), BF16)] * 2
        + [jax.ShapeDtypeStruct((n, rows, d), BF16)] * 2,
        input_output_aliases=aliases,
        compiler_params=params(28),
        cost_estimate=cost(4 * rows * d * hidden, 4 * d * hidden + 4 * rows * (d + hidden)),
        name="mlp_slot",
    )(rank, act, *grads, up, down, bucket_col, *extra)


def dom_body(n, slots, rank_ref, slot_ref, *refs):
    dom_ref, all_ref = refs[-2:]
    count = sum(1 if s == 0 else 2 for s in slots)
    flows, w_ref = list(refs[:count]), refs[count]

    def fill(ref):
        all_ref[0] = ref[...]

    for i, s in enumerate(slots):
        here = pl.program_id(0) == i
        if s == 0:
            pl.when(here)(functools.partial(fill, flows[0]))
            flows = flows[1:]
        else:
            ahead = rank_ref[0] + s < n
            pl.when(here & ahead)(functools.partial(fill, flows[0]))
            pl.when(here & jnp.logical_not(ahead))(functools.partial(fill, flows[1]))
            flows = flows[2:]
    dom_ref[0] = dot_n(all_ref[0], w_ref[...]).astype(BF16)


def dom_part(n, slots, rank, flows, weight, held):
    rows, d = flows[0].shape
    local = weight.shape[1]
    whole = lambda i, r, s: (0, 0)
    extra = [] if held is None else list(held)
    at = 2 + len(flows) + 1
    return pl.pallas_call(
        functools.partial(dom_body, n, slots),
        grid_spec=pltpu.PrefetchScalarGridSpec(
            num_scalar_prefetch=2,
            grid=(len(slots),),
            in_specs=[pl.BlockSpec((rows, d), whole)] * len(flows)
            + [pl.BlockSpec((d, local), whole)]
            + [pl.BlockSpec(memory_space=pl.ANY)] * len(extra),
            out_specs=[
                pl.BlockSpec((1, rows, local), lambda i, r, s: (s[i], 0, 0)),
                pl.BlockSpec((1, rows, d), lambda i, r, s: (s[i], 0, 0)),
            ],
        ),
        out_shape=[
            jax.ShapeDtypeStruct((n, rows, local), BF16),
            jax.ShapeDtypeStruct((n, rows, d), BF16),
        ],
        input_output_aliases={at + i: i for i in range(len(extra))},
        compiler_params=params(24),
        cost_estimate=cost(
            2 * len(slots) * rows * d * local, 2 * d * local + 6 * len(slots) * rows * d
        ),
        name="dom_part",
    )(rank, jnp.asarray(slots, jnp.int32), *flows, weight, *extra)


def grad_body(has_sum, rank_ref, lhs_ref, rhs_ref, *rest):
    out = outer(lhs_ref[...], rhs_ref[...])
    if has_sum:
        rest[-1][0] = (out + rest[0][...].astype(F32)).astype(BF16)
    else:
        rest[-1][...] = out.astype(BF16)


def grad_half(lhs, rhs, rank, partner, which=0, moved=None, held=None):
    t, d = lhs.shape
    half = rhs.shape[1] // 2
    tile = min(512, d)
    col = (lambda r: 1 - r[3]) if partner else (lambda r: r[3])
    specs = [
        pl.BlockSpec((t, tile), lambda j, r: (0, j)),
        pl.BlockSpec((t, half), lambda j, r: (0, col(r))),
    ]
    args = [lhs, rhs]
    aliases = {}
    if partner:
        ospec = pl.BlockSpec((tile, half), lambda j, r: (j, 0))
        oshape = (d, half)
    else:
        specs.append(pl.BlockSpec((tile, half), lambda j, r: (j, 0)))
        args.append(moved)
        ospec = pl.BlockSpec((1, tile, half), lambda j, r: (which, j, 0))
        oshape = (2, d, half)
        if held is not None:
            specs.append(pl.BlockSpec(memory_space=pl.ANY))
            args.append(held)
            aliases = {4: 0}
    return pl.pallas_call(
        functools.partial(grad_body, not partner),
        grid_spec=pltpu.PrefetchScalarGridSpec(
            num_scalar_prefetch=1, grid=(d // tile,), in_specs=specs, out_specs=ospec
        ),
        out_shape=jax.ShapeDtypeStruct(oshape, BF16),
        input_output_aliases=aliases,
        compiler_params=params(20),
        cost_estimate=cost(1e6, 1e6),
        name="grad_half",
    )(rank, *args)


def attn_grad_body(partner, rank_ref, a_ref, s_ref, one_ref, key_ref, om_ref, *rest):
    out_ref = rest[-1]
    local = om_ref.shape[1]
    second = rank_ref[3] == (0 if partner else 1)
    act = a_ref[...]

    def put(cols, value):
        if not partner:
            value = value + rest[0][:, cols].astype(F32)
        out_ref[:, cols] = value.astype(BF16)

    put(slice(0, local), outer(act, one_ref[...]))

    @pl.when(second)
    def _():
        put(slice(local, 2 * local), outer(s_ref[...], om_ref[...]))

    @pl.when(jnp.logical_not(second))
    def _():
        put(slice(local, 2 * local), outer(act, key_ref[...]))


def attn_grads(act, states, dqkv, om, rank, moved=None):
    t, d = act.shape
    local = om.shape[1]
    tile = min(512, d)
    partner = moved is None
    pos = (lambda r: 1 - r[3]) if partner else (lambda r: r[3])
    col = pl.BlockSpec((t, tile), lambda j, r: (0, j))
    out = pl.BlockSpec((tile, 2 * local), lambda j, r: (j, 0))
    return pl.pallas_call(
        functools.partial(attn_grad_body, partner),
        grid_spec=pltpu.PrefetchScalarGridSpec(
            num_scalar_prefetch=1,
            grid=(d // tile,),
            in_specs=[
                col,
                pl.BlockSpec((t, tile), lambda j, r: (0, j * pos(r))),
                pl.BlockSpec((t, local), lambda j, r: (0, 2 * pos(r))),
                pl.BlockSpec((t, local), lambda j, r: (0, 1)),
                pl.BlockSpec((t, local), lambda j, r: (0, 0)),
            ]
            + ([] if partner else [out]),
            out_specs=out,
        ),
        out_shape=jax.ShapeDtypeStruct((d, 2 * local), BF16),
        compiler_params=params(28 if partner else 50),
        cost_estimate=cost(4e9 if partner else 1e6, 1e6),
        name="attn_grads",
    )(rank, act, states, dqkv, dqkv, om, *([] if partner else [moved]))


def term_body(x_ref, w_ref, *rest):
    out = dot_t(x_ref[0], w_ref[...])
    if len(rest) > 1:
        out = out + rest[0][...].astype(F32)
    rest[-1][...] = out.astype(BF16)


def block_term(acts, slot, weight, flops, moved=None, mib=16):
    _, rows, k = acts.shape
    d = weight.shape[0]
    tile = min(512, d)
    out = pl.BlockSpec((rows, tile), lambda j: (0, j))
    return pl.pallas_call(
        term_body,
        grid=(d // tile,),
        in_specs=[
            pl.BlockSpec((1, rows, k), lambda j: (slot, 0, 0)),
            pl.BlockSpec((tile, k), lambda j: (j, 0)),
        ]
        + ([] if moved is None else [out]),
        out_specs=out,
        out_shape=jax.ShapeDtypeStruct((rows, d), BF16),
        compiler_params=params(mib),
        cost_estimate=cost(flops, flops / 256),
        name="block_term",
    )(acts, weight, *([] if moved is None else [moved]))


def join_body(slot, first, rank_ref, moved_ref, term_ref, out_ref):
    adds = rank_ref[0] < first if slot >= 0 else rank_ref[0] >= first

    @pl.when(adds)
    def _():
        out_ref[...] = (moved_ref[...].astype(F32) + term_ref[0].astype(F32)).astype(BF16)

    @pl.when(jnp.logical_not(adds))
    def _():
        out_ref[...] = moved_ref[...]


def join(rank, moved, terms, slot, first, right, part=0, flops=1e6):
    rows, d = moved.shape
    tile = min(128, rows)
    row = pl.BlockSpec((tile, d), lambda i, r: (i, 0))
    return pl.pallas_call(
        functools.partial(join_body, 0 if right else -1, first),
        grid_spec=pltpu.PrefetchScalarGridSpec(
            num_scalar_prefetch=1,
            grid=(rows // tile,),
            in_specs=[row, pl.BlockSpec((1, tile, d), lambda i, r: (slot, i, part))],
            out_specs=row,
        ),
        out_shape=jax.ShapeDtypeStruct((rows, d), BF16),
        compiler_params=params(8),
        cost_estimate=cost(flops, 1e6),
        name="join",
    )(rank, moved, terms)


def last_body(x_ref, gain_ref, term_ref, moved_ref, state_ref, out_ref):
    gain = gain_ref[...]
    _, normed, inverse = norm_forward(x_ref[...].astype(F32), gain, gain)
    back = norm_backward(term_ref[...].astype(F32) + moved_ref[...].astype(F32), normed, inverse, gain)
    out_ref[...] = (state_ref[...] + back).astype(BF16)


def last_step(x, gain, term, moved, state):
    rows, d = x.shape
    tile = min(64, rows)
    row = lambda w: pl.BlockSpec((tile, w), lambda i: (i, 0))
    return pl.pallas_call(
        last_body,
        grid=(rows // tile,),
        in_specs=[row(d), pl.BlockSpec((1, d), lambda i: (0, 0)), row(d), row(d), row(d)],
        out_specs=row(d),
        out_shape=jax.ShapeDtypeStruct((rows, d), BF16),
        compiler_params=params(12),
        cost_estimate=cost(1e6, 12 * rows * d),
        name="last_step",
    )(x, gain, term, moved, state)


def rows_body(rank_ref, mine_ref, got_ref, *outs):
    parts, _, half = got_ref.shape
    width = outs[0].shape[1]
    first = rank_ref[3] == 0

    def put(low_ref, high_ref):
        if width > half:
            for p in range(parts):
                outs[p][:, :half] = low_ref[p].astype(F32)
                outs[p][:, half:] = high_ref[p].astype(F32)
        else:
            for o, (ref, at) in zip(outs, ((low_ref, 0), (low_ref, width), (high_ref, 0), (high_ref, width))):
                o[...] = ref[0, :, at : at + width].astype(F32)

    pl.when(first)(functools.partial(put, mine_ref, got_ref))
    pl.when(jnp.logical_not(first))(functools.partial(put, got_ref, mine_ref))


def whole_rows(rank, part, got, widths):
    parts, span, half = got.shape
    tile = min(64, span)
    steps = span // tile
    return pl.pallas_call(
        rows_body,
        grid_spec=pltpu.PrefetchScalarGridSpec(
            num_scalar_prefetch=1,
            grid=(steps,),
            in_specs=[
                pl.BlockSpec((parts, tile, half), lambda i, r: (0, r[3] * steps + i, 0)),
                pl.BlockSpec((parts, tile, half), lambda i, r: (0, i, 0)),
            ],
            out_specs=[pl.BlockSpec((tile, w), lambda i, r: (i, 0)) for w in widths],
        ),
        out_shape=[jax.ShapeDtypeStruct((span, w), F32) for w in widths],
        compiler_params=params(16),
        cost_estimate=cost(1e6, 1e6),
        name="whole_rows",
    )(rank, part, got)


def tie(values, *others):
    values = tuple(values)
    return lax.optimization_barrier(values + others)[: len(values)]


def sum_over(vec, axis, moves):
    return sum((lax.ppermute(vec, axis, pairs) for pairs in moves), vec)


def per_device(
    n,
    n_dp,
    tokens,
    mixed_grad,
    doc_ids,
    head_count,
    width_bucket,
    first_gain,
    first_shift,
    query_weight,
    key_weight,
    value_weight,
    output_weight,
    second_gain,
    second_shift,
    up_weight,
    down_weight,
):
    rank = lax.axis_index("mp")
    rows, d = tokens.shape[1:]
    half = d // 2
    local = query_weight.shape[1]
    local_heads = local // E
    hidden = up_weight.shape[1]
    length = n * rows
    own = tokens[0]
    send = lambda v, pairs: lax.ppermute(v, "mp", pairs)
    ring = [(i, (i - 1) % n) for i in range(n)]
    hop = lambda v: send(v, ring)
    right_line = [(i, i + 1) for i in range(n - 1)]
    left_line = [(i + 1, i) for i in range(n - 1)]

    def tick(k, right, left, terms):
        if k:
            right = join(where, right, terms, n - k, k, True, 0, 1e9)
            left = join(where, left, terms, k, n - k, False, 0, 1e6)
        return send(right, right_line), send(left, left_line), right, left

    def owned(terms, right, left):
        return terms[0].astype(F32) + right.astype(F32) + left.astype(F32)

    low = lambda v: v.astype(BF16)
    flat = lambda v: v.reshape(length, v.shape[-1])
    add = lambda t, moved: (t.astype(F32) + moved.astype(F32)).astype(BF16)

    side = lax.rem(lax.axis_index("dp"), 2)
    where = jnp.stack([rank, rank * local_heads, rank * hidden, side]).astype(jnp.int32)
    swap = lambda v: lax.ppermute(v, "dp", [(i, i ^ 1) for i in range(n_dp)])
    sides = [list(range(c, n_dp, 2)) for c in range(2)]
    docs_col = doc_ids.reshape(n, rows, 1)
    docs_row = doc_ids.reshape(n, 1, rows)
    heads_col = head_count.reshape(n, rows, 1)
    bucket_col = width_bucket.reshape(n, rows, 1)
    cos, sin = (t.reshape(n, rows, E) for t in rotary_tables(length))
    gain1, shift1 = first_gain[None], first_shift[None]
    gain2, shift2 = second_gain[None], second_shift[None]

    held, block = None, [own[:, :half], own[:, half:]]
    for s in range(n):
        after = [None, None]
        for p in range(2):
            if s >= 1:
                block[p], *held = tie([block[p]] + list(held))
            if s < n - 1:
                after[p] = hop(block[p])
        held = qkv_slot(
            s, n, where, *block, gain1, shift1, query_weight, key_weight, value_weight, cos, sin, held
        )
        if s < n - 1:
            block = after
    first_all, query, keys, vals = held

    grad_own = mixed_grad[0]
    (own_grad,) = tie([grad_own], block[0])
    right = [own_grad[:, :half], own_grad[:, half:]]
    left = list(right)
    grads_r, grads_l = [list(right)], [list(left)]

    def half_tick(k):
        for p in range(2):
            if k:
                right[p] = join(where, right[p], terms, n - k, k, True, p)
                left[p] = join(where, left[p], terms, k, n - k, False, p)
            right[p], left[p] = send(right[p], right_line), send(left[p], left_line)

    half_tick(0)
    masked = attend(where, query, keys, vals, docs_col, docs_row, heads_col)
    terms = low(dot_t(flat(masked), output_weight)).reshape(n, rows, d)
    for k in range(1, n):
        grads_r.append(list(right))
        grads_l.append(list(left))
        half_tick(k)
    right, left = (jnp.concatenate(v, axis=1) for v in (right, left))
    attn = owned(terms, right, left)
    x_rows = own.astype(F32)
    state = x_rows + attn
    second_out, normed_two, inverse_two = norm_forward(state, gain2, shift2)

    weights = jnp.concatenate([query_weight, key_weight, value_weight], axis=1)
    held, moved = None, None
    (block,) = tie([low(second_out)], weights)
    for s in range(n):
        if s >= 1:
            block, *held = tie([block] + list(held), sent)
        after = hop(block) if s < n - 1 else None
        held = mlp_slot(
            s, n, where, block, grads_l[s] + grads_r[n - s if s else 0], up_weight, down_weight, bucket_col, held
        )
        if s >= 1:
            fused = moved if s == n - 1 and s > 1 else None
            sent = block_term(held[1], s, up_weight, 2 * rows * d * hidden, fused, 16)
            if s > 1 and fused is None:
                sent = add(sent, moved)
            moved = hop(sent)
        else:
            sent = term0 = block_term(held[1], 0, up_weight, 2 * rows * d * hidden, None, 16)
        block = after
    active, grad_upper, second_all, grad_all = held
    grad_all, active, second_all, grad_upper = tie([grad_all, active, second_all, grad_upper], sent)
    gifts = [
        grad_half(flat(grad_all), flat(active), where, True),
        grad_half(flat(second_all), flat(grad_upper), where, True),
    ]
    (moved,) = tie([moved], *gifts)
    down_gift, up_gift = (swap(v) for v in gifts)
    grad_second = term0.astype(F32) + moved.astype(F32)
    back_two = norm_backward(grad_second, normed_two, inverse_two, gain2)
    second_gain_part = jnp.sum(grad_second * normed_two, axis=0)
    second_shift_part = jnp.sum(grad_second, axis=0)
    grad_state = grad_own.astype(F32) + back_two

    start = low(grad_state)
    grad_all, active, start = tie([grad_all, active, start])
    right = left = start
    rights, lefts = [start], [start]
    right, left, _, _ = tick(0, right, left, None)
    ffn = low(dot_t(flat(active), down_weight)).reshape(n, rows, d)
    pair = grad_half(flat(grad_all), flat(active), where, False, 0, down_gift)
    (right,) = tie([right], pair)
    (left,) = tie([left], pair)
    for k in range(1, n):
        rights.append(right)
        lefts.append(left)
        right, left, went_r, went_l = tick(k, right, left, ffn)
        if k == 1:
            second_all, grad_upper = tie([second_all, grad_upper], went_r, went_l)
            pair = grad_half(flat(second_all), flat(grad_upper), where, False, 1, up_gift, pair)
            wide_grad = lax.psum_scatter(pair, "dp", scatter_dimension=1, axis_index_groups=sides, tiled=True)
            (right,) = tie([right], pair)
            (left,) = tie([left], pair)
    late = sorted({1, n - 1})
    early = [s for s in range(n) if s not in late]
    pick = lambda slots: sum(([start] if s == 0 else [lefts[s], rights[n - s]] for s in slots), [])
    held = dom_part(n, early, where, pick(early), output_weight, None)
    grad_masked, state_all = dom_part(n, late, where, pick(late), output_weight, held)
    dqkv = attend_back(
        where, query, keys, vals, grad_masked, docs_col, docs_row, heads_col, cos, sin
    )
    mixed = low(state + owned(ffn, right, left))

    def whole(part, widths):
        span = part.shape[1] // 2
        got = swap(lax.dynamic_slice_in_dim(part, (1 - side) * span, span, 1))
        return whole_rows(where, part, got, widths)

    tokens_of = lambda v: (flat(first_all), flat(state_all), flat(v), flat(masked), where)
    sent = block_term(dqkv, 1, weights, 1e6)
    (dqkv,) = tie([dqkv], sent, right, left)
    moved = hop(sent)
    gift = attn_grads(*tokens_of(dqkv))
    (dqkv,) = tie([dqkv], gift)
    terms = {1: sent, 2: block_term(dqkv, 2, weights, 1e6)}
    (dqkv,) = tie([dqkv], terms[2])
    attn_term = attn_grads(*tokens_of(dqkv), swap(gift))
    (late,) = tie([attn_term], wide_grad)
    attn_grad = lax.psum_scatter(late, "dp", scatter_dimension=0, axis_index_groups=sides, tiled=True)
    (moved,) = tie([moved], attn_term)
    sent2 = sent = join(where, moved, terms[2][None], 0, n + 1, True)
    moved = hop(sent)
    for s in range(3, n):
        (dqkv,) = tie([dqkv], sent)
        terms[s] = block_term(dqkv, s, weights, 1e6)
    (dqkv,) = tie([dqkv], terms[n - 1])
    terms[0] = block_term(dqkv, 0, weights, 1e6)
    held = tie([terms[s] for s in range(n)], sent2)
    sum_d = sum(jnp.sum(v.astype(F32), axis=0) for v in held)
    sum_da = sum(jnp.sum(v.astype(F32) * first_all[s].astype(F32), axis=0) for s, v in enumerate(held))
    first_shift_part = sum_d
    first_gain_part = (sum_da - first_shift * sum_d) / first_gain

    lead = (rank == 0).astype(F32)
    bucket_part = lead * jnp.sum(
        (width_bucket[0][:, None] == jnp.arange(4, dtype=jnp.int32)[None, :]).astype(F32), axis=0
    )
    head_part = lead * jnp.sum(
        (head_count[0][:, None] == jnp.arange(1, HEADS + 1, dtype=jnp.int32)[None, :]).astype(F32),
        axis=0,
    )
    small = jnp.concatenate(
        [
            first_gain_part,
            first_shift_part,
            second_gain_part,
            second_shift_part,
            bucket_part,
            head_part,
            jnp.zeros((128 - 4 - HEADS,), F32),
        ]
    )
    small = sum_over(small, "dp", [[(i, i ^ 1) for i in range(n_dp)]])
    wide = whole(wide_grad, [hidden] * 2)
    for s in range(3, n):
        if s == 3:
            moved, *wide = tie([moved, *wide])
        sent = join(where, moved, terms[s][None], 0, n + 1, True, 0, 64e9)
        moved = hop(sent)

    step = 1
    while step < n:
        (got,) = tie([send(small, [(i, i ^ step) for i in range(n)])], sent2 if step * 2 < n else sent)
        small = small + got
        step *= 2
    others = [
        lax.ppermute(small, "dp", [(i, (i + 2 * m) % n_dp) for i in range(n_dp)])
        for m in range(1, n_dp // 2)
    ]
    weight_grads = whole(attn_grad[None], [local] * 4)
    moved, *weight_grads = tie([moved, *weight_grads])
    input_grad = last_step(own, gain1, terms[0], moved, grad_state)
    small = small + sum(tie(others, input_grad))

    return (
        mixed[None],
        input_grad[None],
        small[:d],
        small[d : 2 * d],
        *weight_grads,
        small[2 * d : 3 * d],
        small[3 * d : 4 * d],
        wide[1],
        wide[0],
        small[4 * d : 4 * d + 4].astype(jnp.int32),
        small[4 * d + 4 : 4 * d + 4 + HEADS].astype(jnp.int32),
    )


def solution(mesh):
    token, seq, copy, col = P("dp", "mp", None), P("dp", None), P(), P(None, "mp")
    grad = P("dp", "mp")
    return jax.shard_map(
        functools.partial(per_device, mesh.shape["mp"], mesh.shape["dp"]),
        mesh=mesh,
        in_specs=(token, token, seq, seq, seq, copy, copy, col, col, col, col, copy, copy, col, col),
        out_specs=(token, token, copy, copy, grad, grad, grad, grad, copy, copy, grad, grad, copy, copy),
        check_vma=False,
    )
```
